32 devices in a mesh: fsdp: 32 (over z, y, x, core).
Axes of the slice: x: 2, y: 2, z: 4, core: 2. Of those that a mesh axis runs over, the one named last changes fastest.
Arguments:
- tokens: bfloat16 [8192, 1024], P('fsdp'), may hold values from -6 to 6
- lengths: int32 [4], replicated, may hold values from 1 to 4096, 8192 in all
- seq_order: int32 [4], replicated, may hold values from 0 to 3, each once
- decay_rate: float32 [8], replicated, may hold values from 7.324219e-05 to 0.025
- w_query: bfloat16 [1024, 1024], P('fsdp'), may hold values from -0.1875 to 0.1875
- w_key: bfloat16 [1024, 1024], P('fsdp'), may hold values from -0.1875 to 0.1875
- w_value: bfloat16 [1024, 1024], P('fsdp'), may hold values from -0.1875 to 0.1875
- w_unit: bfloat16 [1024, 1024], P('fsdp'), may hold values from -0.1875 to 0.1875
- w_output: bfloat16 [1024, 1024], P('fsdp'), may hold values from -0.1875 to 0.1875
- norm_gain: bfloat16 [1024], P('fsdp'), may hold values from 0.5 to 1.5
- w_left: bfloat16 [1024, 2816], P('fsdp'), may hold values from -0.1875 to 0.1875
- w_right: bfloat16 [1024, 2816], P('fsdp'), may hold values from -0.1875 to 0.1875
- w_down: bfloat16 [2816, 1024], P('fsdp'), may hold values from -0.109375 to 0.109375
- cotangent: bfloat16 [8192, 1024], P('fsdp'), may hold values from -6 to 6
Outputs:
- block_output: bfloat16 [8192, 1024], P('fsdp')
- grad_tokens: float32 [8192, 1024], P('fsdp')
- grad_query: float32 [1024, 1024], P('fsdp')
- grad_key: float32 [1024, 1024], P('fsdp')
- grad_value: float32 [1024, 1024], P('fsdp')
- grad_unit: float32 [1024, 1024], P('fsdp')
- grad_output: float32 [1024, 1024], P('fsdp')
- grad_gain: float32 [1024], P('fsdp')
- grad_left: float32 [1024, 2816], P('fsdp')
- grad_right: float32 [1024, 2816], P('fsdp')
- grad_down: float32 [2816, 1024], P('fsdp')
The draws below stay inside these ranges and needn't reach their ends.
Inputs may be any that keep to these rules, and one draw needn't show every extreme that they name: lengths of the 4 sequences, summing to 8192; the longest is exactly 4096. Every number below 4 once; the stream holds sequence seq_order[0] first, then seq_order[1], and so on.
All inputs are finite; a program needn't handle non-finite values.
Results may differ from the reference program's by a relative error of at most 0.014.
The reference program's roundings to bfloat16 on the way count: a program that leaves them out, or rounds other values in their place, can miss the bound.
Values may be sent and summed in bfloat16 or wider, within the bound.
A program may use at most 256 MiB of HBM per device.

```python
import math
from functools import partial
import jax
import jax.numpy as jnp
import numpy as np
from jax import lax

D = 1024
H = 8
FF = 2816
SPAN = 256
SEQ_MAX = 4096
TOKENS = 8192
NSEQ = 4


def block_scale(rng, extent, pieces, least, largest):
    loudness = 1.0
    for position, parts in pieces:
        steps = jax.random.uniform(jax.random.fold_in(jax.random.fold_in(rng, 6), position), (parts,), jnp.float32, least / len(pieces), largest / len(pieces))
        loudness = loudness * jnp.repeat(jnp.exp(steps), extent[position] // parts).reshape((-1,) + (1,) * (len(extent) - 1 - position))
    return loudness


def length_profile(amount, total, most, lean):
    loads = [(1 << 20) // math.isqrt(grade ** lean) + 1 for grade in range(2, amount + 1)]
    surplus, counts = total - most - (amount - 1), [1] * (amount - 1)
    while surplus > 0:
        movable = [i for i in range(amount - 1) if counts[i] < most]
        mass, budget = sum([loads[i] for i in movable]), surplus
        for i in movable:
            more = min(most - counts[i], max(1, budget * loads[i] // mass), surplus)
            counts[i] = counts[i] + more
            surplus = surplus - more
    return np.array([most] + counts)


def ragged(stream_key, count, total, reach, lean):
    if count == 2:
        one = jax.random.randint(stream_key, (), max(1, total - reach), min(reach, total - 1) + 1)
        return jnp.stack([one, total - one])
    sizes = jnp.asarray(length_profile(count, total, reach, lean), jnp.int32)
    couples = (count - 1) // 2
    giver, sink = sizes[1:1 + 2 * couples:2], sizes[2:2 + 2 * couples:2]
    margin = jnp.minimum(giver - 1, reach - sink)
    moved = jax.random.randint(jax.random.fold_in(stream_key, 1), (couples,), 0, 1 << 20) % (margin + 1)
    sizes = sizes.at[1:1 + 2 * couples:2].set(giver - moved).at[2:2 + 2 * couples:2].set(sink + moved)
    return sizes[jax.random.permutation(jax.random.fold_in(stream_key, 2), count)]


def scatter_about(stream_key, dims, spread, most, shards=(), held_as=jnp.bfloat16):
    array = spread * jax.random.normal(stream_key, dims, jnp.float32)
    if shards:
        array = array * block_scale(stream_key, dims, shards, -0.22, 0.18)
    return jnp.clip(array, -most, most).astype(held_as)


def setup_inputs(seed: int = 0) -> dict:
    seeds = jax.random.split(jax.random.key(seed), 15)
    return {
        "tokens": scatter_about(seeds[0], (TOKENS, D), 1.0, 6.0, ((0, 32),)),
        "lengths": ragged(seeds[1], NSEQ, TOKENS, SEQ_MAX, 2).astype(jnp.int32),
        "seq_order": jax.random.permutation(seeds[2], NSEQ).astype(jnp.int32),
        "decay_rate": jnp.clip(jnp.exp(jax.random.uniform(seeds[3], (H,), jnp.float32, math.log(7.324219041038305e-05), math.log(0.025))), 7.324219041038305e-05, 0.025),
        "w_query": scatter_about(seeds[4], (D, D), D ** -0.5, 0.1875, ((0, 32),)),
        "w_key": scatter_about(seeds[5], (D, D), D ** -0.5, 0.1875, ((0, 32),)),
        "w_value": scatter_about(seeds[6], (D, D), D ** -0.5, 0.1875, ((0, 32),)),
        "w_unit": scatter_about(seeds[7], (D, D), D ** -0.5, 0.1875, ((0, 32),)),
        "w_output": scatter_about(seeds[8], (D, D), D ** -0.5, 0.1875, ((0, 32),)),
        "norm_gain": jnp.clip(1.0 + 0.1 * jax.random.normal(seeds[9], (D,), jnp.float32), 0.5, 1.5).astype(jnp.bfloat16),
        "w_left": scatter_about(seeds[10], (D, FF), D ** -0.5, 0.1875, ((0, 32),)),
        "w_right": scatter_about(seeds[11], (D, FF), D ** -0.5, 0.1875, ((0, 32),)),
        "w_down": scatter_about(seeds[12], (FF, D), FF ** -0.5, 0.109375, ((0, 32),)),
        "cotangent": scatter_about(seeds[13], (TOKENS, D), 1.0, 6.0, ((0, 32),)),
    }


EPSILON = 1e-05
HIGHEST = lax.Precision.HIGHEST

@jax.custom_vjp
def low(v):
    return lax.optimization_barrier(v.astype(jnp.bfloat16)).astype(jnp.float32)

@jax.custom_vjp
def low_back(v):
    return v

def low_keep(v):
    return (low(v), None)

def low_pass(kept, grad):
    return (grad,)

def back_keep(v):
    return (v, None)

def back_low(kept, grad):
    return (low(grad),)
low.defvjp(low_keep, low_pass)
low_back.defvjp(back_keep, back_low)

def segment_of(places, lengths, seq_order):
    number = lengths.shape[0]
    picked = seq_order[:, None] == jnp.arange(number, dtype=jnp.int32)[None, :]
    packed = lax.optimization_barrier(jnp.sum(jnp.where(picked, lengths[None, :], 0), axis=1, dtype=jnp.int32))
    bounds = jnp.cumsum(packed, dtype=jnp.int32)
    found = lax.optimization_barrier(jnp.sum((bounds[None, :] <= places[:, None]).astype(jnp.int32), axis=1, dtype=jnp.int32))
    return jnp.where(places < 0, -1, found).astype(jnp.int32)

def matmul(left, right):
    return jnp.dot(left, right, precision=HIGHEST, preferred_element_type=jnp.float32)

def span_step(rate, state, item):
    queries, keys, values, segs, prior = item
    size = segs.shape[0]
    steps = jnp.arange(size, dtype=jnp.int32)
    distance = steps[:, None] - steps[None, :]
    same = (segs[:, None] == segs[None, :]) & (distance >= 0)
    within = jnp.where(same[None], jnp.exp(-rate[:, None, None] * jnp.maximum(distance, 0).astype(jnp.float32)[None]), 0.0)
    scores = low_back(jnp.einsum('the,she->hts', queries, keys, precision=HIGHEST))
    mixing = low(scores * within)
    local_out = jnp.einsum('hts,she->the', mixing, values, precision=HIGHEST)
    entry = jnp.where((segs == prior)[:, None], jnp.exp(-rate[None, :] * steps.astype(jnp.float32)[:, None]), 0.0)
    query_held = low(queries * entry[:, :, None])
    state_out = jnp.einsum('the,hef->thf', query_held, low(state), precision=HIGHEST)
    leaving = jnp.where((segs == segs[-1])[:, None], jnp.exp(-rate[None, :] * (size - steps).astype(jnp.float32)[:, None]), 0.0)
    keys_held = low(keys * leaving[:, :, None])
    increment = low_back(jnp.einsum('she,shf->hef', keys_held, values, precision=HIGHEST))
    passing = jnp.where(segs[-1] == prior, jnp.exp(-rate * size), 0.0)
    new_state = passing[:, None, None] * state + increment
    return (new_state, low_back(local_out + state_out))

def layer_block(weights, rate, state, item):
    inputs, segs, prior = item
    w_query, w_key, w_value, w_unit, w_output, gain, w_left, w_right, w_down = weights
    size, width = inputs.shape
    heads = rate.shape[0]
    head_size = width // heads
    count = size // SPAN
    normed = inputs * lax.rsqrt(lax.optimization_barrier(jnp.mean(inputs * inputs, axis=-1, keepdims=True)) + EPSILON)
    hidden = low(normed)
    queries = low(jax.nn.silu(low_back(matmul(hidden, w_query))))
    keys = low(jax.nn.silu(low_back(matmul(hidden, w_key))))
    values = low(low_back(matmul(hidden, w_value)))
    units = low_back(matmul(hidden, w_unit))
    block_shape = (count, SPAN, heads, head_size)
    span_segs = segs.reshape(count, SPAN)
    priors = jnp.concatenate([prior.reshape(1), span_segs[:-1, -1]])
    state, attended = lax.scan(jax.checkpoint(partial(span_step, rate)), state, (queries.reshape(block_shape), keys.reshape(block_shape), values.reshape(block_shape), span_segs, priors))
    attended = attended.reshape(size, heads, head_size)
    unit_norm = (attended * lax.rsqrt(lax.optimization_barrier(jnp.mean(attended * attended, axis=-1, keepdims=True)) + EPSILON)).reshape(size, width)
    mixed_in = low(unit_norm * gain * units)
    middle = inputs + low_back(matmul(mixed_in, w_output))
    second = low(middle * lax.rsqrt(lax.optimization_barrier(jnp.mean(middle * middle, axis=-1, keepdims=True)) + EPSILON))
    product = low(low_back(matmul(second, w_left)) * low_back(matmul(second, w_right)))
    return (state, middle + low_back(matmul(product, w_down)))

def reference(tokens, lengths, seq_order, decay_rate, w_query, w_key, w_value, w_unit, w_output, norm_gain, w_left, w_right, w_down, cotangent):
    total, width = tokens.shape
    heads = decay_rate.shape[0]
    head_size = width // heads
    segs = segment_of(jnp.arange(total, dtype=jnp.int32), lengths, seq_order)
    blocks = total // SEQ_MAX
    block_segs = segs.reshape(blocks, SEQ_MAX)
    priors = jnp.concatenate([jnp.full((1,), -1, jnp.int32), block_segs[:-1, -1]])

    def forward(inputs, *weights):
        stepper = jax.checkpoint(partial(layer_block, weights, decay_rate))
        start_state = jnp.zeros((heads, head_size, head_size), jnp.float32)
        _, outputs = lax.scan(stepper, start_state, (inputs.reshape(blocks, SEQ_MAX, width), block_segs, priors))
        return outputs.reshape(total, width)
    weights = tuple((w.astype(jnp.float32) for w in (w_query, w_key, w_value, w_unit, w_output, norm_gain, w_left, w_right, w_down)))
    result, pullback = jax.vjp(forward, tokens.astype(jnp.float32), *weights)
    grads = pullback(cotangent.astype(jnp.float32))
    return (result.astype(jnp.bfloat16), grads[0], grads[1], grads[2], grads[3], grads[4], grads[5], grads[6], grads[7], grads[8], grads[9])
```

```python
import functools

import jax
import jax.numpy as jnp
from jax import lax
from jax.experimental import pallas as pl
from jax.experimental.pallas import tpu as pltpu
from jax.sharding import PartitionSpec as P

SPAN = 256
AXIS = "fsdp"
TE_DE = "te,de->td"
TD_TE = "td,te->de"
EPSILON = 1e-05
LOGICAL = pl.DeviceIdType.LOGICAL
VMEM_LIMIT = 64000000


class Place:
    def __init__(self):
        me = lax.axis_index(AXIS)
        self.me = me
        self.c = lax.rem(me, 2)
        self.x = lax.rem(me // 2, 2)
        self.y = lax.rem(me // 4, 2)
        self.z = me // 8
        self.inner = (self.z == 1) | (self.z == 2)
        self.even = lax.rem(self.z, 2) == 0
        self.sib = self.z + 1 - 2 * lax.rem(self.z, 2)
        half = self.z // 2
        self.near = 2 - half
        self.far = 3 - 3 * half
        self.cross = 3 - self.z
        self.x1 = 1 - self.x
        self.y1 = 1 - self.y
        self.c1 = 1 - self.c
        self.to = {
            "S": self.dev(self.sib, self.y, self.x, self.c),
            "K": self.dev(self.cross, self.y, self.x, self.c),
            "x": self.dev(self.z, self.y, self.x1, self.c),
            "y": self.dev(self.z, self.y1, self.x, self.c),
            "p": self.dev(self.z, self.y, self.x, self.c1),
        }

    def dev(self, z, y, x, c):
        return ((z * 2 + y) * 2 + x) * 2 + c


def greet(place):
    barrier = pltpu.get_barrier_semaphore()
    for link in ("p", "x", "y", "S"):
        pl.semaphore_signal(barrier, inc=1, device_id=place.to[link], device_id_type=LOGICAL)

    @pl.when(place.inner)
    def _():
        pl.semaphore_signal(barrier, inc=1, device_id=place.to["K"], device_id_type=LOGICAL)

    pl.semaphore_wait(barrier, jnp.where(place.inner, 5, 4))


def arrived(ref, send, recv, place):
    pltpu.make_async_remote_copy(
        src_ref=ref,
        dst_ref=ref,
        send_sem=send,
        recv_sem=recv,
        device_id=place.to["p"],
        device_id_type=LOGICAL,
    ).wait_recv()


class Gather:
    RECV = ("Cs", "Cn", "Cf", "Xo", "Xs", "Xn", "Xf", "Yo", "Ys", "Yn", "Yf", "D0", "D1", "En", "Ef")
    GROUPS = ("C", "X", "Y", "D")
    NRECV = 19
    NSEND = 25

    def __init__(self, place, own, full, send, recv, index):
        self.p, self.own, self.full = place, own, full
        self.send, self.recv, self.index = send, recv, index
        self.sent = []
        p = place
        self.where = {}
        for g, y, x in (("C", p.y, p.x), ("X", p.y, p.x1), ("Y", p.y1, p.x), ("D", p.y1, p.x1)):
            for k, z in (("o", p.z), ("s", p.sib), ("n", p.near), ("f", p.far)):
                self.where[g + k] = (z, y, x, p.c)
        for a, b in (("D0", "Do"), ("D1", "Ds"), ("En", "Dn"), ("Ef", "Df")):
            self.where[a] = self.where[b]

    def slot(self, name):
        return self.full.at[self.where[name]]

    def copy(self, name, link, landing):
        src = self.own if name == "Co" else self.slot(name)
        k = len(self.sent)
        made = pltpu.make_async_remote_copy(
            src_ref=src,
            dst_ref=self.slot(name),
            send_sem=self.send.at[self.index, k],
            recv_sem=self.recv.at[self.index, self.RECV.index(landing)],
            device_id=self.p.to[link],
            device_id_type=LOGICAL,
        )
        return made

    def go(self, name, link, landing, cond=None):
        made = self.copy(name, link, landing)
        self.sent.append((made, cond))
        if cond is None:
            made.start()
        else:
            pl.when(cond)(made.start)

    def wait(self, name):
        arrived(self.slot(name), self.send.at[self.index, 0], self.recv.at[self.index, self.RECV.index(name)], self.p)

    def group(self, g):
        p = self.p
        y = p.y if g in "CX" else p.y1
        x = p.x if g in "CY" else p.x1
        return y, x

    def pair(self, g):
        y, x = self.group(g)
        ref = self.full.at[:, y, x, self.p.c]
        k = len(self.sent)
        made = pltpu.make_async_remote_copy(
            src_ref=ref,
            dst_ref=ref,
            send_sem=self.send.at[self.index, k],
            recv_sem=self.recv.at[self.index, 15 + self.GROUPS.index(g)],
            device_id=self.p.to["p"],
            device_id_type=LOGICAL,
        )
        self.sent.append((made, None))
        made.start()

    def round(self, r):
        p = self.p
        inner, even = p.inner, p.even
        odd = jnp.logical_not(even)
        if r == 0:
            keep = pltpu.make_async_copy(self.own, self.slot("Co"), self.send.at[self.index, self.NSEND])
            self.keep = keep
            keep.start()
            self.go("Co", "S", "Cs")
            self.go("Co", "K", "Cn", inner)
            self.go("Co", "x", "Xo")
            self.go("Co", "y", "Yo")
        if r == 1:
            self.wait("Cs")
            self.go("Cs", "K", "Cf", inner)
            self.go("Cs", "x", "Xs")
            self.go("Cs", "y", "Ys")
            self.wait("Xo")
            self.go("Xo", "y", "D0", even)
            self.wait("Yo")
            self.go("Yo", "x", "D0", odd)
        if r == 2:
            self.wait("Cn")
            self.go("Cn", "S", "Cn", inner)
            self.go("Cn", "x", "Xn")
            self.go("Cn", "y", "Yn")
            self.wait("Xs")
            self.go("Xs", "y", "D1", odd)
            self.wait("Ys")
            self.go("Ys", "x", "D1", even)
            self.wait("D0")
            self.go("D0", "K", "En", inner)
        if r == 3:
            self.wait("Cf")
            self.go("Cf", "S", "Cf", inner)
            self.go("Cf", "x", "Xf")
            self.go("Cf", "y", "Yf")
            self.keep.wait()
            self.pair("C")
            self.wait("D1")
            self.go("D1", "K", "Ef", inner)
            self.wait("Xn")
            self.wait("Yn")
        if r == 4:
            self.wait("En")
            self.go("En", "S", "En", inner)
            self.wait("Xf")
            self.pair("X")
            self.wait("Yf")
            self.pair("Y")
        if r == 5:
            self.wait("Ef")
            self.go("Ef", "S", "Ef", inner)
            self.pair("D")

    def pairs(self):
        for g in self.GROUPS:
            y, x = self.group(g)
            ref = self.full.at[:, y, x, self.p.c1]
            arrived(ref, self.send.at[self.index, 0], self.recv.at[self.index, 15 + self.GROUPS.index(g)], self.p)

    def finish(self):
        for made, cond in self.sent:
            if cond is None:
                made.wait_send()
            else:
                pl.when(cond)(made.wait_send)


def gather_kernel(n, *refs):
    own, full = refs[:n], refs[n : 2 * n]
    send, recv = refs[2 * n :]
    place = Place()
    greet(place)
    made = [Gather(place, own[i], full[i], send, recv, i) for i in range(n)]
    for step in range(n + 5):
        for r in range(6):
            i = step - r
            if 0 <= i < n:
                made[i].round(r)
    for one in made:
        one.pairs()
    for one in made:
        one.finish()


def gather_all(shards):
    n = len(shards)
    return pl.pallas_call(
        functools.partial(gather_kernel, n),
        out_shape=[jax.ShapeDtypeStruct((4, 2, 2, 2) + s.shape, s.dtype) for s in shards],
        in_specs=[pl.BlockSpec(memory_space=pltpu.VMEM)] * n,
        out_specs=[pl.BlockSpec(memory_space=pltpu.HBM)] * n,
        scratch_shapes=[
            pltpu.SemaphoreType.DMA((n, Gather.NSEND + 1)),
            pltpu.SemaphoreType.DMA((n, Gather.NRECV)),
        ],
        compiler_params=pltpu.CompilerParams(
            collective_id=0, has_side_effects=True, vmem_limit_bytes=VMEM_LIMIT
        ),
        name="gather",
    )(*shards)


def add_into(out, parts):
    rows = out.shape[0]
    step = 8 if rows % 16 else 16

    @pl.loop(0, rows // step)
    def _(i):
        at = pl.ds(pl.multiple_of(i * step, step), step)
        total = parts[0][at, :].astype(jnp.float32)
        for part in parts[1:]:
            total = total + part[at, :].astype(jnp.float32)
        out[at, :] = total.astype(out.dtype)


class Scatter:
    NRECV = 20
    NSEND = 22
    SLOTS = ("x0", "x1", "x2", "x3", "Fx", "y0", "y1", "y2", "y3", "Fy", "En", "Ef", "Cn", "Cf", "Co", "De", "Do", "KCs", "KCo")

    def __init__(self, place, part, acc, own, came, out, send, recv, index):
        self.p, self.part, self.acc, self.own, self.came, self.out = place, part, acc, own, came, out
        self.send, self.recv, self.index = send, recv, index
        self.sent = []
        p = place
        half = p.z // 2
        self.ze, self.zo = 2 * half, 2 * half + 1
        self.C = lambda z: (z, p.y, p.x)
        self.X = lambda z: (z, p.y, p.x1)
        self.Y = lambda z: (z, p.y1, p.x)
        self.D = lambda z: (z, p.y1, p.x1)

    def go(self, where, link, slot, cond=None):
        k = len(self.sent)
        at = self.SLOTS.index(slot) if isinstance(slot, str) else slot
        made = pltpu.make_async_remote_copy(
            src_ref=self.acc.at[where],
            dst_ref=self.came.at[at],
            send_sem=self.send.at[self.index, k],
            recv_sem=self.recv.at[self.index, at],
            device_id=self.p.to[link],
            device_id_type=LOGICAL,
        )
        self.sent.append((made, cond))
        if cond is None:
            made.start()
        else:
            pl.when(cond)(made.start)

    def wait(self, slot):
        at = self.SLOTS.index(slot) if isinstance(slot, str) else slot
        arrived(self.came.at[at], self.send.at[self.index, 0], self.recv.at[self.index, at], self.p)
        return self.came.at[at]

    def add(self, where, slots):
        parts = [self.wait(s) for s in slots]
        add_into(self.acc.at[where], [self.acc.at[where]] + parts)

    def round(self, r):
        p = self.p
        inner = p.inner
        outer = jnp.logical_not(inner)
        ze, zo, near, far = self.ze, self.zo, p.near, p.far
        if r == 0:
            made = pltpu.make_async_remote_copy(
                src_ref=self.part.at[:, :, :, p.c1],
                dst_ref=self.acc,
                send_sem=self.send.at[self.index, 0],
                recv_sem=self.recv.at[self.index, 19],
                device_id=p.to["p"],
                device_id_type=LOGICAL,
            )
            self.sent.append((made, None))
            made.start()
            self.load = pltpu.make_async_copy(
                self.part.at[:, :, :, p.c], self.own, self.send.at[self.index, self.NSEND]
            )
            self.load.start()
        if r == 1:
            self.load.wait()
            arrived(self.acc, self.send.at[self.index, 0], self.recv.at[self.index, 19], p)

            @pl.loop(0, 4)
            def _(z):
                for y in range(2):
                    for x in range(2):
                        add_into(self.acc.at[z, y, x], [self.acc.at[z, y, x], self.own.at[z, y, x]])

            self.go(self.D(far), "S", "Ef", outer)
            self.go(self.D(near), "S", "En", outer)
            self.go(self.X(far), "x", far)
            self.go(self.Y(far), "y", far + 5)
            self.go(self.D(ze), "y", "Fy", outer)
            self.go(self.D(zo), "x", "Fx", outer)
            self.go(self.X(near), "x", near)
            self.go(self.Y(near), "y", near + 5)
            self.go(self.X(zo), "x", zo)
            self.go(self.Y(ze), "y", ze + 5)
        if r == 2:

            @pl.when(inner)
            def _():
                self.add(self.D(far), ["Ef"])
                self.add(self.D(near), ["En"])

            self.go(self.D(far), "K", jnp.where(p.z == 1, self.SLOTS.index("Do"), self.SLOTS.index("De")), inner)
            self.go(self.D(near), "K", jnp.where(p.z == 1, self.SLOTS.index("De"), self.SLOTS.index("Do")), inner)
            parts = [self.wait(far), self.wait(far + 5)]
            add_into(self.acc.at[self.C(far)], [self.acc.at[self.C(far)]] + parts)
            self.go(self.C(far), "S", "Cf", outer)
        if r == 3:

            @pl.when(inner)
            def _():
                self.add(self.D(ze), ["De"])
                self.add(self.D(zo), ["Do"])
                self.add(self.C(far), ["Cf"])

            self.go(self.D(ze), "y", "Fy", inner)
            self.go(self.D(zo), "x", "Fx", inner)
            self.go(self.C(far), "K", "KCs", inner)
            parts = [self.wait(near), self.wait(near + 5)]
            add_into(self.acc.at[self.C(near)], [self.acc.at[self.C(near)]] + parts)
            self.go(self.C(near), "S", "Cn", outer)
        if r == 4:
            self.add(self.X(ze), ["Fy"])
            self.add(self.Y(zo), ["Fx"])
            self.go(self.X(ze), "x", ze)
            self.go(self.Y(zo), "y", zo + 5)

            @pl.when(inner)
            def _():
                self.add(self.C(near), ["Cn"])

            self.go(self.C(near), "K", "KCo", inner)
        if r == 5:
            self.add(self.C(p.sib), [p.sib, p.sib + 5])

            @pl.when(inner)
            def _():
                self.add(self.C(p.sib), ["KCs"])

            self.go(self.C(p.sib), "S", "Co")
        if r == 6:
            slots = [p.z, p.z + 5, "Co"]
            parts = [self.acc.at[self.C(p.z)]] + [self.wait(s) for s in slots]
            add_into(self.out, parts)

            @pl.when(inner)
            def _():
                add_into(self.out, [self.out, self.wait("KCo")])

    def finish(self):
        for made, cond in self.sent:
            if cond is None:
                made.wait_send()
            else:
                pl.when(cond)(made.wait_send)


def scatter_kernel(n, *refs):
    part, out = refs[:n], refs[n : 2 * n]
    acc, own, came = refs[2 * n : 3 * n], refs[3 * n : 4 * n], refs[4 * n : 5 * n]
    send, recv = refs[5 * n :]
    place = Place()
    greet(place)
    made = [
        Scatter(place, part[i], acc[i], own[i], came[i], out[i], send, recv, i) for i in range(n)
    ]
    for step in range(n + 6):
        for r in range(7):
            i = step - r
            if 0 <= i < n:
                made[i].round(r)
    for one in made:
        one.finish()


def scatter_all(parts):
    n = len(parts)
    blocks = [(p.shape[4:], p.dtype) for p in parts]
    return pl.pallas_call(
        functools.partial(scatter_kernel, n),
        out_shape=[jax.ShapeDtypeStruct(b, jnp.float32) for b, _ in blocks],
        in_specs=[pl.BlockSpec(memory_space=pltpu.HBM)] * n,
        out_specs=[pl.BlockSpec(memory_space=pltpu.VMEM)] * n,
        scratch_shapes=[pltpu.VMEM((4, 2, 2) + b, t) for b, t in blocks]
        + [pltpu.VMEM((4, 2, 2) + b, t) for b, t in blocks]
        + [pltpu.VMEM((19,) + b, t) for b, t in blocks]
        + [
            pltpu.SemaphoreType.DMA((n, Scatter.NSEND + 1)),
            pltpu.SemaphoreType.DMA((n, Scatter.NRECV)),
        ],
        compiler_params=pltpu.CompilerParams(
            collective_id=3, has_side_effects=True, vmem_limit_bytes=VMEM_LIMIT
        ),
        name="scatter",
    )(*parts)


def states_kernel(reverse, through, value, out, met, planes, ready, send, recv):
    me = lax.axis_index(AXIS)
    z, r = me // 8, lax.rem(me, 8)
    barrier = pltpu.get_barrier_semaphore()
    plane = [z * 8 + lax.bitwise_xor(r, k) for k in range(8)]
    level = [lax.rem(z + k, 4) * 8 + r for k in range(4)]
    for peer in plane[1:] + level[1:]:
        pl.semaphore_signal(barrier, inc=1, device_id=peer, device_id_type=LOGICAL)
    pl.semaphore_wait(barrier, 10)

    def copy(src, dst, k, peer):
        return pltpu.make_async_remote_copy(
            src_ref=src,
            dst_ref=dst,
            send_sem=send.at[k],
            recv_sem=recv.at[k],
            device_id=peer,
            device_id_type=LOGICAL,
        )

    first = [copy(value.at[lax.bitwise_xor(r, k)], met.at[r], k, plane[k]) for k in range(1, 8)]
    for one in first:
        one.start()
    met[r] = value[r]
    for k in range(1, 8):
        copy(value.at[0], met.at[lax.bitwise_xor(r, k)], k, plane[k]).wait_recv()
    order = range(7, -1, -1) if reverse else range(8)
    total = jnp.zeros(met.shape[1:], jnp.float32)
    for i in order:
        total = through[(z * 8 + i) * 8 + r] * total + met[i]
    planes[z] = total
    second = []
    for k in range(1, 4):
        far = z - k if reverse else z + k
        cond = far >= 0 if reverse else far <= 3
        made = copy(planes.at[z], planes.at[z], 7 + k, far * 8 + r)
        second.append((made, cond))
        pl.when(cond)(made.start)
    ready[8] = jnp.zeros(met.shape[1:], jnp.float32)
    for k in range(3, 0, -1):
        far = z + k if reverse else z - k
        cond = far <= 3 if reverse else far >= 0

        @pl.when(cond)
        def _():
            copy(planes.at[z], planes.at[far], 7 + k, plane[0]).wait_recv()
            kept = jnp.float32(1.0)
            for i in range(8):
                kept = kept * through[(far * 8 + i) * 8 + r]
            ready[8] = kept * ready[8] + planes[far]

    total = ready[8]
    for i in order:
        ready[i] = total
        total = through[(z * 8 + i) * 8 + r] * total + met[i]
    third = [
        copy(ready.at[lax.bitwise_xor(r, k)], out.at[r], 10 + k, plane[k]) for k in range(1, 8)
    ]
    for one in third:
        one.start()
    out[r] = ready[r]
    for k in range(1, 8):
        copy(ready.at[0], out.at[lax.bitwise_xor(r, k)], 10 + k, plane[k]).wait_recv()
    for one in first + third:
        one.wait_send()
    for made, cond in second:
        pl.when(cond)(made.wait_send)


def states(value, through, reverse):
    tile = value.shape[1:]
    return pl.pallas_call(
        functools.partial(states_kernel, reverse),
        out_shape=jax.ShapeDtypeStruct(value.shape, jnp.float32),
        in_specs=[
            pl.BlockSpec(memory_space=pltpu.SMEM),
            pl.BlockSpec(memory_space=pltpu.VMEM),
        ],
        out_specs=pl.BlockSpec(memory_space=pltpu.VMEM),
        scratch_shapes=[
            pltpu.VMEM((8,) + tile, jnp.float32),
            pltpu.VMEM((4,) + tile, jnp.float32),
            pltpu.VMEM((9,) + tile, jnp.float32),
            pltpu.SemaphoreType.DMA((18,)),
            pltpu.SemaphoreType.DMA((18,)),
        ],
        compiler_params=pltpu.CompilerParams(
            collective_id=2 if reverse else 1, has_side_effects=True, vmem_limit_bytes=16000000
        ),
        name="states_back" if reverse else "states",
    )(through.reshape(-1), value)

def entering(value, axis, combine, identity, reverse):
    length, here = (lax.axis_size(axis), lax.axis_index(axis))
    everything = jax.tree.map(lambda part: lax.all_gather(part, axis), value)
    start = jax.tree.map(
        lambda part, zero: jnp.broadcast_to(jnp.asarray(zero, part.dtype), part.shape),
        value,
        identity,
    )

    def hop(k, before):
        at = length - 1 - k if reverse else k
        reached = at > here if reverse else at < here
        new = combine(before, jax.tree.map(lambda part: part[at], everything))
        return jax.tree.map(lambda a, b: jnp.where(reached, a, b), new, before)

    return lax.fori_loop(0, length, hop, start)


def segment_of(places, lengths, seq_order):
    number = lengths.shape[0]
    picked = seq_order[:, None] == jnp.arange(number, dtype=jnp.int32)[None, :]
    packed = jnp.sum(jnp.where(picked, lengths[None, :], 0), axis=1, dtype=jnp.int32)
    bounds = jnp.cumsum(packed, dtype=jnp.int32)
    found = jnp.sum((bounds[None, :] <= places[:, None]).astype(jnp.int32), axis=1, dtype=jnp.int32)
    return jnp.where(places < 0, -1, found)


def decay_tables(segments, before, rate, block):
    length = segments.shape[0]
    count = length // block
    spans = segments.reshape(count, block)
    priors = jnp.concatenate([before.reshape(1), spans[:-1, -1]])
    steps = jnp.arange(block, dtype=jnp.int32)
    distance = steps[:, None] - steps[None, :]
    same = (spans[:, :, None] == spans[:, None, :]) & (distance >= 0)[None]
    powers = jnp.exp(-rate[:, None, None] * jnp.maximum(distance, 0).astype(jnp.float32)[None])
    within = jnp.where(same[:, None], powers[None], 0.0)
    entry = jnp.where(
        (spans == priors[:, None])[:, :, None],
        jnp.exp(-rate[None, :] * steps.astype(jnp.float32)[:, None])[None],
        0.0,
    )
    leaving = jnp.where(
        (spans == spans[:, -1:])[:, :, None],
        jnp.exp(-rate[None, :] * (block - steps).astype(jnp.float32)[:, None])[None],
        0.0,
    )
    passing = jnp.where((spans[:, -1] == priors)[:, None], jnp.exp(-rate * block)[None], 0.0)
    offsets = (jnp.arange(count, dtype=jnp.int32) * block).astype(jnp.float32)
    arrival = jnp.where(
        (priors == before)[:, None], jnp.exp(-rate[None, :] * offsets[:, None]), 0.0
    )
    through = jnp.where(segments[-1] == before, jnp.exp(-rate * length), 0.0)
    return (within, entry, leaving, passing, arrival, through)


def chain_states(earlier, later):
    return (earlier[0] * later[0], later[0][:, None, None] * earlier[1] + later[1])


def silu_slope(values):
    sigma = jax.nn.sigmoid(values)
    return sigma * (1.0 + values * (1.0 - sigma))


def row_scale(values):
    return lax.rsqrt(jnp.mean(values * values, axis=-1, keepdims=True) + EPSILON)


def body(
    tokens,
    lengths,
    seq_order,
    decay_rate,
    w_query,
    w_key,
    w_value,
    w_unit,
    w_output,
    norm_gain,
    w_left,
    w_right,
    w_down,
    cotangent,
):
    f32 = jnp.float32
    bf16 = jnp.bfloat16
    length, width = tokens.shape
    heads = decay_rate.shape[0]
    head_size = width // heads
    count = length // SPAN
    first = lax.axis_index(AXIS) * length
    places = first + jnp.arange(length, dtype=jnp.int32)
    segments = segment_of(places, lengths, seq_order)
    before = segment_of(jnp.reshape(first - 1, (1,)), lengths, seq_order)[0]
    within, entry, leaving, passing, arrival, through = decay_tables(
        segments, before, decay_rate, SPAN
    )
    attention_set = (
        lax.all_gather(w_query, AXIS, axis=0, tiled=True),
        lax.all_gather(w_key, AXIS, axis=0, tiled=True),
        lax.all_gather(w_value, AXIS, axis=0, tiled=True),
        lax.all_gather(w_unit, AXIS, axis=0, tiled=True),
        lax.all_gather(w_output, AXIS, axis=0, tiled=True),
        lax.all_gather(norm_gain, AXIS, axis=0, tiled=True),
    )
    feed_set = (
        lax.all_gather(w_left, AXIS, axis=0, tiled=True),
        lax.all_gather(w_right, AXIS, axis=0, tiled=True),
        lax.all_gather(w_down, AXIS, axis=0, tiled=True),
    )
    full_query, full_key, full_value, full_unit, full_output, full_gain = attention_set
    full_left, full_right, full_down = feed_set
    inputs = tokens.astype(f32)
    first_scale = row_scale(inputs)
    normed = inputs * first_scale
    hidden = normed.astype(bf16)
    query_pre = jnp.dot(hidden, full_query, preferred_element_type=f32)
    key_pre = jnp.dot(hidden, full_key, preferred_element_type=f32)
    value_pre = jnp.dot(hidden, full_value, preferred_element_type=f32)
    unit_pre = jnp.dot(hidden, full_unit, preferred_element_type=f32)
    block_shape = (count, SPAN, heads, head_size)
    query_blocks = jax.nn.silu(query_pre).astype(bf16).reshape(block_shape)
    key_blocks = jax.nn.silu(key_pre).astype(bf16).reshape(block_shape)
    value_blocks = value_pre.astype(bf16).reshape(block_shape)
    scores = jnp.einsum("nthe,nshe->nhts", query_blocks, key_blocks, preferred_element_type=f32)
    mixing = (scores * within).astype(bf16)
    local_out = jnp.einsum("nhts,nshe->nthe", mixing, value_blocks, preferred_element_type=f32)
    keys_held = (key_blocks * leaving[..., None]).astype(bf16)
    increments = jnp.einsum("nshe,nshf->nhef", keys_held, value_blocks, preferred_element_type=f32)
    local_states = [jnp.zeros((heads, head_size, head_size), f32)]
    local_states.append(passing[0][:, None, None] * local_states[-1] + increments[0])
    end_state = local_states[count]
    start_pair = (jnp.ones_like(through), jnp.zeros_like(end_state))
    arriving = entering((through, end_state), AXIS, chain_states, start_pair, False)[1]
    states = jnp.stack(local_states[:count]) + arrival[:, :, None, None] * arriving[None]
    state_low = states.astype(bf16)
    query_held = (query_blocks * entry[..., None]).astype(bf16)
    attended = local_out + jnp.einsum(
        "nthe,nhef->nthf", query_held, state_low, preferred_element_type=f32
    )
    attended_heads = attended.reshape(length, heads, head_size)
    head_scale = row_scale(attended_heads)
    unit_norm = (attended_heads * head_scale).reshape(length, width)
    gain = full_gain.astype(f32)
    gated = unit_norm * gain
    mixed_in = (gated * unit_pre).astype(bf16)
    middle = inputs + jnp.dot(mixed_in, full_output, preferred_element_type=f32)
    second_scale = row_scale(middle)
    second_unit = middle * second_scale
    second = second_unit.astype(bf16)
    left_pre = jnp.dot(second, full_left, preferred_element_type=f32)
    right_pre = jnp.dot(second, full_right, preferred_element_type=f32)
    product = (left_pre * right_pre).astype(bf16)
    result = (middle + jnp.dot(product, full_down, preferred_element_type=f32)).astype(bf16)
    back_feed = (
        lax.all_gather(w_left, AXIS, axis=0, tiled=True),
        lax.all_gather(w_right, AXIS, axis=0, tiled=True),
        lax.all_gather(w_down, AXIS, axis=0, tiled=True),
    )
    back_left, back_right, back_down = back_feed
    grad_product = jnp.einsum("td,fd->tf", cotangent, back_down, preferred_element_type=f32)
    grad_left_pre = (grad_product * right_pre).astype(bf16)
    grad_right_pre = (grad_product * left_pre).astype(bf16)
    grad_w_down = jnp.einsum("tf,td->fd", product, cotangent, preferred_element_type=f32)
    grad_w_left = jnp.einsum("td,tf->df", second, grad_left_pre, preferred_element_type=f32)
    grad_w_right = jnp.einsum("td,tf->df", second, grad_right_pre, preferred_element_type=f32)
    feed_grads = (
        lax.psum_scatter(grad_w_left, AXIS, scatter_dimension=0, tiled=True),
        lax.psum_scatter(grad_w_right, AXIS, scatter_dimension=0, tiled=True),
        lax.psum_scatter(grad_w_down, AXIS, scatter_dimension=0, tiled=True),
    )
    grad_second = jnp.einsum(
        "tf,df->td", grad_left_pre, back_left, preferred_element_type=f32
    ) + jnp.einsum("tf,df->td", grad_right_pre, back_right, preferred_element_type=f32)
    grad_middle = cotangent.astype(f32) + second_scale * (
        grad_second - second_unit * jnp.mean(grad_second * second_unit, axis=-1, keepdims=True)
    )
    back_attention = (
        lax.all_gather(w_query, AXIS, axis=0, tiled=True),
        lax.all_gather(w_key, AXIS, axis=0, tiled=True),
        lax.all_gather(w_value, AXIS, axis=0, tiled=True),
        lax.all_gather(w_unit, AXIS, axis=0, tiled=True),
        lax.all_gather(w_output, AXIS, axis=0, tiled=True),
        lax.all_gather(norm_gain, AXIS, axis=0, tiled=True),
    )
    back_query, back_key, back_value, back_unit, back_output, back_gain = back_attention
    grad_branch = grad_middle.astype(bf16)
    grad_w_output = jnp.einsum(TD_TE, mixed_in, grad_branch, preferred_element_type=f32)
    grad_mixed = jnp.einsum(TE_DE, grad_branch, back_output, preferred_element_type=f32)
    grad_gated = grad_mixed * unit_pre
    grad_unit_pre = (grad_mixed * gated).astype(bf16)
    grad_gain = jnp.sum(grad_gated * unit_norm, axis=0)
    grad_norm_heads = (grad_gated * back_gain.astype(f32)).reshape(length, heads, head_size)
    norm_heads = unit_norm.reshape(length, heads, head_size)
    grad_att = head_scale * (
        grad_norm_heads
        - norm_heads * jnp.mean(grad_norm_heads * norm_heads, axis=-1, keepdims=True)
    )
    grad_att_blocks = grad_att.astype(bf16).reshape(block_shape)
    grad_mixing = jnp.einsum(
        "nthf,nshf->nhts", grad_att_blocks, value_blocks, preferred_element_type=f32
    )
    grad_scores = (grad_mixing * within).astype(bf16)
    grad_query_blocks = (
        jnp.einsum("nhts,nshe->nthe", grad_scores, key_blocks, preferred_element_type=f32)
        + jnp.einsum("nthf,nhef->nthe", grad_att_blocks, state_low, preferred_element_type=f32)
        * entry[..., None]
    )
    grad_key_blocks = jnp.einsum(
        "nhts,nthe->nshe", grad_scores, query_blocks, preferred_element_type=f32
    )
    grad_value_blocks = jnp.einsum(
        "nhts,nthf->nshf", mixing, grad_att_blocks, preferred_element_type=f32
    )
    direct = jnp.einsum("nthe,nthf->nhef", query_held, grad_att_blocks, preferred_element_type=f32)
    leaving_sum = jnp.sum(arrival[:, :, None, None] * direct, axis=0)
    later = entering((through, leaving_sum), AXIS, chain_states, start_pair, True)[1]
    next_grads = [later]
    grad_increment = jnp.stack(next_grads[::-1]).astype(bf16)
    grad_keys_held = jnp.einsum(
        "nhef,nshf->nshe", grad_increment, value_blocks, preferred_element_type=f32
    )
    grad_key_blocks = grad_key_blocks + grad_keys_held * leaving[..., None]
    grad_value_blocks = grad_value_blocks + jnp.einsum(
        "nshe,nhef->nshf", keys_held, grad_increment, preferred_element_type=f32
    )
    grad_query_pre = (grad_query_blocks.reshape(length, width) * silu_slope(query_pre)).astype(bf16)
    grad_key_pre = (grad_key_blocks.reshape(length, width) * silu_slope(key_pre)).astype(bf16)
    grad_value_pre = grad_value_blocks.reshape(length, width).astype(bf16)
    grad_w_query = jnp.einsum(TD_TE, hidden, grad_query_pre, preferred_element_type=f32)
    grad_w_key = jnp.einsum(TD_TE, hidden, grad_key_pre, preferred_element_type=f32)
    grad_w_value = jnp.einsum(TD_TE, hidden, grad_value_pre, preferred_element_type=f32)
    grad_w_unit = jnp.einsum(TD_TE, hidden, grad_unit_pre, preferred_element_type=f32)
    attention_grads = (
        lax.psum_scatter(grad_w_query, AXIS, scatter_dimension=0, tiled=True),
        lax.psum_scatter(grad_w_key, AXIS, scatter_dimension=0, tiled=True),
        lax.psum_scatter(grad_w_value, AXIS, scatter_dimension=0, tiled=True),
        lax.psum_scatter(grad_w_unit, AXIS, scatter_dimension=0, tiled=True),
        lax.psum_scatter(grad_w_output, AXIS, scatter_dimension=0, tiled=True),
        lax.psum_scatter(grad_gain, AXIS, scatter_dimension=0, tiled=True),
    )
    grad_hidden = (
        jnp.einsum(TE_DE, grad_query_pre, back_query, preferred_element_type=f32)
        + jnp.einsum(TE_DE, grad_key_pre, back_key, preferred_element_type=f32)
        + jnp.einsum(TE_DE, grad_value_pre, back_value, preferred_element_type=f32)
        + jnp.einsum(TE_DE, grad_unit_pre, back_unit, preferred_element_type=f32)
    )
    grad_inputs = grad_middle + first_scale * (
        grad_hidden - normed * jnp.mean(grad_hidden * normed, axis=-1, keepdims=True)
    )
    return (
        result,
        grad_inputs,
        attention_grads[0],
        attention_grads[1],
        attention_grads[2],
        attention_grads[3],
        attention_grads[4],
        attention_grads[5],
        feed_grads[0],
        feed_grads[1],
        feed_grads[2],
    )


def body_kernels(
    tokens,
    lengths,
    seq_order,
    decay_rate,
    w_query,
    w_key,
    w_value,
    w_unit,
    w_output,
    norm_gain,
    w_left,
    w_right,
    w_down,
    cotangent,
):
    f32 = jnp.float32
    bf16 = jnp.bfloat16
    length, width = tokens.shape
    heads = decay_rate.shape[0]
    head_size = width // heads
    count = length // SPAN
    first = lax.axis_index(AXIS) * length
    places = first + jnp.arange(length, dtype=jnp.int32)
    segments = segment_of(places, lengths, seq_order)
    before = segment_of(jnp.reshape(first - 1, (1,)), lengths, seq_order)[0]
    within, entry, leaving, passing, arrival, through = decay_tables(
        segments, before, decay_rate, SPAN
    )
    devices = lax.axis_size(AXIS)
    me = lax.axis_index(AXIS)
    mine = jnp.arange(devices, dtype=jnp.int32)[:, None] == me
    gain_tile = jnp.where(mine, norm_gain.astype(f32)[None, :], 0.0).reshape(heads, head_size)
    full = gather_all(
        [w_query, w_key, w_value, w_unit, gain_tile, w_output]
        + [w_left[:, : w_left.shape[1] // 2], w_left[:, w_left.shape[1] // 2 :]]
        + [w_right[:, : w_right.shape[1] // 2], w_right[:, w_right.shape[1] // 2 :]]
        + [w_down]
    )
    full_query, full_key, full_value, full_unit = [f.reshape(-1, width) for f in full[:4]]
    full_gain = jnp.sum(full[4].reshape(devices, heads, head_size), axis=0).reshape(width)
    full_output = full[5].reshape(-1, width)
    full_left = jnp.concatenate([f.reshape(width, -1) for f in full[6:8]], axis=1)
    full_right = jnp.concatenate([f.reshape(width, -1) for f in full[8:10]], axis=1)
    full_down = full[10].reshape(-1, width)
    ends = segment_of((jnp.arange(devices + 1, dtype=jnp.int32)) * length - 1, lengths, seq_order)
    through_all = jnp.where(
        (ends[1:] == ends[:-1])[:, None], jnp.exp(-decay_rate * length)[None, :], 0.0
    )
    inputs = tokens.astype(f32)
    first_scale = row_scale(inputs)
    normed = inputs * first_scale
    hidden = normed.astype(bf16)
    query_pre = jnp.dot(hidden, full_query, preferred_element_type=f32)
    key_pre = jnp.dot(hidden, full_key, preferred_element_type=f32)
    value_pre = jnp.dot(hidden, full_value, preferred_element_type=f32)
    unit_pre = jnp.dot(hidden, full_unit, preferred_element_type=f32)
    block_shape = (count, SPAN, heads, head_size)
    query_blocks = jax.nn.silu(query_pre).astype(bf16).reshape(block_shape)
    key_blocks = jax.nn.silu(key_pre).astype(bf16).reshape(block_shape)
    value_blocks = value_pre.astype(bf16).reshape(block_shape)
    scores = jnp.einsum("nthe,nshe->nhts", query_blocks, key_blocks, preferred_element_type=f32)
    mixing = (scores * within).astype(bf16)
    local_out = jnp.einsum("nhts,nshe->nthe", mixing, value_blocks, preferred_element_type=f32)
    keys_held = (key_blocks * leaving[..., None]).astype(bf16)
    increments = jnp.einsum("nshe,nshf->nhef", keys_held, value_blocks, preferred_element_type=f32)
    local_states = [jnp.zeros((heads, head_size, head_size), f32)]
    local_states.append(passing[0][:, None, None] * local_states[-1] + increments[0])
    end_state = local_states[count]
    arriving = states(end_state, through_all, False)
    held = jnp.stack(local_states[:count]) + arrival[:, :, None, None] * arriving[None]
    state_low = held.astype(bf16)
    query_held = (query_blocks * entry[..., None]).astype(bf16)
    attended = local_out + jnp.einsum(
        "nthe,nhef->nthf", query_held, state_low, preferred_element_type=f32
    )
    attended_heads = attended.reshape(length, heads, head_size)
    head_scale = row_scale(attended_heads)
    unit_norm = (attended_heads * head_scale).reshape(length, width)
    gain = full_gain.astype(f32)
    gated = unit_norm * gain
    mixed_in = (gated * unit_pre).astype(bf16)
    middle = inputs + jnp.dot(mixed_in, full_output, preferred_element_type=f32)
    second_scale = row_scale(middle)
    second_unit = middle * second_scale
    second = second_unit.astype(bf16)
    left_pre = jnp.dot(second, full_left, preferred_element_type=f32)
    right_pre = jnp.dot(second, full_right, preferred_element_type=f32)
    product = (left_pre * right_pre).astype(bf16)
    result = (middle + jnp.dot(product, full_down, preferred_element_type=f32)).astype(bf16)
    back_left, back_right, back_down = full_left, full_right, full_down
    grad_product = jnp.einsum("td,fd->tf", cotangent, back_down, preferred_element_type=f32)
    grad_left_pre = (grad_product * right_pre).astype(bf16)
    grad_right_pre = (grad_product * left_pre).astype(bf16)
    grad_w_down = jnp.einsum("tf,td->fd", product, cotangent, preferred_element_type=f32)
    grad_w_left = jnp.einsum("td,tf->df", second, grad_left_pre, preferred_element_type=f32)
    grad_w_right = jnp.einsum("td,tf->df", second, grad_right_pre, preferred_element_type=f32)
    grad_second = jnp.einsum(
        "tf,df->td", grad_left_pre, back_left, preferred_element_type=f32
    ) + jnp.einsum("tf,df->td", grad_right_pre, back_right, preferred_element_type=f32)
    grad_middle = cotangent.astype(f32) + second_scale * (
        grad_second - second_unit * jnp.mean(grad_second * second_unit, axis=-1, keepdims=True)
    )
    back_query, back_key, back_value, back_unit = full_query, full_key, full_value, full_unit
    back_output, back_gain = full_output, full_gain
    grad_branch = grad_middle.astype(bf16)
    grad_w_output = jnp.einsum(TD_TE, mixed_in, grad_branch, preferred_element_type=f32)
    grad_mixed = jnp.einsum(TE_DE, grad_branch, back_output, preferred_element_type=f32)
    grad_gated = grad_mixed * unit_pre
    grad_unit_pre = (grad_mixed * gated).astype(bf16)
    grad_gain = jnp.sum(grad_gated * unit_norm, axis=0)
    grad_norm_heads = (grad_gated * back_gain.astype(f32)).reshape(length, heads, head_size)
    norm_heads = unit_norm.reshape(length, heads, head_size)
    grad_att = head_scale * (
        grad_norm_heads
        - norm_heads * jnp.mean(grad_norm_heads * norm_heads, axis=-1, keepdims=True)
    )
    grad_att_blocks = grad_att.astype(bf16).reshape(block_shape)
    grad_mixing = jnp.einsum(
        "nthf,nshf->nhts", grad_att_blocks, value_blocks, preferred_element_type=f32
    )
    grad_scores = (grad_mixing * within).astype(bf16)
    grad_query_blocks = (
        jnp.einsum("nhts,nshe->nthe", grad_scores, key_blocks, preferred_element_type=f32)
        + jnp.einsum("nthf,nhef->nthe", grad_att_blocks, state_low, preferred_element_type=f32)
        * entry[..., None]
    )
    grad_key_blocks = jnp.einsum(
        "nhts,nthe->nshe", grad_scores, query_blocks, preferred_element_type=f32
    )
    grad_value_blocks = jnp.einsum(
        "nhts,nthf->nshf", mixing, grad_att_blocks, preferred_element_type=f32
    )
    direct = jnp.einsum("nthe,nthf->nhef", query_held, grad_att_blocks, preferred_element_type=f32)
    leaving_sum = jnp.sum(arrival[:, :, None, None] * direct, axis=0)
    later = states(leaving_sum, through_all, True)
    next_grads = [later]
    grad_increment = jnp.stack(next_grads[::-1]).astype(bf16)
    grad_keys_held = jnp.einsum(
        "nhef,nshf->nshe", grad_increment, value_blocks, preferred_element_type=f32
    )
    grad_key_blocks = grad_key_blocks + grad_keys_held * leaving[..., None]
    grad_value_blocks = grad_value_blocks + jnp.einsum(
        "nshe,nhef->nshf", keys_held, grad_increment, preferred_element_type=f32
    )
    grad_query_pre = (grad_query_blocks.reshape(length, width) * silu_slope(query_pre)).astype(bf16)
    grad_key_pre = (grad_key_blocks.reshape(length, width) * silu_slope(key_pre)).astype(bf16)
    grad_value_pre = grad_value_blocks.reshape(length, width).astype(bf16)
    grad_w_query = jnp.einsum(TD_TE, hidden, grad_query_pre, preferred_element_type=f32)
    grad_w_key = jnp.einsum(TD_TE, hidden, grad_key_pre, preferred_element_type=f32)
    grad_w_value = jnp.einsum(TD_TE, hidden, grad_value_pre, preferred_element_type=f32)
    grad_w_unit = jnp.einsum(TD_TE, hidden, grad_unit_pre, preferred_element_type=f32)
    def blocks(grad):
        return grad.astype(bf16).reshape((4, 2, 2, 2, -1) + grad.shape[1:])

    gain_rows = grad_gain.reshape(devices, 1, width // devices)
    gain_rows = jnp.pad(gain_rows, ((0, 0), (0, 7), (0, 128 - width // devices)))
    split = w_left.shape[1] // 2
    grads = scatter_all(
        [blocks(grad_w_down)]
        + [blocks(grad_w_left[:, :split]), blocks(grad_w_left[:, split:])]
        + [blocks(grad_w_right[:, :split]), blocks(grad_w_right[:, split:])]
        + [blocks(grad_w_output), gain_rows.reshape(4, 2, 2, 2, 8, 128)]
        + [blocks(grad_w_unit), blocks(grad_w_value), blocks(grad_w_key), blocks(grad_w_query)]
    )
    feed_grads = (
        jnp.concatenate(grads[1:3], axis=1),
        jnp.concatenate(grads[3:5], axis=1),
        grads[0],
    )
    attention_grads = (
        grads[10],
        grads[9],
        grads[8],
        grads[7],
        grads[5],
        grads[6][0, : width // devices],
    )
    grad_hidden = (
        jnp.einsum(TE_DE, grad_query_pre, back_query, preferred_element_type=f32)
        + jnp.einsum(TE_DE, grad_key_pre, back_key, preferred_element_type=f32)
        + jnp.einsum(TE_DE, grad_value_pre, back_value, preferred_element_type=f32)
        + jnp.einsum(TE_DE, grad_unit_pre, back_unit, preferred_element_type=f32)
    )
    grad_inputs = grad_middle + first_scale * (
        grad_hidden - normed * jnp.mean(grad_hidden * normed, axis=-1, keepdims=True)
    )
    return (
        result,
        grad_inputs,
        attention_grads[0],
        attention_grads[1],
        attention_grads[2],
        attention_grads[3],
        attention_grads[4],
        attention_grads[5],
        feed_grads[0],
        feed_grads[1],
        feed_grads[2],
    )


def solution(mesh):
    placed = (
        P(AXIS, None),
        P(),
        P(),
        P(),
        P(AXIS, None),
        P(AXIS, None),
        P(AXIS, None),
        P(AXIS, None),
        P(AXIS, None),
        P(AXIS),
        P(AXIS, None),
        P(AXIS, None),
        P(AXIS, None),
        P(AXIS, None),
    )
    return jax.shard_map(
        body_kernels if mesh.size == 32 else body,
        mesh=mesh,
        in_specs=placed,
        out_specs=(
            P(AXIS, None),
            P(AXIS, None),
            P(AXIS, None),
            P(AXIS, None),
            P(AXIS, None),
            P(AXIS, None),
            P(AXIS, None),
            P(AXIS),
            P(AXIS, None),
            P(AXIS, None),
            P(AXIS, None),
        ),
        check_vma=False,
    )
```

```python
import functools

import jax
import jax.numpy as jnp
from jax import lax
from jax.experimental import pallas as pl
from jax.experimental.pallas import tpu as pltpu
from jax.sharding import PartitionSpec as P

SPAN = 256
AXIS = "fsdp"
TE_DE = "te,de->td"
TD_TE = "td,te->de"
EPSILON = 1e-05
LOGICAL = pl.DeviceIdType.LOGICAL
VMEM_LIMIT = 64000000


class Place:
    def __init__(self):
        me = lax.axis_index(AXIS)
        self.me = me
        self.c = lax.rem(me, 2)
        self.x = lax.rem(me // 2, 2)
        self.y = lax.rem(me // 4, 2)
        self.z = me // 8
        self.inner = (self.z == 1) | (self.z == 2)
        self.even = lax.rem(self.z, 2) == 0
        self.sib = self.z + 1 - 2 * lax.rem(self.z, 2)
        half = self.z // 2
        self.near = 2 - half
        self.far = 3 - 3 * half
        self.cross = 3 - self.z
        self.x1 = 1 - self.x
        self.y1 = 1 - self.y
        self.c1 = 1 - self.c
        self.to = {
            "S": self.dev(self.sib, self.y, self.x, self.c),
            "K": self.dev(self.cross, self.y, self.x, self.c),
            "x": self.dev(self.z, self.y, self.x1, self.c),
            "y": self.dev(self.z, self.y1, self.x, self.c),
            "p": self.dev(self.z, self.y, self.x, self.c1),
        }

    def dev(self, z, y, x, c):
        return ((z * 2 + y) * 2 + x) * 2 + c


def greet(place):
    barrier = pltpu.get_barrier_semaphore()
    for link in ("p", "x", "y", "S"):
        pl.semaphore_signal(barrier, inc=1, device_id=place.to[link], device_id_type=LOGICAL)

    @pl.when(place.inner)
    def _():
        pl.semaphore_signal(barrier, inc=1, device_id=place.to["K"], device_id_type=LOGICAL)

    pl.semaphore_wait(barrier, jnp.where(place.inner, 5, 4))


def arrived(ref, send, recv, place):
    pltpu.make_async_remote_copy(
        src_ref=ref,
        dst_ref=ref,
        send_sem=send,
        recv_sem=recv,
        device_id=place.to["p"],
        device_id_type=LOGICAL,
    ).wait_recv()


class Gather:
    RECV = ("Cs", "Cn", "Cf", "Xo", "Xs", "Xn", "Xf", "Yo", "Ys", "Yn", "Yf", "D0", "D1", "En", "Ef")
    GROUPS = ("C", "X", "Y", "D")
    NRECV = 19
    NSEND = 25

    def __init__(self, place, own, full, send, recv, index):
        self.p, self.own, self.full = place, own, full
        self.send, self.recv, self.index = send, recv, index
        self.sent = []
        p = place
        self.where = {}
        for g, y, x in (("C", p.y, p.x), ("X", p.y, p.x1), ("Y", p.y1, p.x), ("D", p.y1, p.x1)):
            for k, z in (("o", p.z), ("s", p.sib), ("n", p.near), ("f", p.far)):
                self.where[g + k] = (z, y, x, p.c)
        for a, b in (("D0", "Do"), ("D1", "Ds"), ("En", "Dn"), ("Ef", "Df")):
            self.where[a] = self.where[b]

    def slot(self, name):
        return self.full.at[self.where[name]]

    def copy(self, name, link, landing):
        src = self.own if name == "Co" else self.slot(name)
        k = len(self.sent)
        made = pltpu.make_async_remote_copy(
            src_ref=src,
            dst_ref=self.slot(name),
            send_sem=self.send.at[self.index, k],
            recv_sem=self.recv.at[self.index, self.RECV.index(landing)],
            device_id=self.p.to[link],
            device_id_type=LOGICAL,
        )
        return made

    def go(self, name, link, landing, cond=None):
        made = self.copy(name, link, landing)
        self.sent.append((made, cond))
        if cond is None:
            made.start()
        else:
            pl.when(cond)(made.start)

    def wait(self, name):
        arrived(self.slot(name), self.send.at[self.index, 0], self.recv.at[self.index, self.RECV.index(name)], self.p)

    def group(self, g):
        p = self.p
        y = p.y if g in "CX" else p.y1
        x = p.x if g in "CY" else p.x1
        return y, x

    def pair(self, g):
        y, x = self.group(g)
        ref = self.full.at[:, y, x, self.p.c]
        k = len(self.sent)
        made = pltpu.make_async_remote_copy(
            src_ref=ref,
            dst_ref=ref,
            send_sem=self.send.at[self.index, k],
            recv_sem=self.recv.at[self.index, 15 + self.GROUPS.index(g)],
            device_id=self.p.to["p"],
            device_id_type=LOGICAL,
        )
        self.sent.append((made, None))
        made.start()

    def round(self, r):
        p = self.p
        inner, even = p.inner, p.even
        odd = jnp.logical_not(even)
        if r == 0:
            keep = pltpu.make_async_copy(self.own, self.slot("Co"), self.send.at[self.index, self.NSEND])
            self.keep = keep
            keep.start()
            self.go("Co", "S", "Cs")
            self.go("Co", "K", "Cn", inner)
            self.go("Co", "x", "Xo")
            self.go("Co", "y", "Yo")
        if r == 1:
            self.wait("Cs")
            self.go("Cs", "K", "Cf", inner)
            self.go("Cs", "x", "Xs")
            self.go("Cs", "y", "Ys")
            self.wait("Xo")
            self.go("Xo", "y", "D0", even)
            self.wait("Yo")
            self.go("Yo", "x", "D0", odd)
        if r == 2:
            self.wait("Cn")
            self.go("Cn", "S", "Cn", inner)
            self.go("Cn", "x", "Xn")
            self.go("Cn", "y", "Yn")
            self.wait("Xs")
            self.go("Xs", "y", "D1", odd)
            self.wait("Ys")
            self.go("Ys", "x", "D1", even)
            self.wait("D0")
            self.go("D0", "K", "En", inner)
        if r == 3:
            self.wait("Cf")
            self.go("Cf", "S", "Cf", inner)
            self.go("Cf", "x", "Xf")
            self.go("Cf", "y", "Yf")
            self.keep.wait()
            self.pair("C")
            self.wait("D1")
            self.go("D1", "K", "Ef", inner)
            self.wait("Xn")
            self.wait("Yn")
        if r == 4:
            self.wait("En")
            self.go("En", "S", "En", inner)
            self.wait("Xf")
            self.pair("X")
            self.wait("Yf")
            self.pair("Y")
        if r == 5:
            self.wait("Ef")
            self.go("Ef", "S", "Ef", inner)
            self.pair("D")

    def pairs(self):
        for g in self.GROUPS:
            y, x = self.group(g)
            ref = self.full.at[:, y, x, self.p.c1]
            arrived(ref, self.send.at[self.index, 0], self.recv.at[self.index, 15 + self.GROUPS.index(g)], self.p)

    def finish(self):
        for made, cond in self.sent:
            if cond is None:
                made.wait_send()
            else:
                pl.when(cond)(made.wait_send)


def add_into(out, parts):
    rows = out.shape[0]
    step = 8 if rows % 16 else 16

    @pl.loop(0, rows // step)
    def _(i):
        at = pl.ds(pl.multiple_of(i * step, step), step)
        total = parts[0][at, :].astype(jnp.float32)
        for part in parts[1:]:
            total = total + part[at, :].astype(jnp.float32)
        out[at, :] = total.astype(out.dtype)


class Scatter:
    NRECV = 20
    NSEND = 22
    SLOTS = ("x0", "x1", "x2", "x3", "Fx", "y0", "y1", "y2", "y3", "Fy", "En", "Ef", "Cn", "Cf", "Co", "De", "Do", "KCs", "KCo")

    def __init__(self, place, part, acc, own, came, out, send, recv, index):
        self.p, self.part, self.acc, self.own, self.came, self.out = place, part, acc, own, came, out
        self.send, self.recv, self.index = send, recv, index
        self.sent = []
        p = place
        half = p.z // 2
        self.ze, self.zo = 2 * half, 2 * half + 1
        self.C = lambda z: (z, p.y, p.x)
        self.X = lambda z: (z, p.y, p.x1)
        self.Y = lambda z: (z, p.y1, p.x)
        self.D = lambda z: (z, p.y1, p.x1)

    def go(self, where, link, slot, cond=None):
        k = len(self.sent)
        at = self.SLOTS.index(slot) if isinstance(slot, str) else slot
        made = pltpu.make_async_remote_copy(
            src_ref=self.acc.at[where],
            dst_ref=self.came.at[at],
            send_sem=self.send.at[self.index, k],
            recv_sem=self.recv.at[self.index, at],
            device_id=self.p.to[link],
            device_id_type=LOGICAL,
        )
        self.sent.append((made, cond))
        if cond is None:
            made.start()
        else:
            pl.when(cond)(made.start)

    def wait(self, slot):
        at = self.SLOTS.index(slot) if isinstance(slot, str) else slot
        arrived(self.came.at[at], self.send.at[self.index, 0], self.recv.at[self.index, at], self.p)
        return self.came.at[at]

    def add(self, where, slots):
        parts = [self.wait(s) for s in slots]
        add_into(self.acc.at[where], [self.acc.at[where]] + parts)

    def round(self, r):
        p = self.p
        inner = p.inner
        outer = jnp.logical_not(inner)
        ze, zo, near, far = self.ze, self.zo, p.near, p.far
        if r == 0:
            made = pltpu.make_async_remote_copy(
                src_ref=self.part.at[:, :, :, p.c1],
                dst_ref=self.acc,
                send_sem=self.send.at[self.index, 0],
                recv_sem=self.recv.at[self.index, 19],
                device_id=p.to["p"],
                device_id_type=LOGICAL,
            )
            self.sent.append((made, None))
            made.start()
            self.load = pltpu.make_async_copy(
                self.part.at[:, :, :, p.c], self.own, self.send.at[self.index, self.NSEND]
            )
            self.load.start()
        if r == 1:
            self.load.wait()
            arrived(self.acc, self.send.at[self.index, 0], self.recv.at[self.index, 19], p)

            @pl.loop(0, 4)
            def _(z):
                for y in range(2):
                    for x in range(2):
                        add_into(self.acc.at[z, y, x], [self.acc.at[z, y, x], self.own.at[z, y, x]])

            self.go(self.D(far), "S", "Ef", outer)
            self.go(self.D(near), "S", "En", outer)
            self.go(self.X(far), "x", far)
            self.go(self.Y(far), "y", far + 5)
            self.go(self.D(ze), "y", "Fy", outer)
            self.go(self.D(zo), "x", "Fx", outer)
            self.go(self.X(near), "x", near)
            self.go(self.Y(near), "y", near + 5)
            self.go(self.X(zo), "x", zo)
            self.go(self.Y(ze), "y", ze + 5)
        if r == 2:

            @pl.when(inner)
            def _():
                self.add(self.D(far), ["Ef"])
                self.add(self.D(near), ["En"])

            self.go(self.D(far), "K", jnp.where(p.z == 1, self.SLOTS.index("Do"), self.SLOTS.index("De")), inner)
            self.go(self.D(near), "K", jnp.where(p.z == 1, self.SLOTS.index("De"), self.SLOTS.index("Do")), inner)
            parts = [self.wait(far), self.wait(far + 5)]
            add_into(self.acc.at[self.C(far)], [self.acc.at[self.C(far)]] + parts)
            self.go(self.C(far), "S", "Cf", outer)
        if r == 3:

            @pl.when(inner)
            def _():
                self.add(self.D(ze), ["De"])
                self.add(self.D(zo), ["Do"])
                self.add(self.C(far), ["Cf"])

            self.go(self.D(ze), "y", "Fy", inner)
            self.go(self.D(zo), "x", "Fx", inner)
            self.go(self.C(far), "K", "KCs", inner)
            parts = [self.wait(near), self.wait(near + 5)]
            add_into(self.acc.at[self.C(near)], [self.acc.at[self.C(near)]] + parts)
            self.go(self.C(near), "S", "Cn", outer)
        if r == 4:
            self.add(self.X(ze), ["Fy"])
            self.add(self.Y(zo), ["Fx"])
            self.go(self.X(ze), "x", ze)
            self.go(self.Y(zo), "y", zo + 5)

            @pl.when(inner)
            def _():
                self.add(self.C(near), ["Cn"])

            self.go(self.C(near), "K", "KCo", inner)
        if r == 5:
            self.add(self.C(p.sib), [p.sib, p.sib + 5])

            @pl.when(inner)
            def _():
                self.add(self.C(p.sib), ["KCs"])

            self.go(self.C(p.sib), "S", "Co")
        if r == 6:
            slots = [p.z, p.z + 5, "Co"]
            parts = [self.acc.at[self.C(p.z)]] + [self.wait(s) for s in slots]
            add_into(self.out, parts)

            @pl.when(inner)
            def _():
                add_into(self.out, [self.out, self.wait("KCo")])

    def finish(self):
        for made, cond in self.sent:
            if cond is None:
                made.wait_send()
            else:
                pl.when(cond)(made.wait_send)


def scatter_kernel(n, *refs):
    part, out = refs[:n], refs[n : 2 * n]
    acc, own, came = refs[2 * n : 3 * n], refs[3 * n : 4 * n], refs[4 * n : 5 * n]
    send, recv = refs[5 * n :]
    place = Place()
    greet(place)
    made = [
        Scatter(place, part[i], acc[i], own[i], came[i], out[i], send, recv, i) for i in range(n)
    ]
    for step in range(n + 6):
        for r in range(7):
            i = step - r
            if 0 <= i < n:
                made[i].round(r)
    for one in made:
        one.finish()


def scatter_all(parts):
    n = len(parts)
    blocks = [(p.shape[4:], p.dtype) for p in parts]
    return pl.pallas_call(
        functools.partial(scatter_kernel, n),
        out_shape=[jax.ShapeDtypeStruct(b, jnp.float32) for b, _ in blocks],
        in_specs=[pl.BlockSpec(memory_space=pltpu.HBM)] * n,
        out_specs=[pl.BlockSpec(memory_space=pltpu.VMEM)] * n,
        scratch_shapes=[pltpu.VMEM((4, 2, 2) + b, t) for b, t in blocks]
        + [pltpu.VMEM((4, 2, 2) + b, t) for b, t in blocks]
        + [pltpu.VMEM((19,) + b, t) for b, t in blocks]
        + [
            pltpu.SemaphoreType.DMA((n, Scatter.NSEND + 1)),
            pltpu.SemaphoreType.DMA((n, Scatter.NRECV)),
        ],
        compiler_params=pltpu.CompilerParams(
            collective_id=3, has_side_effects=True, vmem_limit_bytes=VMEM_LIMIT
        ),
        name="scatter",
    )(*parts)


def states_kernel(reverse, through, value, out, met, planes, ready, send, recv):
    me = lax.axis_index(AXIS)
    z, r = me // 8, lax.rem(me, 8)
    barrier = pltpu.get_barrier_semaphore()
    plane = [z * 8 + lax.bitwise_xor(r, k) for k in range(8)]
    level = [lax.rem(z + k, 4) * 8 + r for k in range(4)]
    for peer in plane[1:] + level[1:]:
        pl.semaphore_signal(barrier, inc=1, device_id=peer, device_id_type=LOGICAL)
    pl.semaphore_wait(barrier, 10)

    def copy(src, dst, k, peer):
        return pltpu.make_async_remote_copy(
            src_ref=src,
            dst_ref=dst,
            send_sem=send.at[k],
            recv_sem=recv.at[k],
            device_id=peer,
            device_id_type=LOGICAL,
        )

    first = [copy(value.at[lax.bitwise_xor(r, k)], met.at[r], k, plane[k]) for k in range(1, 8)]
    for one in first:
        one.start()
    met[r] = value[r]
    for k in range(1, 8):
        copy(value.at[0], met.at[lax.bitwise_xor(r, k)], k, plane[k]).wait_recv()
    order = range(7, -1, -1) if reverse else range(8)
    total = jnp.zeros(met.shape[1:], jnp.float32)
    for i in order:
        total = through[(z * 8 + i) * 8 + r] * total + met[i]
    planes[z] = total
    second = []
    for k in range(1, 4):
        far = z - k if reverse else z + k
        cond = far >= 0 if reverse else far <= 3
        made = copy(planes.at[z], planes.at[z], 7 + k, far * 8 + r)
        second.append((made, cond))
        pl.when(cond)(made.start)
    ready[8] = jnp.zeros(met.shape[1:], jnp.float32)
    for k in range(3, 0, -1):
        far = z + k if reverse else z - k
        cond = far <= 3 if reverse else far >= 0

        @pl.when(cond)
        def _():
            copy(planes.at[z], planes.at[far], 7 + k, plane[0]).wait_recv()
            kept = jnp.float32(1.0)
            for i in range(8):
                kept = kept * through[(far * 8 + i) * 8 + r]
            ready[8] = kept * ready[8] + planes[far]

    total = ready[8]
    for i in order:
        ready[i] = total
        total = through[(z * 8 + i) * 8 + r] * total + met[i]
    third = [
        copy(ready.at[lax.bitwise_xor(r, k)], out.at[r], 10 + k, plane[k]) for k in range(1, 8)
    ]
    for one in third:
        one.start()
    out[r] = ready[r]
    for k in range(1, 8):
        copy(ready.at[0], out.at[lax.bitwise_xor(r, k)], 10 + k, plane[k]).wait_recv()
    for one in first + third:
        one.wait_send()
    for made, cond in second:
        pl.when(cond)(made.wait_send)


def states(value, through, reverse):
    tile = value.shape[1:]
    return pl.pallas_call(
        functools.partial(states_kernel, reverse),
        out_shape=jax.ShapeDtypeStruct(value.shape, jnp.float32),
        in_specs=[
            pl.BlockSpec(memory_space=pltpu.SMEM),
            pl.BlockSpec(memory_space=pltpu.VMEM),
        ],
        out_specs=pl.BlockSpec(memory_space=pltpu.VMEM),
        scratch_shapes=[
            pltpu.VMEM((8,) + tile, jnp.float32),
            pltpu.VMEM((4,) + tile, jnp.float32),
            pltpu.VMEM((9,) + tile, jnp.float32),
            pltpu.SemaphoreType.DMA((18,)),
            pltpu.SemaphoreType.DMA((18,)),
        ],
        compiler_params=pltpu.CompilerParams(
            collective_id=2 if reverse else 1, has_side_effects=True, vmem_limit_bytes=16000000
        ),
        name="states_back" if reverse else "states",
    )(through.reshape(-1), value)


def bounds_of(lengths, order):
    total, found = jnp.int32(0), []
    for j in range(lengths.shape[0]):
        total = total + lengths[order[j]]
        found.append(total)
    return found


def segment_at(bounds, places):
    found = jnp.zeros_like(places)
    for bound in bounds:
        found = found + jnp.where(bound <= places, 1, 0)
    return found


def same_segment(bounds, earlier, later):
    same = jnp.int32(0)
    for bound in bounds:
        same = same + jnp.where((bound <= earlier) != (bound <= later), 1, 0)
    return jnp.where((earlier >= 0) & (same == 0), 1.0, 0.0).astype(jnp.float32)


def spans_of(first, bounds, dist, entry, leaving):
    size = dist.shape[0]
    t = lax.broadcasted_iota(jnp.int32, (size, size), 0)
    s = lax.broadcasted_iota(jnp.int32, (size, size), 1)
    same = segment_at(bounds, t + first) == segment_at(bounds, s + first)
    dist[...] = jnp.where(same & (s <= t), t - s, -1).astype(jnp.float32)
    t = lax.broadcasted_iota(jnp.int32, entry.shape, 0)
    here = segment_at(bounds, t + first)
    ahead = segment_at(bounds, jnp.full(entry.shape, first - 1, jnp.int32))
    ahead = jnp.where(jnp.full(entry.shape, first, jnp.int32) == 0, -1, ahead)
    last = segment_at(bounds, jnp.full(entry.shape, first + size - 1, jnp.int32))
    entry[...] = jnp.where(here == ahead, t, -1).astype(jnp.float32)
    leaving[...] = jnp.where(here == last, size - t, -1).astype(jnp.float32)


def decay(distance, rate):
    return jnp.where(distance >= 0, jnp.exp(-rate * distance), 0.0)


def mm(a, b):
    return jnp.dot(a, b, preferred_element_type=jnp.float32)


def mm_nt(a, b):
    return lax.dot_general(a, b, (((1,), (1,)), ((), ())), preferred_element_type=jnp.float32)


def mm_tn(a, b):
    return lax.dot_general(a, b, (((0,), (0,)), ((), ())), preferred_element_type=jnp.float32)


def head_of(h):
    return pl.ds(pl.multiple_of(h * 128, 128), 128)


def norm_scale(values):
    return lax.rsqrt(jnp.mean(values * values, axis=-1, keepdims=True) + EPSILON)


class States:
    PEERS = 10

    def __init__(self, place, bounds, rate, reverse, value, met, planes, ready, out, send, recv):
        self.bounds, self.reverse = bounds, reverse
        self.value, self.met, self.planes, self.ready, self.out = value, met, planes, ready, out
        self.send, self.recv = send, recv
        self.z, self.r = place.z, lax.rem(place.me, 8)
        self.plane = [self.z * 8 + lax.bitwise_xor(self.r, k) for k in range(8)]
        self.level = [lax.rem(self.z + k, 4) * 8 + self.r for k in range(4)]
        self.order = range(7, -1, -1) if reverse else range(8)
        self.step = jnp.exp(jnp.full((1, 128), -SPAN * rate[self.r], jnp.float32))

    def through(self, device):
        return same_segment(self.bounds, device * SPAN - 1, device * SPAN + SPAN - 1)

    def copy(self, src, dst, k, peer):
        return pltpu.make_async_remote_copy(
            src_ref=src,
            dst_ref=dst,
            send_sem=self.send.at[k],
            recv_sem=self.recv.at[k],
            device_id=peer,
            device_id_type=LOGICAL,
        )

    def other(self, k):
        return lax.bitwise_xor(self.r, k)

    def spread(self):
        self.first = [
            self.copy(self.value.at[self.other(k)], self.met.at[self.r], k, self.plane[k])
            for k in range(1, 8)
        ]
        for one in self.first:
            one.start()
        self.met[self.r] = self.value[self.r]

    def total(self):
        for k in range(1, 8):
            self.copy(self.value.at[0], self.met.at[self.other(k)], k, self.plane[k]).wait_recv()
        total = jnp.zeros(self.met.shape[1:], jnp.float32)
        for i in self.order:
            total = self.through(self.z * 8 + i) * self.step * total + self.met[i]
        self.planes[self.z] = total
        self.second = []
        for k in range(1, 4):
            far = self.z - k if self.reverse else self.z + k
            cond = far >= 0 if self.reverse else far <= 3
            made = self.copy(
                self.planes.at[self.z], self.planes.at[self.z], 7 + k, far * 8 + self.r
            )
            self.second.append((made, cond))
            pl.when(cond)(made.start)

    def back(self):
        self.ready[8] = jnp.zeros(self.met.shape[1:], jnp.float32)
        for k in range(3, 0, -1):
            far = self.z + k if self.reverse else self.z - k
            cond = far <= 3 if self.reverse else far >= 0

            @pl.when(cond)
            def _():
                self.copy(
                    self.planes.at[self.z], self.planes.at[far], 7 + k, self.plane[0]
                ).wait_recv()
                kept = jnp.ones((1, 128), jnp.float32)
                for i in range(8):
                    kept = kept * (self.through(far * 8 + i) * self.step)
                self.ready[8] = kept * self.ready[8] + self.planes[far]

        total = self.ready[8]
        for i in self.order:
            self.ready[i] = total
            total = self.through(self.z * 8 + i) * self.step * total + self.met[i]
        self.third = [
            self.copy(self.ready.at[self.other(k)], self.out.at[self.r], 10 + k, self.plane[k])
            for k in range(1, 8)
        ]
        for one in self.third:
            one.start()
        self.out[self.r] = self.ready[self.r]

    def done(self):
        for k in range(1, 8):
            self.copy(self.ready.at[0], self.out.at[self.other(k)], 10 + k, self.plane[k]).wait_recv()

    def finish(self):
        for one in self.first + self.third:
            one.wait_send()
        for made, cond in self.second:
            pl.when(cond)(made.wait_send)


def greet_more(place):
    barrier = pltpu.get_barrier_semaphore()
    r = lax.rem(place.me, 8)
    peers = [place.z * 8 + lax.bitwise_xor(r, k) for k in range(1, 8)]
    peers += [lax.rem(place.z + k, 4) * 8 + r for k in range(1, 4)]
    for peer in peers:
        pl.semaphore_signal(barrier, inc=1, device_id=peer, device_id_type=LOGICAL)
    pl.semaphore_wait(barrier, len(peers))


def forward_kernel(
    lengths,
    order,
    rate,
    tokens,
    gain_own,
    s_key,
    s_value,
    s_query,
    s_unit,
    s_output,
    s_left,
    s_right,
    s_down,
    *refs,
):
    f32, bf16 = jnp.float32, jnp.bfloat16
    n = 11
    full, refs = refs[:n], refs[n:]
    saved, refs = refs[:16], refs[16:]
    kept, refs = refs[:16], refs[16:]
    (hidden, keys, values, queries, key_pre, query_pre, unit_pre, probs) = kept[:8]
    (attended, state_low, mixed, middle, second, left, right, product) = kept[8:]
    (dist, entry, leaving, gains, gain, value, met, planes, ready, arriving) = refs[:10]
    (narrow, wide, send, recv, state_send, state_recv, load_sem, save_sem) = refs[10:]
    place = Place()
    half = s_left.shape[1] // 2
    own = [s_key, s_value, s_query, s_unit, gain_own, s_output]
    own += [s_left.at[:, pl.ds(0, half)], s_left.at[:, pl.ds(half, half)]]
    own += [s_right.at[:, pl.ds(0, half)], s_right.at[:, pl.ds(half, half)], s_down]
    greet_more(place)
    made = [Gather(place, own[i], full[i], send, recv, i) for i in range(n)]
    bounds = bounds_of(lengths, order)
    states = States(
        place, bounds, rate, False, value, met, planes, ready, arriving, state_send, state_recv
    )
    slots = {0: narrow.at[0], 1: narrow.at[1], 2: narrow.at[0], 3: narrow.at[1], 4: gains}
    slots.update({5: narrow.at[0], 6: wide.at[0], 7: wide.at[1], 8: wide.at[0], 9: wide.at[1]})
    saves = []

    def save(*numbers):
        for i in numbers:
            copy = pltpu.make_async_copy(kept[i], saved[i], save_sem.at[i])
            copy.start()
            saves.append(copy)

    def weight(i):
        ref = slots[i]
        return ref[...].reshape(-1, ref.shape[-1])

    def start():
        x = tokens[...].astype(f32)
        hidden[...] = (x * norm_scale(x)).astype(bf16)
        spans_of(place.me * SPAN, bounds, dist, entry, leaving)
        save(0)

    def project(i, pre, low):
        out = mm(hidden[...], weight(i))
        if pre is not None:
            pre[...] = out
            out = out / (1.0 + jnp.exp(-out))
        low[...] = out.astype(bf16)

    def key():
        project(0, key_pre, keys)
        save(1, 4)

    def increments():
        project(1, None, values)

        @pl.loop(0, 8)
        def _(h):
            at = head_of(h)
            held = (keys[:, at].astype(f32) * decay(leaving[...], rate[h])).astype(bf16)
            value[h] = mm_tn(held, values[:, at])

        states.spread()
        save(2)

    def query():
        project(2, query_pre, queries)

        @pl.loop(0, 8)
        def _(h):
            at = head_of(h)
            scores = mm_nt(queries[:, at], keys[:, at])
            low = (scores * decay(dist[...], rate[h])).astype(bf16)
            probs[h] = low
            attended[:, at] = mm(low, values[:, at])

        save(3, 5, 7)

    def unit():
        unit_pre[...] = mm(hidden[...], weight(3))
        save(6)

    def attend():
        gain[...] = jnp.sum(gains[...].reshape(-1, 8, 128), axis=0)

        @pl.loop(0, 8)
        def _(h):
            at = head_of(h)
            low = arriving[h].astype(bf16)
            state_low[h] = low
            held = (queries[:, at].astype(f32) * decay(entry[...], rate[h])).astype(bf16)
            out = attended[:, at] + mm(held, low)
            attended[:, at] = out
            mixed[:, at] = (
                out * norm_scale(out) * gain[pl.ds(h, 1), :] * unit_pre[:, at]
            ).astype(bf16)

        save(8, 9, 10)

    def output():
        out = tokens[...].astype(f32) + mm(mixed[...], weight(5))
        middle[...] = out
        second[...] = (out * norm_scale(out)).astype(bf16)
        save(11, 12)

    def gate(i, side, part):
        side[:, pl.ds(part * half, half)] = mm(second[...], weight(i))

    def multiply():
        @pl.loop(0, SPAN // 16)
        def _(i):
            at = pl.ds(pl.multiple_of(i * 16, 16), 16)
            product[at, :] = (left[at, :] * right[at, :]).astype(bf16)

        save(13, 14, 15)

    tasks = {0: [start], 7: [key], 8: [increments], 9: [states.total, query], 10: [states.back, unit]}
    tasks[11] = [states.done, attend]
    tasks[12] = [output]
    tasks[13] = [lambda: gate(6, left, 0)]
    tasks[14] = [lambda: gate(7, left, 1)]
    tasks[15] = [lambda: gate(8, right, 0)]
    tasks[16] = [lambda: gate(9, right, 1), multiply]
    loads = {}
    for step in range(n + 6):
        for r in range(6):
            if 0 <= step - r < n:
                made[step - r].round(r)
        i = step - 6
        if 0 <= i < n:
            made[i].pairs()
        if i - 1 in loads:
            loads[i - 1].wait()
        if i in slots:
            loads[i] = pltpu.make_async_copy(full[i], slots[i], load_sem.at[i])
            loads[i].start()
        for task in tasks.get(step, []):
            task()
    for one in made:
        one.finish()
    states.finish()
    for copy in saves:
        copy.wait()


def forward(lengths, order, rate, tokens, gain_tile, shards):
    f32, bf16 = jnp.float32, jnp.bfloat16
    size, width = tokens.shape
    wide = shards[5].shape[1]
    half = wide // 2
    blocks = [(s.shape, s.dtype) for s in shards[:4]] + [(gain_tile.shape, f32)]
    blocks += [(shards[4].shape, bf16)] + [((32, half), bf16)] * 4 + [(shards[7].shape, bf16)]
    square, cube = (size, width), (8, 128, 128)
    kept = [(square, bf16)] * 4 + [(square, f32)] * 3 + [((8, size, size), bf16)]
    kept += [(square, f32), (cube, bf16), (square, bf16), (square, f32), (square, bf16)]
    kept += [((size, wide), f32)] * 2 + [((size, wide), bf16)]
    vmem, hbm = pl.BlockSpec(memory_space=pltpu.VMEM), pl.BlockSpec(memory_space=pltpu.HBM)
    smem = pl.BlockSpec(memory_space=pltpu.SMEM)
    n = len(blocks)
    out = pl.pallas_call(
        forward_kernel,
        out_shape=[jax.ShapeDtypeStruct((4, 2, 2, 2) + s, t) for s, t in blocks]
        + [jax.ShapeDtypeStruct(s, t) for s, t in kept],
        in_specs=[smem] * 3 + [vmem] * 10,
        out_specs=[hbm] * (n + len(kept)),
        scratch_shapes=[pltpu.VMEM(s, t) for s, t in kept]
        + [pltpu.VMEM((size, size), f32), pltpu.VMEM((size, 128), f32), pltpu.VMEM((size, 128), f32)]
        + [pltpu.VMEM((4, 2, 2, 2, 8, 128), f32), pltpu.VMEM((8, 128), f32)]
        + [pltpu.VMEM(cube, f32), pltpu.VMEM(cube, f32), pltpu.VMEM((4, 128, 128), f32)]
        + [pltpu.VMEM((9, 128, 128), f32), pltpu.VMEM(cube, f32)]
        + [
            pltpu.VMEM((2, 4, 2, 2, 2, 32, width), bf16),
            pltpu.VMEM((2, 4, 2, 2, 2, 32, half), bf16),
            pltpu.SemaphoreType.DMA((n, Gather.NSEND + 1)),
            pltpu.SemaphoreType.DMA((n, Gather.NRECV)),
            pltpu.SemaphoreType.DMA((18,)),
            pltpu.SemaphoreType.DMA((18,)),
            pltpu.SemaphoreType.DMA((n,)),
            pltpu.SemaphoreType.DMA((len(kept),)),
        ],
        compiler_params=pltpu.CompilerParams(
            collective_id=0, has_side_effects=True, vmem_limit_bytes=VMEM_LIMIT
        ),
        name="forward",
    )(lengths, order, rate, tokens, gain_tile, *shards)
    return out[:n], out[n:]

def entering(value, axis, combine, identity, reverse):
    length, here = (lax.axis_size(axis), lax.axis_index(axis))
    everything = jax.tree.map(lambda part: lax.all_gather(part, axis), value)
    start = jax.tree.map(
        lambda part, zero: jnp.broadcast_to(jnp.asarray(zero, part.dtype), part.shape),
        value,
        identity,
    )

    def hop(k, before):
        at = length - 1 - k if reverse else k
        reached = at > here if reverse else at < here
        new = combine(before, jax.tree.map(lambda part: part[at], everything))
        return jax.tree.map(lambda a, b: jnp.where(reached, a, b), new, before)

    return lax.fori_loop(0, length, hop, start)


def segment_of(places, lengths, seq_order):
    number = lengths.shape[0]
    picked = seq_order[:, None] == jnp.arange(number, dtype=jnp.int32)[None, :]
    packed = jnp.sum(jnp.where(picked, lengths[None, :], 0), axis=1, dtype=jnp.int32)
    bounds = jnp.cumsum(packed, dtype=jnp.int32)
    found = jnp.sum((bounds[None, :] <= places[:, None]).astype(jnp.int32), axis=1, dtype=jnp.int32)
    return jnp.where(places < 0, -1, found)


def decay_tables(segments, before, rate, block):
    length = segments.shape[0]
    count = length // block
    spans = segments.reshape(count, block)
    priors = jnp.concatenate([before.reshape(1), spans[:-1, -1]])
    steps = jnp.arange(block, dtype=jnp.int32)
    distance = steps[:, None] - steps[None, :]
    same = (spans[:, :, None] == spans[:, None, :]) & (distance >= 0)[None]
    powers = jnp.exp(-rate[:, None, None] * jnp.maximum(distance, 0).astype(jnp.float32)[None])
    within = jnp.where(same[:, None], powers[None], 0.0)
    entry = jnp.where(
        (spans == priors[:, None])[:, :, None],
        jnp.exp(-rate[None, :] * steps.astype(jnp.float32)[:, None])[None],
        0.0,
    )
    leaving = jnp.where(
        (spans == spans[:, -1:])[:, :, None],
        jnp.exp(-rate[None, :] * (block - steps).astype(jnp.float32)[:, None])[None],
        0.0,
    )
    passing = jnp.where((spans[:, -1] == priors)[:, None], jnp.exp(-rate * block)[None], 0.0)
    offsets = (jnp.arange(count, dtype=jnp.int32) * block).astype(jnp.float32)
    arrival = jnp.where(
        (priors == before)[:, None], jnp.exp(-rate[None, :] * offsets[:, None]), 0.0
    )
    through = jnp.where(segments[-1] == before, jnp.exp(-rate * length), 0.0)
    return (within, entry, leaving, passing, arrival, through)


def chain_states(earlier, later):
    return (earlier[0] * later[0], later[0][:, None, None] * earlier[1] + later[1])


def silu_slope(values):
    sigma = jax.nn.sigmoid(values)
    return sigma * (1.0 + values * (1.0 - sigma))


def row_scale(values):
    return lax.rsqrt(jnp.mean(values * values, axis=-1, keepdims=True) + EPSILON)


def body(
    tokens,
    lengths,
    seq_order,
    decay_rate,
    w_query,
    w_key,
    w_value,
    w_unit,
    w_output,
    norm_gain,
    w_left,
    w_right,
    w_down,
    cotangent,
):
    f32 = jnp.float32
    bf16 = jnp.bfloat16
    length, width = tokens.shape
    heads = decay_rate.shape[0]
    head_size = width // heads
    count = length // SPAN
    first = lax.axis_index(AXIS) * length
    places = first + jnp.arange(length, dtype=jnp.int32)
    segments = segment_of(places, lengths, seq_order)
    before = segment_of(jnp.reshape(first - 1, (1,)), lengths, seq_order)[0]
    within, entry, leaving, passing, arrival, through = decay_tables(
        segments, before, decay_rate, SPAN
    )
    attention_set = (
        lax.all_gather(w_query, AXIS, axis=0, tiled=True),
        lax.all_gather(w_key, AXIS, axis=0, tiled=True),
        lax.all_gather(w_value, AXIS, axis=0, tiled=True),
        lax.all_gather(w_unit, AXIS, axis=0, tiled=True),
        lax.all_gather(w_output, AXIS, axis=0, tiled=True),
        lax.all_gather(norm_gain, AXIS, axis=0, tiled=True),
    )
    feed_set = (
        lax.all_gather(w_left, AXIS, axis=0, tiled=True),
        lax.all_gather(w_right, AXIS, axis=0, tiled=True),
        lax.all_gather(w_down, AXIS, axis=0, tiled=True),
    )
    full_query, full_key, full_value, full_unit, full_output, full_gain = attention_set
    full_left, full_right, full_down = feed_set
    inputs = tokens.astype(f32)
    first_scale = row_scale(inputs)
    normed = inputs * first_scale
    hidden = normed.astype(bf16)
    query_pre = jnp.dot(hidden, full_query, preferred_element_type=f32)
    key_pre = jnp.dot(hidden, full_key, preferred_element_type=f32)
    value_pre = jnp.dot(hidden, full_value, preferred_element_type=f32)
    unit_pre = jnp.dot(hidden, full_unit, preferred_element_type=f32)
    block_shape = (count, SPAN, heads, head_size)
    query_blocks = jax.nn.silu(query_pre).astype(bf16).reshape(block_shape)
    key_blocks = jax.nn.silu(key_pre).astype(bf16).reshape(block_shape)
    value_blocks = value_pre.astype(bf16).reshape(block_shape)
    scores = jnp.einsum("nthe,nshe->nhts", query_blocks, key_blocks, preferred_element_type=f32)
    mixing = (scores * within).astype(bf16)
    local_out = jnp.einsum("nhts,nshe->nthe", mixing, value_blocks, preferred_element_type=f32)
    keys_held = (key_blocks * leaving[..., None]).astype(bf16)
    increments = jnp.einsum("nshe,nshf->nhef", keys_held, value_blocks, preferred_element_type=f32)
    local_states = [jnp.zeros((heads, head_size, head_size), f32)]
    local_states.append(passing[0][:, None, None] * local_states[-1] + increments[0])
    end_state = local_states[count]
    start_pair = (jnp.ones_like(through), jnp.zeros_like(end_state))
    arriving = entering((through, end_state), AXIS, chain_states, start_pair, False)[1]
    states = jnp.stack(local_states[:count]) + arrival[:, :, None, None] * arriving[None]
    state_low = states.astype(bf16)
    query_held = (query_blocks * entry[..., None]).astype(bf16)
    attended = local_out + jnp.einsum(
        "nthe,nhef->nthf", query_held, state_low, preferred_element_type=f32
    )
    attended_heads = attended.reshape(length, heads, head_size)
    head_scale = row_scale(attended_heads)
    unit_norm = (attended_heads * head_scale).reshape(length, width)
    gain = full_gain.astype(f32)
    gated = unit_norm * gain
    mixed_in = (gated * unit_pre).astype(bf16)
    middle = inputs + jnp.dot(mixed_in, full_output, preferred_element_type=f32)
    second_scale = row_scale(middle)
    second_unit = middle * second_scale
    second = second_unit.astype(bf16)
    left_pre = jnp.dot(second, full_left, preferred_element_type=f32)
    right_pre = jnp.dot(second, full_right, preferred_element_type=f32)
    product = (left_pre * right_pre).astype(bf16)
    result = (middle + jnp.dot(product, full_down, preferred_element_type=f32)).astype(bf16)
    back_feed = (
        lax.all_gather(w_left, AXIS, axis=0, tiled=True),
        lax.all_gather(w_right, AXIS, axis=0, tiled=True),
        lax.all_gather(w_down, AXIS, axis=0, tiled=True),
    )
    back_left, back_right, back_down = back_feed
    grad_product = jnp.einsum("td,fd->tf", cotangent, back_down, preferred_element_type=f32)
    grad_left_pre = (grad_product * right_pre).astype(bf16)
    grad_right_pre = (grad_product * left_pre).astype(bf16)
    grad_w_down = jnp.einsum("tf,td->fd", product, cotangent, preferred_element_type=f32)
    grad_w_left = jnp.einsum("td,tf->df", second, grad_left_pre, preferred_element_type=f32)
    grad_w_right = jnp.einsum("td,tf->df", second, grad_right_pre, preferred_element_type=f32)
    feed_grads = (
        lax.psum_scatter(grad_w_left, AXIS, scatter_dimension=0, tiled=True),
        lax.psum_scatter(grad_w_right, AXIS, scatter_dimension=0, tiled=True),
        lax.psum_scatter(grad_w_down, AXIS, scatter_dimension=0, tiled=True),
    )
    grad_second = jnp.einsum(
        "tf,df->td", grad_left_pre, back_left, preferred_element_type=f32
    ) + jnp.einsum("tf,df->td", grad_right_pre, back_right, preferred_element_type=f32)
    grad_middle = cotangent.astype(f32) + second_scale * (
        grad_second - second_unit * jnp.mean(grad_second * second_unit, axis=-1, keepdims=True)
    )
    back_attention = (
        lax.all_gather(w_query, AXIS, axis=0, tiled=True),
        lax.all_gather(w_key, AXIS, axis=0, tiled=True),
        lax.all_gather(w_value, AXIS, axis=0, tiled=True),
        lax.all_gather(w_unit, AXIS, axis=0, tiled=True),
        lax.all_gather(w_output, AXIS, axis=0, tiled=True),
        lax.all_gather(norm_gain, AXIS, axis=0, tiled=True),
    )
    back_query, back_key, back_value, back_unit, back_output, back_gain = back_attention
    grad_branch = grad_middle.astype(bf16)
    grad_w_output = jnp.einsum(TD_TE, mixed_in, grad_branch, preferred_element_type=f32)
    grad_mixed = jnp.einsum(TE_DE, grad_branch, back_output, preferred_element_type=f32)
    grad_gated = grad_mixed * unit_pre
    grad_unit_pre = (grad_mixed * gated).astype(bf16)
    grad_gain = jnp.sum(grad_gated * unit_norm, axis=0)
    grad_norm_heads = (grad_gated * back_gain.astype(f32)).reshape(length, heads, head_size)
    norm_heads = unit_norm.reshape(length, heads, head_size)
    grad_att = head_scale * (
        grad_norm_heads
        - norm_heads * jnp.mean(grad_norm_heads * norm_heads, axis=-1, keepdims=True)
    )
    grad_att_blocks = grad_att.astype(bf16).reshape(block_shape)
    grad_mixing = jnp.einsum(
        "nthf,nshf->nhts", grad_att_blocks, value_blocks, preferred_element_type=f32
    )
    grad_scores = (grad_mixing * within).astype(bf16)
    grad_query_blocks = (
        jnp.einsum("nhts,nshe->nthe", grad_scores, key_blocks, preferred_element_type=f32)
        + jnp.einsum("nthf,nhef->nthe", grad_att_blocks, state_low, preferred_element_type=f32)
        * entry[..., None]
    )
    grad_key_blocks = jnp.einsum(
        "nhts,nthe->nshe", grad_scores, query_blocks, preferred_element_type=f32
    )
    grad_value_blocks = jnp.einsum(
        "nhts,nthf->nshf", mixing, grad_att_blocks, preferred_element_type=f32
    )
    direct = jnp.einsum("nthe,nthf->nhef", query_held, grad_att_blocks, preferred_element_type=f32)
    leaving_sum = jnp.sum(arrival[:, :, None, None] * direct, axis=0)
    later = entering((through, leaving_sum), AXIS, chain_states, start_pair, True)[1]
    next_grads = [later]
    grad_increment = jnp.stack(next_grads[::-1]).astype(bf16)
    grad_keys_held = jnp.einsum(
        "nhef,nshf->nshe", grad_increment, value_blocks, preferred_element_type=f32
    )
    grad_key_blocks = grad_key_blocks + grad_keys_held * leaving[..., None]
    grad_value_blocks = grad_value_blocks + jnp.einsum(
        "nshe,nhef->nshf", keys_held, grad_increment, preferred_element_type=f32
    )
    grad_query_pre = (grad_query_blocks.reshape(length, width) * silu_slope(query_pre)).astype(bf16)
    grad_key_pre = (grad_key_blocks.reshape(length, width) * silu_slope(key_pre)).astype(bf16)
    grad_value_pre = grad_value_blocks.reshape(length, width).astype(bf16)
    grad_w_query = jnp.einsum(TD_TE, hidden, grad_query_pre, preferred_element_type=f32)
    grad_w_key = jnp.einsum(TD_TE, hidden, grad_key_pre, preferred_element_type=f32)
    grad_w_value = jnp.einsum(TD_TE, hidden, grad_value_pre, preferred_element_type=f32)
    grad_w_unit = jnp.einsum(TD_TE, hidden, grad_unit_pre, preferred_element_type=f32)
    attention_grads = (
        lax.psum_scatter(grad_w_query, AXIS, scatter_dimension=0, tiled=True),
        lax.psum_scatter(grad_w_key, AXIS, scatter_dimension=0, tiled=True),
        lax.psum_scatter(grad_w_value, AXIS, scatter_dimension=0, tiled=True),
        lax.psum_scatter(grad_w_unit, AXIS, scatter_dimension=0, tiled=True),
        lax.psum_scatter(grad_w_output, AXIS, scatter_dimension=0, tiled=True),
        lax.psum_scatter(grad_gain, AXIS, scatter_dimension=0, tiled=True),
    )
    grad_hidden = (
        jnp.einsum(TE_DE, grad_query_pre, back_query, preferred_element_type=f32)
        + jnp.einsum(TE_DE, grad_key_pre, back_key, preferred_element_type=f32)
        + jnp.einsum(TE_DE, grad_value_pre, back_value, preferred_element_type=f32)
        + jnp.einsum(TE_DE, grad_unit_pre, back_unit, preferred_element_type=f32)
    )
    grad_inputs = grad_middle + first_scale * (
        grad_hidden - normed * jnp.mean(grad_hidden * normed, axis=-1, keepdims=True)
    )
    return (
        result,
        grad_inputs,
        attention_grads[0],
        attention_grads[1],
        attention_grads[2],
        attention_grads[3],
        attention_grads[4],
        attention_grads[5],
        feed_grads[0],
        feed_grads[1],
        feed_grads[2],
    )


def body_kernels(
    tokens,
    lengths,
    seq_order,
    decay_rate,
    w_query,
    w_key,
    w_value,
    w_unit,
    w_output,
    norm_gain,
    w_left,
    w_right,
    w_down,
    cotangent,
):
    f32 = jnp.float32
    bf16 = jnp.bfloat16
    length, width = tokens.shape
    heads = decay_rate.shape[0]
    head_size = width // heads
    count = length // SPAN
    first = lax.axis_index(AXIS) * length
    places = first + jnp.arange(length, dtype=jnp.int32)
    segments = segment_of(places, lengths, seq_order)
    before = segment_of(jnp.reshape(first - 1, (1,)), lengths, seq_order)[0]
    within, entry, leaving, passing, arrival, through = decay_tables(
        segments, before, decay_rate, SPAN
    )
    devices = lax.axis_size(AXIS)
    me = lax.axis_index(AXIS)
    mine = jnp.arange(devices, dtype=jnp.int32)[:, None] == me
    gain_tile = jnp.where(mine, norm_gain.astype(f32)[None, :], 0.0).reshape(heads, head_size)
    full, kept = forward(
        lengths,
        seq_order,
        decay_rate,
        tokens,
        gain_tile,
        [w_key, w_value, w_query, w_unit, w_output, w_left, w_right, w_down],
    )
    full_key, full_value, full_query, full_unit = [f.reshape(-1, width) for f in full[:4]]
    full_gain = jnp.sum(full[4].reshape(devices, heads, head_size), axis=0).reshape(width)
    full_output = full[5].reshape(-1, width)
    full_left = jnp.concatenate([f.reshape(width, -1) for f in full[6:8]], axis=1)
    full_right = jnp.concatenate([f.reshape(width, -1) for f in full[8:10]], axis=1)
    full_down = full[10].reshape(-1, width)
    ends = segment_of((jnp.arange(devices + 1, dtype=jnp.int32)) * length - 1, lengths, seq_order)
    through_all = jnp.where(
        (ends[1:] == ends[:-1])[:, None], jnp.exp(-decay_rate * length)[None, :], 0.0
    )
    hidden, keys, values, queries, key_pre, query_pre, unit_pre, mixing = kept[:8]
    attended, state_low, mixed_in, middle, second, left_pre, right_pre, product = kept[8:]
    block_shape = (count, SPAN, heads, head_size)
    query_blocks = queries.reshape(block_shape)
    key_blocks = keys.reshape(block_shape)
    value_blocks = values.reshape(block_shape)
    mixing, state_low = mixing[None], state_low[None]
    inputs = tokens.astype(f32)
    first_scale = row_scale(inputs)
    normed = inputs * first_scale
    keys_held = (key_blocks * leaving[..., None]).astype(bf16)
    query_held = (query_blocks * entry[..., None]).astype(bf16)
    attended_heads = attended.reshape(length, heads, head_size)
    head_scale = row_scale(attended_heads)
    unit_norm = (attended_heads * head_scale).reshape(length, width)
    gated = unit_norm * full_gain
    second_scale = row_scale(middle)
    second_unit = middle * second_scale
    result = (middle + jnp.dot(product, full_down, preferred_element_type=f32)).astype(bf16)
    back_left, back_right, back_down = full_left, full_right, full_down
    grad_product = jnp.einsum("td,fd->tf", cotangent, back_down, preferred_element_type=f32)
    grad_left_pre = (grad_product * right_pre).astype(bf16)
    grad_right_pre = (grad_product * left_pre).astype(bf16)
    grad_w_down = jnp.einsum("tf,td->fd", product, cotangent, preferred_element_type=f32)
    grad_w_left = jnp.einsum("td,tf->df", second, grad_left_pre, preferred_element_type=f32)
    grad_w_right = jnp.einsum("td,tf->df", second, grad_right_pre, preferred_element_type=f32)
    grad_second = jnp.einsum(
        "tf,df->td", grad_left_pre, back_left, preferred_element_type=f32
    ) + jnp.einsum("tf,df->td", grad_right_pre, back_right, preferred_element_type=f32)
    grad_middle = cotangent.astype(f32) + second_scale * (
        grad_second - second_unit * jnp.mean(grad_second * second_unit, axis=-1, keepdims=True)
    )
    back_query, back_key, back_value, back_unit = full_query, full_key, full_value, full_unit
    back_output, back_gain = full_output, full_gain
    grad_branch = grad_middle.astype(bf16)
    grad_w_output = jnp.einsum(TD_TE, mixed_in, grad_branch, preferred_element_type=f32)
    grad_mixed = jnp.einsum(TE_DE, grad_branch, back_output, preferred_element_type=f32)
    grad_gated = grad_mixed * unit_pre
    grad_unit_pre = (grad_mixed * gated).astype(bf16)
    grad_gain = jnp.sum(grad_gated * unit_norm, axis=0)
    grad_norm_heads = (grad_gated * back_gain.astype(f32)).reshape(length, heads, head_size)
    norm_heads = unit_norm.reshape(length, heads, head_size)
    grad_att = head_scale * (
        grad_norm_heads
        - norm_heads * jnp.mean(grad_norm_heads * norm_heads, axis=-1, keepdims=True)
    )
    grad_att_blocks = grad_att.astype(bf16).reshape(block_shape)
    grad_mixing = jnp.einsum(
        "nthf,nshf->nhts", grad_att_blocks, value_blocks, preferred_element_type=f32
    )
    grad_scores = (grad_mixing * within).astype(bf16)
    grad_query_blocks = (
        jnp.einsum("nhts,nshe->nthe", grad_scores, key_blocks, preferred_element_type=f32)
        + jnp.einsum("nthf,nhef->nthe", grad_att_blocks, state_low, preferred_element_type=f32)
        * entry[..., None]
    )
    grad_key_blocks = jnp.einsum(
        "nhts,nthe->nshe", grad_scores, query_blocks, preferred_element_type=f32
    )
    grad_value_blocks = jnp.einsum(
        "nhts,nthf->nshf", mixing, grad_att_blocks, preferred_element_type=f32
    )
    direct = jnp.einsum("nthe,nthf->nhef", query_held, grad_att_blocks, preferred_element_type=f32)
    leaving_sum = jnp.sum(arrival[:, :, None, None] * direct, axis=0)
    later = states(leaving_sum, through_all, True)
    next_grads = [later]
    grad_increment = jnp.stack(next_grads[::-1]).astype(bf16)
    grad_keys_held = jnp.einsum(
        "nhef,nshf->nshe", grad_increment, value_blocks, preferred_element_type=f32
    )
    grad_key_blocks = grad_key_blocks + grad_keys_held * leaving[..., None]
    grad_value_blocks = grad_value_blocks + jnp.einsum(
        "nshe,nhef->nshf", keys_held, grad_increment, preferred_element_type=f32
    )
    grad_query_pre = (grad_query_blocks.reshape(length, width) * silu_slope(query_pre)).astype(bf16)
    grad_key_pre = (grad_key_blocks.reshape(length, width) * silu_slope(key_pre)).astype(bf16)
    grad_value_pre = grad_value_blocks.reshape(length, width).astype(bf16)
    grad_w_query = jnp.einsum(TD_TE, hidden, grad_query_pre, preferred_element_type=f32)
    grad_w_key = jnp.einsum(TD_TE, hidden, grad_key_pre, preferred_element_type=f32)
    grad_w_value = jnp.einsum(TD_TE, hidden, grad_value_pre, preferred_element_type=f32)
    grad_w_unit = jnp.einsum(TD_TE, hidden, grad_unit_pre, preferred_element_type=f32)
    def blocks(grad):
        return grad.astype(bf16).reshape((4, 2, 2, 2, -1) + grad.shape[1:])

    gain_rows = grad_gain.reshape(devices, 1, width // devices)
    gain_rows = jnp.pad(gain_rows, ((0, 0), (0, 7), (0, 128 - width // devices)))
    split = w_left.shape[1] // 2
    grads = scatter_all(
        [blocks(grad_w_down)]
        + [blocks(grad_w_left[:, :split]), blocks(grad_w_left[:, split:])]
        + [blocks(grad_w_right[:, :split]), blocks(grad_w_right[:, split:])]
        + [blocks(grad_w_output), gain_rows.reshape(4, 2, 2, 2, 8, 128)]
        + [blocks(grad_w_unit), blocks(grad_w_value), blocks(grad_w_key), blocks(grad_w_query)]
    )
    feed_grads = (
        jnp.concatenate(grads[1:3], axis=1),
        jnp.concatenate(grads[3:5], axis=1),
        grads[0],
    )
    attention_grads = (
        grads[10],
        grads[9],
        grads[8],
        grads[7],
        grads[5],
        grads[6][0, : width // devices],
    )
    grad_hidden = (
        jnp.einsum(TE_DE, grad_query_pre, back_query, preferred_element_type=f32)
        + jnp.einsum(TE_DE, grad_key_pre, back_key, preferred_element_type=f32)
        + jnp.einsum(TE_DE, grad_value_pre, back_value, preferred_element_type=f32)
        + jnp.einsum(TE_DE, grad_unit_pre, back_unit, preferred_element_type=f32)
    )
    grad_inputs = grad_middle + first_scale * (
        grad_hidden - normed * jnp.mean(grad_hidden * normed, axis=-1, keepdims=True)
    )
    return (
        result,
        grad_inputs,
        attention_grads[0],
        attention_grads[1],
        attention_grads[2],
        attention_grads[3],
        attention_grads[4],
        attention_grads[5],
        feed_grads[0],
        feed_grads[1],
        feed_grads[2],
    )


def solution(mesh):
    placed = (
        P(AXIS, None),
        P(),
        P(),
        P(),
        P(AXIS, None),
        P(AXIS, None),
        P(AXIS, None),
        P(AXIS, None),
        P(AXIS, None),
        P(AXIS),
        P(AXIS, None),
        P(AXIS, None),
        P(AXIS, None),
        P(AXIS, None),
    )
    return jax.shard_map(
        body_kernels if mesh.size == 32 else body,
        mesh=mesh,
        in_specs=placed,
        out_specs=(
            P(AXIS, None),
            P(AXIS, None),
            P(AXIS, None),
            P(AXIS, None),
            P(AXIS, None),
            P(AXIS, None),
            P(AXIS, None),
            P(AXIS),
            P(AXIS, None),
            P(AXIS, None),
            P(AXIS, None),
        ),
        check_vma=False,
    )
```

```python
import functools

import jax
import jax.numpy as jnp
from jax import lax
from jax.experimental import pallas as pl
from jax.experimental.pallas import tpu as pltpu
from jax.sharding import PartitionSpec as P

SPAN = 256
AXIS = "fsdp"
TE_DE = "te,de->td"
TD_TE = "td,te->de"
EPSILON = 1e-05
LOGICAL = pl.DeviceIdType.LOGICAL
VMEM_LIMIT = 64000000


class Place:
    def __init__(self):
        me = lax.axis_index(AXIS)
        self.me = me
        self.c = lax.rem(me, 2)
        self.x = lax.rem(me // 2, 2)
        self.y = lax.rem(me // 4, 2)
        self.z = me // 8
        self.inner = (self.z == 1) | (self.z == 2)
        self.even = lax.rem(self.z, 2) == 0
        self.sib = self.z + 1 - 2 * lax.rem(self.z, 2)
        half = self.z // 2
        self.near = 2 - half
        self.far = 3 - 3 * half
        self.cross = 3 - self.z
        self.x1 = 1 - self.x
        self.y1 = 1 - self.y
        self.c1 = 1 - self.c
        self.to = {
            "S": self.dev(self.sib, self.y, self.x, self.c),
            "K": self.dev(self.cross, self.y, self.x, self.c),
            "x": self.dev(self.z, self.y, self.x1, self.c),
            "y": self.dev(self.z, self.y1, self.x, self.c),
            "p": self.dev(self.z, self.y, self.x, self.c1),
        }

    def dev(self, z, y, x, c):
        return ((z * 2 + y) * 2 + x) * 2 + c


def arrived(ref, send, recv, place):
    pltpu.make_async_remote_copy(
        src_ref=ref,
        dst_ref=ref,
        send_sem=send,
        recv_sem=recv,
        device_id=place.to["p"],
        device_id_type=LOGICAL,
    ).wait_recv()


class Gather:
    RECV = ("Cs", "Cn", "Cf", "Xo", "Xs", "Xn", "Xf", "Yo", "Ys", "Yn", "Yf", "D0", "D1", "En", "Ef")
    GROUPS = ("C", "X", "Y", "D")
    NRECV = 19
    NSEND = 25

    def __init__(self, place, own, full, send, recv, index):
        self.p, self.own, self.full = place, own, full
        self.send, self.recv, self.index = send, recv, index
        self.sent = []
        p = place
        self.where = {}
        for g, y, x in (("C", p.y, p.x), ("X", p.y, p.x1), ("Y", p.y1, p.x), ("D", p.y1, p.x1)):
            for k, z in (("o", p.z), ("s", p.sib), ("n", p.near), ("f", p.far)):
                self.where[g + k] = (z, y, x, p.c)
        for a, b in (("D0", "Do"), ("D1", "Ds"), ("En", "Dn"), ("Ef", "Df")):
            self.where[a] = self.where[b]

    def slot(self, name):
        return self.full.at[self.where[name]]

    def copy(self, name, link, landing):
        src = self.own if name == "Co" else self.slot(name)
        k = len(self.sent)
        made = pltpu.make_async_remote_copy(
            src_ref=src,
            dst_ref=self.slot(name),
            send_sem=self.send.at[self.index, k],
            recv_sem=self.recv.at[self.index, self.RECV.index(landing)],
            device_id=self.p.to[link],
            device_id_type=LOGICAL,
        )
        return made

    def go(self, name, link, landing, cond=None):
        made = self.copy(name, link, landing)
        self.sent.append((made, cond))
        if cond is None:
            made.start()
        else:
            pl.when(cond)(made.start)

    def wait(self, name):
        arrived(self.slot(name), self.send.at[self.index, 0], self.recv.at[self.index, self.RECV.index(name)], self.p)

    def group(self, g):
        p = self.p
        y = p.y if g in "CX" else p.y1
        x = p.x if g in "CY" else p.x1
        return y, x

    def pair(self, g):
        y, x = self.group(g)
        ref = self.full.at[:, y, x, self.p.c]
        k = len(self.sent)
        made = pltpu.make_async_remote_copy(
            src_ref=ref,
            dst_ref=ref,
            send_sem=self.send.at[self.index, k],
            recv_sem=self.recv.at[self.index, 15 + self.GROUPS.index(g)],
            device_id=self.p.to["p"],
            device_id_type=LOGICAL,
        )
        self.sent.append((made, None))
        made.start()

    def round(self, r):
        p = self.p
        inner, even = p.inner, p.even
        odd = jnp.logical_not(even)
        if r == 0:
            keep = pltpu.make_async_copy(self.own, self.slot("Co"), self.send.at[self.index, self.NSEND])
            self.keep = keep
            keep.start()
            self.go("Co", "S", "Cs")
            self.go("Co", "K", "Cn", inner)
            self.go("Co", "x", "Xo")
            self.go("Co", "y", "Yo")
        if r == 1:
            self.wait("Cs")
            self.go("Cs", "K", "Cf", inner)
            self.go("Cs", "x", "Xs")
            self.go("Cs", "y", "Ys")
            self.wait("Xo")
            self.go("Xo", "y", "D0", even)
            self.wait("Yo")
            self.go("Yo", "x", "D0", odd)
        if r == 2:
            self.wait("Cn")
            self.go("Cn", "S", "Cn", inner)
            self.go("Cn", "x", "Xn")
            self.go("Cn", "y", "Yn")
            self.wait("Xs")
            self.go("Xs", "y", "D1", odd)
            self.wait("Ys")
            self.go("Ys", "x", "D1", even)
            self.wait("D0")
            self.go("D0", "K", "En", inner)
        if r == 3:
            self.wait("Cf")
            self.go("Cf", "S", "Cf", inner)
            self.go("Cf", "x", "Xf")
            self.go("Cf", "y", "Yf")
            self.keep.wait()
            self.pair("C")
            self.wait("D1")
            self.go("D1", "K", "Ef", inner)
            self.wait("Xn")
            self.wait("Yn")
        if r == 4:
            self.wait("En")
            self.go("En", "S", "En", inner)
            self.wait("Xf")
            self.pair("X")
            self.wait("Yf")
            self.pair("Y")
        if r == 5:
            self.wait("Ef")
            self.go("Ef", "S", "Ef", inner)
            self.pair("D")

    def pairs(self):
        for g in self.GROUPS:
            y, x = self.group(g)
            ref = self.full.at[:, y, x, self.p.c1]
            arrived(ref, self.send.at[self.index, 0], self.recv.at[self.index, 15 + self.GROUPS.index(g)], self.p)

    def finish(self):
        for made, cond in self.sent:
            if cond is None:
                made.wait_send()
            else:
                pl.when(cond)(made.wait_send)


def add_into(out, parts):
    rows = out.shape[0]
    step = 8 if rows % 16 else 16

    @pl.loop(0, rows // step)
    def _(i):
        at = pl.ds(pl.multiple_of(i * step, step), step)
        total = parts[0][at, :].astype(jnp.float32)
        for part in parts[1:]:
            total = total + part[at, :].astype(jnp.float32)
        out[at, :] = total.astype(out.dtype)


class Scatter:
    NRECV = 20
    NSEND = 22
    SLOTS = ("x0", "x1", "x2", "x3", "Fx", "y0", "y1", "y2", "y3", "Fy", "En", "Ef", "Cn", "Cf", "Co", "De", "Do", "KCs", "KCo")

    def __init__(self, place, part, acc, term, came, out, send, recv, index):
        self.p, self.part, self.acc, self.term, self.came, self.out = place, part, acc, term, came, out
        self.send, self.recv, self.index = send, recv, index
        self.sent = []
        p = place
        half = p.z // 2
        self.ze, self.zo = 2 * half, 2 * half + 1
        self.C = lambda z: (z, p.y, p.x)
        self.X = lambda z: (z, p.y, p.x1)
        self.Y = lambda z: (z, p.y1, p.x)
        self.D = lambda z: (z, p.y1, p.x1)

    def go(self, where, link, slot, cond=None):
        k = len(self.sent)
        at = self.SLOTS.index(slot) if isinstance(slot, str) else slot
        made = pltpu.make_async_remote_copy(
            src_ref=self.acc.at[where],
            dst_ref=self.came.at[at],
            send_sem=self.send.at[self.index, k],
            recv_sem=self.recv.at[self.index, at],
            device_id=self.p.to[link],
            device_id_type=LOGICAL,
        )
        self.sent.append((made, cond))
        if cond is None:
            made.start()
        else:
            pl.when(cond)(made.start)

    def wait(self, slot):
        at = self.SLOTS.index(slot) if isinstance(slot, str) else slot
        arrived(self.came.at[at], self.send.at[self.index, 0], self.recv.at[self.index, at], self.p)
        return self.came.at[at]

    def add(self, where, slots):
        parts = [self.wait(s) for s in slots]
        add_into(self.acc.at[where], [self.acc.at[where]] + parts)

    def round(self, r):
        p = self.p
        inner = p.inner
        outer = jnp.logical_not(inner)
        ze, zo, near, far = self.ze, self.zo, p.near, p.far
        if r == 0:
            self.given = pltpu.make_async_remote_copy(
                src_ref=self.part,
                dst_ref=self.acc,
                send_sem=self.send.at[self.index, self.NSEND],
                recv_sem=self.recv.at[self.index, 19],
                device_id=p.to["p"],
                device_id_type=LOGICAL,
            )
            self.given.start()
        if r == 1:
            arrived(self.acc, self.send.at[self.index, 0], self.recv.at[self.index, 19], p)
            self.term.second(self.acc)
            self.go(self.D(far), "S", "Ef", outer)
            self.go(self.D(near), "S", "En", outer)
            self.go(self.X(far), "x", far)
            self.go(self.Y(far), "y", far + 5)
            self.go(self.D(ze), "y", "Fy", outer)
            self.go(self.D(zo), "x", "Fx", outer)
            self.go(self.X(near), "x", near)
            self.go(self.Y(near), "y", near + 5)
            self.go(self.X(zo), "x", zo)
            self.go(self.Y(ze), "y", ze + 5)
        if r == 2:

            @pl.when(inner)
            def _():
                self.add(self.D(far), ["Ef"])
                self.add(self.D(near), ["En"])

            self.go(self.D(far), "K", jnp.where(p.z == 1, self.SLOTS.index("Do"), self.SLOTS.index("De")), inner)
            self.go(self.D(near), "K", jnp.where(p.z == 1, self.SLOTS.index("De"), self.SLOTS.index("Do")), inner)
            parts = [self.wait(far), self.wait(far + 5)]
            add_into(self.acc.at[self.C(far)], [self.acc.at[self.C(far)]] + parts)
            self.go(self.C(far), "S", "Cf", outer)
        if r == 3:

            @pl.when(inner)
            def _():
                self.add(self.D(ze), ["De"])
                self.add(self.D(zo), ["Do"])
                self.add(self.C(far), ["Cf"])

            self.go(self.D(ze), "y", "Fy", inner)
            self.go(self.D(zo), "x", "Fx", inner)
            self.go(self.C(far), "K", "KCs", inner)
            parts = [self.wait(near), self.wait(near + 5)]
            add_into(self.acc.at[self.C(near)], [self.acc.at[self.C(near)]] + parts)
            self.go(self.C(near), "S", "Cn", outer)
        if r == 4:
            self.add(self.X(ze), ["Fy"])
            self.add(self.Y(zo), ["Fx"])
            self.go(self.X(ze), "x", ze)
            self.go(self.Y(zo), "y", zo + 5)

            @pl.when(inner)
            def _():
                self.add(self.C(near), ["Cn"])

            self.go(self.C(near), "K", "KCo", inner)
        if r == 5:
            self.add(self.C(p.sib), [p.sib, p.sib + 5])

            @pl.when(inner)
            def _():
                self.add(self.C(p.sib), ["KCs"])

            self.go(self.C(p.sib), "S", "Co")
        if r == 6:
            slots = [p.z, p.z + 5, "Co"]
            parts = [self.acc.at[self.C(p.z)]] + [self.wait(s) for s in slots]
            add_into(self.out, parts)

            @pl.when(inner)
            def _():
                add_into(self.out, [self.out, self.wait("KCo")])

    def handed(self):
        self.given.wait_send()

    def finish(self):
        for made, cond in self.sent:
            if cond is None:
                made.wait_send()
            else:
                pl.when(cond)(made.wait_send)


def bounds_of(lengths, order):
    total, found = jnp.int32(0), []
    for j in range(lengths.shape[0]):
        total = total + lengths[order[j]]
        found.append(total)
    return found


def segment_at(bounds, places):
    found = jnp.zeros_like(places)
    for bound in bounds:
        found = found + jnp.where(bound <= places, 1, 0)
    return found


def same_segment(bounds, earlier, later):
    same = jnp.int32(0)
    for bound in bounds:
        same = same + jnp.where((bound <= earlier) != (bound <= later), 1, 0)
    return jnp.where((earlier >= 0) & (same == 0), 1.0, 0.0).astype(jnp.float32)


def spans_of(first, bounds, dist, entry, leaving):
    size = dist.shape[0]
    t = lax.broadcasted_iota(jnp.int32, (size, size), 0)
    s = lax.broadcasted_iota(jnp.int32, (size, size), 1)
    same = segment_at(bounds, t + first) == segment_at(bounds, s + first)
    dist[...] = jnp.where(same & (s <= t), t - s, -1).astype(jnp.float32)
    t = lax.broadcasted_iota(jnp.int32, entry.shape, 0)
    here = segment_at(bounds, t + first)
    ahead = segment_at(bounds, jnp.full(entry.shape, first - 1, jnp.int32))
    ahead = jnp.where(jnp.full(entry.shape, first, jnp.int32) == 0, -1, ahead)
    last = segment_at(bounds, jnp.full(entry.shape, first + size - 1, jnp.int32))
    entry[...] = jnp.where(here == ahead, t, -1).astype(jnp.float32)
    leaving[...] = jnp.where(here == last, size - t, -1).astype(jnp.float32)


def decay(distance, rate):
    return jnp.where(distance >= 0, jnp.exp(-rate * distance), 0.0)


def mm(a, b):
    return jnp.dot(a, b, preferred_element_type=jnp.float32)


def mm_nt(a, b):
    return lax.dot_general(a, b, (((1,), (1,)), ((), ())), preferred_element_type=jnp.float32)


def mm_tn(a, b):
    return lax.dot_general(a, b, (((0,), (0,)), ((), ())), preferred_element_type=jnp.float32)


def head_of(h):
    return pl.ds(pl.multiple_of(h * 128, 128), 128)


def norm_scale(values):
    return lax.rsqrt(jnp.mean(values * values, axis=-1, keepdims=True) + EPSILON)


def slope(a):
    sigma = 1.0 / (1.0 + jnp.exp(-a))
    return sigma * (1.0 + a * (1.0 - sigma))


def flat_rows(value):
    return value.astype(jnp.float32).reshape(-1, value.shape[-1]).astype(jnp.bfloat16)


SAVED_BACK = 18


class States:
    PEERS = 10

    def __init__(self, place, bounds, rate, reverse, value, met, planes, ready, out, send, recv):
        self.bounds, self.reverse = bounds, reverse
        self.value, self.met, self.planes, self.ready, self.out = value, met, planes, ready, out
        self.send, self.recv = send, recv
        self.z, self.r = place.z, lax.rem(place.me, 8)
        self.plane = [self.z * 8 + lax.bitwise_xor(self.r, k) for k in range(8)]
        self.level = [lax.rem(self.z + k, 4) * 8 + self.r for k in range(4)]
        self.order = range(7, -1, -1) if reverse else range(8)
        self.step = jnp.exp(jnp.full((1, 128), -SPAN * rate[self.r], jnp.float32))

    def through(self, device):
        return same_segment(self.bounds, device * SPAN - 1, device * SPAN + SPAN - 1)

    def copy(self, src, dst, k, peer):
        return pltpu.make_async_remote_copy(
            src_ref=src,
            dst_ref=dst,
            send_sem=self.send.at[k],
            recv_sem=self.recv.at[k],
            device_id=peer,
            device_id_type=LOGICAL,
        )

    def other(self, k):
        return lax.bitwise_xor(self.r, k)

    def spread(self):
        self.first = [
            self.copy(self.value.at[self.other(k)], self.met.at[self.r], k, self.plane[k])
            for k in range(1, 8)
        ]
        for one in self.first:
            one.start()
        self.met[self.r] = self.value[self.r]

    def total(self):
        for k in range(1, 8):
            self.copy(self.value.at[0], self.met.at[self.other(k)], k, self.plane[k]).wait_recv()
        total = jnp.zeros(self.met.shape[1:], jnp.float32)
        for i in self.order:
            total = self.through(self.z * 8 + i) * self.step * total + self.met[i]
        self.planes[self.z] = total
        self.second = []
        for k in range(1, 4):
            far = self.z - k if self.reverse else self.z + k
            cond = far >= 0 if self.reverse else far <= 3
            made = self.copy(
                self.planes.at[self.z], self.planes.at[self.z], 7 + k, far * 8 + self.r
            )
            self.second.append((made, cond))
            pl.when(cond)(made.start)

    def back(self):
        self.ready[8] = jnp.zeros(self.met.shape[1:], jnp.float32)
        for k in range(3, 0, -1):
            far = self.z + k if self.reverse else self.z - k
            cond = far <= 3 if self.reverse else far >= 0

            @pl.when(cond)
            def _():
                self.copy(
                    self.planes.at[self.z], self.planes.at[far], 7 + k, self.plane[0]
                ).wait_recv()
                kept = jnp.ones((1, 128), jnp.float32)
                for i in range(8):
                    kept = kept * (self.through(far * 8 + i) * self.step)
                self.ready[8] = kept * self.ready[8] + self.planes[far]

        total = self.ready[8]
        for i in self.order:
            self.ready[i] = total
            total = self.through(self.z * 8 + i) * self.step * total + self.met[i]
        self.third = [
            self.copy(self.ready.at[self.other(k)], self.out.at[self.r], 10 + k, self.plane[k])
            for k in range(1, 8)
        ]
        for one in self.third:
            one.start()
        self.out[self.r] = self.ready[self.r]

    def done(self):
        for k in range(1, 8):
            self.copy(self.ready.at[0], self.out.at[self.other(k)], 10 + k, self.plane[k]).wait_recv()

    def finish(self):
        for one in self.first + self.third:
            one.wait_send()
        for made, cond in self.second:
            pl.when(cond)(made.wait_send)


def greet_more(place):
    barrier = pltpu.get_barrier_semaphore()
    r = lax.rem(place.me, 8)
    peers = [place.z * 8 + lax.bitwise_xor(r, k) for k in range(1, 8)]
    peers += [lax.rem(place.z + k, 4) * 8 + r for k in range(1, 4)]
    for peer in peers:
        pl.semaphore_signal(barrier, inc=1, device_id=peer, device_id_type=LOGICAL)
    pl.semaphore_wait(barrier, len(peers))


def forward_kernel(
    lengths,
    order,
    rate,
    tokens,
    cot,
    gain_own,
    s_key,
    s_value,
    s_query,
    s_unit,
    s_output,
    s_left,
    s_right,
    s_down,
    *refs,
):
    f32, bf16 = jnp.float32, jnp.bfloat16
    n = 11
    full, refs = refs[:n], refs[n:]
    saved, refs = refs[:SAVED_BACK], refs[SAVED_BACK:]
    kept, refs = refs[:SAVED_BACK], refs[SAVED_BACK:]
    (hidden_rows, keys, values, queries, key_pre, query_pre, unit_pre, probs) = kept[:8]
    (attended, state_low, mixed_rows, middle, second_rows, left, right, product) = kept[8:16]
    gain, down_term = kept[16:]
    (hidden, mixed, second, turned) = refs[:4]
    (dist, entry, leaving, gains, value, met, planes, ready, arriving) = refs[4:13]
    (narrow, wide, send, recv, state_send, state_recv, load_sem, save_sem) = refs[13:]
    place = Place()
    half = s_left.shape[1] // 2
    own = [s_key, s_value, s_query, s_unit, gain_own, s_output]
    own += [s_left.at[:, pl.ds(0, half)], s_left.at[:, pl.ds(half, half)]]
    own += [s_right.at[:, pl.ds(0, half)], s_right.at[:, pl.ds(half, half)], s_down]
    greet_more(place)
    made = [Gather(place, own[i], full[i], send, recv, i) for i in range(n)]
    bounds = bounds_of(lengths, order)
    states = States(
        place, bounds, rate, False, value, met, planes, ready, arriving, state_send, state_recv
    )
    slots = {0: narrow.at[0], 1: narrow.at[1], 2: narrow.at[0], 3: narrow.at[1], 4: gains}
    slots.update({5: narrow.at[0], 6: wide.at[0], 7: wide.at[1], 8: wide.at[0], 9: wide.at[1]})
    saves = []

    def save(*numbers):
        for i in numbers:
            copy = pltpu.make_async_copy(kept[i], saved[i], save_sem.at[i])
            copy.start()
            saves.append(copy)

    def weight(i):
        ref = slots[i]
        return ref[...].reshape(-1, ref.shape[-1])

    def turn(ref, rows):
        @pl.loop(0, 8)
        def _(i):
            block = ref[:, head_of(i)].astype(f32).T
            rows[i // 2, i % 2] = block.reshape((2, 2) + rows.shape[4:]).astype(bf16)

    def start():
        x = tokens[...].astype(f32)
        hidden[...] = (x * norm_scale(x)).astype(bf16)
        spans_of(place.me * SPAN, bounds, dist, entry, leaving)
        turn(hidden, hidden_rows)
        save(0)

    def project(i, pre, low):
        out = mm(hidden[...], weight(i))
        if pre is not None:
            pre[...] = out
            out = out / (1.0 + jnp.exp(-out))
        low[...] = out.astype(bf16)

    def key():
        project(0, key_pre, keys)
        save(1, 4)

    def increments():
        project(1, None, values)

        @pl.loop(0, 8)
        def _(h):
            at = head_of(h)
            held = (keys[:, at].astype(f32) * decay(leaving[...], rate[h])).astype(bf16)
            value[h] = mm_tn(held, values[:, at])

        states.spread()
        save(2)

    def query():
        project(2, query_pre, queries)

        @pl.loop(0, 8)
        def _(h):
            at = head_of(h)
            scores = mm_nt(queries[:, at], keys[:, at])
            low = (scores * decay(dist[...], rate[h])).astype(bf16)
            probs[h] = low
            attended[:, at] = mm(low, values[:, at])

        save(3, 5, 7)

    def unit():
        unit_pre[...] = mm(hidden[...], weight(3))
        save(6)

    def attend():
        gain[...] = jnp.sum(gains[...].reshape(-1, 8, 128), axis=0)

        @pl.loop(0, 8)
        def _(h):
            at = head_of(h)
            low = arriving[h].astype(bf16)
            state_low[h] = low
            held = (queries[:, at].astype(f32) * decay(entry[...], rate[h])).astype(bf16)
            out = attended[:, at] + mm(held, low)
            attended[:, at] = out
            mixed[:, at] = (
                out * norm_scale(out) * gain[pl.ds(h, 1), :] * unit_pre[:, at]
            ).astype(bf16)

        turn(mixed, mixed_rows)
        save(8, 9, 10, 16)

    def output():
        out = tokens[...].astype(f32) + mm(mixed[...], weight(5))
        middle[...] = out
        second[...] = (out * norm_scale(out)).astype(bf16)
        turn(second, second_rows)
        save(11, 12)

    def gate(i, side, part):
        side[:, pl.ds(part * half, half)] = mm(second[...], weight(i))

    def multiply():
        cols = cot.shape[1] // 2

        @pl.loop(0, 2)
        def _(j):
            @pl.loop(0, half // 128)
            def _(i):
                at = pl.ds(pl.multiple_of(j * half + i * 128, 128), 128)
                block = (left[:, at] * right[:, at]).astype(bf16).astype(f32)
                turned[pl.ds(pl.multiple_of(i * 128, 128), 128), :] = block.T

            both = pl.ds(2 * j, 2)
            block = turned[...].reshape((2,) + product.shape[1:])
            product[both] = block.astype(bf16)
            rows = flat_rows(product[both, :, :, place.c1])
            for m in range(2):
                term = mm(rows, cot[:, pl.ds(m * cols, cols)])
                down_term[m, both] = term.reshape((2,) + down_term.shape[2:]).astype(bf16)

        save(13, 14, 15, 17)

    tasks = {0: [start], 7: [key], 8: [increments], 9: [states.total, query], 10: [states.back, unit]}
    tasks[11] = [states.done, attend]
    tasks[12] = [output]
    tasks[13] = [lambda: gate(6, left, 0)]
    tasks[14] = [lambda: gate(7, left, 1)]
    tasks[15] = [lambda: gate(8, right, 0)]
    tasks[16] = [lambda: gate(9, right, 1), multiply]
    loads = {}
    for step in range(n + 6):
        for r in range(6):
            if 0 <= step - r < n:
                made[step - r].round(r)
        i = step - 6
        if i - 1 in loads:
            loads[i - 1].wait()
        for task in tasks.get(step, []):
            task()
        if 0 <= i < n:
            made[i].pairs()
        if i in slots:
            loads[i] = pltpu.make_async_copy(full[i], slots[i], load_sem.at[i])
            loads[i].start()
    for one in made:
        one.finish()
    states.finish()
    for copy in saves:
        copy.wait()


def forward(lengths, order, rate, tokens, cot, gain_tile, shards):
    f32, bf16 = jnp.float32, jnp.bfloat16
    size, width = tokens.shape
    wide = shards[5].shape[1]
    half = wide // 2
    blocks = [(s.shape, s.dtype) for s in shards[:4]] + [(gain_tile.shape, f32)]
    blocks += [(shards[4].shape, bf16)] + [((32, half), bf16)] * 4 + [(shards[7].shape, bf16)]
    square, cube = (size, width), (8, 128, 128)
    rows, down_rows = shards[4].shape[0], shards[7].shape[0]
    across = ((4, 2, 2, 2, rows, size), bf16)
    kept = [across] + [(square, bf16)] * 3 + [(square, f32)] * 3 + [((8, size, size), bf16)]
    kept += [(square, f32), (cube, bf16), across, (square, f32), across]
    kept += [((size, wide), f32)] * 2 + [((4, 2, 2, 2, down_rows, size), bf16), ((8, 128), f32)]
    kept += [((2, 4, 2, 2, down_rows, width // 2), bf16)]
    vmem, hbm = pl.BlockSpec(memory_space=pltpu.VMEM), pl.BlockSpec(memory_space=pltpu.HBM)
    smem = pl.BlockSpec(memory_space=pltpu.SMEM)
    n = len(blocks)
    out = pl.pallas_call(
        forward_kernel,
        out_shape=[jax.ShapeDtypeStruct((4, 2, 2, 2) + s, t) for s, t in blocks]
        + [jax.ShapeDtypeStruct(s, t) for s, t in kept],
        in_specs=[smem] * 3 + [vmem] * 11,
        out_specs=[hbm] * (n + len(kept)),
        scratch_shapes=[pltpu.VMEM(s, t) for s, t in kept]
        + [pltpu.VMEM(square, bf16)] * 3
        + [pltpu.VMEM((half, size), f32)]
        + [pltpu.VMEM((size, size), f32), pltpu.VMEM((size, 128), f32), pltpu.VMEM((size, 128), f32)]
        + [pltpu.VMEM((4, 2, 2, 2, 8, 128), f32)]
        + [pltpu.VMEM(cube, f32), pltpu.VMEM(cube, f32), pltpu.VMEM((4, 128, 128), f32)]
        + [pltpu.VMEM((9, 128, 128), f32), pltpu.VMEM(cube, f32)]
        + [
            pltpu.VMEM((2, 4, 2, 2, 2, 32, width), bf16),
            pltpu.VMEM((2, 4, 2, 2, 2, 32, half), bf16),
            pltpu.SemaphoreType.DMA((n, Gather.NSEND + 1)),
            pltpu.SemaphoreType.DMA((n, Gather.NRECV)),
            pltpu.SemaphoreType.DMA((18,)),
            pltpu.SemaphoreType.DMA((18,)),
            pltpu.SemaphoreType.DMA((n,)),
            pltpu.SemaphoreType.DMA((len(kept),)),
        ],
        compiler_params=pltpu.CompilerParams(
            collective_id=0, has_side_effects=True, vmem_limit_bytes=VMEM_LIMIT
        ),
        name="forward",
    )(lengths, order, rate, tokens, cot, gain_tile, *shards)
    return out[:n], out[n:]

def backward_kernel(lengths, order, rate, tokens, cot, *refs):
    f32, bf16 = jnp.float32, jnp.bfloat16
    n = 12
    saved, refs = refs[:SAVED_BACK], refs[SAVED_BACK:]
    (h_hidden, h_keys, h_values, h_queries, h_key_pre, h_query_pre, h_unit_pre, h_probs) = saved[:8]
    (h_attended, h_state_low, h_mixed, h_middle, h_second, h_left, h_right, h_product) = saved[8:16]
    h_gain, h_down = saved[16:]
    w_in, refs = refs[:10], refs[10:]
    (w_key, w_value, w_query, w_unit, w_output, w_l0, w_l1, w_r0, w_r1, w_down) = w_in
    out, result_out, tokens_out, refs = refs[:n], refs[n], refs[n + 1], refs[n + 2 :]
    acc, came, refs = refs[:n], refs[n : 2 * n], refs[2 * n :]
    (part, gain_part, wd, down, wl, left, right, f1, f2, f3, f4) = refs[:11]
    (branch, ga, gup, gkp, gvp, result, glp, grp, rows, mixed, product) = refs[11:22]
    (probs, state_low, gain, gg, dist, entry, leaving) = refs[22:29]
    (value, met, planes, ready, arriving) = refs[29:34]
    (send, recv, state_send, state_recv, load_sem) = refs[34:]
    place = Place()
    half = h_left.shape[1] // 2
    width = tokens.shape[1]
    left_w, right_w = left.at[:, pl.ds(0, width)], right.at[:, pl.ds(0, width)]
    queries, keys = glp.at[:, pl.ds(0, width)], glp.at[:, pl.ds(width, width)]
    values, gqp = grp.at[:, pl.ds(0, width)], grp.at[:, pl.ds(width, width)]
    wn = wl.at[:, :, :, :, :, pl.ds(0, width)]
    greet_more(place)
    bounds = bounds_of(lengths, order)
    states = States(
        place, bounds, rate, True, value, met, planes, ready, arriving, state_send, state_recv
    )
    loads = {}

    def load(name, src, dst):
        copy = pltpu.make_async_copy(src, dst, load_sem.at[len(loads)])
        loads[name] = copy
        copy.start()

    def loaded(*names):
        for name in names:
            loads[name].wait()

    def weight(cols):
        return wl[:, :, :, :, :, pl.ds(0, cols)].reshape(-1, cols)

    def side(i):
        return pl.ds(i * half, half)

    def product_of(i):
        return flat_rows(product[pl.ds(2 * i, 2)])

    class Piece:
        def __init__(self, rows, core_rows, grad, cols, need=()):
            self.rows, self.core_rows, self.grad, self.cols, self.need = rows, core_rows, grad, cols, need

        def term(self, zh, core):
            lhs = self.rows[pl.ds(zh * 2, 2), :, :, core]
            lhs = flat_rows(lhs) if self.core_rows % 16 else lhs.reshape(-1, lhs.shape[-1])
            out = mm(lhs, self.grad[...])
            return out.reshape(2, 2, 2, self.core_rows, self.cols)

        def first(self):
            @pl.loop(0, 2)
            def _(zh):
                part[pl.ds(zh * 2, 2), :, :, :, pl.ds(0, self.cols)] = self.term(
                    zh, place.c1
                ).astype(bf16)

        def second(self, acc):
            @pl.loop(0, 2)
            def _(zh):
                at = pl.ds(zh * 2, 2)
                acc[at] = (acc[at].astype(f32) + self.term(zh, place.c)).astype(bf16)

    class Gain:
        def first(self):
            gain_part[...] = jnp.broadcast_to(gg[...][None, None, None], gain_part.shape)

        def second(self, acc):
            acc[...] = acc[...] + gg[...][None, None, None]

    wide = part.at[:, :, :, :, pl.ds(0, half)]
    narrow = part.at[:, :, :, :, pl.ds(0, width)]
    cols = width // 2
    pieces = [(h_down.at[m], Piece(product, 88, cot.at[:, pl.ds(m * cols, cols)], cols)) for m in (0, 1)]
    pieces += [(wide, Piece(rows, 32, glp.at[:, side(i)], half)) for i in (0, 1)]
    pieces += [(wide, Piece(rows, 32, grp.at[:, side(i)], half)) for i in (0, 1)]
    pieces += [(narrow, Piece(mixed, 32, branch, width)), (gain_part, Gain())]
    pieces += [(narrow, Piece(rows, 32, g, width)) for g in (gup, gqp, gvp, gkp)]
    made = [
        Scatter(place, pieces[i][0], acc[i], pieces[i][1], came[i], out[i], send, recv, i)
        for i in range(n)
    ]

    def begin():
        spans_of(place.me * SPAN, bounds, dist, entry, leaving)

    def gates(i):
        loaded("down%d" % i, "left%d" % i, "right%d" % i)
        pair = 2 * wd.shape[4]

        @pl.loop(0, 8)
        def _(k):
            at = pl.ds(pl.multiple_of(k * pair, 16), pair)
            down[at, :] = flat_rows(wd[k // 4, (k // 2) % 2, k % 2])

        grad = mm_nt(cot[...], down[...])
        glp[:, side(i)] = (grad * right[...]).astype(bf16)
        grp[:, side(i)] = (grad * left[...]).astype(bf16)
        if i == 0:
            loaded("middle")
            f3[...] = f2[...] + mm_tn(product_of(0), down[...])
            load("down1", w_down.at[pl.ds(2, 2)], wd)
            load("left1", h_left.at[:, side(1)], left)
            load("right1", h_right.at[:, side(1)], right)
        else:
            result[...] = (f3[...] + mm_tn(product_of(1), down[...])).astype(bf16)
            load("unit_pre", h_unit_pre, left_w)
            load("result", result, result_out)

    def second_part(name, grad, i, following, start):
        loaded(name)
        term = mm_nt(grad[:, side(i)], weight(half))
        f1[...] = term if start else f1[...] + term
        load(*following)

    def middle():
        @pl.loop(0, SPAN // 16)
        def _(i):
            at = pl.ds(pl.multiple_of(i * 16, 16), 16)
            x, g = f2[at, :], f1[at, :]
            scale = norm_scale(x)
            unit = x * scale
            grad = cot[at, :].astype(f32) + scale * (
                g - unit * jnp.mean(g * unit, axis=-1, keepdims=True)
            )
            f3[at, :] = grad
            branch[at, :] = grad.astype(bf16)

        load("attended", h_attended, f2)

    def spare():
        load("queries", h_queries, queries)
        load("keys", h_keys, keys)
        load("values", h_values, values)
        load("hidden", h_hidden, rows)

    def attention():
        loaded("output")
        f1[...] = mm_nt(branch[...], weight(width))
        load("unit", w_unit, wn)
        loaded("attended", "unit_pre", "queries", "gain")

        @pl.loop(0, 8)
        def _(h):
            at = head_of(h)
            att, up, gm = f2[:, at], left_w[:, at], f1[:, at]
            scale = norm_scale(att)
            unit = att * scale
            row = gain[pl.ds(h, 1), :]
            gated = gm * up
            gg[pl.ds(h, 1), :] = jnp.sum(gated * unit, axis=0, keepdims=True)
            gup[:, at] = (gm * unit * row).astype(bf16)
            g = gated * row
            low = (
                scale * (g - unit * jnp.mean(g * unit, axis=-1, keepdims=True))
            ).astype(bf16)
            ga[:, at] = low
            held = (queries[:, at].astype(f32) * decay(entry[...], rate[h])).astype(bf16)
            value[h] = mm_tn(held, low)

        states.spread()
        load("key_pre", h_key_pre, f2)

    def scores():
        loaded("keys", "values", "query_pre", "probs", "state_low")

        @pl.loop(0, 8)
        def _(h):
            at = head_of(h)
            low = ga[:, at]
            grads = (mm_nt(low, values[:, at]) * decay(dist[...], rate[h])).astype(bf16)
            grad_q = mm(grads, keys[:, at])
            grad_q = grad_q + mm_nt(low, state_low[h]) * decay(entry[...], rate[h])
            gqp[:, at] = (grad_q * slope(f4[:, at])).astype(bf16)
            f1[:, at] = mm_tn(grads, queries[:, at])
            right_w[:, at] = mm_tn(probs[h], low)

        states.total()

    def hidden_part(name, grad, following, start):
        loaded(name)
        term = mm_nt(grad[...], weight(width))
        f4[...] = term if start else f4[...] + term
        if following:
            load(*following)

    def unit_rest():
        states.back()
        hidden_part("unit", gup, ("query", w_query, wn), True)

    def last_grads():
        hidden_part("query", gqp, ("value", w_value, wn), False)
        states.done()
        loaded("key_pre")

        @pl.loop(0, 8)
        def _(h):
            at = head_of(h)
            grad = arriving[h].astype(bf16)
            fall = decay(leaving[...], rate[h])
            held = (keys[:, at].astype(f32) * fall).astype(bf16)
            grad_k = f1[:, at] + mm_nt(values[:, at], grad) * fall
            gkp[:, at] = (grad_k * slope(f2[:, at])).astype(bf16)
            gvp[:, at] = (right_w[:, at] + mm(held, grad)).astype(bf16)

    def value_rest():
        hidden_part("value", gvp, ("key", w_key, wn), False)

    def inputs():
        hidden_part("key", gkp, None, False)

        @pl.loop(0, SPAN // 16)
        def _(i):
            at = pl.ds(pl.multiple_of(i * 16, 16), 16)
            x, g = tokens[at, :].astype(f32), f4[at, :]
            scale = norm_scale(x)
            unit = x * scale
            f3[at, :] = f3[at, :] + scale * (g - unit * jnp.mean(g * unit, axis=-1, keepdims=True))

        load("tokens", f3, tokens_out)

    before = {1: lambda: loaded("product"), 2: lambda: loaded("second"), 6: lambda: loaded("mixed")}
    before[8] = lambda: loaded("hidden")
    tasks = {0: [begin], 1: [lambda: gates(0)], 2: [lambda: gates(1)]}
    tasks[3] = [lambda: second_part("l0", glp, 0, ("l1", w_l1, wl), True)]
    tasks[4] = [lambda: second_part("l1", glp, 1, ("r0", w_r0, wl), False)]
    tasks[5] = [
        lambda: second_part("r0", grp, 0, ("r1", w_r1, wl), False),
        lambda: second_part("r1", grp, 1, ("output", w_output, wn), False),
        middle,
    ]
    tasks[6] = [spare, attention]
    tasks[7] = [scores]
    tasks[8] = [unit_rest]
    tasks[9] = [last_grads]
    tasks[10] = [value_rest]
    tasks[11] = [inputs]
    load("product", h_product, product)
    load("down0", w_down.at[pl.ds(0, 2)], wd)
    load("left0", h_left.at[:, side(0)], left)
    load("right0", h_right.at[:, side(0)], right)
    load("middle", h_middle, f2)
    load("second", h_second, rows)
    load("l0", w_l0, wl)
    load("mixed", h_mixed, mixed)
    load("gain", h_gain, gain)
    load("query_pre", h_query_pre, f4)
    load("probs", h_probs, probs)
    load("state_low", h_state_low, state_low)
    for step in range(n + 6):
        if step < n:
            if step in before:
                before[step]()
            if step > 2:
                made[step - 1].handed()
            if step > 1:
                pieces[step][1].first()
            made[step].round(0)
        if 0 < step <= n:
            made[step - 1].round(1)
        for task in tasks.get(step, []):
            task()
        for r in range(2, 7):
            if 0 <= step - r < n:
                made[step - r].round(r)
    for i, one in enumerate(made):
        if i < 2 or i == n - 1:
            one.handed()
        one.finish()
    states.finish()
    loaded("result", "tokens")


def backward(lengths, order, rate, tokens, cot, saved, weights):
    f32, bf16 = jnp.float32, jnp.bfloat16
    size, width = tokens.shape
    wide = saved[13].shape[1]
    half = wide // 2
    rows = width // 32
    down_rows = wide // 32
    blocks = [((down_rows, width // 2), bf16)] * 2 + [((rows, half), bf16)] * 4
    blocks += [((rows, width), bf16), ((8, 128), f32)] + [((rows, width), bf16)] * 4
    n = len(blocks)
    square, cube = (size, width), (8, 128, 128)
    vmem, hbm = pl.BlockSpec(memory_space=pltpu.VMEM), pl.BlockSpec(memory_space=pltpu.HBM)
    smem = pl.BlockSpec(memory_space=pltpu.SMEM)
    out = pl.pallas_call(
        backward_kernel,
        out_shape=[jax.ShapeDtypeStruct(b, f32) for b, _ in blocks]
        + [jax.ShapeDtypeStruct(square, bf16), jax.ShapeDtypeStruct(square, f32)],
        in_specs=[smem] * 3 + [vmem] * 2 + [hbm] * (len(saved) + len(weights)),
        out_specs=[vmem] * n + [hbm] * 2,
        scratch_shapes=[pltpu.VMEM((4, 2, 2) + b, t) for b, t in blocks]
        + [pltpu.VMEM((19,) + b, t) for b, t in blocks]
        + [
            pltpu.VMEM((4, 2, 2, rows, half), bf16),
            pltpu.VMEM((4, 2, 2, 8, 128), f32),
            pltpu.VMEM((2, 2, 2, 2, down_rows, width), bf16),
            pltpu.VMEM((half, width), bf16),
            pltpu.VMEM((4, 2, 2, 2, rows, half), bf16),
            pltpu.VMEM((size, half), f32),
            pltpu.VMEM((size, half), f32),
        ]
        + [pltpu.VMEM(square, f32)] * 4
        + [pltpu.VMEM(square, bf16)] * 6
        + [pltpu.VMEM((size, wide), bf16)] * 2
        + [pltpu.VMEM((4, 2, 2, 2, rows, size), bf16)] * 2
        + [pltpu.VMEM((4, 2, 2, 2, down_rows, size), bf16)]
        + [pltpu.VMEM((8, size, size), bf16), pltpu.VMEM(cube, bf16)]
        + [pltpu.VMEM((8, 128), f32)] * 2
        + [pltpu.VMEM((size, size), f32), pltpu.VMEM((size, 128), f32), pltpu.VMEM((size, 128), f32)]
        + [pltpu.VMEM(cube, f32), pltpu.VMEM(cube, f32), pltpu.VMEM((4, 128, 128), f32)]
        + [pltpu.VMEM((9, 128, 128), f32), pltpu.VMEM(cube, f32)]
        + [
            pltpu.SemaphoreType.DMA((n, Scatter.NSEND + 1)),
            pltpu.SemaphoreType.DMA((n, Scatter.NRECV)),
            pltpu.SemaphoreType.DMA((18,)),
            pltpu.SemaphoreType.DMA((18,)),
            pltpu.SemaphoreType.DMA((40,)),
        ],
        compiler_params=pltpu.CompilerParams(
            collective_id=3, has_side_effects=True, vmem_limit_bytes=67000000
        ),
        name="backward",
    )(lengths, order, rate, tokens, cot, *saved, *weights)
    return out[:n], out[n], out[n + 1]


def entering(value, axis, combine, identity, reverse):
    length, here = (lax.axis_size(axis), lax.axis_index(axis))
    everything = jax.tree.map(lambda part: lax.all_gather(part, axis), value)
    start = jax.tree.map(
        lambda part, zero: jnp.broadcast_to(jnp.asarray(zero, part.dtype), part.shape),
        value,
        identity,
    )

    def hop(k, before):
        at = length - 1 - k if reverse else k
        reached = at > here if reverse else at < here
        new = combine(before, jax.tree.map(lambda part: part[at], everything))
        return jax.tree.map(lambda a, b: jnp.where(reached, a, b), new, before)

    return lax.fori_loop(0, length, hop, start)


def segment_of(places, lengths, seq_order):
    number = lengths.shape[0]
    picked = seq_order[:, None] == jnp.arange(number, dtype=jnp.int32)[None, :]
    packed = jnp.sum(jnp.where(picked, lengths[None, :], 0), axis=1, dtype=jnp.int32)
    bounds = jnp.cumsum(packed, dtype=jnp.int32)
    found = jnp.sum((bounds[None, :] <= places[:, None]).astype(jnp.int32), axis=1, dtype=jnp.int32)
    return jnp.where(places < 0, -1, found)


def decay_tables(segments, before, rate, block):
    length = segments.shape[0]
    count = length // block
    spans = segments.reshape(count, block)
    priors = jnp.concatenate([before.reshape(1), spans[:-1, -1]])
    steps = jnp.arange(block, dtype=jnp.int32)
    distance = steps[:, None] - steps[None, :]
    same = (spans[:, :, None] == spans[:, None, :]) & (distance >= 0)[None]
    powers = jnp.exp(-rate[:, None, None] * jnp.maximum(distance, 0).astype(jnp.float32)[None])
    within = jnp.where(same[:, None], powers[None], 0.0)
    entry = jnp.where(
        (spans == priors[:, None])[:, :, None],
        jnp.exp(-rate[None, :] * steps.astype(jnp.float32)[:, None])[None],
        0.0,
    )
    leaving = jnp.where(
        (spans == spans[:, -1:])[:, :, None],
        jnp.exp(-rate[None, :] * (block - steps).astype(jnp.float32)[:, None])[None],
        0.0,
    )
    passing = jnp.where((spans[:, -1] == priors)[:, None], jnp.exp(-rate * block)[None], 0.0)
    offsets = (jnp.arange(count, dtype=jnp.int32) * block).astype(jnp.float32)
    arrival = jnp.where(
        (priors == before)[:, None], jnp.exp(-rate[None, :] * offsets[:, None]), 0.0
    )
    through = jnp.where(segments[-1] == before, jnp.exp(-rate * length), 0.0)
    return (within, entry, leaving, passing, arrival, through)


def chain_states(earlier, later):
    return (earlier[0] * later[0], later[0][:, None, None] * earlier[1] + later[1])


def silu_slope(values):
    sigma = jax.nn.sigmoid(values)
    return sigma * (1.0 + values * (1.0 - sigma))


def row_scale(values):
    return lax.rsqrt(jnp.mean(values * values, axis=-1, keepdims=True) + EPSILON)


def body(
    tokens,
    lengths,
    seq_order,
    decay_rate,
    w_query,
    w_key,
    w_value,
    w_unit,
    w_output,
    norm_gain,
    w_left,
    w_right,
    w_down,
    cotangent,
):
    f32 = jnp.float32
    bf16 = jnp.bfloat16
    length, width = tokens.shape
    heads = decay_rate.shape[0]
    head_size = width // heads
    count = length // SPAN
    first = lax.axis_index(AXIS) * length
    places = first + jnp.arange(length, dtype=jnp.int32)
    segments = segment_of(places, lengths, seq_order)
    before = segment_of(jnp.reshape(first - 1, (1,)), lengths, seq_order)[0]
    within, entry, leaving, passing, arrival, through = decay_tables(
        segments, before, decay_rate, SPAN
    )
    attention_set = (
        lax.all_gather(w_query, AXIS, axis=0, tiled=True),
        lax.all_gather(w_key, AXIS, axis=0, tiled=True),
        lax.all_gather(w_value, AXIS, axis=0, tiled=True),
        lax.all_gather(w_unit, AXIS, axis=0, tiled=True),
        lax.all_gather(w_output, AXIS, axis=0, tiled=True),
        lax.all_gather(norm_gain, AXIS, axis=0, tiled=True),
    )
    feed_set = (
        lax.all_gather(w_left, AXIS, axis=0, tiled=True),
        lax.all_gather(w_right, AXIS, axis=0, tiled=True),
        lax.all_gather(w_down, AXIS, axis=0, tiled=True),
    )
    full_query, full_key, full_value, full_unit, full_output, full_gain = attention_set
    full_left, full_right, full_down = feed_set
    inputs = tokens.astype(f32)
    first_scale = row_scale(inputs)
    normed = inputs * first_scale
    hidden = normed.astype(bf16)
    query_pre = jnp.dot(hidden, full_query, preferred_element_type=f32)
    key_pre = jnp.dot(hidden, full_key, preferred_element_type=f32)
    value_pre = jnp.dot(hidden, full_value, preferred_element_type=f32)
    unit_pre = jnp.dot(hidden, full_unit, preferred_element_type=f32)
    block_shape = (count, SPAN, heads, head_size)
    query_blocks = jax.nn.silu(query_pre).astype(bf16).reshape(block_shape)
    key_blocks = jax.nn.silu(key_pre).astype(bf16).reshape(block_shape)
    value_blocks = value_pre.astype(bf16).reshape(block_shape)
    scores = jnp.einsum("nthe,nshe->nhts", query_blocks, key_blocks, preferred_element_type=f32)
    mixing = (scores * within).astype(bf16)
    local_out = jnp.einsum("nhts,nshe->nthe", mixing, value_blocks, preferred_element_type=f32)
    keys_held = (key_blocks * leaving[..., None]).astype(bf16)
    increments = jnp.einsum("nshe,nshf->nhef", keys_held, value_blocks, preferred_element_type=f32)
    local_states = [jnp.zeros((heads, head_size, head_size), f32)]
    local_states.append(passing[0][:, None, None] * local_states[-1] + increments[0])
    end_state = local_states[count]
    start_pair = (jnp.ones_like(through), jnp.zeros_like(end_state))
    arriving = entering((through, end_state), AXIS, chain_states, start_pair, False)[1]
    states = jnp.stack(local_states[:count]) + arrival[:, :, None, None] * arriving[None]
    state_low = states.astype(bf16)
    query_held = (query_blocks * entry[..., None]).astype(bf16)
    attended = local_out + jnp.einsum(
        "nthe,nhef->nthf", query_held, state_low, preferred_element_type=f32
    )
    attended_heads = attended.reshape(length, heads, head_size)
    head_scale = row_scale(attended_heads)
    unit_norm = (attended_heads * head_scale).reshape(length, width)
    gain = full_gain.astype(f32)
    gated = unit_norm * gain
    mixed_in = (gated * unit_pre).astype(bf16)
    middle = inputs + jnp.dot(mixed_in, full_output, preferred_element_type=f32)
    second_scale = row_scale(middle)
    second_unit = middle * second_scale
    second = second_unit.astype(bf16)
    left_pre = jnp.dot(second, full_left, preferred_element_type=f32)
    right_pre = jnp.dot(second, full_right, preferred_element_type=f32)
    product = (left_pre * right_pre).astype(bf16)
    result = (middle + jnp.dot(product, full_down, preferred_element_type=f32)).astype(bf16)
    back_feed = (
        lax.all_gather(w_left, AXIS, axis=0, tiled=True),
        lax.all_gather(w_right, AXIS, axis=0, tiled=True),
        lax.all_gather(w_down, AXIS, axis=0, tiled=True),
    )
    back_left, back_right, back_down = back_feed
    grad_product = jnp.einsum("td,fd->tf", cotangent, back_down, preferred_element_type=f32)
    grad_left_pre = (grad_product * right_pre).astype(bf16)
    grad_right_pre = (grad_product * left_pre).astype(bf16)
    grad_w_down = jnp.einsum("tf,td->fd", product, cotangent, preferred_element_type=f32)
    grad_w_left = jnp.einsum("td,tf->df", second, grad_left_pre, preferred_element_type=f32)
    grad_w_right = jnp.einsum("td,tf->df", second, grad_right_pre, preferred_element_type=f32)
    feed_grads = (
        lax.psum_scatter(grad_w_left, AXIS, scatter_dimension=0, tiled=True),
        lax.psum_scatter(grad_w_right, AXIS, scatter_dimension=0, tiled=True),
        lax.psum_scatter(grad_w_down, AXIS, scatter_dimension=0, tiled=True),
    )
    grad_second = jnp.einsum(
        "tf,df->td", grad_left_pre, back_left, preferred_element_type=f32
    ) + jnp.einsum("tf,df->td", grad_right_pre, back_right, preferred_element_type=f32)
    grad_middle = cotangent.astype(f32) + second_scale * (
        grad_second - second_unit * jnp.mean(grad_second * second_unit, axis=-1, keepdims=True)
    )
    back_attention = (
        lax.all_gather(w_query, AXIS, axis=0, tiled=True),
        lax.all_gather(w_key, AXIS, axis=0, tiled=True),
        lax.all_gather(w_value, AXIS, axis=0, tiled=True),
        lax.all_gather(w_unit, AXIS, axis=0, tiled=True),
        lax.all_gather(w_output, AXIS, axis=0, tiled=True),
        lax.all_gather(norm_gain, AXIS, axis=0, tiled=True),
    )
    back_query, back_key, back_value, back_unit, back_output, back_gain = back_attention
    grad_branch = grad_middle.astype(bf16)
    grad_w_output = jnp.einsum(TD_TE, mixed_in, grad_branch, preferred_element_type=f32)
    grad_mixed = jnp.einsum(TE_DE, grad_branch, back_output, preferred_element_type=f32)
    grad_gated = grad_mixed * unit_pre
    grad_unit_pre = (grad_mixed * gated).astype(bf16)
    grad_gain = jnp.sum(grad_gated * unit_norm, axis=0)
    grad_norm_heads = (grad_gated * back_gain.astype(f32)).reshape(length, heads, head_size)
    norm_heads = unit_norm.reshape(length, heads, head_size)
    grad_att = head_scale * (
        grad_norm_heads
        - norm_heads * jnp.mean(grad_norm_heads * norm_heads, axis=-1, keepdims=True)
    )
    grad_att_blocks = grad_att.astype(bf16).reshape(block_shape)
    grad_mixing = jnp.einsum(
        "nthf,nshf->nhts", grad_att_blocks, value_blocks, preferred_element_type=f32
    )
    grad_scores = (grad_mixing * within).astype(bf16)
    grad_query_blocks = (
        jnp.einsum("nhts,nshe->nthe", grad_scores, key_blocks, preferred_element_type=f32)
        + jnp.einsum("nthf,nhef->nthe", grad_att_blocks, state_low, preferred_element_type=f32)
        * entry[..., None]
    )
    grad_key_blocks = jnp.einsum(
        "nhts,nthe->nshe", grad_scores, query_blocks, preferred_element_type=f32
    )
    grad_value_blocks = jnp.einsum(
        "nhts,nthf->nshf", mixing, grad_att_blocks, preferred_element_type=f32
    )
    direct = jnp.einsum("nthe,nthf->nhef", query_held, grad_att_blocks, preferred_element_type=f32)
    leaving_sum = jnp.sum(arrival[:, :, None, None] * direct, axis=0)
    later = entering((through, leaving_sum), AXIS, chain_states, start_pair, True)[1]
    next_grads = [later]
    grad_increment = jnp.stack(next_grads[::-1]).astype(bf16)
    grad_keys_held = jnp.einsum(
        "nhef,nshf->nshe", grad_increment, value_blocks, preferred_element_type=f32
    )
    grad_key_blocks = grad_key_blocks + grad_keys_held * leaving[..., None]
    grad_value_blocks = grad_value_blocks + jnp.einsum(
        "nshe,nhef->nshf", keys_held, grad_increment, preferred_element_type=f32
    )
    grad_query_pre = (grad_query_blocks.reshape(length, width) * silu_slope(query_pre)).astype(bf16)
    grad_key_pre = (grad_key_blocks.reshape(length, width) * silu_slope(key_pre)).astype(bf16)
    grad_value_pre = grad_value_blocks.reshape(length, width).astype(bf16)
    grad_w_query = jnp.einsum(TD_TE, hidden, grad_query_pre, preferred_element_type=f32)
    grad_w_key = jnp.einsum(TD_TE, hidden, grad_key_pre, preferred_element_type=f32)
    grad_w_value = jnp.einsum(TD_TE, hidden, grad_value_pre, preferred_element_type=f32)
    grad_w_unit = jnp.einsum(TD_TE, hidden, grad_unit_pre, preferred_element_type=f32)
    attention_grads = (
        lax.psum_scatter(grad_w_query, AXIS, scatter_dimension=0, tiled=True),
        lax.psum_scatter(grad_w_key, AXIS, scatter_dimension=0, tiled=True),
        lax.psum_scatter(grad_w_value, AXIS, scatter_dimension=0, tiled=True),
        lax.psum_scatter(grad_w_unit, AXIS, scatter_dimension=0, tiled=True),
        lax.psum_scatter(grad_w_output, AXIS, scatter_dimension=0, tiled=True),
        lax.psum_scatter(grad_gain, AXIS, scatter_dimension=0, tiled=True),
    )
    grad_hidden = (
        jnp.einsum(TE_DE, grad_query_pre, back_query, preferred_element_type=f32)
        + jnp.einsum(TE_DE, grad_key_pre, back_key, preferred_element_type=f32)
        + jnp.einsum(TE_DE, grad_value_pre, back_value, preferred_element_type=f32)
        + jnp.einsum(TE_DE, grad_unit_pre, back_unit, preferred_element_type=f32)
    )
    grad_inputs = grad_middle + first_scale * (
        grad_hidden - normed * jnp.mean(grad_hidden * normed, axis=-1, keepdims=True)
    )
    return (
        result,
        grad_inputs,
        attention_grads[0],
        attention_grads[1],
        attention_grads[2],
        attention_grads[3],
        attention_grads[4],
        attention_grads[5],
        feed_grads[0],
        feed_grads[1],
        feed_grads[2],
    )


def body_kernels(
    tokens,
    lengths,
    seq_order,
    decay_rate,
    w_query,
    w_key,
    w_value,
    w_unit,
    w_output,
    norm_gain,
    w_left,
    w_right,
    w_down,
    cotangent,
):
    f32 = jnp.float32
    heads = decay_rate.shape[0]
    devices = lax.axis_size(AXIS)
    me = lax.axis_index(AXIS)
    mine = jnp.arange(devices, dtype=jnp.int32)[:, None] == me
    gain_tile = jnp.where(mine, norm_gain.astype(f32)[None, :], 0.0).reshape(heads, -1)
    full, saved = forward(
        lengths,
        seq_order,
        decay_rate,
        tokens,
        cotangent,
        gain_tile,
        [w_key, w_value, w_query, w_unit, w_output, w_left, w_right, w_down],
    )
    grads, result, grad_inputs = backward(
        lengths, seq_order, decay_rate, tokens, cotangent, saved, full[:4] + full[5:]
    )
    own = norm_gain.shape[0]
    return (
        result,
        grad_inputs,
        grads[9],
        grads[11],
        grads[10],
        grads[8],
        grads[6],
        lax.dynamic_slice(grads[7].reshape(-1), (me * own,), (own,)),
        jnp.concatenate(grads[2:4], axis=1),
        jnp.concatenate(grads[4:6], axis=1),
        jnp.concatenate(grads[0:2], axis=1),
    )


def solution(mesh):
    placed = (
        P(AXIS, None),
        P(),
        P(),
        P(),
        P(AXIS, None),
        P(AXIS, None),
        P(AXIS, None),
        P(AXIS, None),
        P(AXIS, None),
        P(AXIS),
        P(AXIS, None),
        P(AXIS, None),
        P(AXIS, None),
        P(AXIS, None),
    )
    return jax.shard_map(
        body_kernels if mesh.size == 32 else body,
        mesh=mesh,
        in_specs=placed,
        out_specs=(
            P(AXIS, None),
            P(AXIS, None),
            P(AXIS, None),
            P(AXIS, None),
            P(AXIS, None),
            P(AXIS, None),
            P(AXIS, None),
            P(AXIS),
            P(AXIS, None),
            P(AXIS, None),
            P(AXIS, None),
        ),
        check_vma=False,
    )
```

```python
import functools

import jax
import jax.numpy as jnp
from jax import lax
from jax.experimental import pallas as pl
from jax.experimental.pallas import tpu as pltpu
from jax.sharding import PartitionSpec as P

SPAN = 256
AXIS = "fsdp"
TE_DE = "te,de->td"
TD_TE = "td,te->de"
EPSILON = 1e-05
LOGICAL = pl.DeviceIdType.LOGICAL
VMEM_LIMIT = 64000000


class Place:
    def __init__(self):
        me = lax.axis_index(AXIS)
        self.me = me
        self.c = lax.rem(me, 2)
        self.x = lax.rem(me // 2, 2)
        self.y = lax.rem(me // 4, 2)
        self.z = me // 8
        self.inner = (self.z == 1) | (self.z == 2)
        self.even = lax.rem(self.z, 2) == 0
        self.sib = self.z + 1 - 2 * lax.rem(self.z, 2)
        half = self.z // 2
        self.near = 2 - half
        self.far = 3 - 3 * half
        self.cross = 3 - self.z
        self.x1 = 1 - self.x
        self.y1 = 1 - self.y
        self.c1 = 1 - self.c
        self.to = {
            "S": self.dev(self.sib, self.y, self.x, self.c),
            "K": self.dev(self.cross, self.y, self.x, self.c),
            "x": self.dev(self.z, self.y, self.x1, self.c),
            "y": self.dev(self.z, self.y1, self.x, self.c),
            "p": self.dev(self.z, self.y, self.x, self.c1),
        }

    def dev(self, z, y, x, c):
        return ((z * 2 + y) * 2 + x) * 2 + c


def arrived(ref, send, recv, place):
    pltpu.make_async_remote_copy(
        src_ref=ref,
        dst_ref=ref,
        send_sem=send,
        recv_sem=recv,
        device_id=place.to["p"],
        device_id_type=LOGICAL,
    ).wait_recv()


class Gather:
    RECV = ("Cs", "Cn", "Cf", "Xo", "Xs", "Xn", "Xf", "Yo", "Ys", "Yn", "Yf", "D0", "D1", "En", "Ef")
    GROUPS = ("C", "X", "Y", "D")
    NRECV = 19
    NSEND = 25

    def __init__(self, place, own, full, send, recv, index):
        self.p, self.own, self.full = place, own, full
        self.send, self.recv, self.index = send, recv, index
        self.sent = []
        p = place
        self.where = {}
        for g, y, x in (("C", p.y, p.x), ("X", p.y, p.x1), ("Y", p.y1, p.x), ("D", p.y1, p.x1)):
            for k, z in (("o", p.z), ("s", p.sib), ("n", p.near), ("f", p.far)):
                self.where[g + k] = (z, y, x, p.c)
        for a, b in (("D0", "Do"), ("D1", "Ds"), ("En", "Dn"), ("Ef", "Df")):
            self.where[a] = self.where[b]

    def slot(self, name):
        return self.full.at[self.where[name]]

    def copy(self, name, link, landing):
        src = self.own if name == "Co" else self.slot(name)
        k = len(self.sent)
        made = pltpu.make_async_remote_copy(
            src_ref=src,
            dst_ref=self.slot(name),
            send_sem=self.send.at[self.index, k],
            recv_sem=self.recv.at[self.index, self.RECV.index(landing)],
            device_id=self.p.to[link],
            device_id_type=LOGICAL,
        )
        return made

    def go(self, name, link, landing, cond=None):
        made = self.copy(name, link, landing)
        self.sent.append((made, cond))
        if cond is None:
            made.start()
        else:
            pl.when(cond)(made.start)

    def wait(self, name):
        arrived(self.slot(name), self.send.at[self.index, 0], self.recv.at[self.index, self.RECV.index(name)], self.p)

    def group(self, g):
        p = self.p
        y = p.y if g in "CX" else p.y1
        x = p.x if g in "CY" else p.x1
        return y, x

    def pair(self, g):
        y, x = self.group(g)
        ref = self.full.at[:, y, x, self.p.c]
        k = len(self.sent)
        made = pltpu.make_async_remote_copy(
            src_ref=ref,
            dst_ref=ref,
            send_sem=self.send.at[self.index, k],
            recv_sem=self.recv.at[self.index, 15 + self.GROUPS.index(g)],
            device_id=self.p.to["p"],
            device_id_type=LOGICAL,
        )
        self.sent.append((made, None))
        made.start()

    def round(self, r):
        p = self.p
        inner, even = p.inner, p.even
        odd = jnp.logical_not(even)
        if r == 0:
            keep = pltpu.make_async_copy(self.own, self.slot("Co"), self.send.at[self.index, self.NSEND])
            self.keep = keep
            keep.start()
            self.go("Co", "S", "Cs")
            self.go("Co", "K", "Cn", inner)
            self.go("Co", "x", "Xo")
            self.go("Co", "y", "Yo")
        if r == 1:
            self.wait("Cs")
            self.go("Cs", "K", "Cf", inner)
            self.go("Cs", "x", "Xs")
            self.go("Cs", "y", "Ys")
            self.wait("Xo")
            self.go("Xo", "y", "D0", even)
            self.wait("Yo")
            self.go("Yo", "x", "D0", odd)
        if r == 2:
            self.wait("Cn")
            self.go("Cn", "S", "Cn", inner)
            self.go("Cn", "x", "Xn")
            self.go("Cn", "y", "Yn")
            self.wait("Xs")
            self.go("Xs", "y", "D1", odd)
            self.wait("Ys")
            self.go("Ys", "x", "D1", even)
            self.wait("D0")
            self.go("D0", "K", "En", inner)
        if r == 3:
            self.wait("Cf")
            self.go("Cf", "S", "Cf", inner)
            self.go("Cf", "x", "Xf")
            self.go("Cf", "y", "Yf")
            self.keep.wait()
            self.pair("C")
            self.wait("D1")
            self.go("D1", "K", "Ef", inner)
            self.wait("Xn")
            self.wait("Yn")
        if r == 4:
            self.wait("En")
            self.go("En", "S", "En", inner)
            self.wait("Xf")
            self.pair("X")
            self.wait("Yf")
            self.pair("Y")
        if r == 5:
            self.wait("Ef")
            self.go("Ef", "S", "Ef", inner)
            self.pair("D")

    def pairs(self):
        for g in self.GROUPS:
            y, x = self.group(g)
            ref = self.full.at[:, y, x, self.p.c1]
            arrived(ref, self.send.at[self.index, 0], self.recv.at[self.index, 15 + self.GROUPS.index(g)], self.p)

    def finish(self):
        for made, cond in self.sent:
            if cond is None:
                made.wait_send()
            else:
                pl.when(cond)(made.wait_send)


def add_into(out, parts):
    rows = out.shape[0]
    step = 8 if rows % 16 else 16

    @pl.loop(0, rows // step)
    def _(i):
        at = pl.ds(pl.multiple_of(i * step, step), step)
        total = parts[0][at, :].astype(jnp.float32)
        for part in parts[1:]:
            total = total + part[at, :].astype(jnp.float32)
        out[at, :] = total.astype(out.dtype)


class Scatter:
    NRECV = 20
    NSEND = 22
    SLOTS = ("x0", "x1", "x2", "x3", "Fx", "y0", "y1", "y2", "y3", "Fy", "En", "Ef", "Cn", "Cf", "Co", "De", "Do", "KCs", "KCo")

    def __init__(self, place, part, acc, term, came, out, send, recv, index):
        self.p, self.part, self.acc, self.term, self.came, self.out = place, part, acc, term, came, out
        self.send, self.recv, self.index = send, recv, index
        self.sent = []
        p = place
        half = p.z // 2
        self.ze, self.zo = 2 * half, 2 * half + 1
        self.C = lambda z: (z, p.y, p.x)
        self.X = lambda z: (z, p.y, p.x1)
        self.Y = lambda z: (z, p.y1, p.x)
        self.D = lambda z: (z, p.y1, p.x1)

    def go(self, where, link, slot, cond=None):
        k = len(self.sent)
        at = self.SLOTS.index(slot) if isinstance(slot, str) else slot
        made = pltpu.make_async_remote_copy(
            src_ref=self.acc.at[where],
            dst_ref=self.came.at[at],
            send_sem=self.send.at[self.index, k],
            recv_sem=self.recv.at[self.index, at],
            device_id=self.p.to[link],
            device_id_type=LOGICAL,
        )
        self.sent.append((made, cond))
        if cond is None:
            made.start()
        else:
            pl.when(cond)(made.start)

    def wait(self, slot):
        at = self.SLOTS.index(slot) if isinstance(slot, str) else slot
        arrived(self.came.at[at], self.send.at[self.index, 0], self.recv.at[self.index, at], self.p)
        return self.came.at[at]

    def add(self, where, slots):
        parts = [self.wait(s) for s in slots]
        add_into(self.acc.at[where], [self.acc.at[where]] + parts)

    def round(self, r):
        p = self.p
        inner = p.inner
        outer = jnp.logical_not(inner)
        ze, zo, near, far = self.ze, self.zo, p.near, p.far
        if r == 0:
            self.given = pltpu.make_async_remote_copy(
                src_ref=self.part,
                dst_ref=self.acc,
                send_sem=self.send.at[self.index, self.NSEND],
                recv_sem=self.recv.at[self.index, 19],
                device_id=p.to["p"],
                device_id_type=LOGICAL,
            )
            self.given.start()
        if r == 1:
            arrived(self.acc, self.send.at[self.index, 0], self.recv.at[self.index, 19], p)
            self.term.second(self.acc)
            self.go(self.D(far), "S", "Ef", outer)
            self.go(self.D(near), "S", "En", outer)
            self.go(self.X(far), "x", far)
            self.go(self.Y(far), "y", far + 5)
            self.go(self.D(ze), "y", "Fy", outer)
            self.go(self.D(zo), "x", "Fx", outer)
            self.go(self.X(near), "x", near)
            self.go(self.Y(near), "y", near + 5)
            self.go(self.X(zo), "x", zo)
            self.go(self.Y(ze), "y", ze + 5)
        if r == 2:

            @pl.when(inner)
            def _():
                self.add(self.D(far), ["Ef"])
                self.add(self.D(near), ["En"])

            self.go(self.D(far), "K", jnp.where(p.z == 1, self.SLOTS.index("Do"), self.SLOTS.index("De")), inner)
            self.go(self.D(near), "K", jnp.where(p.z == 1, self.SLOTS.index("De"), self.SLOTS.index("Do")), inner)
            parts = [self.wait(far), self.wait(far + 5)]
            add_into(self.acc.at[self.C(far)], [self.acc.at[self.C(far)]] + parts)
            self.go(self.C(far), "S", "Cf", outer)
        if r == 3:

            @pl.when(inner)
            def _():
                self.add(self.D(ze), ["De"])
                self.add(self.D(zo), ["Do"])
                self.add(self.C(far), ["Cf"])

            self.go(self.D(ze), "y", "Fy", inner)
            self.go(self.D(zo), "x", "Fx", inner)
            self.go(self.C(far), "K", "KCs", inner)
            parts = [self.wait(near), self.wait(near + 5)]
            add_into(self.acc.at[self.C(near)], [self.acc.at[self.C(near)]] + parts)
            self.go(self.C(near), "S", "Cn", outer)
        if r == 4:
            self.add(self.X(ze), ["Fy"])
            self.add(self.Y(zo), ["Fx"])
            self.go(self.X(ze), "x", ze)
            self.go(self.Y(zo), "y", zo + 5)

            @pl.when(inner)
            def _():
                self.add(self.C(near), ["Cn"])

            self.go(self.C(near), "K", "KCo", inner)
        if r == 5:
            self.add(self.C(p.sib), [p.sib, p.sib + 5])

            @pl.when(inner)
            def _():
                self.add(self.C(p.sib), ["KCs"])

            self.go(self.C(p.sib), "S", "Co")
        if r == 6:
            slots = [p.z, p.z + 5, "Co"]
            parts = [self.acc.at[self.C(p.z)]] + [self.wait(s) for s in slots]
            add_into(self.out, parts)

            @pl.when(inner)
            def _():
                add_into(self.out, [self.out, self.wait("KCo")])

    def handed(self):
        self.given.wait_send()

    def finish(self):
        for made, cond in self.sent:
            if cond is None:
                made.wait_send()
            else:
                pl.when(cond)(made.wait_send)


def bounds_of(lengths, order):
    total, found = jnp.int32(0), []
    for j in range(lengths.shape[0]):
        total = total + lengths[order[j]]
        found.append(total)
    return found


def segment_at(bounds, places):
    found = jnp.zeros_like(places)
    for bound in bounds:
        found = found + jnp.where(bound <= places, 1, 0)
    return found


def same_segment(bounds, earlier, later):
    same = jnp.int32(0)
    for bound in bounds:
        same = same + jnp.where((bound <= earlier) != (bound <= later), 1, 0)
    return jnp.where((earlier >= 0) & (same == 0), 1.0, 0.0).astype(jnp.float32)


def spans_of(first, bounds, dist, entry, leaving):
    size = dist.shape[0]
    t = lax.broadcasted_iota(jnp.int32, (size, size), 0)
    s = lax.broadcasted_iota(jnp.int32, (size, size), 1)
    same = segment_at(bounds, t + first) == segment_at(bounds, s + first)
    dist[...] = jnp.where(same & (s <= t), t - s, -1).astype(jnp.float32)
    t = lax.broadcasted_iota(jnp.int32, entry.shape, 0)
    here = segment_at(bounds, t + first)
    ahead = segment_at(bounds, jnp.full(entry.shape, first - 1, jnp.int32))
    ahead = jnp.where(jnp.full(entry.shape, first, jnp.int32) == 0, -1, ahead)
    last = segment_at(bounds, jnp.full(entry.shape, first + size - 1, jnp.int32))
    entry[...] = jnp.where(here == ahead, t, -1).astype(jnp.float32)
    leaving[...] = jnp.where(here == last, size - t, -1).astype(jnp.float32)


def decay(distance, rate):
    return jnp.where(distance >= 0, jnp.exp(-rate * distance), 0.0)


def mm(a, b):
    return jnp.dot(a, b, preferred_element_type=jnp.float32)


def mm_nt(a, b):
    return lax.dot_general(a, b, (((1,), (1,)), ((), ())), preferred_element_type=jnp.float32)


def mm_tn(a, b):
    return lax.dot_general(a, b, (((0,), (0,)), ((), ())), preferred_element_type=jnp.float32)


def head_of(h):
    return pl.ds(pl.multiple_of(h * 128, 128), 128)


def norm_scale(values):
    return lax.rsqrt(jnp.mean(values * values, axis=-1, keepdims=True) + EPSILON)


def slope(a):
    sigma = 1.0 / (1.0 + jnp.exp(-a))
    return sigma * (1.0 + a * (1.0 - sigma))


def flat_rows(value):
    return value.astype(jnp.float32).reshape(-1, value.shape[-1]).astype(jnp.bfloat16)


SAVED_BACK = 18


class States:
    def __init__(self, place, bounds, rate, reverse, value, buffers, send, recv):
        self.bounds, self.reverse, self.rate = bounds, reverse, rate
        self.value = value
        self.theirs, self.sums, self.met, self.planes, self.ready, self.entered, self.give, self.out, self.sum = buffers
        self.send, self.recv = send, recv
        self.z, self.c, self.c1 = place.z, place.c, place.c1
        self.me, self.partner = place.me, place.to["p"]
        self.q = lax.rem(place.me // 2, 4)
        self.chip = [self.at(self.z, lax.bitwise_xor(self.q, k)) for k in range(4)]
        self.level = [self.at(lax.rem(self.z + k, 4), self.q) for k in range(4)]
        self.order = range(3, -1, -1) if reverse else range(4)
        lead = 1 if reverse else 0
        self.lead = jnp.where(self.c == lead, 1.0, 0.0).astype(jnp.float32)
        base = self.me - self.c
        self.lead_through = self.through(base + lead, 1)
        self.last_through = self.through(base + 1 - lead, 1)
        mine = rate[4 * self.c + self.q]
        self.chip_step = jnp.exp(jnp.full((1, 128), -2 * SPAN * mine, jnp.float32))
        self.plane_step = jnp.exp(jnp.full((1, 128), -8 * SPAN * mine, jnp.float32))

    def at(self, z, q):
        return (z * 4 + q) * 2 + self.c

    def through(self, device, count):
        return same_segment(self.bounds, device * SPAN - 1, (device + count) * SPAN - 1)

    def step(self, k):
        return jnp.exp(jnp.full((1, 128), -SPAN * self.rate[4 * self.c + k], jnp.float32))

    def copy(self, src, dst, k, peer):
        return pltpu.make_async_remote_copy(
            src_ref=src,
            dst_ref=dst,
            send_sem=self.send.at[k],
            recv_sem=self.recv.at[k],
            device_id=peer,
            device_id_type=LOGICAL,
        )

    def other(self, k):
        return lax.bitwise_xor(self.q, k)

    def begin(self, made):
        for one in made:
            one.start()
        return made

    def terms(self, k):
        mine, theirs = self.value[4 * self.c + k], self.theirs[k]
        rest = 1.0 - self.lead
        return self.lead * mine + rest * theirs, rest * mine + self.lead * theirs

    def spread(self):
        half = self.value.at[pl.ds(4 * self.c1, 4)]
        self.sent = self.begin([self.copy(half, self.theirs, 0, self.partner)])

    def join(self):
        self.copy(self.theirs, self.theirs, 0, self.partner).wait_recv()
        for k in range(4):
            first, last = self.terms(k)
            self.sums[k] = (self.last_through * self.step(k) * first + last).astype(jnp.bfloat16)
        self.sent += self.begin(
            [
                self.copy(self.sums.at[self.other(k)], self.met.at[self.q], k, self.chip[k])
                for k in range(1, 4)
            ]
        )
        self.met[self.q] = self.sums[self.q]

    def total(self):
        for k in range(1, 4):
            self.copy(self.sums.at[0], self.met.at[self.other(k)], k, self.chip[k]).wait_recv()
        total = jnp.zeros(self.met.shape[1:], jnp.float32)
        for i in self.order:
            through = self.through(self.z * 8 + 2 * i, 2)
            total = through * self.chip_step * total + self.met[i].astype(jnp.float32)
        self.planes[self.z] = total.astype(jnp.bfloat16)
        self.second = []
        for k in range(1, 4):
            far = self.z - k if self.reverse else self.z + k
            cond = far >= 0 if self.reverse else far <= 3
            made = self.copy(
                self.planes.at[self.z], self.planes.at[self.z], 3 + k, self.at(far, self.q)
            )
            self.second.append((made, cond))
            pl.when(cond)(made.start)

    def back(self):
        self.sum[...] = jnp.zeros(self.sum.shape, jnp.float32)
        for k in range(3, 0, -1):
            far = self.z + k if self.reverse else self.z - k
            cond = far <= 3 if self.reverse else far >= 0

            @pl.when(cond)
            def _():
                self.copy(
                    self.planes.at[self.z], self.planes.at[far], 3 + k, self.partner
                ).wait_recv()
                kept = self.through(far * 8, 8) * self.plane_step
                self.sum[...] = kept * self.sum[...] + self.planes[far].astype(jnp.float32)

        total = self.sum[...]
        for i in self.order:
            self.ready[i] = total.astype(jnp.bfloat16)
            through = self.through(self.z * 8 + 2 * i, 2)
            total = through * self.chip_step * total + self.met[i].astype(jnp.float32)
        self.sent += self.begin(
            [
                self.copy(self.ready.at[self.other(k)], self.entered.at[self.q], 6 + k, self.chip[k])
                for k in range(1, 4)
            ]
        )
        self.entered[self.q] = self.ready[self.q]

    def part(self):
        for k in range(1, 4):
            self.copy(self.ready.at[0], self.entered.at[self.other(k)], 6 + k, self.chip[k]).wait_recv()
        rest = 1.0 - self.lead
        for k in range(4):
            first, _ = self.terms(k)
            entering = self.entered[k].astype(jnp.float32)
            later = self.lead_through * self.step(k) * entering + first
            self.out[4 * self.c + k] = (self.lead * entering + rest * later).astype(jnp.bfloat16)
            self.give[k] = (self.lead * later + rest * entering).astype(jnp.bfloat16)
        at = pl.ds(4 * self.c, 4)
        self.sent += self.begin([self.copy(self.give, self.out.at[at], 10, self.partner)])

    def done(self):
        at = pl.ds(4 * self.c1, 4)
        self.copy(self.give, self.out.at[at], 10, self.partner).wait_recv()

    def finish(self):
        for one in self.sent:
            one.wait_send()
        for made, cond in self.second:
            pl.when(cond)(made.wait_send)


def state_buffers():
    cube, low = (4, 128, 128), jnp.bfloat16
    return (
        [pltpu.VMEM(cube, jnp.float32)]
        + [pltpu.VMEM(cube, low)] * 6
        + [pltpu.VMEM((8, 128, 128), low), pltpu.VMEM((128, 128), jnp.float32)]
    )


def greet_more(place):
    barrier = pltpu.get_barrier_semaphore()
    r = lax.rem(place.me, 8)
    peers = [place.z * 8 + lax.bitwise_xor(r, k) for k in range(1, 8)]
    peers += [lax.rem(place.z + k, 4) * 8 + r for k in range(1, 4)]
    for peer in peers:
        pl.semaphore_signal(barrier, inc=1, device_id=peer, device_id_type=LOGICAL)
    pl.semaphore_wait(barrier, len(peers))


def forward_kernel(
    lengths,
    order,
    rate,
    tokens,
    cot,
    gain_own,
    s_key,
    s_value,
    s_query,
    s_unit,
    s_output,
    s_left,
    s_right,
    s_down,
    *refs,
):
    f32, bf16 = jnp.float32, jnp.bfloat16
    n = 12
    full, refs = refs[:n], refs[n:]
    saved, refs = refs[:SAVED_BACK], refs[SAVED_BACK:]
    kept, refs = refs[:SAVED_BACK], refs[SAVED_BACK:]
    (hidden_rows, keys, values, queries, key_pre, query_pre, unit_pre, probs) = kept[:8]
    (attended, state_low, mixed_rows, middle, second_rows, left, right, product) = kept[8:16]
    gain, down_term = kept[16:]
    (hidden, mixed, second, turned) = refs[:4]
    (dist, entry, leaving, gains, value) = refs[4:9]
    state_refs, arriving = refs[9:18], refs[16]
    (narrow, wide, send, recv, state_send, state_recv, load_sem, save_sem) = refs[18:]
    place = Place()
    half = s_left.shape[1] // 2
    own = [s_key, s_value, s_query, s_unit, gain_own, s_output]
    own += [s_left.at[:, pl.ds(0, half)], s_left.at[:, pl.ds(half, half)]]
    own += [s_right.at[:, pl.ds(0, half)], s_right.at[:, pl.ds(half, half)]]
    down_cols = s_down.shape[1] // 2
    own += [s_down.at[:, pl.ds(i * down_cols, down_cols)] for i in (0, 1)]
    greet_more(place)
    made = [Gather(place, own[i], full[i], send, recv, i) for i in range(n)]
    bounds = bounds_of(lengths, order)
    states = States(
        place, bounds, rate, False, value, state_refs, state_send, state_recv
    )
    slots = {0: narrow.at[0], 1: narrow.at[1], 2: narrow.at[0], 3: narrow.at[1], 4: gains}
    slots.update({5: narrow.at[0], 6: wide.at[0], 7: wide.at[1], 8: wide.at[0], 9: wide.at[1]})
    saves = []

    def save(*numbers):
        for i in numbers:
            copy = pltpu.make_async_copy(kept[i], saved[i], save_sem.at[i])
            copy.start()
            saves.append(copy)

    def weight(i):
        ref = slots[i]
        return ref[...].reshape(-1, ref.shape[-1])

    def turn(ref, rows):
        @pl.loop(0, 8)
        def _(i):
            block = ref[:, head_of(i)].astype(f32).T
            rows[i // 2, i % 2] = block.reshape((2, 2) + rows.shape[4:]).astype(bf16)

    def start():
        x = tokens[...].astype(f32)
        hidden[...] = (x * norm_scale(x)).astype(bf16)
        spans_of(place.me * SPAN, bounds, dist, entry, leaving)
        turn(hidden, hidden_rows)
        save(0)

    def project(i, pre, low):
        out = mm(hidden[...], weight(i))
        if pre is not None:
            pre[...] = out
            out = out / (1.0 + jnp.exp(-out))
        low[...] = out.astype(bf16)

    def key():
        project(0, key_pre, keys)
        save(1, 4)

    def increments():
        project(1, None, values)

        @pl.loop(0, 8)
        def _(h):
            at = head_of(h)
            held = (keys[:, at].astype(f32) * decay(leaving[...], rate[h])).astype(bf16)
            value[h] = mm_tn(held, values[:, at])

        states.spread()
        save(2)

    def query():
        project(2, query_pre, queries)

        @pl.loop(0, 8)
        def _(h):
            at = head_of(h)
            scores = mm_nt(queries[:, at], keys[:, at])
            low = (scores * decay(dist[...], rate[h])).astype(bf16)
            probs[h] = low
            attended[:, at] = mm(low, values[:, at])

        save(3, 5, 7)

    def unit():
        unit_pre[...] = mm(hidden[...], weight(3))
        save(6)

    def attend():
        gain[...] = jnp.sum(gains[...].reshape(-1, 8, 128), axis=0)

        @pl.loop(0, 8)
        def _(h):
            at = head_of(h)
            low = arriving[h].astype(bf16)
            state_low[h] = low
            held = (queries[:, at].astype(f32) * decay(entry[...], rate[h])).astype(bf16)
            out = attended[:, at] + mm(held, low)
            attended[:, at] = out
            mixed[:, at] = (
                out * norm_scale(out) * gain[pl.ds(h, 1), :] * unit_pre[:, at]
            ).astype(bf16)

        turn(mixed, mixed_rows)
        save(8, 9, 10, 16)

    def output():
        out = tokens[...].astype(f32) + mm(mixed[...], weight(5))
        middle[...] = out
        second[...] = (out * norm_scale(out)).astype(bf16)
        turn(second, second_rows)
        save(11, 12)

    def gate(i, side, part):
        side[:, pl.ds(part * half, half)] = mm(second[...], weight(i))

    def multiply(j):
        cols = cot.shape[1] // 2

        @pl.loop(0, half // 128)
        def _(i):
            at = pl.ds(pl.multiple_of(j * half + i * 128, 128), 128)
            block = (left[:, at] * right[:, at]).astype(bf16).astype(f32)
            turned[pl.ds(pl.multiple_of(i * 128, 128), 128), :] = block.T

        both = pl.ds(2 * j, 2)
        block = turned[...].reshape((2,) + product.shape[1:])
        product[both] = block.astype(bf16)
        rows = flat_rows(product[both, :, :, place.c1])
        for m in range(2):
            term = mm(rows, cot[:, pl.ds(m * cols, cols)])
            down_term[m, both] = term.reshape((2,) + down_term.shape[2:]).astype(bf16)

    tasks = {2: [start], 7: [key], 8: [increments], 8.5: [states.join], 9: [query], 9.5: [states.total]}
    tasks.update({10: [unit], 10.5: [states.back], 11.5: [states.part], 12: [states.done, attend]})
    tasks[12.5] = [output]
    tasks[13] = [lambda: gate(6, left, 0)]
    tasks[14] = [lambda: gate(7, left, 1), lambda: save(13)]
    tasks[15] = [lambda: gate(8, right, 0), lambda: multiply(0)]
    tasks[16] = [lambda: gate(9, right, 1), lambda: multiply(1), lambda: save(17, 15, 14)]
    loads = {}
    for step in range(n + 6):
        i = step - 6
        for r in range(6):
            if 0 <= step - r < n:
                made[step - r].round(r)
            if r == 0:
                if i - 1 in loads:
                    loads[i - 1].wait()
                for task in tasks.get(step, []):
                    task()
            if r == 3:
                for task in tasks.get(step + 0.5, []):
                    task()
        if 0 <= i < n:
            made[i].pairs()
        if i in slots:
            loads[i] = pltpu.make_async_copy(full[i], slots[i], load_sem.at[i])
            loads[i].start()
    for one in made:
        one.finish()
    states.finish()
    for copy in saves:
        copy.wait()


def forward(lengths, order, rate, tokens, cot, gain_tile, shards):
    f32, bf16 = jnp.float32, jnp.bfloat16
    size, width = tokens.shape
    wide = shards[5].shape[1]
    half = wide // 2
    blocks = [(s.shape, s.dtype) for s in shards[:4]] + [(gain_tile.shape, f32)]
    blocks += [(shards[4].shape, bf16)] + [((32, half), bf16)] * 4
    blocks += [((shards[7].shape[0], width // 2), bf16)] * 2
    square, cube = (size, width), (8, 128, 128)
    rows, down_rows = shards[4].shape[0], shards[7].shape[0]
    across = ((4, 2, 2, 2, rows, size), bf16)
    kept = [across] + [(square, bf16)] * 3 + [(square, f32)] * 3 + [((8, size, size), bf16)]
    kept += [(square, f32), (cube, bf16), across, (square, f32), across]
    kept += [((size, wide), f32)] * 2 + [((4, 2, 2, 2, down_rows, size), bf16), ((8, 128), f32)]
    kept += [((2, 4, 2, 2, down_rows, width // 2), bf16)]
    vmem, hbm = pl.BlockSpec(memory_space=pltpu.VMEM), pl.BlockSpec(memory_space=pltpu.HBM)
    smem = pl.BlockSpec(memory_space=pltpu.SMEM)
    n = len(blocks)
    out = pl.pallas_call(
        forward_kernel,
        out_shape=[jax.ShapeDtypeStruct((4, 2, 2, 2) + s, t) for s, t in blocks]
        + [jax.ShapeDtypeStruct(s, t) for s, t in kept],
        in_specs=[smem] * 3 + [vmem] * 11,
        out_specs=[hbm] * (n + len(kept)),
        scratch_shapes=[pltpu.VMEM(s, t) for s, t in kept]
        + [pltpu.VMEM(square, bf16)] * 3
        + [pltpu.VMEM((half, size), f32)]
        + [pltpu.VMEM((size, size), f32), pltpu.VMEM((size, 128), f32), pltpu.VMEM((size, 128), f32)]
        + [pltpu.VMEM((4, 2, 2, 2, 8, 128), f32)]
        + [pltpu.VMEM(cube, f32)]
        + state_buffers()
        + [
            pltpu.VMEM((2, 4, 2, 2, 2, 32, width), bf16),
            pltpu.VMEM((2, 4, 2, 2, 2, 32, half), bf16),
            pltpu.SemaphoreType.DMA((n, Gather.NSEND + 1)),
            pltpu.SemaphoreType.DMA((n, Gather.NRECV)),
            pltpu.SemaphoreType.DMA((18,)),
            pltpu.SemaphoreType.DMA((18,)),
            pltpu.SemaphoreType.DMA((n,)),
            pltpu.SemaphoreType.DMA((len(kept),)),
        ],
        compiler_params=pltpu.CompilerParams(
            collective_id=0, has_side_effects=True, vmem_limit_bytes=VMEM_LIMIT
        ),
        name="forward",
    )(lengths, order, rate, tokens, cot, gain_tile, *shards)
    return out[:n], out[n:]

def backward_kernel(lengths, order, rate, tokens, cot, *refs):
    f32, bf16 = jnp.float32, jnp.bfloat16
    n = 12
    saved, refs = refs[:SAVED_BACK], refs[SAVED_BACK:]
    (h_hidden, h_keys, h_values, h_queries, h_key_pre, h_query_pre, h_unit_pre, h_probs) = saved[:8]
    (h_attended, h_state_low, h_mixed, h_middle, h_second, h_left, h_right, h_product) = saved[8:16]
    h_gain, h_down = saved[16:]
    w_in, refs = refs[:11], refs[11:]
    (w_key, w_value, w_query, w_unit, w_output, w_l0, w_l1, w_r0, w_r1) = w_in[:9]
    w_down = w_in[9:]
    out, result_out, tokens_out, refs = refs[:n], refs[n], refs[n + 1], refs[n + 2 :]
    acc, came, refs = refs[:n], refs[n : 2 * n], refs[2 * n :]
    (part, gain_part, wd, down, wl, left, right, f1, f2, f3, f4) = refs[:11]
    (branch, ga, gup, gkp, gvp, result, glp, grp, rows, mixed, product) = refs[11:22]
    (probs, state_low, gain, gg, dist, entry, leaving) = refs[22:29]
    value, state_refs, arriving = refs[29], refs[30:39], refs[37]
    (send, recv, state_send, state_recv, load_sem) = refs[39:]
    place = Place()
    half = h_left.shape[1] // 2
    width = tokens.shape[1]
    left_w, right_w = left.at[:, pl.ds(0, width)], right.at[:, pl.ds(0, width)]
    queries, keys = glp.at[:, pl.ds(0, width)], glp.at[:, pl.ds(width, width)]
    values, gqp = grp.at[:, pl.ds(0, width)], grp.at[:, pl.ds(width, width)]
    wn = wl.at[:, :, :, :, :, pl.ds(0, width)]
    greet_more(place)
    bounds = bounds_of(lengths, order)
    states = States(
        place, bounds, rate, True, value, state_refs, state_send, state_recv
    )
    loads = {}

    def load(name, src, dst):
        copy = pltpu.make_async_copy(src, dst, load_sem.at[len(loads)])
        loads[name] = copy
        copy.start()

    def load_down(i):
        for m in range(2):
            dst = wd.at[:, :, :, :, :, pl.ds(m * cols, cols)]
            load("down%d%d" % (i, m), w_down[m].at[pl.ds(2 * i, 2)], dst)

    def loaded(*names):
        for name in names:
            loads[name].wait()

    def weight(cols):
        return wl[:, :, :, :, :, pl.ds(0, cols)].reshape(-1, cols)

    def side(i):
        return pl.ds(i * half, half)

    def product_of(i):
        return flat_rows(product[pl.ds(2 * i, 2)])

    class Piece:
        def __init__(self, rows, core_rows, grad, cols, need=()):
            self.rows, self.core_rows, self.grad, self.cols, self.need = rows, core_rows, grad, cols, need

        def term(self, zh, core):
            lhs = self.rows[pl.ds(zh * 2, 2), :, :, core]
            lhs = flat_rows(lhs) if self.core_rows % 16 else lhs.reshape(-1, lhs.shape[-1])
            out = mm(lhs, self.grad[...])
            return out.reshape(2, 2, 2, self.core_rows, self.cols)

        def first(self):
            @pl.loop(0, 2)
            def _(zh):
                part[pl.ds(zh * 2, 2), :, :, :, pl.ds(0, self.cols)] = self.term(
                    zh, place.c1
                ).astype(bf16)

        def second(self, acc):
            @pl.loop(0, 2)
            def _(zh):
                at = pl.ds(zh * 2, 2)
                acc[at] = (acc[at].astype(f32) + self.term(zh, place.c)).astype(bf16)

    class Gain:
        def first(self):
            gain_part[...] = jnp.broadcast_to(gg[...][None, None, None], gain_part.shape)

        def second(self, acc):
            acc[...] = acc[...] + gg[...][None, None, None]

    wide = part.at[:, :, :, :, pl.ds(0, half)]
    narrow = part.at[:, :, :, :, pl.ds(0, width)]
    cols = width // 2
    pieces = [(h_down.at[m], Piece(product, 88, cot.at[:, pl.ds(m * cols, cols)], cols)) for m in (0, 1)]
    pieces += [(wide, Piece(rows, 32, glp.at[:, side(i)], half)) for i in (0, 1)]
    pieces += [(wide, Piece(rows, 32, grp.at[:, side(i)], half)) for i in (0, 1)]
    pieces += [(narrow, Piece(mixed, 32, branch, width)), (gain_part, Gain())]
    pieces += [(narrow, Piece(rows, 32, g, width)) for g in (gup, gqp, gvp, gkp)]
    made = [
        Scatter(place, pieces[i][0], acc[i], pieces[i][1], came[i], out[i], send, recv, i)
        for i in range(n)
    ]

    def begin():
        spans_of(place.me * SPAN, bounds, dist, entry, leaving)

    def gates(i):
        loaded("down%d0" % i, "down%d1" % i, "left%d" % i, "right%d" % i)
        pair = 2 * wd.shape[4]

        @pl.loop(0, 8)
        def _(k):
            at = pl.ds(pl.multiple_of(k * pair, 16), pair)
            down[at, :] = flat_rows(wd[k // 4, (k // 2) % 2, k % 2])

        grad = mm_nt(cot[...], down[...])
        glp[:, side(i)] = (grad * right[...]).astype(bf16)
        grp[:, side(i)] = (grad * left[...]).astype(bf16)
        if i == 0:
            loaded("middle")
            f3[...] = f2[...] + mm_tn(product_of(0), down[...])
            load_down(1)
            load("left1", h_left.at[:, side(1)], left)
            load("right1", h_right.at[:, side(1)], right)
        else:
            result[...] = (f3[...] + mm_tn(product_of(1), down[...])).astype(bf16)
            load("unit_pre", h_unit_pre, left_w)
            load("result", result, result_out)

    def second_part(name, grad, i, following, start):
        loaded(name)
        term = mm_nt(grad[:, side(i)], weight(half))
        f1[...] = term if start else f1[...] + term
        load(*following)

    def middle():
        @pl.loop(0, SPAN // 16)
        def _(i):
            at = pl.ds(pl.multiple_of(i * 16, 16), 16)
            x, g = f2[at, :], f1[at, :]
            scale = norm_scale(x)
            unit = x * scale
            grad = cot[at, :].astype(f32) + scale * (
                g - unit * jnp.mean(g * unit, axis=-1, keepdims=True)
            )
            f3[at, :] = grad
            branch[at, :] = grad.astype(bf16)

        load("attended", h_attended, f2)

    def spare():
        load("queries", h_queries, queries)
        load("keys", h_keys, keys)
        load("values", h_values, values)
        load("hidden", h_hidden, rows)

    def attention():
        loaded("output")
        f1[...] = mm_nt(branch[...], weight(width))
        load("unit", w_unit, wn)
        loaded("attended", "unit_pre", "queries", "gain")

        @pl.loop(0, 8)
        def _(h):
            at = head_of(h)
            att, up, gm = f2[:, at], left_w[:, at], f1[:, at]
            scale = norm_scale(att)
            unit = att * scale
            row = gain[pl.ds(h, 1), :]
            gated = gm * up
            gg[pl.ds(h, 1), :] = jnp.sum(gated * unit, axis=0, keepdims=True)
            gup[:, at] = (gm * unit * row).astype(bf16)
            g = gated * row
            low = (
                scale * (g - unit * jnp.mean(g * unit, axis=-1, keepdims=True))
            ).astype(bf16)
            ga[:, at] = low
            held = (queries[:, at].astype(f32) * decay(entry[...], rate[h])).astype(bf16)
            value[h] = mm_tn(held, low)

        states.spread()
        load("key_pre", h_key_pre, f2)

    def scores():
        loaded("keys", "values", "query_pre", "probs", "state_low")

        @pl.loop(0, 8)
        def _(h):
            at = head_of(h)
            low = ga[:, at]
            grads = (mm_nt(low, values[:, at]) * decay(dist[...], rate[h])).astype(bf16)
            grad_q = mm(grads, keys[:, at])
            grad_q = grad_q + mm_nt(low, state_low[h]) * decay(entry[...], rate[h])
            gqp[:, at] = (grad_q * slope(f4[:, at])).astype(bf16)
            f1[:, at] = mm_tn(grads, queries[:, at])
            right_w[:, at] = mm_tn(probs[h], low)

    def hidden_part(name, grad, following, start):
        loaded(name)
        term = mm_nt(grad[...], weight(width))
        f4[...] = term if start else f4[...] + term
        if following:
            load(*following)

    def unit_rest():
        hidden_part("unit", gup, ("query", w_query, wn), True)

    def last_grads():
        hidden_part("query", gqp, ("value", w_value, wn), False)
        states.done()
        loaded("key_pre")

        @pl.loop(0, 8)
        def _(h):
            at = head_of(h)
            grad = arriving[h].astype(bf16)
            fall = decay(leaving[...], rate[h])
            held = (keys[:, at].astype(f32) * fall).astype(bf16)
            grad_k = f1[:, at] + mm_nt(values[:, at], grad) * fall
            gkp[:, at] = (grad_k * slope(f2[:, at])).astype(bf16)
            gvp[:, at] = (right_w[:, at] + mm(held, grad)).astype(bf16)

    def value_rest():
        hidden_part("value", gvp, ("key", w_key, wn), False)

    def inputs():
        hidden_part("key", gkp, None, False)

        @pl.loop(0, SPAN // 16)
        def _(i):
            at = pl.ds(pl.multiple_of(i * 16, 16), 16)
            x, g = tokens[at, :].astype(f32), f4[at, :]
            scale = norm_scale(x)
            unit = x * scale
            f3[at, :] = f3[at, :] + scale * (g - unit * jnp.mean(g * unit, axis=-1, keepdims=True))

        load("tokens", f3, tokens_out)

    before = {1: lambda: loaded("product"), 2: lambda: loaded("second"), 6: lambda: loaded("mixed")}
    before[8] = lambda: loaded("hidden")
    tasks = {0: [begin], 1: [lambda: gates(0)], 2: [lambda: gates(1)]}
    tasks[3] = [lambda: second_part("l0", glp, 0, ("l1", w_l1, wl), True)]
    tasks[4] = [lambda: second_part("l1", glp, 1, ("r0", w_r0, wl), False)]
    tasks[5] = [
        lambda: second_part("r0", grp, 0, ("r1", w_r1, wl), False),
        lambda: second_part("r1", grp, 1, ("output", w_output, wn), False),
        middle,
    ]
    tasks[6] = [spare, attention]
    tasks[6.5] = [states.join]
    tasks[7] = [scores]
    tasks[7.5] = [states.total]
    tasks[8] = [unit_rest, states.back]
    tasks[8.5] = [states.part]
    tasks[9] = [last_grads]
    tasks[10] = [value_rest]
    tasks[11] = [inputs]
    load("product", h_product, product)
    load_down(0)
    load("left0", h_left.at[:, side(0)], left)
    load("right0", h_right.at[:, side(0)], right)
    load("middle", h_middle, f2)
    load("second", h_second, rows)
    load("l0", w_l0, wl)
    load("mixed", h_mixed, mixed)
    load("gain", h_gain, gain)
    load("query_pre", h_query_pre, f4)
    load("probs", h_probs, probs)
    load("state_low", h_state_low, state_low)
    for step in range(n + 6):
        if step < n:
            if step in before:
                before[step]()
            if step > 2:
                made[step - 1].handed()
            if step > 1:
                pieces[step][1].first()
            made[step].round(0)
        if 0 < step <= n:
            made[step - 1].round(1)
        for task in tasks.get(step, []):
            task()
        for r in range(2, 7):
            if 0 <= step - r < n:
                made[step - r].round(r)
            if r == 4:
                for task in tasks.get(step + 0.5, []):
                    task()
    for i, one in enumerate(made):
        if i < 2 or i == n - 1:
            one.handed()
        one.finish()
    states.finish()
    loaded("result", "tokens")


def backward(lengths, order, rate, tokens, cot, saved, weights):
    f32, bf16 = jnp.float32, jnp.bfloat16
    size, width = tokens.shape
    wide = saved[13].shape[1]
    half = wide // 2
    rows = width // 32
    down_rows = wide // 32
    blocks = [((down_rows, width // 2), bf16)] * 2 + [((rows, half), bf16)] * 4
    blocks += [((rows, width), bf16), ((8, 128), f32)] + [((rows, width), bf16)] * 4
    n = len(blocks)
    square, cube = (size, width), (8, 128, 128)
    vmem, hbm = pl.BlockSpec(memory_space=pltpu.VMEM), pl.BlockSpec(memory_space=pltpu.HBM)
    smem = pl.BlockSpec(memory_space=pltpu.SMEM)
    out = pl.pallas_call(
        backward_kernel,
        out_shape=[jax.ShapeDtypeStruct(b, f32) for b, _ in blocks]
        + [jax.ShapeDtypeStruct(square, bf16), jax.ShapeDtypeStruct(square, f32)],
        in_specs=[smem] * 3 + [vmem] * 2 + [hbm] * (len(saved) + len(weights)),
        out_specs=[vmem] * n + [hbm] * 2,
        scratch_shapes=[pltpu.VMEM((4, 2, 2) + b, t) for b, t in blocks]
        + [pltpu.VMEM((19,) + b, t) for b, t in blocks]
        + [
            pltpu.VMEM((4, 2, 2, rows, half), bf16),
            pltpu.VMEM((4, 2, 2, 8, 128), f32),
            pltpu.VMEM((2, 2, 2, 2, down_rows, width), bf16),
            pltpu.VMEM((half, width), bf16),
            pltpu.VMEM((4, 2, 2, 2, rows, half), bf16),
            pltpu.VMEM((size, half), f32),
            pltpu.VMEM((size, half), f32),
        ]
        + [pltpu.VMEM(square, f32)] * 4
        + [pltpu.VMEM(square, bf16)] * 6
        + [pltpu.VMEM((size, wide), bf16)] * 2
        + [pltpu.VMEM((4, 2, 2, 2, rows, size), bf16)] * 2
        + [pltpu.VMEM((4, 2, 2, 2, down_rows, size), bf16)]
        + [pltpu.VMEM((8, size, size), bf16), pltpu.VMEM(cube, bf16)]
        + [pltpu.VMEM((8, 128), f32)] * 2
        + [pltpu.VMEM((size, size), f32), pltpu.VMEM((size, 128), f32), pltpu.VMEM((size, 128), f32)]
        + [pltpu.VMEM(cube, f32)]
        + state_buffers()
        + [
            pltpu.SemaphoreType.DMA((n, Scatter.NSEND + 1)),
            pltpu.SemaphoreType.DMA((n, Scatter.NRECV)),
            pltpu.SemaphoreType.DMA((18,)),
            pltpu.SemaphoreType.DMA((18,)),
            pltpu.SemaphoreType.DMA((40,)),
        ],
        compiler_params=pltpu.CompilerParams(
            collective_id=3, has_side_effects=True, vmem_limit_bytes=67000000
        ),
        name="backward",
    )(lengths, order, rate, tokens, cot, *saved, *weights)
    return out[:n], out[n], out[n + 1]


def deliver_kernel(result, inputs, *refs):
    grads, out = refs[:12], refs[12:]
    out[0][...] = result[...]
    out[1][...] = inputs[...]
    for i, k in enumerate((9, 11, 10, 8, 6)):
        out[2 + i][...] = grads[k][...]
    me = lax.axis_index(AXIS)
    row = grads[7][pl.ds(me // 4, 1), :]
    own = jnp.zeros((1, 32), jnp.float32)
    for k in range(4):
        own = own + jnp.where(lax.rem(me, 4) == k, 1.0, 0.0) * row[:, 32 * k : 32 * k + 32]
    out[7][...] = own
    for i, k in enumerate((2, 4, 0)):
        out[8 + i][...] = jnp.concatenate([grads[k][...], grads[k + 1][...]], axis=1)


def deliver(result, inputs, grads):
    f32 = jnp.float32
    narrow = [grads[k].shape for k in (9, 11, 10, 8, 6)]
    wide = [(grads[k].shape[0], 2 * grads[k].shape[1]) for k in (2, 4, 0)]
    shapes = narrow + [(1, 32)] + wide
    vmem = pl.BlockSpec(memory_space=pltpu.VMEM)
    out = pl.pallas_call(
        deliver_kernel,
        out_shape=[
            jax.ShapeDtypeStruct(result.shape, result.dtype),
            jax.ShapeDtypeStruct(inputs.shape, f32),
        ]
        + [jax.ShapeDtypeStruct(s, f32) for s in shapes],
        in_specs=[vmem] * 14,
        out_specs=[vmem] * 11,
        name="deliver",
    )(result, inputs, *grads)
    return (*out[:7], out[7].reshape(-1), *out[8:])


def entering(value, axis, combine, identity, reverse):
    length, here = (lax.axis_size(axis), lax.axis_index(axis))
    everything = jax.tree.map(lambda part: lax.all_gather(part, axis), value)
    start = jax.tree.map(
        lambda part, zero: jnp.broadcast_to(jnp.asarray(zero, part.dtype), part.shape),
        value,
        identity,
    )

    def hop(k, before):
        at = length - 1 - k if reverse else k
        reached = at > here if reverse else at < here
        new = combine(before, jax.tree.map(lambda part: part[at], everything))
        return jax.tree.map(lambda a, b: jnp.where(reached, a, b), new, before)

    return lax.fori_loop(0, length, hop, start)


def segment_of(places, lengths, seq_order):
    number = lengths.shape[0]
    picked = seq_order[:, None] == jnp.arange(number, dtype=jnp.int32)[None, :]
    packed = jnp.sum(jnp.where(picked, lengths[None, :], 0), axis=1, dtype=jnp.int32)
    bounds = jnp.cumsum(packed, dtype=jnp.int32)
    found = jnp.sum((bounds[None, :] <= places[:, None]).astype(jnp.int32), axis=1, dtype=jnp.int32)
    return jnp.where(places < 0, -1, found)


def decay_tables(segments, before, rate, block):
    length = segments.shape[0]
    count = length // block
    spans = segments.reshape(count, block)
    priors = jnp.concatenate([before.reshape(1), spans[:-1, -1]])
    steps = jnp.arange(block, dtype=jnp.int32)
    distance = steps[:, None] - steps[None, :]
    same = (spans[:, :, None] == spans[:, None, :]) & (distance >= 0)[None]
    powers = jnp.exp(-rate[:, None, None] * jnp.maximum(distance, 0).astype(jnp.float32)[None])
    within = jnp.where(same[:, None], powers[None], 0.0)
    entry = jnp.where(
        (spans == priors[:, None])[:, :, None],
        jnp.exp(-rate[None, :] * steps.astype(jnp.float32)[:, None])[None],
        0.0,
    )
    leaving = jnp.where(
        (spans == spans[:, -1:])[:, :, None],
        jnp.exp(-rate[None, :] * (block - steps).astype(jnp.float32)[:, None])[None],
        0.0,
    )
    passing = jnp.where((spans[:, -1] == priors)[:, None], jnp.exp(-rate * block)[None], 0.0)
    offsets = (jnp.arange(count, dtype=jnp.int32) * block).astype(jnp.float32)
    arrival = jnp.where(
        (priors == before)[:, None], jnp.exp(-rate[None, :] * offsets[:, None]), 0.0
    )
    through = jnp.where(segments[-1] == before, jnp.exp(-rate * length), 0.0)
    return (within, entry, leaving, passing, arrival, through)


def chain_states(earlier, later):
    return (earlier[0] * later[0], later[0][:, None, None] * earlier[1] + later[1])


def silu_slope(values):
    sigma = jax.nn.sigmoid(values)
    return sigma * (1.0 + values * (1.0 - sigma))


def row_scale(values):
    return lax.rsqrt(jnp.mean(values * values, axis=-1, keepdims=True) + EPSILON)


def body(
    tokens,
    lengths,
    seq_order,
    decay_rate,
    w_query,
    w_key,
    w_value,
    w_unit,
    w_output,
    norm_gain,
    w_left,
    w_right,
    w_down,
    cotangent,
):
    f32 = jnp.float32
    bf16 = jnp.bfloat16
    length, width = tokens.shape
    heads = decay_rate.shape[0]
    head_size = width // heads
    count = length // SPAN
    first = lax.axis_index(AXIS) * length
    places = first + jnp.arange(length, dtype=jnp.int32)
    segments = segment_of(places, lengths, seq_order)
    before = segment_of(jnp.reshape(first - 1, (1,)), lengths, seq_order)[0]
    within, entry, leaving, passing, arrival, through = decay_tables(
        segments, before, decay_rate, SPAN
    )
    attention_set = (
        lax.all_gather(w_query, AXIS, axis=0, tiled=True),
        lax.all_gather(w_key, AXIS, axis=0, tiled=True),
        lax.all_gather(w_value, AXIS, axis=0, tiled=True),
        lax.all_gather(w_unit, AXIS, axis=0, tiled=True),
        lax.all_gather(w_output, AXIS, axis=0, tiled=True),
        lax.all_gather(norm_gain, AXIS, axis=0, tiled=True),
    )
    feed_set = (
        lax.all_gather(w_left, AXIS, axis=0, tiled=True),
        lax.all_gather(w_right, AXIS, axis=0, tiled=True),
        lax.all_gather(w_down, AXIS, axis=0, tiled=True),
    )
    full_query, full_key, full_value, full_unit, full_output, full_gain = attention_set
    full_left, full_right, full_down = feed_set
    inputs = tokens.astype(f32)
    first_scale = row_scale(inputs)
    normed = inputs * first_scale
    hidden = normed.astype(bf16)
    query_pre = jnp.dot(hidden, full_query, preferred_element_type=f32)
    key_pre = jnp.dot(hidden, full_key, preferred_element_type=f32)
    value_pre = jnp.dot(hidden, full_value, preferred_element_type=f32)
    unit_pre = jnp.dot(hidden, full_unit, preferred_element_type=f32)
    block_shape = (count, SPAN, heads, head_size)
    query_blocks = jax.nn.silu(query_pre).astype(bf16).reshape(block_shape)
    key_blocks = jax.nn.silu(key_pre).astype(bf16).reshape(block_shape)
    value_blocks = value_pre.astype(bf16).reshape(block_shape)
    scores = jnp.einsum("nthe,nshe->nhts", query_blocks, key_blocks, preferred_element_type=f32)
    mixing = (scores * within).astype(bf16)
    local_out = jnp.einsum("nhts,nshe->nthe", mixing, value_blocks, preferred_element_type=f32)
    keys_held = (key_blocks * leaving[..., None]).astype(bf16)
    increments = jnp.einsum("nshe,nshf->nhef", keys_held, value_blocks, preferred_element_type=f32)
    local_states = [jnp.zeros((heads, head_size, head_size), f32)]
    local_states.append(passing[0][:, None, None] * local_states[-1] + increments[0])
    end_state = local_states[count]
    start_pair = (jnp.ones_like(through), jnp.zeros_like(end_state))
    arriving = entering((through, end_state), AXIS, chain_states, start_pair, False)[1]
    states = jnp.stack(local_states[:count]) + arrival[:, :, None, None] * arriving[None]
    state_low = states.astype(bf16)
    query_held = (query_blocks * entry[..., None]).astype(bf16)
    attended = local_out + jnp.einsum(
        "nthe,nhef->nthf", query_held, state_low, preferred_element_type=f32
    )
    attended_heads = attended.reshape(length, heads, head_size)
    head_scale = row_scale(attended_heads)
    unit_norm = (attended_heads * head_scale).reshape(length, width)
    gain = full_gain.astype(f32)
    gated = unit_norm * gain
    mixed_in = (gated * unit_pre).astype(bf16)
    middle = inputs + jnp.dot(mixed_in, full_output, preferred_element_type=f32)
    second_scale = row_scale(middle)
    second_unit = middle * second_scale
    second = second_unit.astype(bf16)
    left_pre = jnp.dot(second, full_left, preferred_element_type=f32)
    right_pre = jnp.dot(second, full_right, preferred_element_type=f32)
    product = (left_pre * right_pre).astype(bf16)
    result = (middle + jnp.dot(product, full_down, preferred_element_type=f32)).astype(bf16)
    back_feed = (
        lax.all_gather(w_left, AXIS, axis=0, tiled=True),
        lax.all_gather(w_right, AXIS, axis=0, tiled=True),
        lax.all_gather(w_down, AXIS, axis=0, tiled=True),
    )
    back_left, back_right, back_down = back_feed
    grad_product = jnp.einsum("td,fd->tf", cotangent, back_down, preferred_element_type=f32)
    grad_left_pre = (grad_product * right_pre).astype(bf16)
    grad_right_pre = (grad_product * left_pre).astype(bf16)
    grad_w_down = jnp.einsum("tf,td->fd", product, cotangent, preferred_element_type=f32)
    grad_w_left = jnp.einsum("td,tf->df", second, grad_left_pre, preferred_element_type=f32)
    grad_w_right = jnp.einsum("td,tf->df", second, grad_right_pre, preferred_element_type=f32)
    feed_grads = (
        lax.psum_scatter(grad_w_left, AXIS, scatter_dimension=0, tiled=True),
        lax.psum_scatter(grad_w_right, AXIS, scatter_dimension=0, tiled=True),
        lax.psum_scatter(grad_w_down, AXIS, scatter_dimension=0, tiled=True),
    )
    grad_second = jnp.einsum(
        "tf,df->td", grad_left_pre, back_left, preferred_element_type=f32
    ) + jnp.einsum("tf,df->td", grad_right_pre, back_right, preferred_element_type=f32)
    grad_middle = cotangent.astype(f32) + second_scale * (
        grad_second - second_unit * jnp.mean(grad_second * second_unit, axis=-1, keepdims=True)
    )
    back_attention = (
        lax.all_gather(w_query, AXIS, axis=0, tiled=True),
        lax.all_gather(w_key, AXIS, axis=0, tiled=True),
        lax.all_gather(w_value, AXIS, axis=0, tiled=True),
        lax.all_gather(w_unit, AXIS, axis=0, tiled=True),
        lax.all_gather(w_output, AXIS, axis=0, tiled=True),
        lax.all_gather(norm_gain, AXIS, axis=0, tiled=True),
    )
    back_query, back_key, back_value, back_unit, back_output, back_gain = back_attention
    grad_branch = grad_middle.astype(bf16)
    grad_w_output = jnp.einsum(TD_TE, mixed_in, grad_branch, preferred_element_type=f32)
    grad_mixed = jnp.einsum(TE_DE, grad_branch, back_output, preferred_element_type=f32)
    grad_gated = grad_mixed * unit_pre
    grad_unit_pre = (grad_mixed * gated).astype(bf16)
    grad_gain = jnp.sum(grad_gated * unit_norm, axis=0)
    grad_norm_heads = (grad_gated * back_gain.astype(f32)).reshape(length, heads, head_size)
    norm_heads = unit_norm.reshape(length, heads, head_size)
    grad_att = head_scale * (
        grad_norm_heads
        - norm_heads * jnp.mean(grad_norm_heads * norm_heads, axis=-1, keepdims=True)
    )
    grad_att_blocks = grad_att.astype(bf16).reshape(block_shape)
    grad_mixing = jnp.einsum(
        "nthf,nshf->nhts", grad_att_blocks, value_blocks, preferred_element_type=f32
    )
    grad_scores = (grad_mixing * within).astype(bf16)
    grad_query_blocks = (
        jnp.einsum("nhts,nshe->nthe", grad_scores, key_blocks, preferred_element_type=f32)
        + jnp.einsum("nthf,nhef->nthe", grad_att_blocks, state_low, preferred_element_type=f32)
        * entry[..., None]
    )
    grad_key_blocks = jnp.einsum(
        "nhts,nthe->nshe", grad_scores, query_blocks, preferred_element_type=f32
    )
    grad_value_blocks = jnp.einsum(
        "nhts,nthf->nshf", mixing, grad_att_blocks, preferred_element_type=f32
    )
    direct = jnp.einsum("nthe,nthf->nhef", query_held, grad_att_blocks, preferred_element_type=f32)
    leaving_sum = jnp.sum(arrival[:, :, None, None] * direct, axis=0)
    later = entering((through, leaving_sum), AXIS, chain_states, start_pair, True)[1]
    next_grads = [later]
    grad_increment = jnp.stack(next_grads[::-1]).astype(bf16)
    grad_keys_held = jnp.einsum(
        "nhef,nshf->nshe", grad_increment, value_blocks, preferred_element_type=f32
    )
    grad_key_blocks = grad_key_blocks + grad_keys_held * leaving[..., None]
    grad_value_blocks = grad_value_blocks + jnp.einsum(
        "nshe,nhef->nshf", keys_held, grad_increment, preferred_element_type=f32
    )
    grad_query_pre = (grad_query_blocks.reshape(length, width) * silu_slope(query_pre)).astype(bf16)
    grad_key_pre = (grad_key_blocks.reshape(length, width) * silu_slope(key_pre)).astype(bf16)
    grad_value_pre = grad_value_blocks.reshape(length, width).astype(bf16)
    grad_w_query = jnp.einsum(TD_TE, hidden, grad_query_pre, preferred_element_type=f32)
    grad_w_key = jnp.einsum(TD_TE, hidden, grad_key_pre, preferred_element_type=f32)
    grad_w_value = jnp.einsum(TD_TE, hidden, grad_value_pre, preferred_element_type=f32)
    grad_w_unit = jnp.einsum(TD_TE, hidden, grad_unit_pre, preferred_element_type=f32)
    attention_grads = (
        lax.psum_scatter(grad_w_query, AXIS, scatter_dimension=0, tiled=True),
        lax.psum_scatter(grad_w_key, AXIS, scatter_dimension=0, tiled=True),
        lax.psum_scatter(grad_w_value, AXIS, scatter_dimension=0, tiled=True),
        lax.psum_scatter(grad_w_unit, AXIS, scatter_dimension=0, tiled=True),
        lax.psum_scatter(grad_w_output, AXIS, scatter_dimension=0, tiled=True),
        lax.psum_scatter(grad_gain, AXIS, scatter_dimension=0, tiled=True),
    )
    grad_hidden = (
        jnp.einsum(TE_DE, grad_query_pre, back_query, preferred_element_type=f32)
        + jnp.einsum(TE_DE, grad_key_pre, back_key, preferred_element_type=f32)
        + jnp.einsum(TE_DE, grad_value_pre, back_value, preferred_element_type=f32)
        + jnp.einsum(TE_DE, grad_unit_pre, back_unit, preferred_element_type=f32)
    )
    grad_inputs = grad_middle + first_scale * (
        grad_hidden - normed * jnp.mean(grad_hidden * normed, axis=-1, keepdims=True)
    )
    return (
        result,
        grad_inputs,
        attention_grads[0],
        attention_grads[1],
        attention_grads[2],
        attention_grads[3],
        attention_grads[4],
        attention_grads[5],
        feed_grads[0],
        feed_grads[1],
        feed_grads[2],
    )


def body_kernels(
    tokens,
    lengths,
    seq_order,
    decay_rate,
    w_query,
    w_key,
    w_value,
    w_unit,
    w_output,
    norm_gain,
    w_left,
    w_right,
    w_down,
    cotangent,
):
    f32 = jnp.float32
    heads = decay_rate.shape[0]
    devices = lax.axis_size(AXIS)
    me = lax.axis_index(AXIS)
    mine = jnp.arange(devices, dtype=jnp.int32)[:, None] == me
    gain_tile = jnp.where(mine, norm_gain.astype(f32)[None, :], 0.0).reshape(heads, -1)
    full, saved = forward(
        lengths,
        seq_order,
        decay_rate,
        tokens,
        cotangent,
        gain_tile,
        [w_key, w_value, w_query, w_unit, w_output, w_left, w_right, w_down],
    )
    grads, result, grad_inputs = backward(
        lengths, seq_order, decay_rate, tokens, cotangent, saved, full[:4] + full[5:]
    )
    return deliver(result, grad_inputs, grads)


def solution(mesh):
    placed = (
        P(AXIS, None),
        P(),
        P(),
        P(),
        P(AXIS, None),
        P(AXIS, None),
        P(AXIS, None),
        P(AXIS, None),
        P(AXIS, None),
        P(AXIS),
        P(AXIS, None),
        P(AXIS, None),
        P(AXIS, None),
        P(AXIS, None),
    )
    return jax.shard_map(
        body_kernels if mesh.size == 32 else body,
        mesh=mesh,
        in_specs=placed,
        out_specs=(
            P(AXIS, None),
            P(AXIS, None),
            P(AXIS, None),
            P(AXIS, None),
            P(AXIS, None),
            P(AXIS, None),
            P(AXIS, None),
            P(AXIS),
            P(AXIS, None),
            P(AXIS, None),
            P(AXIS, None),
        ),
        check_vma=False,
    )
```

```python
import functools

import jax
import jax.numpy as jnp
from jax import lax
from jax.experimental import pallas as pl
from jax.experimental.pallas import tpu as pltpu
from jax.sharding import PartitionSpec as P

SPAN = 256
AXIS = "fsdp"
TE_DE = "te,de->td"
TD_TE = "td,te->de"
EPSILON = 1e-05
LOGICAL = pl.DeviceIdType.LOGICAL
VMEM_LIMIT = 64000000


class Place:
    def __init__(self):
        me = lax.axis_index(AXIS)
        self.me = me
        self.c = lax.rem(me, 2)
        self.x = lax.rem(me // 2, 2)
        self.y = lax.rem(me // 4, 2)
        self.z = me // 8
        self.inner = (self.z == 1) | (self.z == 2)
        self.even = lax.rem(self.z, 2) == 0
        self.sib = self.z + 1 - 2 * lax.rem(self.z, 2)
        half = self.z // 2
        self.near = 2 - half
        self.far = 3 - 3 * half
        self.cross = 3 - self.z
        self.x1 = 1 - self.x
        self.y1 = 1 - self.y
        self.c1 = 1 - self.c
        self.to = {
            "S": self.dev(self.sib, self.y, self.x, self.c),
            "K": self.dev(self.cross, self.y, self.x, self.c),
            "x": self.dev(self.z, self.y, self.x1, self.c),
            "y": self.dev(self.z, self.y1, self.x, self.c),
            "p": self.dev(self.z, self.y, self.x, self.c1),
        }

    def dev(self, z, y, x, c):
        return ((z * 2 + y) * 2 + x) * 2 + c


def arrived(ref, send, recv, place):
    pltpu.make_async_remote_copy(
        src_ref=ref,
        dst_ref=ref,
        send_sem=send,
        recv_sem=recv,
        device_id=place.to["p"],
        device_id_type=LOGICAL,
    ).wait_recv()


class Gather:
    RECV = ("Cs", "Cn", "Cf", "Xo", "Xs", "Xn", "Xf", "Yo", "Ys", "Yn", "Yf", "D0", "D1", "En", "Ef")
    GROUPS = ("C", "X", "Y", "D")
    NRECV = 19
    NSEND = 25

    def __init__(self, place, own, full, send, recv, index):
        self.p, self.own, self.full = place, own, full
        self.send, self.recv, self.index = send, recv, index
        self.sent = []
        p = place
        self.where = {}
        for g, y, x in (("C", p.y, p.x), ("X", p.y, p.x1), ("Y", p.y1, p.x), ("D", p.y1, p.x1)):
            for k, z in (("o", p.z), ("s", p.sib), ("n", p.near), ("f", p.far)):
                self.where[g + k] = (z, y, x, p.c)
        for a, b in (("D0", "Do"), ("D1", "Ds"), ("En", "Dn"), ("Ef", "Df")):
            self.where[a] = self.where[b]

    def slot(self, name):
        return self.full.at[self.where[name]]

    def copy(self, name, link, landing):
        src = self.own if name == "Co" else self.slot(name)
        k = len(self.sent)
        made = pltpu.make_async_remote_copy(
            src_ref=src,
            dst_ref=self.slot(name),
            send_sem=self.send.at[self.index, k],
            recv_sem=self.recv.at[self.index, self.RECV.index(landing)],
            device_id=self.p.to[link],
            device_id_type=LOGICAL,
        )
        return made

    def go(self, name, link, landing, cond=None):
        made = self.copy(name, link, landing)
        self.sent.append((made, cond))
        if cond is None:
            made.start()
        else:
            pl.when(cond)(made.start)

    def wait(self, name):
        arrived(self.slot(name), self.send.at[self.index, 0], self.recv.at[self.index, self.RECV.index(name)], self.p)

    def group(self, g):
        p = self.p
        y = p.y if g in "CX" else p.y1
        x = p.x if g in "CY" else p.x1
        return y, x

    def pair(self, g):
        y, x = self.group(g)
        ref = self.full.at[:, y, x, self.p.c]
        k = len(self.sent)
        made = pltpu.make_async_remote_copy(
            src_ref=ref,
            dst_ref=ref,
            send_sem=self.send.at[self.index, k],
            recv_sem=self.recv.at[self.index, 15 + self.GROUPS.index(g)],
            device_id=self.p.to["p"],
            device_id_type=LOGICAL,
        )
        self.sent.append((made, None))
        made.start()

    def round(self, r):
        p = self.p
        inner, even = p.inner, p.even
        odd = jnp.logical_not(even)
        if r == 0:
            keep = pltpu.make_async_copy(self.own, self.slot("Co"), self.send.at[self.index, self.NSEND])
            self.keep = keep
            keep.start()
            self.go("Co", "S", "Cs")
            self.go("Co", "K", "Cn", inner)
            self.go("Co", "x", "Xo")
            self.go("Co", "y", "Yo")
        outer = jnp.logical_not(inner)
        if r == 1:
            self.wait("Cs")
            self.go("Cs", "K", "Cf", inner)
            self.go("Cs", "x", "Xs")
            self.go("Cs", "y", "Ys")
            self.wait("Xo")
            self.go("Xo", "y", "D0", even)
            self.wait("Yo")
            self.go("Yo", "x", "D0", odd)
            self.relay("Cn")
        if r == 2:
            pl.when(outer)(lambda: self.wait("Cn"))
            self.go("Cn", "x", "Xn")
            self.go("Cn", "y", "Yn")
            self.wait("Xs")
            self.go("Xs", "y", "D1", odd)
            self.wait("Ys")
            self.go("Ys", "x", "D1", even)
            self.wait("D0")
            self.go("D0", "K", "En", inner)
            self.relay("Cf")
        if r == 3:
            pl.when(outer)(lambda: self.wait("Cf"))
            self.go("Cf", "x", "Xf")
            self.go("Cf", "y", "Yf")
            self.keep.wait()
            self.pair("C")
            self.wait("D1")
            self.go("D1", "K", "Ef", inner)
            self.wait("Xn")
            self.wait("Yn")
            self.relay("En")
        if r == 4:
            pl.when(outer)(lambda: self.wait("En"))
            self.wait("Xf")
            self.pair("X")
            self.wait("Yf")
            self.pair("Y")
            self.relay("Ef")
        if r == 5:
            pl.when(outer)(lambda: self.wait("Ef"))
            self.pair("D")

    def relay(self, name):
        pl.when(self.p.inner)(lambda: self.wait(name))
        self.go(name, "S", name, self.p.inner)

    def pairs(self):
        for g in self.GROUPS:
            y, x = self.group(g)
            ref = self.full.at[:, y, x, self.p.c1]
            arrived(ref, self.send.at[self.index, 0], self.recv.at[self.index, 15 + self.GROUPS.index(g)], self.p)

    def finish(self):
        for made, cond in self.sent:
            if cond is None:
                made.wait_send()
            else:
                pl.when(cond)(made.wait_send)


def add_into(out, parts):
    rows = out.shape[0]
    step = 8 if rows % 16 else 16

    @pl.loop(0, rows // step)
    def _(i):
        at = pl.ds(pl.multiple_of(i * step, step), step)
        total = parts[0][at, :].astype(jnp.float32)
        for part in parts[1:]:
            total = total + part[at, :].astype(jnp.float32)
        out[at, :] = total.astype(out.dtype)


class Scatter:
    NRECV = 20
    NSEND = 22
    SLOTS = ("x0", "x1", "x2", "x3", "Fx", "y0", "y1", "y2", "y3", "Fy", "En", "Ef", "Cn", "Cf", "Co", "De", "Do", "KCs", "KCo")

    def __init__(self, place, part, acc, term, came, out, send, recv, index):
        self.p, self.part, self.acc, self.term, self.came, self.out = place, part, acc, term, came, out
        self.send, self.recv, self.index = send, recv, index
        self.sent = []
        p = place
        half = p.z // 2
        self.ze, self.zo = 2 * half, 2 * half + 1
        self.C = lambda z: (z, p.y, p.x)
        self.X = lambda z: (z, p.y, p.x1)
        self.Y = lambda z: (z, p.y1, p.x)
        self.D = lambda z: (z, p.y1, p.x1)

    def go(self, where, link, slot, cond=None):
        k = len(self.sent)
        at = self.SLOTS.index(slot) if isinstance(slot, str) else slot
        made = pltpu.make_async_remote_copy(
            src_ref=self.acc.at[where],
            dst_ref=self.came.at[at],
            send_sem=self.send.at[self.index, k],
            recv_sem=self.recv.at[self.index, at],
            device_id=self.p.to[link],
            device_id_type=LOGICAL,
        )
        self.sent.append((made, cond))
        if cond is None:
            made.start()
        else:
            pl.when(cond)(made.start)

    def wait(self, slot):
        at = self.SLOTS.index(slot) if isinstance(slot, str) else slot
        arrived(self.came.at[at], self.send.at[self.index, 0], self.recv.at[self.index, at], self.p)
        return self.came.at[at]

    def add(self, where, slots):
        parts = [self.wait(s) for s in slots]
        add_into(self.acc.at[where], [self.acc.at[where]] + parts)

    def round(self, r):
        p = self.p
        inner = p.inner
        outer = jnp.logical_not(inner)
        ze, zo, near, far = self.ze, self.zo, p.near, p.far
        if r == 0:
            self.given = pltpu.make_async_remote_copy(
                src_ref=self.part,
                dst_ref=self.acc,
                send_sem=self.send.at[self.index, self.NSEND],
                recv_sem=self.recv.at[self.index, 19],
                device_id=p.to["p"],
                device_id_type=LOGICAL,
            )
            self.given.start()
        if r == 1:
            arrived(self.acc, self.send.at[self.index, 0], self.recv.at[self.index, 19], p)
            self.term.second(self.acc)
            self.go(self.D(far), "S", "Ef", outer)
            self.go(self.D(near), "S", "En", outer)
            self.go(self.X(far), "x", far)
            self.go(self.Y(far), "y", far + 5)
            self.go(self.D(ze), "y", "Fy", outer)
            self.go(self.D(zo), "x", "Fx", outer)
            self.go(self.X(near), "x", near)
            self.go(self.Y(near), "y", near + 5)
            self.go(self.X(zo), "x", zo)
            self.go(self.Y(ze), "y", ze + 5)
        if r == 2:

            @pl.when(inner)
            def _():
                self.add(self.D(far), ["Ef"])
                self.add(self.D(near), ["En"])

            self.go(self.D(far), "K", jnp.where(p.z == 1, self.SLOTS.index("Do"), self.SLOTS.index("De")), inner)
            self.go(self.D(near), "K", jnp.where(p.z == 1, self.SLOTS.index("De"), self.SLOTS.index("Do")), inner)
            parts = [self.wait(far), self.wait(far + 5)]
            add_into(self.acc.at[self.C(far)], [self.acc.at[self.C(far)]] + parts)
            self.go(self.C(far), "S", "Cf", outer)
        if r == 3:

            @pl.when(inner)
            def _():
                self.add(self.D(ze), ["De"])
                self.add(self.D(zo), ["Do"])
                self.add(self.C(far), ["Cf"])

            self.go(self.D(ze), "y", "Fy", inner)
            self.go(self.D(zo), "x", "Fx", inner)
            self.go(self.C(far), "K", "KCs", inner)
            parts = [self.wait(near), self.wait(near + 5)]
            add_into(self.acc.at[self.C(near)], [self.acc.at[self.C(near)]] + parts)
            self.go(self.C(near), "S", "Cn", outer)
        if r == 4:
            self.add(self.X(ze), ["Fy"])
            self.add(self.Y(zo), ["Fx"])
            self.go(self.X(ze), "x", ze)
            self.go(self.Y(zo), "y", zo + 5)

            @pl.when(inner)
            def _():
                self.add(self.C(near), ["Cn"])

            self.go(self.C(near), "K", "KCo", inner)
        if r == 5:
            self.add(self.C(p.sib), [p.sib, p.sib + 5])

            @pl.when(inner)
            def _():
                self.add(self.C(p.sib), ["KCs"])

            self.go(self.C(p.sib), "S", "Co")
        if r == 6:
            slots = [p.z, p.z + 5, "Co"]
            parts = [self.acc.at[self.C(p.z)]] + [self.wait(s) for s in slots]
            add_into(self.out, parts)

            @pl.when(inner)
            def _():
                add_into(self.out, [self.out, self.wait("KCo")])

    def handed(self):
        self.given.wait_send()

    def finish(self):
        for made, cond in self.sent:
            if cond is None:
                made.wait_send()
            else:
                pl.when(cond)(made.wait_send)


def bounds_of(lengths, order):
    total, found = jnp.int32(0), []
    for j in range(lengths.shape[0]):
        total = total + lengths[order[j]]
        found.append(total)
    return found


def segment_at(bounds, places):
    found = jnp.zeros_like(places)
    for bound in bounds:
        found = found + jnp.where(bound <= places, 1, 0)
    return found


def same_segment(bounds, earlier, later):
    same = jnp.int32(0)
    for bound in bounds:
        same = same + jnp.where((bound <= earlier) != (bound <= later), 1, 0)
    return jnp.where((earlier >= 0) & (same == 0), 1.0, 0.0).astype(jnp.float32)


def spans_of(first, bounds, dist, entry, leaving):
    size = dist.shape[0]
    t = lax.broadcasted_iota(jnp.int32, (size, size), 0)
    s = lax.broadcasted_iota(jnp.int32, (size, size), 1)
    same = segment_at(bounds, t + first) == segment_at(bounds, s + first)
    dist[...] = jnp.where(same & (s <= t), t - s, -1).astype(jnp.float32)
    t = lax.broadcasted_iota(jnp.int32, entry.shape, 0)
    here = segment_at(bounds, t + first)
    ahead = segment_at(bounds, jnp.full(entry.shape, first - 1, jnp.int32))
    ahead = jnp.where(jnp.full(entry.shape, first, jnp.int32) == 0, -1, ahead)
    last = segment_at(bounds, jnp.full(entry.shape, first + size - 1, jnp.int32))
    entry[...] = jnp.where(here == ahead, t, -1).astype(jnp.float32)
    leaving[...] = jnp.where(here == last, size - t, -1).astype(jnp.float32)


def decay(distance, rate):
    return jnp.where(distance >= 0, jnp.exp(-rate * distance), 0.0)


def mm(a, b):
    return jnp.dot(a, b, preferred_element_type=jnp.float32)


def mm_nt(a, b):
    return lax.dot_general(a, b, (((1,), (1,)), ((), ())), preferred_element_type=jnp.float32)


def mm_tn(a, b):
    return lax.dot_general(a, b, (((0,), (0,)), ((), ())), preferred_element_type=jnp.float32)


def head_of(h):
    return pl.ds(pl.multiple_of(h * 128, 128), 128)


def norm_scale(values):
    return lax.rsqrt(jnp.mean(values * values, axis=-1, keepdims=True) + EPSILON)


def slope(a):
    sigma = 1.0 / (1.0 + jnp.exp(-a))
    return sigma * (1.0 + a * (1.0 - sigma))


def flat_rows(value):
    return value.astype(jnp.float32).reshape(-1, value.shape[-1]).astype(jnp.bfloat16)


SAVED_BACK = 20


def parts_of(width, last):
    cuts = (0, width // 2, width - last, width)
    return [(a, b - a) for a, b in zip(cuts, cuts[1:])]


class States:
    def __init__(self, place, bounds, rate, reverse, value, buffers, send, recv):
        self.bounds, self.reverse, self.rate = bounds, reverse, rate
        self.value = value
        self.theirs, self.sums, self.met, self.planes, self.ready, self.entered, self.give, self.out, self.sum = buffers
        self.send, self.recv = send, recv
        self.z, self.c, self.c1 = place.z, place.c, place.c1
        self.me, self.partner = place.me, place.to["p"]
        self.q = lax.rem(place.me // 2, 4)
        self.chip = [self.at(self.z, lax.bitwise_xor(self.q, k)) for k in range(4)]
        self.level = [self.at(lax.rem(self.z + k, 4), self.q) for k in range(4)]
        self.order = range(3, -1, -1) if reverse else range(4)
        lead = 1 if reverse else 0
        self.lead = jnp.where(self.c == lead, 1.0, 0.0).astype(jnp.float32)
        base = self.me - self.c
        self.lead_through = self.through(base + lead, 1)
        self.last_through = self.through(base + 1 - lead, 1)
        mine = rate[4 * self.c + self.q]
        self.chip_step = jnp.exp(jnp.full((1, 128), -2 * SPAN * mine, jnp.float32))
        self.plane_step = jnp.exp(jnp.full((1, 128), -8 * SPAN * mine, jnp.float32))

    def at(self, z, q):
        return (z * 4 + q) * 2 + self.c

    def through(self, device, count):
        return same_segment(self.bounds, device * SPAN - 1, (device + count) * SPAN - 1)

    def step(self, k):
        return jnp.exp(jnp.full((1, 128), -SPAN * self.rate[4 * self.c + k], jnp.float32))

    def copy(self, src, dst, k, peer):
        return pltpu.make_async_remote_copy(
            src_ref=src,
            dst_ref=dst,
            send_sem=self.send.at[k],
            recv_sem=self.recv.at[k],
            device_id=peer,
            device_id_type=LOGICAL,
        )

    def other(self, k):
        return lax.bitwise_xor(self.q, k)

    def begin(self, made):
        for one in made:
            one.start()
        return made

    def terms(self, k):
        mine, theirs = self.value[4 * self.c + k], self.theirs[k]
        rest = 1.0 - self.lead
        return self.lead * mine + rest * theirs, rest * mine + self.lead * theirs

    def spread(self):
        half = self.value.at[pl.ds(4 * self.c1, 4)]
        self.sent = self.begin([self.copy(half, self.theirs, 0, self.partner)])

    def join(self):
        self.copy(self.theirs, self.theirs, 0, self.partner).wait_recv()
        for k in range(4):
            first, last = self.terms(k)
            self.sums[k] = (self.last_through * self.step(k) * first + last).astype(jnp.bfloat16)
        self.sent += self.begin(
            [
                self.copy(self.sums.at[self.other(k)], self.met.at[self.q], k, self.chip[k])
                for k in range(1, 4)
            ]
        )
        self.met[self.q] = self.sums[self.q]

    def total(self):
        for k in range(1, 4):
            self.copy(self.sums.at[0], self.met.at[self.other(k)], k, self.chip[k]).wait_recv()
        total = jnp.zeros(self.met.shape[1:], jnp.float32)
        for i in self.order:
            through = self.through(self.z * 8 + 2 * i, 2)
            total = through * self.chip_step * total + self.met[i].astype(jnp.float32)
        self.planes[self.z] = total.astype(jnp.bfloat16)
        self.second = []
        for k in range(1, 4):
            far = self.z - k if self.reverse else self.z + k
            cond = far >= 0 if self.reverse else far <= 3
            made = self.copy(
                self.planes.at[self.z], self.planes.at[self.z], 3 + k, self.at(far, self.q)
            )
            self.second.append((made, cond))
            pl.when(cond)(made.start)

    def back(self):
        self.sum[...] = jnp.zeros(self.sum.shape, jnp.float32)
        for k in range(3, 0, -1):
            far = self.z + k if self.reverse else self.z - k
            cond = far <= 3 if self.reverse else far >= 0

            @pl.when(cond)
            def _():
                self.copy(
                    self.planes.at[self.z], self.planes.at[far], 3 + k, self.partner
                ).wait_recv()
                kept = self.through(far * 8, 8) * self.plane_step
                self.sum[...] = kept * self.sum[...] + self.planes[far].astype(jnp.float32)

        total = self.sum[...]
        for i in self.order:
            self.ready[i] = total.astype(jnp.bfloat16)
            through = self.through(self.z * 8 + 2 * i, 2)
            total = through * self.chip_step * total + self.met[i].astype(jnp.float32)
        self.sent += self.begin(
            [
                self.copy(self.ready.at[self.other(k)], self.entered.at[self.q], 6 + k, self.chip[k])
                for k in range(1, 4)
            ]
        )
        self.entered[self.q] = self.ready[self.q]

    def part(self):
        for k in range(1, 4):
            self.copy(self.ready.at[0], self.entered.at[self.other(k)], 6 + k, self.chip[k]).wait_recv()
        rest = 1.0 - self.lead
        for k in range(4):
            first, _ = self.terms(k)
            entering = self.entered[k].astype(jnp.float32)
            later = self.lead_through * self.step(k) * entering + first
            self.out[4 * self.c + k] = (self.lead * entering + rest * later).astype(jnp.bfloat16)
            self.give[k] = (self.lead * later + rest * entering).astype(jnp.bfloat16)
        at = pl.ds(4 * self.c, 4)
        self.sent += self.begin([self.copy(self.give, self.out.at[at], 10, self.partner)])

    def done(self):
        at = pl.ds(4 * self.c1, 4)
        self.copy(self.give, self.out.at[at], 10, self.partner).wait_recv()

    def finish(self):
        for one in self.sent:
            one.wait_send()
        for made, cond in self.second:
            pl.when(cond)(made.wait_send)


def state_buffers():
    cube, low = (4, 128, 128), jnp.bfloat16
    return (
        [pltpu.VMEM(cube, jnp.float32)]
        + [pltpu.VMEM(cube, low)] * 6
        + [pltpu.VMEM((8, 128, 128), low), pltpu.VMEM((128, 128), jnp.float32)]
    )


def greet_more(place):
    barrier = pltpu.get_barrier_semaphore()
    r = lax.rem(place.me, 8)
    peers = [place.z * 8 + lax.bitwise_xor(r, k) for k in range(1, 8)]
    peers += [lax.rem(place.z + k, 4) * 8 + r for k in range(1, 4)]
    for peer in peers:
        pl.semaphore_signal(barrier, inc=1, device_id=peer, device_id_type=LOGICAL)
    pl.semaphore_wait(barrier, len(peers))


def forward_kernel(
    lengths,
    order,
    rate,
    tokens,
    cot,
    gain_own,
    s_key,
    s_value,
    s_query,
    s_unit,
    s_output,
    s_left,
    s_right,
    s_down,
    *refs,
):
    f32, bf16 = jnp.float32, jnp.bfloat16
    n = 13
    full, refs = refs[:n], refs[n:]
    saved, refs = refs[:SAVED_BACK], refs[SAVED_BACK:]
    kept, refs = refs[:SAVED_BACK], refs[SAVED_BACK:]
    (hidden_rows, keys, values, queries, key_pre, query_pre, unit_pre, probs) = kept[:8]
    (attended, state_low, mixed_rows, middle, second_rows, left, right, product) = kept[8:16]
    gain, down_terms = kept[16], kept[17:]
    (hidden, mixed, second, turned, gain_tile) = refs[:5]
    refs = refs[1:]
    (dist, entry, leaving, gains, value) = refs[4:9]
    state_refs, arriving = refs[9:18], refs[16]
    (narrow, wide, send, recv, state_send, state_recv, load_sem, save_sem) = refs[18:]
    place = Place()
    half = s_left.shape[1] // 2
    own = [s_key, s_value, s_query, s_unit, gain_tile, s_output]
    own += [s_left.at[:, pl.ds(0, half)], s_left.at[:, pl.ds(half, half)]]
    own += [s_right.at[:, pl.ds(0, half)], s_right.at[:, pl.ds(half, half)]]
    parts = parts_of(s_down.shape[1], 128)
    own += [s_down.at[:, pl.ds(a, size)] for a, size in parts]
    lane = lax.broadcasted_iota(jnp.int32, gain_tile.shape, 1)
    line = lax.broadcasted_iota(jnp.int32, gain_tile.shape, 0)
    row = jnp.concatenate([gain_own[...].astype(f32)] * 4, axis=1)
    here = (lane // 32 == lax.rem(place.me, 4)) & (line == place.me // 4)
    gain_tile[...] = jnp.where(here, jnp.broadcast_to(row, gain_tile.shape), 0.0)
    greet_more(place)
    made = [Gather(place, own[i], full[i], send, recv, i) for i in range(n)]
    bounds = bounds_of(lengths, order)
    states = States(
        place, bounds, rate, False, value, state_refs, state_send, state_recv
    )
    slots = {0: narrow.at[0], 1: narrow.at[1], 2: narrow.at[0], 3: narrow.at[1], 4: gains}
    slots.update({5: narrow.at[0], 6: wide.at[0], 7: wide.at[1], 8: wide.at[0], 9: wide.at[1]})
    saves = []

    def save(*numbers):
        for i in numbers:
            copy = pltpu.make_async_copy(kept[i], saved[i], save_sem.at[i])
            copy.start()
            saves.append(copy)

    def weight(i):
        ref = slots[i]
        return ref[...].reshape(-1, ref.shape[-1])

    def turn(ref, rows):
        @pl.loop(0, 8)
        def _(i):
            block = ref[:, head_of(i)].astype(f32).T
            rows[i // 2, i % 2] = block.reshape((2, 2) + rows.shape[4:]).astype(bf16)

    def start():
        x = tokens[...].astype(f32)
        hidden[...] = (x * norm_scale(x)).astype(bf16)
        spans_of(place.me * SPAN, bounds, dist, entry, leaving)
        turn(hidden, hidden_rows)
        save(0)

    def project(i, pre, low):
        out = mm(hidden[...], weight(i))
        if pre is not None:
            pre[...] = out
            out = out / (1.0 + jnp.exp(-out))
        low[...] = out.astype(bf16)

    def key():
        project(0, key_pre, keys)
        save(1, 4)

    def increments():
        project(1, None, values)

        @pl.loop(0, 8)
        def _(h):
            at = head_of(h)
            held = (keys[:, at].astype(f32) * decay(leaving[...], rate[h])).astype(bf16)
            value[h] = mm_tn(held, values[:, at])

        states.spread()
        save(2)

    def query():
        project(2, query_pre, queries)

        @pl.loop(0, 8)
        def _(h):
            at = head_of(h)
            scores = mm_nt(queries[:, at], keys[:, at])
            low = (scores * decay(dist[...], rate[h])).astype(bf16)
            probs[h] = low
            attended[:, at] = mm(low, values[:, at])

        save(3, 5, 7)

    def unit():
        unit_pre[...] = mm(hidden[...], weight(3))
        save(6)

    def attend():
        gain[...] = jnp.sum(gains[...].reshape(-1, 8, 128), axis=0)

        @pl.loop(0, 8)
        def _(h):
            at = head_of(h)
            low = arriving[h].astype(bf16)
            state_low[h] = low
            held = (queries[:, at].astype(f32) * decay(entry[...], rate[h])).astype(bf16)
            out = attended[:, at] + mm(held, low)
            attended[:, at] = out
            mixed[:, at] = (
                out * norm_scale(out) * gain[pl.ds(h, 1), :] * unit_pre[:, at]
            ).astype(bf16)

        turn(mixed, mixed_rows)
        save(8, 9, 10, 16)

    def output():
        out = tokens[...].astype(f32) + mm(mixed[...], weight(5))
        middle[...] = out
        second[...] = (out * norm_scale(out)).astype(bf16)
        turn(second, second_rows)
        save(11, 12)

    def gate(i, side, part):
        side[:, pl.ds(part * half, half)] = mm(second[...], weight(i))

    def multiply(j):
        @pl.loop(0, half // 128)
        def _(i):
            at = pl.ds(pl.multiple_of(j * half + i * 128, 128), 128)
            block = (left[:, at] * right[:, at]).astype(bf16).astype(f32)
            turned[pl.ds(pl.multiple_of(i * 128, 128), 128), :] = block.T

        both = pl.ds(2 * j, 2)
        block = turned[...].reshape((2,) + product.shape[1:])
        product[both] = block.astype(bf16)
        rows = flat_rows(product[both, :, :, place.c1])
        for (a, size), out in zip(parts, down_terms):
            term = mm(rows, cot[:, pl.ds(a, size)])
            out[both] = term.reshape((2,) + out.shape[1:]).astype(bf16)

    tasks = {2: [start], 7: [key], 8: [increments], 8.5: [states.join], 9: [query], 9.5: [states.total]}
    tasks.update({10: [unit], 10.5: [states.back], 11.5: [states.part], 12: [states.done, attend]})
    tasks[12.5] = [output]
    tasks[13] = [lambda: gate(6, left, 0)]
    tasks[14] = [lambda: gate(7, left, 1), lambda: save(13)]
    tasks[15] = [lambda: gate(8, right, 0), lambda: multiply(0)]
    tasks[16] = [lambda: gate(9, right, 1), lambda: multiply(1), lambda: save(19, 18, 17, 15, 14)]
    loads = {}
    for step in range(n + 6):
        i = step - 6
        for r in range(6):
            if r == 0:
                for k in (range(min(n, 1 + 2)) if step == 0 else [step + 2]):
                    if k < n:
                        made[k].round(0)
            elif 0 <= step - r < n:
                made[step - r].round(r)
            if r == 0:
                if i - 1 in loads:
                    loads[i - 1].wait()
                for task in tasks.get(step, []):
                    task()
            if r == 3:
                for task in tasks.get(step + 0.5, []):
                    task()
        if 0 <= i < n:
            made[i].pairs()
        if i in slots:
            loads[i] = pltpu.make_async_copy(full[i], slots[i], load_sem.at[i])
            loads[i].start()
    for one in made:
        one.finish()
    states.finish()
    for copy in saves:
        copy.wait()


def forward(lengths, order, rate, tokens, cot, gain, shards):
    f32, bf16 = jnp.float32, jnp.bfloat16
    size, width = tokens.shape
    wide = shards[5].shape[1]
    half = wide // 2
    blocks = [(s.shape, s.dtype) for s in shards[:4]] + [((8, 128), f32)]
    blocks += [(shards[4].shape, bf16)] + [((32, half), bf16)] * 4
    parts = parts_of(width, 128)
    blocks += [((shards[7].shape[0], p), bf16) for _, p in parts]
    square, cube = (size, width), (8, 128, 128)
    rows, down_rows = shards[4].shape[0], shards[7].shape[0]
    across = ((4, 2, 2, 2, rows, size), bf16)
    kept = [across] + [(square, bf16)] * 3 + [(square, f32)] * 3 + [((8, size, size), bf16)]
    kept += [(square, f32), (cube, bf16), across, (square, f32), across]
    kept += [((size, wide), f32)] * 2 + [((4, 2, 2, 2, down_rows, size), bf16), ((8, 128), f32)]
    kept += [((4, 2, 2, down_rows, p), bf16) for _, p in parts]
    vmem, hbm = pl.BlockSpec(memory_space=pltpu.VMEM), pl.BlockSpec(memory_space=pltpu.HBM)
    smem = pl.BlockSpec(memory_space=pltpu.SMEM)
    n = len(blocks)
    out = pl.pallas_call(
        forward_kernel,
        out_shape=[jax.ShapeDtypeStruct((4, 2, 2, 2) + s, t) for s, t in blocks]
        + [jax.ShapeDtypeStruct(s, t) for s, t in kept],
        in_specs=[smem] * 3 + [vmem] * 11,
        out_specs=[hbm] * (n + len(kept)),
        scratch_shapes=[pltpu.VMEM(s, t) for s, t in kept]
        + [pltpu.VMEM(square, bf16)] * 3
        + [pltpu.VMEM((half, size), f32), pltpu.VMEM((8, 128), f32)]
        + [pltpu.VMEM((size, size), f32), pltpu.VMEM((size, 128), f32), pltpu.VMEM((size, 128), f32)]
        + [pltpu.VMEM((4, 2, 2, 2, 8, 128), f32)]
        + [pltpu.VMEM(cube, f32)]
        + state_buffers()
        + [
            pltpu.VMEM((2, 4, 2, 2, 2, 32, width), bf16),
            pltpu.VMEM((2, 4, 2, 2, 2, 32, half), bf16),
            pltpu.SemaphoreType.DMA((n, Gather.NSEND + 1)),
            pltpu.SemaphoreType.DMA((n, Gather.NRECV)),
            pltpu.SemaphoreType.DMA((18,)),
            pltpu.SemaphoreType.DMA((18,)),
            pltpu.SemaphoreType.DMA((n,)),
            pltpu.SemaphoreType.DMA((len(kept),)),
        ],
        compiler_params=pltpu.CompilerParams(
            collective_id=0, has_side_effects=True, vmem_limit_bytes=VMEM_LIMIT
        ),
        name="forward",
    )(lengths, order, rate, tokens, cot, gain, *shards)
    return out[:n], out[n:]

def backward_kernel(lengths, order, rate, tokens, cot, *refs):
    f32, bf16 = jnp.float32, jnp.bfloat16
    n = 14
    saved, refs = refs[:SAVED_BACK], refs[SAVED_BACK:]
    (h_hidden, h_keys, h_values, h_queries, h_key_pre, h_query_pre, h_unit_pre, h_probs) = saved[:8]
    (h_attended, h_state_low, h_mixed, h_middle, h_second, h_left, h_right, h_product) = saved[8:16]
    h_gain, h_down = saved[16], saved[17:]
    w_in, refs = refs[:12], refs[12:]
    (w_key, w_value, w_query, w_unit, w_output, w_l0, w_l1, w_r0, w_r1) = w_in[:9]
    w_down = w_in[9:]
    out, result_out, tokens_out, refs = refs[:n], refs[n], refs[n + 1], refs[n + 2 :]
    acc, came, refs = refs[:n], refs[n : 2 * n], refs[2 * n :]
    (part, gain_part, wd, down, wl, left, right, f1, f2, f3, f4) = refs[:11]
    (branch, ga, gup, gkp, gvp, result, glp, grp, rows, mixed, product) = refs[11:22]
    (probs, state_low, gain, gg, dist, entry, leaving) = refs[22:29]
    value, state_refs, arriving = refs[29], refs[30:39], refs[37]
    (send, recv, state_send, state_recv, load_sem) = refs[39:]
    place = Place()
    half = h_left.shape[1] // 2
    width = tokens.shape[1]
    left_w, right_w = left.at[:, pl.ds(0, width)], right.at[:, pl.ds(0, width)]
    queries, keys = glp.at[:, pl.ds(0, width)], glp.at[:, pl.ds(width, width)]
    values, gqp = grp.at[:, pl.ds(0, width)], grp.at[:, pl.ds(width, width)]
    wn = wl.at[:, :, :, :, :, pl.ds(0, width)]
    greet_more(place)
    bounds = bounds_of(lengths, order)
    states = States(
        place, bounds, rate, True, value, state_refs, state_send, state_recv
    )
    loads = {}

    def load(name, src, dst):
        copy = pltpu.make_async_copy(src, dst, load_sem.at[len(loads)])
        loads[name] = copy
        copy.start()

    def load_down(i):
        for m, (a, size) in enumerate(parts):
            dst = wd.at[:, :, :, :, :, pl.ds(a, size)]
            load("down%d%d" % (i, m), w_down[m].at[pl.ds(2 * i, 2)], dst)

    def loaded(*names):
        for name in names:
            loads[name].wait()

    def weight(cols):
        return wl[:, :, :, :, :, pl.ds(0, cols)].reshape(-1, cols)

    def side(i):
        return pl.ds(i * half, half)

    def product_of(i):
        return flat_rows(product[pl.ds(2 * i, 2)])

    class Piece:
        def __init__(self, rows, core_rows, grad, cols, need=()):
            self.rows, self.core_rows, self.grad, self.cols, self.need = rows, core_rows, grad, cols, need

        def term(self, zh, core):
            lhs = self.rows[pl.ds(zh * 2, 2), :, :, core]
            lhs = flat_rows(lhs) if self.core_rows % 16 else lhs.reshape(-1, lhs.shape[-1])
            out = mm(lhs, self.grad[...])
            return out.reshape(2, 2, 2, self.core_rows, self.cols)

        def first(self):
            @pl.loop(0, 2)
            def _(zh):
                part[pl.ds(zh * 2, 2), :, :, :, pl.ds(0, self.cols)] = self.term(
                    zh, place.c1
                ).astype(bf16)

        def second(self, acc):
            @pl.loop(0, 2)
            def _(zh):
                at = pl.ds(zh * 2, 2)
                acc[at] = (acc[at].astype(f32) + self.term(zh, place.c)).astype(bf16)

    class Gain:
        def first(self):
            gain_part[...] = jnp.broadcast_to(gg[...][None, None, None], gain_part.shape)

        def second(self, acc):
            acc[...] = acc[...] + gg[...][None, None, None]

    wide = part.at[:, :, :, :, pl.ds(0, half)]
    narrow = part.at[:, :, :, :, pl.ds(0, width)]
    parts = parts_of(width, 128)
    pieces = []
    for m in (2, 1, 0):
        a, size = parts[m]
        pieces.append((h_down[m], Piece(product, 88, cot.at[:, pl.ds(a, size)], size)))
    pieces += [(wide, Piece(rows, 32, glp.at[:, side(i)], half)) for i in (0, 1)]
    pieces += [(wide, Piece(rows, 32, grp.at[:, side(i)], half)) for i in (0, 1)]
    pieces += [(narrow, Piece(mixed, 32, branch, width)), (gain_part, Gain())]
    pieces += [(narrow, Piece(rows, 32, g, width)) for g in (gup, gqp, gvp)]
    last = width // 4
    for a, size in ((0, width - last), (width - last, last)):
        view = part.at[:, :, :, :, pl.ds(0, size)]
        pieces.append((view, Piece(rows, 32, gkp.at[:, pl.ds(a, size)], size)))
    made = [
        Scatter(place, pieces[i][0], acc[i], pieces[i][1], came[i], out[i], send, recv, i)
        for i in range(n)
    ]

    def begin():
        spans_of(place.me * SPAN, bounds, dist, entry, leaving)

    def gates(i):
        loaded("down%d0" % i, "down%d1" % i, "down%d2" % i, "left%d" % i, "right%d" % i)
        pair = 2 * wd.shape[4]

        @pl.loop(0, 8)
        def _(k):
            at = pl.ds(pl.multiple_of(k * pair, 16), pair)
            down[at, :] = flat_rows(wd[k // 4, (k // 2) % 2, k % 2])

        grad = mm_nt(cot[...], down[...])
        glp[:, side(i)] = (grad * right[...]).astype(bf16)
        grp[:, side(i)] = (grad * left[...]).astype(bf16)
        if i == 0:
            loaded("middle")
            f3[...] = f2[...] + mm_tn(product_of(0), down[...])
            load_down(1)
            load("left1", h_left.at[:, side(1)], left)
            load("right1", h_right.at[:, side(1)], right)
        else:
            result[...] = (f3[...] + mm_tn(product_of(1), down[...])).astype(bf16)
            load("unit_pre", h_unit_pre, left_w)
            load("result", result, result_out)

    def second_part(name, grad, i, following, start):
        loaded(name)
        term = mm_nt(grad[:, side(i)], weight(half))
        f1[...] = term if start else f1[...] + term
        load(*following)

    def middle():
        @pl.loop(0, SPAN // 16)
        def _(i):
            at = pl.ds(pl.multiple_of(i * 16, 16), 16)
            x, g = f2[at, :], f1[at, :]
            scale = norm_scale(x)
            unit = x * scale
            grad = cot[at, :].astype(f32) + scale * (
                g - unit * jnp.mean(g * unit, axis=-1, keepdims=True)
            )
            f3[at, :] = grad
            branch[at, :] = grad.astype(bf16)

        load("attended", h_attended, f2)

    def spare():
        load("queries", h_queries, queries)
        load("keys", h_keys, keys)
        load("values", h_values, values)
        load("hidden", h_hidden, rows)

    def attention():
        loaded("output")
        f1[...] = mm_nt(branch[...], weight(width))
        load("unit", w_unit, wn)
        loaded("attended", "unit_pre", "queries", "gain")

        @pl.loop(0, 8)
        def _(h):
            at = head_of(h)
            att, up, gm = f2[:, at], left_w[:, at], f1[:, at]
            scale = norm_scale(att)
            unit = att * scale
            row = gain[pl.ds(h, 1), :]
            gated = gm * up
            gg[pl.ds(h, 1), :] = jnp.sum(gated * unit, axis=0, keepdims=True)
            gup[:, at] = (gm * unit * row).astype(bf16)
            g = gated * row
            low = (
                scale * (g - unit * jnp.mean(g * unit, axis=-1, keepdims=True))
            ).astype(bf16)
            ga[:, at] = low
            held = (queries[:, at].astype(f32) * decay(entry[...], rate[h])).astype(bf16)
            value[h] = mm_tn(held, low)

        states.spread()
        load("key_pre", h_key_pre, f2)

    def scores():
        loaded("keys", "values", "query_pre", "probs", "state_low")

        @pl.loop(0, 8)
        def _(h):
            at = head_of(h)
            low = ga[:, at]
            grads = (mm_nt(low, values[:, at]) * decay(dist[...], rate[h])).astype(bf16)
            grad_q = mm(grads, keys[:, at])
            grad_q = grad_q + mm_nt(low, state_low[h]) * decay(entry[...], rate[h])
            gqp[:, at] = (grad_q * slope(f4[:, at])).astype(bf16)
            f1[:, at] = mm_tn(grads, queries[:, at])
            right_w[:, at] = mm_tn(probs[h], low)

    def hidden_part(name, grad, following, start):
        loaded(name)
        term = mm_nt(grad[...], weight(width))
        f4[...] = term if start else f4[...] + term
        if following:
            load(*following)

    def unit_rest():
        hidden_part("unit", gup, ("query", w_query, wn), True)

    def last_grads():
        hidden_part("query", gqp, ("value", w_value, wn), False)
        states.done()
        loaded("key_pre")

        @pl.loop(0, 8)
        def _(h):
            at = head_of(h)
            grad = arriving[h].astype(bf16)
            fall = decay(leaving[...], rate[h])
            held = (keys[:, at].astype(f32) * fall).astype(bf16)
            grad_k = f1[:, at] + mm_nt(values[:, at], grad) * fall
            gkp[:, at] = (grad_k * slope(f2[:, at])).astype(bf16)
            gvp[:, at] = (right_w[:, at] + mm(held, grad)).astype(bf16)

    def value_rest():
        hidden_part("value", gvp, ("key", w_key, wn), False)

    def inputs():
        hidden_part("key", gkp, None, False)

        @pl.loop(0, SPAN // 16)
        def _(i):
            at = pl.ds(pl.multiple_of(i * 16, 16), 16)
            x, g = tokens[at, :].astype(f32), f4[at, :]
            scale = norm_scale(x)
            unit = x * scale
            f3[at, :] = f3[at, :] + scale * (g - unit * jnp.mean(g * unit, axis=-1, keepdims=True))

        load("tokens", f3, tokens_out)

    before = {1: lambda: loaded("product"), 3: lambda: loaded("second"), 7: lambda: loaded("mixed")}
    before[9] = lambda: loaded("hidden")
    tasks = {0: [begin], 2: [lambda: gates(0)], 3: [lambda: gates(1)]}
    tasks[4] = [lambda: second_part("l0", glp, 0, ("l1", w_l1, wl), True)]
    tasks[5] = [lambda: second_part("l1", glp, 1, ("r0", w_r0, wl), False)]
    tasks[6] = [
        lambda: second_part("r0", grp, 0, ("r1", w_r1, wl), False),
        lambda: second_part("r1", grp, 1, ("output", w_output, wn), False),
        middle,
    ]
    tasks[7] = [spare, attention]
    tasks[7.5] = [states.join]
    tasks[8] = [scores]
    tasks[8.5] = [states.total]
    tasks[9] = [unit_rest, states.back]
    tasks[9.5] = [states.part]
    tasks[10] = [last_grads]
    tasks[11] = [value_rest]
    tasks[12] = [inputs]
    load("product", h_product, product)
    load_down(0)
    load("left0", h_left.at[:, side(0)], left)
    load("right0", h_right.at[:, side(0)], right)
    load("middle", h_middle, f2)
    load("second", h_second, rows)
    load("l0", w_l0, wl)
    load("mixed", h_mixed, mixed)
    load("gain", h_gain, gain)
    load("query_pre", h_query_pre, f4)
    load("probs", h_probs, probs)
    load("state_low", h_state_low, state_low)
    for step in range(n + 6):
        if step == 0:
            for i in range(3):
                made[i].round(0)
        if step in before:
            before[step]()
        if 2 < step < n:
            if step > 3:
                made[step - 1].handed()
            pieces[step][1].first()
            made[step].round(0)
        if 0 < step <= n:
            made[step - 1].round(1)
        for task in tasks.get(step, []):
            task()
        for r in range(2, 7):
            if 0 <= step - r < n:
                made[step - r].round(r)
            if r == 4:
                for task in tasks.get(step + 0.5, []):
                    task()
    for i, one in enumerate(made):
        if i < 3 or i == n - 1:
            one.handed()
        one.finish()
    states.finish()
    loaded("result", "tokens")


def backward(lengths, order, rate, tokens, cot, saved, weights):
    f32, bf16 = jnp.float32, jnp.bfloat16
    size, width = tokens.shape
    wide = saved[13].shape[1]
    half = wide // 2
    rows = width // 32
    down_rows = wide // 32
    parts, last = parts_of(width, 128), width // 4
    blocks = [((down_rows, parts[m][1]), bf16) for m in (2, 1, 0)] + [((rows, half), bf16)] * 4
    blocks += [((rows, width), bf16), ((8, 128), f32)] + [((rows, width), bf16)] * 3
    blocks += [((rows, width - last), bf16), ((rows, last), bf16)]
    n = len(blocks)
    square, cube = (size, width), (8, 128, 128)
    vmem, hbm = pl.BlockSpec(memory_space=pltpu.VMEM), pl.BlockSpec(memory_space=pltpu.HBM)
    smem = pl.BlockSpec(memory_space=pltpu.SMEM)
    out = pl.pallas_call(
        backward_kernel,
        out_shape=[jax.ShapeDtypeStruct(b, f32) for b, _ in blocks]
        + [jax.ShapeDtypeStruct(square, bf16), jax.ShapeDtypeStruct(square, f32)],
        in_specs=[smem] * 3 + [vmem] * 2 + [hbm] * (len(saved) + len(weights)),
        out_specs=[vmem] * n + [hbm] * 2,
        scratch_shapes=[pltpu.VMEM((4, 2, 2) + b, t) for b, t in blocks]
        + [pltpu.VMEM((19,) + b, t) for b, t in blocks]
        + [
            pltpu.VMEM((4, 2, 2, rows, half), bf16),
            pltpu.VMEM((4, 2, 2, 8, 128), f32),
            pltpu.VMEM((2, 2, 2, 2, down_rows, width), bf16),
            pltpu.VMEM((half, width), bf16),
            pltpu.VMEM((4, 2, 2, 2, rows, half), bf16),
            pltpu.VMEM((size, half), f32),
            pltpu.VMEM((size, half), f32),
        ]
        + [pltpu.VMEM(square, f32)] * 4
        + [pltpu.VMEM(square, bf16)] * 6
        + [pltpu.VMEM((size, wide), bf16)] * 2
        + [pltpu.VMEM((4, 2, 2, 2, rows, size), bf16)] * 2
        + [pltpu.VMEM((4, 2, 2, 2, down_rows, size), bf16)]
        + [pltpu.VMEM((8, size, size), bf16), pltpu.VMEM(cube, bf16)]
        + [pltpu.VMEM((8, 128), f32)] * 2
        + [pltpu.VMEM((size, size), f32), pltpu.VMEM((size, 128), f32), pltpu.VMEM((size, 128), f32)]
        + [pltpu.VMEM(cube, f32)]
        + state_buffers()
        + [
            pltpu.SemaphoreType.DMA((n, Scatter.NSEND + 1)),
            pltpu.SemaphoreType.DMA((n, Scatter.NRECV)),
            pltpu.SemaphoreType.DMA((18,)),
            pltpu.SemaphoreType.DMA((18,)),
            pltpu.SemaphoreType.DMA((40,)),
        ],
        compiler_params=pltpu.CompilerParams(
            collective_id=3, has_side_effects=True, vmem_limit_bytes=67000000
        ),
        name="backward",
    )(lengths, order, rate, tokens, cot, *saved, *weights)
    return out[:n], out[n], out[n + 1]


RESULTS = ((10,), (12, 13), (11,), (9,), (7,), (8,), (3, 4), (5, 6), (2, 1, 0))


def deliver_kernel(result, inputs, *refs):
    grads, out = refs[:14], refs[14:]
    out[0][...] = result[...]
    out[1][...] = inputs[...]
    for dst, found in zip(out[2:], RESULTS):
        if found == (8,):
            me = lax.axis_index(AXIS)
            row = grads[8][pl.ds(me // 4, 1), :]
            own = jnp.zeros((1, 32), jnp.float32)
            for k in range(4):
                own = own + jnp.where(lax.rem(me, 4) == k, 1.0, 0.0) * row[:, 32 * k : 32 * k + 32]
            dst[...] = own
        else:
            at = 0
            for k in found:
                size = grads[k].shape[1]
                dst[:, pl.ds(at, size)] = grads[k][...]
                at += size


def deliver(result, inputs, grads):
    f32 = jnp.float32
    shapes = [(grads[k[0]].shape[0], sum(grads[i].shape[1] for i in k)) for k in RESULTS]
    shapes[5] = (1, 32)
    vmem = pl.BlockSpec(memory_space=pltpu.VMEM)
    out = pl.pallas_call(
        deliver_kernel,
        out_shape=[
            jax.ShapeDtypeStruct(result.shape, result.dtype),
            jax.ShapeDtypeStruct(inputs.shape, f32),
        ]
        + [jax.ShapeDtypeStruct(s, f32) for s in shapes],
        in_specs=[vmem] * 16,
        out_specs=[vmem] * 11,
        name="deliver",
    )(result, inputs, *grads)
    return (*out[:7], out[7].reshape(-1), *out[8:])


def entering(value, axis, combine, identity, reverse):
    length, here = (lax.axis_size(axis), lax.axis_index(axis))
    everything = jax.tree.map(lambda part: lax.all_gather(part, axis), value)
    start = jax.tree.map(
        lambda part, zero: jnp.broadcast_to(jnp.asarray(zero, part.dtype), part.shape),
        value,
        identity,
    )

    def hop(k, before):
        at = length - 1 - k if reverse else k
        reached = at > here if reverse else at < here
        new = combine(before, jax.tree.map(lambda part: part[at], everything))
        return jax.tree.map(lambda a, b: jnp.where(reached, a, b), new, before)

    return lax.fori_loop(0, length, hop, start)


def segment_of(places, lengths, seq_order):
    number = lengths.shape[0]
    picked = seq_order[:, None] == jnp.arange(number, dtype=jnp.int32)[None, :]
    packed = jnp.sum(jnp.where(picked, lengths[None, :], 0), axis=1, dtype=jnp.int32)
    bounds = jnp.cumsum(packed, dtype=jnp.int32)
    found = jnp.sum((bounds[None, :] <= places[:, None]).astype(jnp.int32), axis=1, dtype=jnp.int32)
    return jnp.where(places < 0, -1, found)


def decay_tables(segments, before, rate, block):
    length = segments.shape[0]
    count = length // block
    spans = segments.reshape(count, block)
    priors = jnp.concatenate([before.reshape(1), spans[:-1, -1]])
    steps = jnp.arange(block, dtype=jnp.int32)
    distance = steps[:, None] - steps[None, :]
    same = (spans[:, :, None] == spans[:, None, :]) & (distance >= 0)[None]
    powers = jnp.exp(-rate[:, None, None] * jnp.maximum(distance, 0).astype(jnp.float32)[None])
    within = jnp.where(same[:, None], powers[None], 0.0)
    entry = jnp.where(
        (spans == priors[:, None])[:, :, None],
        jnp.exp(-rate[None, :] * steps.astype(jnp.float32)[:, None])[None],
        0.0,
    )
    leaving = jnp.where(
        (spans == spans[:, -1:])[:, :, None],
        jnp.exp(-rate[None, :] * (block - steps).astype(jnp.float32)[:, None])[None],
        0.0,
    )
    passing = jnp.where((spans[:, -1] == priors)[:, None], jnp.exp(-rate * block)[None], 0.0)
    offsets = (jnp.arange(count, dtype=jnp.int32) * block).astype(jnp.float32)
    arrival = jnp.where(
        (priors == before)[:, None], jnp.exp(-rate[None, :] * offsets[:, None]), 0.0
    )
    through = jnp.where(segments[-1] == before, jnp.exp(-rate * length), 0.0)
    return (within, entry, leaving, passing, arrival, through)


def chain_states(earlier, later):
    return (earlier[0] * later[0], later[0][:, None, None] * earlier[1] + later[1])


def silu_slope(values):
    sigma = jax.nn.sigmoid(values)
    return sigma * (1.0 + values * (1.0 - sigma))


def row_scale(values):
    return lax.rsqrt(jnp.mean(values * values, axis=-1, keepdims=True) + EPSILON)


def body(
    tokens,
    lengths,
    seq_order,
    decay_rate,
    w_query,
    w_key,
    w_value,
    w_unit,
    w_output,
    norm_gain,
    w_left,
    w_right,
    w_down,
    cotangent,
):
    f32 = jnp.float32
    bf16 = jnp.bfloat16
    length, width = tokens.shape
    heads = decay_rate.shape[0]
    head_size = width // heads
    count = length // SPAN
    first = lax.axis_index(AXIS) * length
    places = first + jnp.arange(length, dtype=jnp.int32)
    segments = segment_of(places, lengths, seq_order)
    before = segment_of(jnp.reshape(first - 1, (1,)), lengths, seq_order)[0]
    within, entry, leaving, passing, arrival, through = decay_tables(
        segments, before, decay_rate, SPAN
    )
    attention_set = (
        lax.all_gather(w_query, AXIS, axis=0, tiled=True),
        lax.all_gather(w_key, AXIS, axis=0, tiled=True),
        lax.all_gather(w_value, AXIS, axis=0, tiled=True),
        lax.all_gather(w_unit, AXIS, axis=0, tiled=True),
        lax.all_gather(w_output, AXIS, axis=0, tiled=True),
        lax.all_gather(norm_gain, AXIS, axis=0, tiled=True),
    )
    feed_set = (
        lax.all_gather(w_left, AXIS, axis=0, tiled=True),
        lax.all_gather(w_right, AXIS, axis=0, tiled=True),
        lax.all_gather(w_down, AXIS, axis=0, tiled=True),
    )
    full_query, full_key, full_value, full_unit, full_output, full_gain = attention_set
    full_left, full_right, full_down = feed_set
    inputs = tokens.astype(f32)
    first_scale = row_scale(inputs)
    normed = inputs * first_scale
    hidden = normed.astype(bf16)
    query_pre = jnp.dot(hidden, full_query, preferred_element_type=f32)
    key_pre = jnp.dot(hidden, full_key, preferred_element_type=f32)
    value_pre = jnp.dot(hidden, full_value, preferred_element_type=f32)
    unit_pre = jnp.dot(hidden, full_unit, preferred_element_type=f32)
    block_shape = (count, SPAN, heads, head_size)
    query_blocks = jax.nn.silu(query_pre).astype(bf16).reshape(block_shape)
    key_blocks = jax.nn.silu(key_pre).astype(bf16).reshape(block_shape)
    value_blocks = value_pre.astype(bf16).reshape(block_shape)
    scores = jnp.einsum("nthe,nshe->nhts", query_blocks, key_blocks, preferred_element_type=f32)
    mixing = (scores * within).astype(bf16)
    local_out = jnp.einsum("nhts,nshe->nthe", mixing, value_blocks, preferred_element_type=f32)
    keys_held = (key_blocks * leaving[..., None]).astype(bf16)
    increments = jnp.einsum("nshe,nshf->nhef", keys_held, value_blocks, preferred_element_type=f32)
    local_states = [jnp.zeros((heads, head_size, head_size), f32)]
    local_states.append(passing[0][:, None, None] * local_states[-1] + increments[0])
    end_state = local_states[count]
    start_pair = (jnp.ones_like(through), jnp.zeros_like(end_state))
    arriving = entering((through, end_state), AXIS, chain_states, start_pair, False)[1]
    states = jnp.stack(local_states[:count]) + arrival[:, :, None, None] * arriving[None]
    state_low = states.astype(bf16)
    query_held = (query_blocks * entry[..., None]).astype(bf16)
    attended = local_out + jnp.einsum(
        "nthe,nhef->nthf", query_held, state_low, preferred_element_type=f32
    )
    attended_heads = attended.reshape(length, heads, head_size)
    head_scale = row_scale(attended_heads)
    unit_norm = (attended_heads * head_scale).reshape(length, width)
    gain = full_gain.astype(f32)
    gated = unit_norm * gain
    mixed_in = (gated * unit_pre).astype(bf16)
    middle = inputs + jnp.dot(mixed_in, full_output, preferred_element_type=f32)
    second_scale = row_scale(middle)
    second_unit = middle * second_scale
    second = second_unit.astype(bf16)
    left_pre = jnp.dot(second, full_left, preferred_element_type=f32)
    right_pre = jnp.dot(second, full_right, preferred_element_type=f32)
    product = (left_pre * right_pre).astype(bf16)
    result = (middle + jnp.dot(product, full_down, preferred_element_type=f32)).astype(bf16)
    back_feed = (
        lax.all_gather(w_left, AXIS, axis=0, tiled=True),
        lax.all_gather(w_right, AXIS, axis=0, tiled=True),
        lax.all_gather(w_down, AXIS, axis=0, tiled=True),
    )
    back_left, back_right, back_down = back_feed
    grad_product = jnp.einsum("td,fd->tf", cotangent, back_down, preferred_element_type=f32)
    grad_left_pre = (grad_product * right_pre).astype(bf16)
    grad_right_pre = (grad_product * left_pre).astype(bf16)
    grad_w_down = jnp.einsum("tf,td->fd", product, cotangent, preferred_element_type=f32)
    grad_w_left = jnp.einsum("td,tf->df", second, grad_left_pre, preferred_element_type=f32)
    grad_w_right = jnp.einsum("td,tf->df", second, grad_right_pre, preferred_element_type=f32)
    feed_grads = (
        lax.psum_scatter(grad_w_left, AXIS, scatter_dimension=0, tiled=True),
        lax.psum_scatter(grad_w_right, AXIS, scatter_dimension=0, tiled=True),
        lax.psum_scatter(grad_w_down, AXIS, scatter_dimension=0, tiled=True),
    )
    grad_second = jnp.einsum(
        "tf,df->td", grad_left_pre, back_left, preferred_element_type=f32
    ) + jnp.einsum("tf,df->td", grad_right_pre, back_right, preferred_element_type=f32)
    grad_middle = cotangent.astype(f32) + second_scale * (
        grad_second - second_unit * jnp.mean(grad_second * second_unit, axis=-1, keepdims=True)
    )
    back_attention = (
        lax.all_gather(w_query, AXIS, axis=0, tiled=True),
        lax.all_gather(w_key, AXIS, axis=0, tiled=True),
        lax.all_gather(w_value, AXIS, axis=0, tiled=True),
        lax.all_gather(w_unit, AXIS, axis=0, tiled=True),
        lax.all_gather(w_output, AXIS, axis=0, tiled=True),
        lax.all_gather(norm_gain, AXIS, axis=0, tiled=True),
    )
    back_query, back_key, back_value, back_unit, back_output, back_gain = back_attention
    grad_branch = grad_middle.astype(bf16)
    grad_w_output = jnp.einsum(TD_TE, mixed_in, grad_branch, preferred_element_type=f32)
    grad_mixed = jnp.einsum(TE_DE, grad_branch, back_output, preferred_element_type=f32)
    grad_gated = grad_mixed * unit_pre
    grad_unit_pre = (grad_mixed * gated).astype(bf16)
    grad_gain = jnp.sum(grad_gated * unit_norm, axis=0)
    grad_norm_heads = (grad_gated * back_gain.astype(f32)).reshape(length, heads, head_size)
    norm_heads = unit_norm.reshape(length, heads, head_size)
    grad_att = head_scale * (
        grad_norm_heads
        - norm_heads * jnp.mean(grad_norm_heads * norm_heads, axis=-1, keepdims=True)
    )
    grad_att_blocks = grad_att.astype(bf16).reshape(block_shape)
    grad_mixing = jnp.einsum(
        "nthf,nshf->nhts", grad_att_blocks, value_blocks, preferred_element_type=f32
    )
    grad_scores = (grad_mixing * within).astype(bf16)
    grad_query_blocks = (
        jnp.einsum("nhts,nshe->nthe", grad_scores, key_blocks, preferred_element_type=f32)
        + jnp.einsum("nthf,nhef->nthe", grad_att_blocks, state_low, preferred_element_type=f32)
        * entry[..., None]
    )
    grad_key_blocks = jnp.einsum(
        "nhts,nthe->nshe", grad_scores, query_blocks, preferred_element_type=f32
    )
    grad_value_blocks = jnp.einsum(
        "nhts,nthf->nshf", mixing, grad_att_blocks, preferred_element_type=f32
    )
    direct = jnp.einsum("nthe,nthf->nhef", query_held, grad_att_blocks, preferred_element_type=f32)
    leaving_sum = jnp.sum(arrival[:, :, None, None] * direct, axis=0)
    later = entering((through, leaving_sum), AXIS, chain_states, start_pair, True)[1]
    next_grads = [later]
    grad_increment = jnp.stack(next_grads[::-1]).astype(bf16)
    grad_keys_held = jnp.einsum(
        "nhef,nshf->nshe", grad_increment, value_blocks, preferred_element_type=f32
    )
    grad_key_blocks = grad_key_blocks + grad_keys_held * leaving[..., None]
    grad_value_blocks = grad_value_blocks + jnp.einsum(
        "nshe,nhef->nshf", keys_held, grad_increment, preferred_element_type=f32
    )
    grad_query_pre = (grad_query_blocks.reshape(length, width) * silu_slope(query_pre)).astype(bf16)
    grad_key_pre = (grad_key_blocks.reshape(length, width) * silu_slope(key_pre)).astype(bf16)
    grad_value_pre = grad_value_blocks.reshape(length, width).astype(bf16)
    grad_w_query = jnp.einsum(TD_TE, hidden, grad_query_pre, preferred_element_type=f32)
    grad_w_key = jnp.einsum(TD_TE, hidden, grad_key_pre, preferred_element_type=f32)
    grad_w_value = jnp.einsum(TD_TE, hidden, grad_value_pre, preferred_element_type=f32)
    grad_w_unit = jnp.einsum(TD_TE, hidden, grad_unit_pre, preferred_element_type=f32)
    attention_grads = (
        lax.psum_scatter(grad_w_query, AXIS, scatter_dimension=0, tiled=True),
        lax.psum_scatter(grad_w_key, AXIS, scatter_dimension=0, tiled=True),
        lax.psum_scatter(grad_w_value, AXIS, scatter_dimension=0, tiled=True),
        lax.psum_scatter(grad_w_unit, AXIS, scatter_dimension=0, tiled=True),
        lax.psum_scatter(grad_w_output, AXIS, scatter_dimension=0, tiled=True),
        lax.psum_scatter(grad_gain, AXIS, scatter_dimension=0, tiled=True),
    )
    grad_hidden = (
        jnp.einsum(TE_DE, grad_query_pre, back_query, preferred_element_type=f32)
        + jnp.einsum(TE_DE, grad_key_pre, back_key, preferred_element_type=f32)
        + jnp.einsum(TE_DE, grad_value_pre, back_value, preferred_element_type=f32)
        + jnp.einsum(TE_DE, grad_unit_pre, back_unit, preferred_element_type=f32)
    )
    grad_inputs = grad_middle + first_scale * (
        grad_hidden - normed * jnp.mean(grad_hidden * normed, axis=-1, keepdims=True)
    )
    return (
        result,
        grad_inputs,
        attention_grads[0],
        attention_grads[1],
        attention_grads[2],
        attention_grads[3],
        attention_grads[4],
        attention_grads[5],
        feed_grads[0],
        feed_grads[1],
        feed_grads[2],
    )


def body_kernels(
    tokens,
    lengths,
    seq_order,
    decay_rate,
    w_query,
    w_key,
    w_value,
    w_unit,
    w_output,
    norm_gain,
    w_left,
    w_right,
    w_down,
    cotangent,
):
    full, saved = forward(
        lengths,
        seq_order,
        decay_rate,
        tokens,
        cotangent,
        norm_gain.reshape(1, -1),
        [w_key, w_value, w_query, w_unit, w_output, w_left, w_right, w_down],
    )
    grads, result, grad_inputs = backward(
        lengths, seq_order, decay_rate, tokens, cotangent, saved, full[:4] + full[5:]
    )
    return deliver(result, grad_inputs, grads)


def solution(mesh):
    placed = (
        P(AXIS, None),
        P(),
        P(),
        P(),
        P(AXIS, None),
        P(AXIS, None),
        P(AXIS, None),
        P(AXIS, None),
        P(AXIS, None),
        P(AXIS),
        P(AXIS, None),
        P(AXIS, None),
        P(AXIS, None),
        P(AXIS, None),
    )
    return jax.shard_map(
        body_kernels if mesh.size == 32 else body,
        mesh=mesh,
        in_specs=placed,
        out_specs=(
            P(AXIS, None),
            P(AXIS, None),
            P(AXIS, None),
            P(AXIS, None),
            P(AXIS, None),
            P(AXIS, None),
            P(AXIS, None),
            P(AXIS),
            P(AXIS, None),
            P(AXIS, None),
            P(AXIS, None),
        ),
        check_vma=False,
    )
```

```python
import functools

import jax
import jax.numpy as jnp
from jax import lax
from jax.experimental import pallas as pl
from jax.experimental.pallas import tpu as pltpu
from jax.sharding import PartitionSpec as P

SPAN = 256
AXIS = "fsdp"
TE_DE = "te,de->td"
TD_TE = "td,te->de"
EPSILON = 1e-05
LOGICAL = pl.DeviceIdType.LOGICAL
VMEM_LIMIT = 64000000


class Place:
    def __init__(self):
        me = lax.axis_index(AXIS)
        self.me = me
        self.c = lax.rem(me, 2)
        self.x = lax.rem(me // 2, 2)
        self.y = lax.rem(me // 4, 2)
        self.z = me // 8
        self.inner = (self.z == 1) | (self.z == 2)
        self.even = lax.rem(self.z, 2) == 0
        self.sib = self.z + 1 - 2 * lax.rem(self.z, 2)
        half = self.z // 2
        self.near = 2 - half
        self.far = 3 - 3 * half
        self.cross = 3 - self.z
        self.x1 = 1 - self.x
        self.y1 = 1 - self.y
        self.c1 = 1 - self.c
        self.to = {
            "S": self.dev(self.sib, self.y, self.x, self.c),
            "K": self.dev(self.cross, self.y, self.x, self.c),
            "x": self.dev(self.z, self.y, self.x1, self.c),
            "y": self.dev(self.z, self.y1, self.x, self.c),
            "p": self.dev(self.z, self.y, self.x, self.c1),
        }

    def dev(self, z, y, x, c):
        return ((z * 2 + y) * 2 + x) * 2 + c


def arrived(ref, send, recv, place):
    pltpu.make_async_remote_copy(
        src_ref=ref,
        dst_ref=ref,
        send_sem=send,
        recv_sem=recv,
        device_id=place.to["p"],
        device_id_type=LOGICAL,
    ).wait_recv()


class Gather:
    RECV = ("Cs", "Cn", "Cf", "Xo", "Xs", "Xn", "Xf", "Yo", "Ys", "Yn", "Yf", "D0", "D1", "En", "Ef")
    GROUPS = ("C", "X", "Y", "D")
    NRECV = 19
    NSEND = 25

    def __init__(self, place, own, full, send, recv, index):
        self.p, self.own, self.full = place, own, full
        self.send, self.recv, self.index = send, recv, index
        self.sent = []
        p = place
        self.where = {}
        for g, y, x in (("C", p.y, p.x), ("X", p.y, p.x1), ("Y", p.y1, p.x), ("D", p.y1, p.x1)):
            for k, z in (("o", p.z), ("s", p.sib), ("n", p.near), ("f", p.far)):
                self.where[g + k] = (z, y, x, p.c)
        for a, b in (("D0", "Do"), ("D1", "Ds"), ("En", "Dn"), ("Ef", "Df")):
            self.where[a] = self.where[b]

    def slot(self, name):
        return self.full.at[self.where[name]]

    def copy(self, name, link, landing):
        src = self.own if name == "Co" else self.slot(name)
        k = len(self.sent)
        made = pltpu.make_async_remote_copy(
            src_ref=src,
            dst_ref=self.slot(name),
            send_sem=self.send.at[self.index, k],
            recv_sem=self.recv.at[self.index, self.RECV.index(landing)],
            device_id=self.p.to[link],
            device_id_type=LOGICAL,
        )
        return made

    def go(self, name, link, landing, cond=None):
        made = self.copy(name, link, landing)
        self.sent.append((made, cond))
        if cond is None:
            made.start()
        else:
            pl.when(cond)(made.start)

    def wait(self, name):
        arrived(self.slot(name), self.send.at[self.index, 0], self.recv.at[self.index, self.RECV.index(name)], self.p)

    def group(self, g):
        p = self.p
        y = p.y if g in "CX" else p.y1
        x = p.x if g in "CY" else p.x1
        return y, x

    def pair(self, g):
        y, x = self.group(g)
        ref = self.full.at[:, y, x, self.p.c]
        k = len(self.sent)
        made = pltpu.make_async_remote_copy(
            src_ref=ref,
            dst_ref=ref,
            send_sem=self.send.at[self.index, k],
            recv_sem=self.recv.at[self.index, 15 + self.GROUPS.index(g)],
            device_id=self.p.to["p"],
            device_id_type=LOGICAL,
        )
        self.sent.append((made, None))
        made.start()

    def round(self, r):
        p = self.p
        inner, even = p.inner, p.even
        odd = jnp.logical_not(even)
        if r == 0:
            keep = pltpu.make_async_copy(self.own, self.slot("Co"), self.send.at[self.index, self.NSEND])
            self.keep = keep
            keep.start()
            self.go("Co", "S", "Cs")
            self.go("Co", "K", "Cn", inner)
            self.go("Co", "x", "Xo")
            self.go("Co", "y", "Yo")
        outer = jnp.logical_not(inner)
        if r == 1:
            self.wait("Cs")
            self.go("Cs", "K", "Cf", inner)
            self.go("Cs", "x", "Xs")
            self.go("Cs", "y", "Ys")
            self.wait("Xo")
            self.go("Xo", "y", "D0", even)
            self.wait("Yo")
            self.go("Yo", "x", "D0", odd)
            self.relay("Cn")
        if r == 2:
            pl.when(outer)(lambda: self.wait("Cn"))
            self.go("Cn", "x", "Xn")
            self.go("Cn", "y", "Yn")
            self.wait("Xs")
            self.go("Xs", "y", "D1", odd)
            self.wait("Ys")
            self.go("Ys", "x", "D1", even)
            self.wait("D0")
            self.go("D0", "K", "En", inner)
            self.relay("Cf")
        if r == 3:
            pl.when(outer)(lambda: self.wait("Cf"))
            self.go("Cf", "x", "Xf")
            self.go("Cf", "y", "Yf")
            self.keep.wait()
            self.pair("C")
            self.wait("D1")
            self.go("D1", "K", "Ef", inner)
            self.wait("Xn")
            self.wait("Yn")
            self.relay("En")
        if r == 4:
            pl.when(outer)(lambda: self.wait("En"))
            self.wait("Xf")
            self.pair("X")
            self.wait("Yf")
            self.pair("Y")
            self.relay("Ef")
        if r == 5:
            pl.when(outer)(lambda: self.wait("Ef"))
            self.pair("D")

    def relay(self, name):
        pl.when(self.p.inner)(lambda: self.wait(name))
        self.go(name, "S", name, self.p.inner)

    def pairs(self):
        for g in self.GROUPS:
            y, x = self.group(g)
            ref = self.full.at[:, y, x, self.p.c1]
            arrived(ref, self.send.at[self.index, 0], self.recv.at[self.index, 15 + self.GROUPS.index(g)], self.p)

    def finish(self):
        for made, cond in self.sent:
            if cond is None:
                made.wait_send()
            else:
                pl.when(cond)(made.wait_send)


def add_into(out, parts):
    rows = out.shape[0]
    step = 8 if rows % 16 else 16

    @pl.loop(0, rows // step)
    def _(i):
        at = pl.ds(pl.multiple_of(i * step, step), step)
        total = parts[0][at, :].astype(jnp.float32)
        for part in parts[1:]:
            total = total + part[at, :].astype(jnp.float32)
        out[at, :] = total.astype(out.dtype)


class Scatter:
    NRECV = 20
    NSEND = 22
    SLOTS = ("x0", "x1", "x2", "x3", "Fx", "y0", "y1", "y2", "y3", "Fy", "En", "Ef", "Cn", "Cf", "Co", "De", "Do", "KCs", "KCo")

    def __init__(self, place, part, acc, term, came, out, send, recv, index):
        self.p, self.part, self.acc, self.term, self.came, self.out = place, part, acc, term, came, out
        self.send, self.recv, self.index = send, recv, index
        self.sent = []
        p = place
        half = p.z // 2
        self.ze, self.zo = 2 * half, 2 * half + 1
        self.C = lambda z: (z, p.y, p.x)
        self.X = lambda z: (z, p.y, p.x1)
        self.Y = lambda z: (z, p.y1, p.x)
        self.D = lambda z: (z, p.y1, p.x1)

    def go(self, where, link, slot, cond=None):
        k = len(self.sent)
        at = self.SLOTS.index(slot) if isinstance(slot, str) else slot
        made = pltpu.make_async_remote_copy(
            src_ref=self.acc.at[where],
            dst_ref=self.came.at[at],
            send_sem=self.send.at[self.index, k],
            recv_sem=self.recv.at[self.index, at],
            device_id=self.p.to[link],
            device_id_type=LOGICAL,
        )
        self.sent.append((made, cond))
        if cond is None:
            made.start()
        else:
            pl.when(cond)(made.start)

    def wait(self, slot):
        at = self.SLOTS.index(slot) if isinstance(slot, str) else slot
        arrived(self.came.at[at], self.send.at[self.index, 0], self.recv.at[self.index, at], self.p)
        return self.came.at[at]

    def add(self, where, slots):
        parts = [self.wait(s) for s in slots]
        add_into(self.acc.at[where], [self.acc.at[where]] + parts)

    def round(self, r):
        p = self.p
        inner = p.inner
        outer = jnp.logical_not(inner)
        ze, zo, near, far = self.ze, self.zo, p.near, p.far
        if r == 0:
            if self.term is None:
                self.given = pltpu.make_async_copy(self.part, self.acc, self.send.at[self.index, self.NSEND])
                self.given.start()
                return
            self.given = pltpu.make_async_remote_copy(
                src_ref=self.part,
                dst_ref=self.acc,
                send_sem=self.send.at[self.index, self.NSEND],
                recv_sem=self.recv.at[self.index, 19],
                device_id=p.to["p"],
                device_id_type=LOGICAL,
            )
            self.given.start()
        if r == 1:
            if self.term is None:
                self.given.wait()
            else:
                arrived(self.acc, self.send.at[self.index, 0], self.recv.at[self.index, 19], p)
                self.term.second(self.acc)
            self.go(self.D(far), "S", "Ef", outer)
            self.go(self.D(near), "S", "En", outer)
            self.go(self.X(far), "x", far)
            self.go(self.Y(far), "y", far + 5)
            self.go(self.D(ze), "y", "Fy", outer)
            self.go(self.D(zo), "x", "Fx", outer)
            self.go(self.X(near), "x", near)
            self.go(self.Y(near), "y", near + 5)
            self.go(self.X(zo), "x", zo)
            self.go(self.Y(ze), "y", ze + 5)
        if r == 2:

            @pl.when(inner)
            def _():
                self.add(self.D(far), ["Ef"])
                self.add(self.D(near), ["En"])

            self.go(self.D(far), "K", jnp.where(p.z == 1, self.SLOTS.index("Do"), self.SLOTS.index("De")), inner)
            self.go(self.D(near), "K", jnp.where(p.z == 1, self.SLOTS.index("De"), self.SLOTS.index("Do")), inner)
            parts = [self.wait(far), self.wait(far + 5)]
            add_into(self.acc.at[self.C(far)], [self.acc.at[self.C(far)]] + parts)
            self.go(self.C(far), "S", "Cf", outer)
        if r == 3:

            @pl.when(inner)
            def _():
                self.add(self.D(ze), ["De"])
                self.add(self.D(zo), ["Do"])
                self.add(self.C(far), ["Cf"])

            self.go(self.D(ze), "y", "Fy", inner)
            self.go(self.D(zo), "x", "Fx", inner)
            self.go(self.C(far), "K", "KCs", inner)
            parts = [self.wait(near), self.wait(near + 5)]
            add_into(self.acc.at[self.C(near)], [self.acc.at[self.C(near)]] + parts)
            self.go(self.C(near), "S", "Cn", outer)
        if r == 4:
            self.add(self.X(ze), ["Fy"])
            self.add(self.Y(zo), ["Fx"])
            self.go(self.X(ze), "x", ze)
            self.go(self.Y(zo), "y", zo + 5)

            @pl.when(inner)
            def _():
                self.add(self.C(near), ["Cn"])

            self.go(self.C(near), "K", "KCo", inner)
        if r == 5:
            self.add(self.C(p.sib), [p.sib, p.sib + 5])

            @pl.when(inner)
            def _():
                self.add(self.C(p.sib), ["KCs"])

            self.go(self.C(p.sib), "S", "Co")
        if r == 6:
            slots = [p.z, p.z + 5, "Co"]
            parts = [self.acc.at[self.C(p.z)]] + [self.wait(s) for s in slots]
            add_into(self.out, parts)

            @pl.when(inner)
            def _():
                add_into(self.out, [self.out, self.wait("KCo")])

    def handed(self):
        self.given.wait_send()

    def finish(self):
        for made, cond in self.sent:
            if cond is None:
                made.wait_send()
            else:
                pl.when(cond)(made.wait_send)


def bounds_of(lengths, order):
    total, found = jnp.int32(0), []
    for j in range(lengths.shape[0]):
        total = total + lengths[order[j]]
        found.append(total)
    return found


def segment_at(bounds, places):
    found = jnp.zeros_like(places)
    for bound in bounds:
        found = found + jnp.where(bound <= places, 1, 0)
    return found


def same_segment(bounds, earlier, later):
    same = jnp.int32(0)
    for bound in bounds:
        same = same + jnp.where((bound <= earlier) != (bound <= later), 1, 0)
    return jnp.where((earlier >= 0) & (same == 0), 1.0, 0.0).astype(jnp.float32)


def spans_of(first, bounds, dist, entry, leaving):
    size = dist.shape[0]
    t = lax.broadcasted_iota(jnp.int32, (size, size), 0)
    s = lax.broadcasted_iota(jnp.int32, (size, size), 1)
    same = segment_at(bounds, t + first) == segment_at(bounds, s + first)
    dist[...] = jnp.where(same & (s <= t), t - s, -1).astype(jnp.float32)
    t = lax.broadcasted_iota(jnp.int32, entry.shape, 0)
    here = segment_at(bounds, t + first)
    ahead = segment_at(bounds, jnp.full(entry.shape, first - 1, jnp.int32))
    ahead = jnp.where(jnp.full(entry.shape, first, jnp.int32) == 0, -1, ahead)
    last = segment_at(bounds, jnp.full(entry.shape, first + size - 1, jnp.int32))
    entry[...] = jnp.where(here == ahead, t, -1).astype(jnp.float32)
    leaving[...] = jnp.where(here == last, size - t, -1).astype(jnp.float32)


def decay(distance, rate):
    return jnp.where(distance >= 0, jnp.exp(-rate * distance), 0.0)


def mm(a, b):
    return jnp.dot(a, b, preferred_element_type=jnp.float32)


def mm_nt(a, b):
    return lax.dot_general(a, b, (((1,), (1,)), ((), ())), preferred_element_type=jnp.float32)


def mm_tn(a, b):
    return lax.dot_general(a, b, (((0,), (0,)), ((), ())), preferred_element_type=jnp.float32)


def head_of(h):
    return pl.ds(pl.multiple_of(h * 128, 128), 128)


def norm_scale(values):
    return lax.rsqrt(jnp.mean(values * values, axis=-1, keepdims=True) + EPSILON)


def slope(a):
    sigma = 1.0 / (1.0 + jnp.exp(-a))
    return sigma * (1.0 + a * (1.0 - sigma))


def flat_rows(value):
    return value.astype(jnp.float32).reshape(-1, value.shape[-1]).astype(jnp.bfloat16)


SAVED_BACK = 20
FIRST = 1
ORDER = (FIRST, 2, 0)


def parts_of(width, last):
    cuts = (0, width // 2, width - last, width)
    return [(a, b - a) for a, b in zip(cuts, cuts[1:])]


class States:
    def __init__(self, place, bounds, rate, reverse, value, buffers, send, recv):
        self.bounds, self.reverse, self.rate = bounds, reverse, rate
        self.value = value
        self.theirs, self.sums, self.met, self.planes, self.ready, self.entered, self.give, self.out, self.sum = buffers
        self.send, self.recv = send, recv
        self.z, self.c, self.c1 = place.z, place.c, place.c1
        self.me, self.partner = place.me, place.to["p"]
        self.q = lax.rem(place.me // 2, 4)
        self.chip = [self.at(self.z, lax.bitwise_xor(self.q, k)) for k in range(4)]
        self.level = [self.at(lax.rem(self.z + k, 4), self.q) for k in range(4)]
        self.order = range(3, -1, -1) if reverse else range(4)
        lead = 1 if reverse else 0
        self.lead = jnp.where(self.c == lead, 1.0, 0.0).astype(jnp.float32)
        base = self.me - self.c
        self.lead_through = self.through(base + lead, 1)
        self.last_through = self.through(base + 1 - lead, 1)
        mine = rate[4 * self.c + self.q]
        self.chip_step = jnp.exp(jnp.full((1, 128), -2 * SPAN * mine, jnp.float32))
        self.plane_step = jnp.exp(jnp.full((1, 128), -8 * SPAN * mine, jnp.float32))

    def at(self, z, q):
        return (z * 4 + q) * 2 + self.c

    def through(self, device, count):
        return same_segment(self.bounds, device * SPAN - 1, (device + count) * SPAN - 1)

    def step(self, k):
        return jnp.exp(jnp.full((1, 128), -SPAN * self.rate[4 * self.c + k], jnp.float32))

    def copy(self, src, dst, k, peer):
        return pltpu.make_async_remote_copy(
            src_ref=src,
            dst_ref=dst,
            send_sem=self.send.at[k],
            recv_sem=self.recv.at[k],
            device_id=peer,
            device_id_type=LOGICAL,
        )

    def other(self, k):
        return lax.bitwise_xor(self.q, k)

    def begin(self, made):
        for one in made:
            one.start()
        return made

    def terms(self, k):
        mine, theirs = self.value[4 * self.c + k], self.theirs[k]
        rest = 1.0 - self.lead
        return self.lead * mine + rest * theirs, rest * mine + self.lead * theirs

    def spread(self):
        half = self.value.at[pl.ds(4 * self.c1, 4)]
        self.sent = self.begin([self.copy(half, self.theirs, 0, self.partner)])

    def join(self):
        self.copy(self.theirs, self.theirs, 0, self.partner).wait_recv()
        for k in range(4):
            first, last = self.terms(k)
            self.sums[k] = (self.last_through * self.step(k) * first + last).astype(jnp.bfloat16)
        self.sent += self.begin(
            [
                self.copy(self.sums.at[self.other(k)], self.met.at[self.q], k, self.chip[k])
                for k in range(1, 4)
            ]
        )
        self.met[self.q] = self.sums[self.q]

    def total(self):
        for k in range(1, 4):
            self.copy(self.sums.at[0], self.met.at[self.other(k)], k, self.chip[k]).wait_recv()
        total = jnp.zeros(self.met.shape[1:], jnp.float32)
        for i in self.order:
            through = self.through(self.z * 8 + 2 * i, 2)
            total = through * self.chip_step * total + self.met[i].astype(jnp.float32)
        self.planes[self.z] = total.astype(jnp.bfloat16)
        self.second = []
        for k in range(1, 4):
            far = self.z - k if self.reverse else self.z + k
            cond = far >= 0 if self.reverse else far <= 3
            made = self.copy(
                self.planes.at[self.z], self.planes.at[self.z], 3 + k, self.at(far, self.q)
            )
            self.second.append((made, cond))
            pl.when(cond)(made.start)

    def back(self):
        self.sum[...] = jnp.zeros(self.sum.shape, jnp.float32)
        for k in range(3, 0, -1):
            far = self.z + k if self.reverse else self.z - k
            cond = far <= 3 if self.reverse else far >= 0

            @pl.when(cond)
            def _():
                self.copy(
                    self.planes.at[self.z], self.planes.at[far], 3 + k, self.partner
                ).wait_recv()
                kept = self.through(far * 8, 8) * self.plane_step
                self.sum[...] = kept * self.sum[...] + self.planes[far].astype(jnp.float32)

        total = self.sum[...]
        for i in self.order:
            self.ready[i] = total.astype(jnp.bfloat16)
            through = self.through(self.z * 8 + 2 * i, 2)
            total = through * self.chip_step * total + self.met[i].astype(jnp.float32)
        self.sent += self.begin(
            [
                self.copy(self.ready.at[self.other(k)], self.entered.at[self.q], 6 + k, self.chip[k])
                for k in range(1, 4)
            ]
        )
        self.entered[self.q] = self.ready[self.q]

    def part(self):
        for k in range(1, 4):
            self.copy(self.ready.at[0], self.entered.at[self.other(k)], 6 + k, self.chip[k]).wait_recv()
        rest = 1.0 - self.lead
        for k in range(4):
            first, _ = self.terms(k)
            entering = self.entered[k].astype(jnp.float32)
            later = self.lead_through * self.step(k) * entering + first
            self.out[4 * self.c + k] = (self.lead * entering + rest * later).astype(jnp.bfloat16)
            self.give[k] = (self.lead * later + rest * entering).astype(jnp.bfloat16)
        at = pl.ds(4 * self.c, 4)
        self.sent += self.begin([self.copy(self.give, self.out.at[at], 10, self.partner)])

    def done(self):
        at = pl.ds(4 * self.c1, 4)
        self.copy(self.give, self.out.at[at], 10, self.partner).wait_recv()

    def finish(self):
        for one in self.sent:
            one.wait_send()
        for made, cond in self.second:
            pl.when(cond)(made.wait_send)


def state_buffers():
    cube, low = (4, 128, 128), jnp.bfloat16
    return (
        [pltpu.VMEM(cube, jnp.float32)]
        + [pltpu.VMEM(cube, low)] * 6
        + [pltpu.VMEM((8, 128, 128), low), pltpu.VMEM((128, 128), jnp.float32)]
    )


def greet_more(place):
    barrier = pltpu.get_barrier_semaphore()
    r = lax.rem(place.me, 8)
    peers = [place.z * 8 + lax.bitwise_xor(r, k) for k in range(1, 8)]
    peers += [lax.rem(place.z + k, 4) * 8 + r for k in range(1, 4)]
    for peer in peers:
        pl.semaphore_signal(barrier, inc=1, device_id=peer, device_id_type=LOGICAL)
    pl.semaphore_wait(barrier, len(peers))


def forward_kernel(lengths, order, rate, gain_own, *refs):
    inputs, refs = refs[:10], refs[10:]
    f32, bf16 = jnp.float32, jnp.bfloat16
    n = 13
    full, refs = refs[:n], refs[n:]
    saved, refs = refs[:SAVED_BACK], refs[SAVED_BACK:]
    kept, refs = refs[:SAVED_BACK], refs[SAVED_BACK:]
    (hidden_rows, keys, values, queries, key_pre, query_pre, unit_pre, probs) = kept[:8]
    (attended, state_low, mixed_rows, middle, second_rows, left, right, product) = kept[8:16]
    gain, down_terms = kept[16], kept[17:]
    held, refs = refs[:10], refs[10:]
    (s_key, s_value, s_query, s_unit, s_output, tokens, s_left, s_right, s_down, cot) = held
    (in_sem, first_send, first_recv, down_first), refs = refs[:4], refs[4:]
    (hidden, mixed, second, turned, gain_tile) = refs[:5]
    refs = refs[1:]
    fetched = [
        pltpu.make_async_copy(src, dst, in_sem.at[i])
        for i, (src, dst) in enumerate(zip(inputs, held))
    ]
    for copy in fetched:
        copy.start()
    (dist, entry, leaving, gains, value) = refs[4:9]
    state_refs, arriving = refs[9:18], refs[16]
    (narrow, wide, send, recv, state_send, state_recv, load_sem, save_sem) = refs[18:]
    place = Place()
    half = s_left.shape[1] // 2
    own = [s_key, s_value, s_query, s_unit, gain_tile, s_output]
    own += [s_left.at[:, pl.ds(0, half)], s_left.at[:, pl.ds(half, half)]]
    own += [s_right.at[:, pl.ds(0, half)], s_right.at[:, pl.ds(half, half)]]
    parts = parts_of(s_down.shape[1], 128)
    own += [s_down.at[:, pl.ds(a, size)] for a, size in parts]
    lane = lax.broadcasted_iota(jnp.int32, gain_tile.shape, 1)
    line = lax.broadcasted_iota(jnp.int32, gain_tile.shape, 0)
    row = jnp.concatenate([gain_own[...].astype(f32)] * 4, axis=1)
    here = (lane // 32 == lax.rem(place.me, 4)) & (line == place.me // 4)
    gain_tile[...] = jnp.where(here, jnp.broadcast_to(row, gain_tile.shape), 0.0)
    greet_more(place)
    made = [Gather(place, own[i], full[i], send, recv, i) for i in range(n)]
    bounds = bounds_of(lengths, order)
    states = States(
        place, bounds, rate, False, value, state_refs, state_send, state_recv
    )
    slots = {0: narrow.at[0], 1: narrow.at[1], 2: narrow.at[0], 3: narrow.at[1], 4: gains}
    slots.update({5: narrow.at[0], 6: wide.at[0], 7: wide.at[1], 8: wide.at[0], 9: wide.at[1]})
    saves = []

    def save(*numbers):
        for i in numbers:
            copy = pltpu.make_async_copy(kept[i], saved[i], save_sem.at[i])
            copy.start()
            saves.append(copy)

    def weight(i):
        ref = slots[i]
        return ref[...].reshape(-1, ref.shape[-1])

    def turn(ref, rows):
        @pl.loop(0, 8)
        def _(i):
            block = ref[:, head_of(i)].astype(f32).T
            rows[i // 2, i % 2] = block.reshape((2, 2) + rows.shape[4:]).astype(bf16)

    def start():
        fetched[5].wait()
        fetched[9].wait()
        x = tokens[...].astype(f32)
        hidden[...] = (x * norm_scale(x)).astype(bf16)
        spans_of(place.me * SPAN, bounds, dist, entry, leaving)
        turn(hidden, hidden_rows)
        save(0)

    def project(i, pre, low):
        out = mm(hidden[...], weight(i))
        if pre is not None:
            pre[...] = out
            out = out / (1.0 + jnp.exp(-out))
        low[...] = out.astype(bf16)

    def key():
        project(0, key_pre, keys)
        save(1, 4)

    def increments():
        project(1, None, values)

        @pl.loop(0, 8)
        def _(h):
            at = head_of(h)
            held = (keys[:, at].astype(f32) * decay(leaving[...], rate[h])).astype(bf16)
            value[h] = mm_tn(held, values[:, at])

        states.spread()
        save(2)

    def query():
        project(2, query_pre, queries)

        @pl.loop(0, 8)
        def _(h):
            at = head_of(h)
            scores = mm_nt(queries[:, at], keys[:, at])
            low = (scores * decay(dist[...], rate[h])).astype(bf16)
            probs[h] = low
            attended[:, at] = mm(low, values[:, at])

        save(3, 5, 7)

    def unit():
        unit_pre[...] = mm(hidden[...], weight(3))
        save(6)

    def attend():
        gain[...] = jnp.sum(gains[...].reshape(-1, 8, 128), axis=0)

        @pl.loop(0, 8)
        def _(h):
            at = head_of(h)
            low = arriving[h].astype(bf16)
            state_low[h] = low
            held = (queries[:, at].astype(f32) * decay(entry[...], rate[h])).astype(bf16)
            out = attended[:, at] + mm(held, low)
            attended[:, at] = out
            mixed[:, at] = (
                out * norm_scale(out) * gain[pl.ds(h, 1), :] * unit_pre[:, at]
            ).astype(bf16)

        turn(mixed, mixed_rows)
        save(8, 9, 10, 16)

    def output():
        out = tokens[...].astype(f32) + mm(mixed[...], weight(5))
        middle[...] = out
        second[...] = (out * norm_scale(out)).astype(bf16)
        turn(second, second_rows)
        save(11, 12)

    def gate(i, side, part):
        side[:, pl.ds(part * half, half)] = mm(second[...], weight(i))

    def multiply(j):
        @pl.loop(0, half // 128)
        def _(i):
            at = pl.ds(pl.multiple_of(j * half + i * 128, 128), 128)
            block = (left[:, at] * right[:, at]).astype(bf16).astype(f32)
            turned[pl.ds(pl.multiple_of(i * 128, 128), 128), :] = block.T

        both = pl.ds(2 * j, 2)
        block = turned[...].reshape((2,) + product.shape[1:])
        product[both] = block.astype(bf16)
        rows = flat_rows(product[both, :, :, place.c1])
        for m, (a, size) in enumerate(parts):
            out = down_first if m == FIRST else down_terms[m]
            term = mm(rows, cot[:, pl.ds(a, size)])
            out[both] = term.reshape((2,) + out.shape[1:]).astype(bf16)
        exchange(j).start()

    def exchange(j):
        both = pl.ds(2 * j, 2)
        return pltpu.make_async_remote_copy(
            src_ref=down_first.at[both],
            dst_ref=down_terms[FIRST].at[both],
            send_sem=first_send.at[j],
            recv_sem=first_recv.at[j],
            device_id=place.to["p"],
            device_id_type=LOGICAL,
        )

    def joined(j):
        exchange(j).wait_recv()
        both, out = pl.ds(2 * j, 2), down_terms[FIRST]
        a, size = parts[FIRST]
        rows = flat_rows(product[both, :, :, place.c])
        term = mm(rows, cot[:, pl.ds(a, size)]).reshape((2,) + out.shape[1:])
        out[both] = (out[both].astype(f32) + term).astype(bf16)

    tasks = {2: [start], 7: [key], 8: [increments], 8.5: [states.join], 9: [query], 9.5: [states.total]}
    tasks.update({10: [unit], 10.5: [states.back], 11.5: [states.part], 12: [states.done, attend]})
    tasks[12.5] = [output]
    tasks[13] = [lambda: gate(6, left, 0)]
    tasks[14] = [lambda: gate(7, left, 1), lambda: save(13)]
    tasks[15] = [lambda: gate(8, right, 0), lambda: multiply(0)]
    tasks[16] = [lambda: gate(9, right, 1), lambda: multiply(1), lambda: save(19, 17, 15, 14)]
    tasks[16] += [lambda: joined(0)]
    tasks[18] = [lambda: joined(1), lambda: save(18)]
    needs = {0: 0, 1: 1, 2: 2, 3: 3, 5: 4, 6: 6, 8: 7, 10: 8}
    loads = {}
    for step in range(n + 6):
        i = step - 6
        for r in range(6):
            if r == 0:
                for k in range(3) if step == 0 else [step + 2]:
                    if k in needs:
                        fetched[needs[k]].wait()
                    if k < n:
                        made[k].round(0)
            elif 0 <= step - r < n:
                made[step - r].round(r)
            if r == 0:
                if i - 1 in loads:
                    loads[i - 1].wait()
                for task in tasks.get(step, []):
                    task()
            if r == 3:
                for task in tasks.get(step + 0.5, []):
                    task()
        if 0 <= i < n:
            made[i].pairs()
        if i in slots:
            loads[i] = pltpu.make_async_copy(full[i], slots[i], load_sem.at[i])
            loads[i].start()
    for one in made:
        one.finish()
    states.finish()
    for j in range(2):
        exchange(j).wait_send()
    for copy in saves:
        copy.wait()


def forward(lengths, order, rate, tokens, cot, gain, shards):
    f32, bf16 = jnp.float32, jnp.bfloat16
    size, width = tokens.shape
    wide = shards[5].shape[1]
    half = wide // 2
    blocks = [(s.shape, s.dtype) for s in shards[:4]] + [((8, 128), f32)]
    blocks += [(shards[4].shape, bf16)] + [((32, half), bf16)] * 4
    parts = parts_of(width, 128)
    blocks += [((shards[7].shape[0], p), bf16) for _, p in parts]
    square, cube = (size, width), (8, 128, 128)
    rows, down_rows = shards[4].shape[0], shards[7].shape[0]
    across = ((4, 2, 2, 2, rows, size), bf16)
    kept = [across] + [(square, bf16)] * 3 + [(square, f32)] * 3 + [((8, size, size), bf16)]
    kept += [(square, f32), (cube, bf16), across, (square, f32), across]
    kept += [((size, wide), f32)] * 2 + [((4, 2, 2, 2, down_rows, size), bf16), ((8, 128), f32)]
    kept += [((4, 2, 2, down_rows, p), bf16) for _, p in parts]
    vmem, hbm = pl.BlockSpec(memory_space=pltpu.VMEM), pl.BlockSpec(memory_space=pltpu.HBM)
    smem = pl.BlockSpec(memory_space=pltpu.SMEM)
    n = len(blocks)
    inputs = [*shards[:5], tokens, *shards[5:], cot]
    out = pl.pallas_call(
        forward_kernel,
        out_shape=[jax.ShapeDtypeStruct((4, 2, 2, 2) + s, t) for s, t in blocks]
        + [jax.ShapeDtypeStruct(s, t) for s, t in kept],
        in_specs=[smem] * 3 + [vmem] + [hbm] * 10,
        out_specs=[hbm] * (n + len(kept)),
        scratch_shapes=[pltpu.VMEM(s, t) for s, t in kept]
        + [pltpu.VMEM(s.shape, s.dtype) for s in inputs]
        + [pltpu.SemaphoreType.DMA((10,))]
        + [pltpu.SemaphoreType.DMA((2,))] * 2
        + [pltpu.VMEM((4, 2, 2, down_rows, parts[FIRST][1]), bf16)]
        + [pltpu.VMEM(square, bf16)] * 3
        + [pltpu.VMEM((half, size), f32), pltpu.VMEM((8, 128), f32)]
        + [pltpu.VMEM((size, size), f32), pltpu.VMEM((size, 128), f32), pltpu.VMEM((size, 128), f32)]
        + [pltpu.VMEM((4, 2, 2, 2, 8, 128), f32)]
        + [pltpu.VMEM(cube, f32)]
        + state_buffers()
        + [
            pltpu.VMEM((2, 4, 2, 2, 2, 32, width), bf16),
            pltpu.VMEM((2, 4, 2, 2, 2, 32, half), bf16),
            pltpu.SemaphoreType.DMA((n, Gather.NSEND + 1)),
            pltpu.SemaphoreType.DMA((n, Gather.NRECV)),
            pltpu.SemaphoreType.DMA((18,)),
            pltpu.SemaphoreType.DMA((18,)),
            pltpu.SemaphoreType.DMA((n,)),
            pltpu.SemaphoreType.DMA((len(kept),)),
        ],
        compiler_params=pltpu.CompilerParams(
            collective_id=0, has_side_effects=True, vmem_limit_bytes=VMEM_LIMIT
        ),
        name="forward",
    )(lengths, order, rate, gain, *inputs)
    return out[:n], out[n:]

def backward_kernel(lengths, order, rate, h_tokens, h_cot, *refs):
    f32, bf16 = jnp.float32, jnp.bfloat16
    n = 14
    saved, refs = refs[:SAVED_BACK], refs[SAVED_BACK:]
    (h_hidden, h_keys, h_values, h_queries, h_key_pre, h_query_pre, h_unit_pre, h_probs) = saved[:8]
    (h_attended, h_state_low, h_mixed, h_middle, h_second, h_left, h_right, h_product) = saved[8:16]
    h_gain, h_down = saved[16], saved[17:]
    w_in, refs = refs[:12], refs[12:]
    (w_key, w_value, w_query, w_unit, w_output, w_l0, w_l1, w_r0, w_r1) = w_in[:9]
    w_down = w_in[9:]
    sums, result_out, tokens_out, refs = refs[:n], refs[n], refs[n + 1], refs[n + 2 :]
    out, tokens, cot, refs = refs[:n], refs[n], refs[n + 1], refs[n + 2 :]
    acc, came, refs = refs[:n], refs[n : 2 * n], refs[2 * n :]
    (part, gain_part, wd, down, wl, left, right, f1, f2, f3, f4) = refs[:11]
    (branch, ga, gup, gkp, gvp, result, glp, grp, rows, mixed, product) = refs[11:22]
    (probs, state_low, gain, gg, dist, entry, leaving) = refs[22:29]
    value, state_refs, arriving = refs[29], refs[30:39], refs[37]
    (send, recv, state_send, state_recv, load_sem, out_sem) = refs[39:]
    place = Place()
    half = h_left.shape[1] // 2
    width = tokens.shape[1]
    left_w, right_w = left.at[:, pl.ds(0, width)], right.at[:, pl.ds(0, width)]
    queries, keys = glp.at[:, pl.ds(0, width)], glp.at[:, pl.ds(width, width)]
    values, gqp = grp.at[:, pl.ds(0, width)], grp.at[:, pl.ds(width, width)]
    wn = wl.at[:, :, :, :, :, pl.ds(0, width)]
    greet_more(place)
    bounds = bounds_of(lengths, order)
    states = States(
        place, bounds, rate, True, value, state_refs, state_send, state_recv
    )
    loads = {}

    def load(name, src, dst):
        copy = pltpu.make_async_copy(src, dst, load_sem.at[len(loads)])
        loads[name] = copy
        copy.start()

    def load_down(i):
        for m, (a, size) in enumerate(parts):
            dst = wd.at[:, :, :, :, :, pl.ds(a, size)]
            load("down%d%d" % (i, m), w_down[m].at[pl.ds(2 * i, 2)], dst)

    def loaded(*names):
        for name in names:
            loads[name].wait()

    def weight(cols):
        return wl[:, :, :, :, :, pl.ds(0, cols)].reshape(-1, cols)

    def side(i):
        return pl.ds(i * half, half)

    def product_of(i):
        return flat_rows(product[pl.ds(2 * i, 2)])

    class Piece:
        def __init__(self, rows, core_rows, grad, cols, need=()):
            self.rows, self.core_rows, self.grad, self.cols, self.need = rows, core_rows, grad, cols, need

        def term(self, zh, core):
            lhs = self.rows[pl.ds(zh * 2, 2), :, :, core]
            lhs = flat_rows(lhs) if self.core_rows % 16 else lhs.reshape(-1, lhs.shape[-1])
            out = mm(lhs, self.grad[...])
            return out.reshape(2, 2, 2, self.core_rows, self.cols)

        def first(self):
            @pl.loop(0, 2)
            def _(zh):
                part[pl.ds(zh * 2, 2), :, :, :, pl.ds(0, self.cols)] = self.term(
                    zh, place.c1
                ).astype(bf16)

        def second(self, acc):
            @pl.loop(0, 2)
            def _(zh):
                at = pl.ds(zh * 2, 2)
                acc[at] = (acc[at].astype(f32) + self.term(zh, place.c)).astype(bf16)

    class Gain:
        def first(self):
            gain_part[...] = jnp.broadcast_to(gg[...][None, None, None], gain_part.shape)

        def second(self, acc):
            acc[...] = acc[...] + gg[...][None, None, None]

    wide = part.at[:, :, :, :, pl.ds(0, half)]
    narrow = part.at[:, :, :, :, pl.ds(0, width)]
    parts = parts_of(width, 128)
    pieces = []
    for m in ORDER:
        a, size = parts[m]
        piece = None if m == FIRST else Piece(product, 88, cot.at[:, pl.ds(a, size)], size)
        pieces.append((h_down[m], piece))
    pieces += [(wide, Piece(rows, 32, glp.at[:, side(i)], half)) for i in (0, 1)]
    pieces += [(wide, Piece(rows, 32, grp.at[:, side(i)], half)) for i in (0, 1)]
    pieces += [(narrow, Piece(mixed, 32, branch, width)), (gain_part, Gain())]
    pieces += [(narrow, Piece(rows, 32, g, width)) for g in (gup, gqp, gvp)]
    last = width // 4
    for a, size in ((0, width - last), (width - last, last)):
        view = part.at[:, :, :, :, pl.ds(0, size)]
        pieces.append((view, Piece(rows, 32, gkp.at[:, pl.ds(a, size)], size)))
    made = [
        Scatter(place, pieces[i][0], acc[i], pieces[i][1], came[i], out[i], send, recv, i)
        for i in range(n)
    ]

    def begin():
        spans_of(place.me * SPAN, bounds, dist, entry, leaving)

    def gates(i):
        loaded("down%d0" % i, "down%d1" % i, "down%d2" % i, "left%d" % i, "right%d" % i)
        pair = 2 * wd.shape[4]

        @pl.loop(0, 8)
        def _(k):
            at = pl.ds(pl.multiple_of(k * pair, 16), pair)
            down[at, :] = flat_rows(wd[k // 4, (k // 2) % 2, k % 2])

        grad = mm_nt(cot[...], down[...])
        glp[:, side(i)] = (grad * right[...]).astype(bf16)
        grp[:, side(i)] = (grad * left[...]).astype(bf16)
        if i == 0:
            loaded("middle")
            f3[...] = f2[...] + mm_tn(product_of(0), down[...])
            load_down(1)
            load("left1", h_left.at[:, side(1)], left)
            load("right1", h_right.at[:, side(1)], right)
        else:
            result[...] = (f3[...] + mm_tn(product_of(1), down[...])).astype(bf16)
            load("unit_pre", h_unit_pre, left_w)
            load("result", result, result_out)

    def second_part(name, grad, i, following, start):
        loaded(name)
        term = mm_nt(grad[:, side(i)], weight(half))
        f1[...] = term if start else f1[...] + term
        load(*following)

    def middle():
        @pl.loop(0, SPAN // 16)
        def _(i):
            at = pl.ds(pl.multiple_of(i * 16, 16), 16)
            x, g = f2[at, :], f1[at, :]
            scale = norm_scale(x)
            unit = x * scale
            grad = cot[at, :].astype(f32) + scale * (
                g - unit * jnp.mean(g * unit, axis=-1, keepdims=True)
            )
            f3[at, :] = grad
            branch[at, :] = grad.astype(bf16)

        load("attended", h_attended, f2)

    def spare():
        load("queries", h_queries, queries)
        load("keys", h_keys, keys)
        load("values", h_values, values)
        load("hidden", h_hidden, rows)

    def attention():
        loaded("output")
        f1[...] = mm_nt(branch[...], weight(width))
        load("unit", w_unit, wn)
        loaded("attended", "unit_pre", "queries", "gain")

        @pl.loop(0, 8)
        def _(h):
            at = head_of(h)
            att, up, gm = f2[:, at], left_w[:, at], f1[:, at]
            scale = norm_scale(att)
            unit = att * scale
            row = gain[pl.ds(h, 1), :]
            gated = gm * up
            gg[pl.ds(h, 1), :] = jnp.sum(gated * unit, axis=0, keepdims=True)
            gup[:, at] = (gm * unit * row).astype(bf16)
            g = gated * row
            low = (
                scale * (g - unit * jnp.mean(g * unit, axis=-1, keepdims=True))
            ).astype(bf16)
            ga[:, at] = low
            held = (queries[:, at].astype(f32) * decay(entry[...], rate[h])).astype(bf16)
            value[h] = mm_tn(held, low)

        states.spread()
        load("key_pre", h_key_pre, f2)

    def scores():
        loaded("keys", "values", "query_pre", "probs", "state_low")

        @pl.loop(0, 8)
        def _(h):
            at = head_of(h)
            low = ga[:, at]
            grads = (mm_nt(low, values[:, at]) * decay(dist[...], rate[h])).astype(bf16)
            grad_q = mm(grads, keys[:, at])
            grad_q = grad_q + mm_nt(low, state_low[h]) * decay(entry[...], rate[h])
            gqp[:, at] = (grad_q * slope(f4[:, at])).astype(bf16)
            f1[:, at] = mm_tn(grads, queries[:, at])
            right_w[:, at] = mm_tn(probs[h], low)

    def hidden_part(name, grad, following, start):
        loaded(name)
        term = mm_nt(grad[...], weight(width))
        f4[...] = term if start else f4[...] + term
        if following:
            load(*following)

    def unit_rest():
        hidden_part("unit", gup, ("query", w_query, wn), True)

    def last_grads():
        hidden_part("query", gqp, ("value", w_value, wn), False)
        states.done()
        loaded("key_pre")

        @pl.loop(0, 8)
        def _(h):
            at = head_of(h)
            grad = arriving[h].astype(bf16)
            fall = decay(leaving[...], rate[h])
            held = (keys[:, at].astype(f32) * fall).astype(bf16)
            grad_k = f1[:, at] + mm_nt(values[:, at], grad) * fall
            gkp[:, at] = (grad_k * slope(f2[:, at])).astype(bf16)
            gvp[:, at] = (right_w[:, at] + mm(held, grad)).astype(bf16)

    def value_rest():
        hidden_part("value", gvp, ("key", w_key, wn), False)

    def inputs():
        hidden_part("key", gkp, None, False)
        loaded("input")

        @pl.loop(0, SPAN // 16)
        def _(i):
            at = pl.ds(pl.multiple_of(i * 16, 16), 16)
            x, g = tokens[at, :].astype(f32), f4[at, :]
            scale = norm_scale(x)
            unit = x * scale
            f3[at, :] = f3[at, :] + scale * (g - unit * jnp.mean(g * unit, axis=-1, keepdims=True))

        load("tokens", f3, tokens_out)

    before = {2: lambda: loaded("product", "cot"), 3: lambda: loaded("second"), 7: lambda: loaded("mixed")}
    before[9] = lambda: loaded("hidden")
    tasks = {0: [begin], 2: [lambda: gates(0)], 3: [lambda: gates(1)]}
    tasks[4] = [lambda: second_part("l0", glp, 0, ("l1", w_l1, wl), True)]
    tasks[5] = [lambda: second_part("l1", glp, 1, ("r0", w_r0, wl), False)]
    tasks[6] = [
        lambda: second_part("r0", grp, 0, ("r1", w_r1, wl), False),
        lambda: second_part("r1", grp, 1, ("output", w_output, wn), False),
        middle,
    ]
    tasks[7] = [spare, attention]
    tasks[7.5] = [states.join]
    tasks[8] = [scores]
    tasks[8.5] = [states.total]
    tasks[9] = [unit_rest, states.back]
    tasks[9.5] = [states.part]
    tasks[10] = [last_grads]
    tasks[11] = [value_rest]
    tasks[12] = [inputs]
    for i in range(3):
        made[i].round(0)
    load("product", h_product, product)
    load("cot", h_cot, cot)
    load_down(0)
    load("left0", h_left.at[:, side(0)], left)
    load("right0", h_right.at[:, side(0)], right)
    load("middle", h_middle, f2)
    load("second", h_second, rows)
    load("l0", w_l0, wl)
    load("mixed", h_mixed, mixed)
    load("gain", h_gain, gain)
    load("query_pre", h_query_pre, f4)
    load("probs", h_probs, probs)
    load("state_low", h_state_low, state_low)
    load("input", h_tokens, tokens)
    def given(i):
        return pltpu.make_async_copy(out[i], sums[i], out_sem.at[i])

    for step in range(n + 6):
        if step in before:
            before[step]()
        if 2 < step < n:
            if step > 3:
                made[step - 1].handed()
            pieces[step][1].first()
            made[step].round(0)
        if 0 < step <= n:
            made[step - 1].round(1)
        for task in tasks.get(step, []):
            task()
        for r in range(2, 7):
            if 0 <= step - r < n:
                made[step - r].round(r)
                if r == 6:
                    given(step - r).start()
            if r == 4:
                for task in tasks.get(step + 0.5, []):
                    task()
    for i, one in enumerate(made):
        if i in (1, 2, n - 1):
            one.handed()
        given(i).wait()
        one.finish()
    states.finish()
    loaded("result", "tokens")


def backward(lengths, order, rate, tokens, cot, saved, weights):
    f32, bf16 = jnp.float32, jnp.bfloat16
    size, width = tokens.shape
    wide = saved[13].shape[1]
    half = wide // 2
    rows = width // 32
    down_rows = wide // 32
    parts, last = parts_of(width, 128), width // 4
    blocks = [((down_rows, parts[m][1]), bf16) for m in ORDER] + [((rows, half), bf16)] * 4
    blocks += [((rows, width), bf16), ((8, 128), f32)] + [((rows, width), bf16)] * 3
    blocks += [((rows, width - last), bf16), ((rows, last), bf16)]
    n = len(blocks)
    square, cube = (size, width), (8, 128, 128)
    hbm = pl.BlockSpec(memory_space=pltpu.HBM)
    smem = pl.BlockSpec(memory_space=pltpu.SMEM)
    out = pl.pallas_call(
        backward_kernel,
        out_shape=[jax.ShapeDtypeStruct(b, f32) for b, _ in blocks]
        + [jax.ShapeDtypeStruct(square, bf16), jax.ShapeDtypeStruct(square, f32)],
        in_specs=[smem] * 3 + [hbm] * (2 + len(saved) + len(weights)),
        out_specs=[hbm] * (n + 2),
        scratch_shapes=[pltpu.VMEM(b, f32) for b, _ in blocks]
        + [pltpu.VMEM(square, bf16)] * 2
        + [pltpu.VMEM((4, 2, 2) + b, t) for b, t in blocks]
        + [pltpu.VMEM((19,) + b, t) for b, t in blocks]
        + [
            pltpu.VMEM((4, 2, 2, rows, half), bf16),
            pltpu.VMEM((4, 2, 2, 8, 128), f32),
            pltpu.VMEM((2, 2, 2, 2, down_rows, width), bf16),
            pltpu.VMEM((half, width), bf16),
            pltpu.VMEM((4, 2, 2, 2, rows, half), bf16),
            pltpu.VMEM((size, half), f32),
            pltpu.VMEM((size, half), f32),
        ]
        + [pltpu.VMEM(square, f32)] * 4
        + [pltpu.VMEM(square, bf16)] * 6
        + [pltpu.VMEM((size, wide), bf16)] * 2
        + [pltpu.VMEM((4, 2, 2, 2, rows, size), bf16)] * 2
        + [pltpu.VMEM((4, 2, 2, 2, down_rows, size), bf16)]
        + [pltpu.VMEM((8, size, size), bf16), pltpu.VMEM(cube, bf16)]
        + [pltpu.VMEM((8, 128), f32)] * 2
        + [pltpu.VMEM((size, size), f32), pltpu.VMEM((size, 128), f32), pltpu.VMEM((size, 128), f32)]
        + [pltpu.VMEM(cube, f32)]
        + state_buffers()
        + [
            pltpu.SemaphoreType.DMA((n, Scatter.NSEND + 1)),
            pltpu.SemaphoreType.DMA((n, Scatter.NRECV)),
            pltpu.SemaphoreType.DMA((18,)),
            pltpu.SemaphoreType.DMA((18,)),
            pltpu.SemaphoreType.DMA((48,)),
            pltpu.SemaphoreType.DMA((n,)),
        ],
        compiler_params=pltpu.CompilerParams(
            collective_id=3, has_side_effects=True, vmem_limit_bytes=67000000
        ),
        name="backward",
    )(lengths, order, rate, tokens, cot, *saved, *weights)
    return out[:n], out[n], out[n + 1]


RESULTS = ((10,), (12, 13), (11,), (9,), (7,), (8,), (3, 4), (5, 6), (2, 0, 1))


def deliver_kernel(*refs):
    given, out, held, gain, own = refs[:16], refs[16:27], refs[27:38], refs[38], refs[39]
    in_sem, out_sem = refs[40:]
    sources = [(0,), (1,)] + [tuple(k + 2 for k in found) for found in RESULTS]
    copies = []
    for dst, found in zip(held, sources):
        at, mine = 0, []
        for k in found:
            size = given[k].shape[1]
            place = gain if k == 10 else dst.at[:, pl.ds(at, size)]
            mine.append(pltpu.make_async_copy(given[k], place, in_sem.at[k]))
            at += size
        for copy in mine:
            copy.start()
        copies.append(mine)
    made = []
    for i, mine in enumerate(copies):
        for copy in mine:
            copy.wait()
        src = held[i]
        if i == 7:
            me = lax.axis_index(AXIS)
            row = gain[pl.ds(me // 4, 1), :]
            found = jnp.zeros((1, 32), jnp.float32)
            for k in range(4):
                found = found + jnp.where(lax.rem(me, 4) == k, 1.0, 0.0) * row[:, 32 * k : 32 * k + 32]
            own[...] = found
            src = own
        copy = pltpu.make_async_copy(src, out[i], out_sem.at[i])
        copy.start()
        made.append(copy)
    for copy in made:
        copy.wait()


def deliver(result, inputs, grads):
    f32 = jnp.float32
    shapes = [(grads[k[0]].shape[0], sum(grads[i].shape[1] for i in k)) for k in RESULTS]
    shapes[5] = (1, 32)
    shapes = [(result.shape, result.dtype), (inputs.shape, f32)] + [(s, f32) for s in shapes]
    hbm = pl.BlockSpec(memory_space=pltpu.HBM)
    out = pl.pallas_call(
        deliver_kernel,
        out_shape=[jax.ShapeDtypeStruct(s, t) for s, t in shapes],
        in_specs=[hbm] * 16,
        out_specs=[hbm] * 11,
        scratch_shapes=[pltpu.VMEM(s, t) for s, t in shapes]
        + [
            pltpu.VMEM((8, 128), f32),
            pltpu.VMEM((1, 32), f32),
            pltpu.SemaphoreType.DMA((16,)),
            pltpu.SemaphoreType.DMA((11,)),
        ],
        name="deliver",
    )(result, inputs, *grads)
    return (*out[:7], out[7].reshape(-1), *out[8:])


def entering(value, axis, combine, identity, reverse):
    length, here = (lax.axis_size(axis), lax.axis_index(axis))
    everything = jax.tree.map(lambda part: lax.all_gather(part, axis), value)
    start = jax.tree.map(
        lambda part, zero: jnp.broadcast_to(jnp.asarray(zero, part.dtype), part.shape),
        value,
        identity,
    )

    def hop(k, before):
        at = length - 1 - k if reverse else k
        reached = at > here if reverse else at < here
        new = combine(before, jax.tree.map(lambda part: part[at], everything))
        return jax.tree.map(lambda a, b: jnp.where(reached, a, b), new, before)

    return lax.fori_loop(0, length, hop, start)


def segment_of(places, lengths, seq_order):
    number = lengths.shape[0]
    picked = seq_order[:, None] == jnp.arange(number, dtype=jnp.int32)[None, :]
    packed = jnp.sum(jnp.where(picked, lengths[None, :], 0), axis=1, dtype=jnp.int32)
    bounds = jnp.cumsum(packed, dtype=jnp.int32)
    found = jnp.sum((bounds[None, :] <= places[:, None]).astype(jnp.int32), axis=1, dtype=jnp.int32)
    return jnp.where(places < 0, -1, found)


def decay_tables(segments, before, rate, block):
    length = segments.shape[0]
    count = length // block
    spans = segments.reshape(count, block)
    priors = jnp.concatenate([before.reshape(1), spans[:-1, -1]])
    steps = jnp.arange(block, dtype=jnp.int32)
    distance = steps[:, None] - steps[None, :]
    same = (spans[:, :, None] == spans[:, None, :]) & (distance >= 0)[None]
    powers = jnp.exp(-rate[:, None, None] * jnp.maximum(distance, 0).astype(jnp.float32)[None])
    within = jnp.where(same[:, None], powers[None], 0.0)
    entry = jnp.where(
        (spans == priors[:, None])[:, :, None],
        jnp.exp(-rate[None, :] * steps.astype(jnp.float32)[:, None])[None],
        0.0,
    )
    leaving = jnp.where(
        (spans == spans[:, -1:])[:, :, None],
        jnp.exp(-rate[None, :] * (block - steps).astype(jnp.float32)[:, None])[None],
        0.0,
    )
    passing = jnp.where((spans[:, -1] == priors)[:, None], jnp.exp(-rate * block)[None], 0.0)
    offsets = (jnp.arange(count, dtype=jnp.int32) * block).astype(jnp.float32)
    arrival = jnp.where(
        (priors == before)[:, None], jnp.exp(-rate[None, :] * offsets[:, None]), 0.0
    )
    through = jnp.where(segments[-1] == before, jnp.exp(-rate * length), 0.0)
    return (within, entry, leaving, passing, arrival, through)


def chain_states(earlier, later):
    return (earlier[0] * later[0], later[0][:, None, None] * earlier[1] + later[1])


def silu_slope(values):
    sigma = jax.nn.sigmoid(values)
    return sigma * (1.0 + values * (1.0 - sigma))


def row_scale(values):
    return lax.rsqrt(jnp.mean(values * values, axis=-1, keepdims=True) + EPSILON)


def body(
    tokens,
    lengths,
    seq_order,
    decay_rate,
    w_query,
    w_key,
    w_value,
    w_unit,
    w_output,
    norm_gain,
    w_left,
    w_right,
    w_down,
    cotangent,
):
    f32 = jnp.float32
    bf16 = jnp.bfloat16
    length, width = tokens.shape
    heads = decay_rate.shape[0]
    head_size = width // heads
    count = length // SPAN
    first = lax.axis_index(AXIS) * length
    places = first + jnp.arange(length, dtype=jnp.int32)
    segments = segment_of(places, lengths, seq_order)
    before = segment_of(jnp.reshape(first - 1, (1,)), lengths, seq_order)[0]
    within, entry, leaving, passing, arrival, through = decay_tables(
        segments, before, decay_rate, SPAN
    )
    attention_set = (
        lax.all_gather(w_query, AXIS, axis=0, tiled=True),
        lax.all_gather(w_key, AXIS, axis=0, tiled=True),
        lax.all_gather(w_value, AXIS, axis=0, tiled=True),
        lax.all_gather(w_unit, AXIS, axis=0, tiled=True),
        lax.all_gather(w_output, AXIS, axis=0, tiled=True),
        lax.all_gather(norm_gain, AXIS, axis=0, tiled=True),
    )
    feed_set = (
        lax.all_gather(w_left, AXIS, axis=0, tiled=True),
        lax.all_gather(w_right, AXIS, axis=0, tiled=True),
        lax.all_gather(w_down, AXIS, axis=0, tiled=True),
    )
    full_query, full_key, full_value, full_unit, full_output, full_gain = attention_set
    full_left, full_right, full_down = feed_set
    inputs = tokens.astype(f32)
    first_scale = row_scale(inputs)
    normed = inputs * first_scale
    hidden = normed.astype(bf16)
    query_pre = jnp.dot(hidden, full_query, preferred_element_type=f32)
    key_pre = jnp.dot(hidden, full_key, preferred_element_type=f32)
    value_pre = jnp.dot(hidden, full_value, preferred_element_type=f32)
    unit_pre = jnp.dot(hidden, full_unit, preferred_element_type=f32)
    block_shape = (count, SPAN, heads, head_size)
    query_blocks = jax.nn.silu(query_pre).astype(bf16).reshape(block_shape)
    key_blocks = jax.nn.silu(key_pre).astype(bf16).reshape(block_shape)
    value_blocks = value_pre.astype(bf16).reshape(block_shape)
    scores = jnp.einsum("nthe,nshe->nhts", query_blocks, key_blocks, preferred_element_type=f32)
    mixing = (scores * within).astype(bf16)
    local_out = jnp.einsum("nhts,nshe->nthe", mixing, value_blocks, preferred_element_type=f32)
    keys_held = (key_blocks * leaving[..., None]).astype(bf16)
    increments = jnp.einsum("nshe,nshf->nhef", keys_held, value_blocks, preferred_element_type=f32)
    local_states = [jnp.zeros((heads, head_size, head_size), f32)]
    local_states.append(passing[0][:, None, None] * local_states[-1] + increments[0])
    end_state = local_states[count]
    start_pair = (jnp.ones_like(through), jnp.zeros_like(end_state))
    arriving = entering((through, end_state), AXIS, chain_states, start_pair, False)[1]
    states = jnp.stack(local_states[:count]) + arrival[:, :, None, None] * arriving[None]
    state_low = states.astype(bf16)
    query_held = (query_blocks * entry[..., None]).astype(bf16)
    attended = local_out + jnp.einsum(
        "nthe,nhef->nthf", query_held, state_low, preferred_element_type=f32
    )
    attended_heads = attended.reshape(length, heads, head_size)
    head_scale = row_scale(attended_heads)
    unit_norm = (attended_heads * head_scale).reshape(length, width)
    gain = full_gain.astype(f32)
    gated = unit_norm * gain
    mixed_in = (gated * unit_pre).astype(bf16)
    middle = inputs + jnp.dot(mixed_in, full_output, preferred_element_type=f32)
    second_scale = row_scale(middle)
    second_unit = middle * second_scale
    second = second_unit.astype(bf16)
    left_pre = jnp.dot(second, full_left, preferred_element_type=f32)
    right_pre = jnp.dot(second, full_right, preferred_element_type=f32)
    product = (left_pre * right_pre).astype(bf16)
    result = (middle + jnp.dot(product, full_down, preferred_element_type=f32)).astype(bf16)
    back_feed = (
        lax.all_gather(w_left, AXIS, axis=0, tiled=True),
        lax.all_gather(w_right, AXIS, axis=0, tiled=True),
        lax.all_gather(w_down, AXIS, axis=0, tiled=True),
    )
    back_left, back_right, back_down = back_feed
    grad_product = jnp.einsum("td,fd->tf", cotangent, back_down, preferred_element_type=f32)
    grad_left_pre = (grad_product * right_pre).astype(bf16)
    grad_right_pre = (grad_product * left_pre).astype(bf16)
    grad_w_down = jnp.einsum("tf,td->fd", product, cotangent, preferred_element_type=f32)
    grad_w_left = jnp.einsum("td,tf->df", second, grad_left_pre, preferred_element_type=f32)
    grad_w_right = jnp.einsum("td,tf->df", second, grad_right_pre, preferred_element_type=f32)
    feed_grads = (
        lax.psum_scatter(grad_w_left, AXIS, scatter_dimension=0, tiled=True),
        lax.psum_scatter(grad_w_right, AXIS, scatter_dimension=0, tiled=True),
        lax.psum_scatter(grad_w_down, AXIS, scatter_dimension=0, tiled=True),
    )
    grad_second = jnp.einsum(
        "tf,df->td", grad_left_pre, back_left, preferred_element_type=f32
    ) + jnp.einsum("tf,df->td", grad_right_pre, back_right, preferred_element_type=f32)
    grad_middle = cotangent.astype(f32) + second_scale * (
        grad_second - second_unit * jnp.mean(grad_second * second_unit, axis=-1, keepdims=True)
    )
    back_attention = (
        lax.all_gather(w_query, AXIS, axis=0, tiled=True),
        lax.all_gather(w_key, AXIS, axis=0, tiled=True),
        lax.all_gather(w_value, AXIS, axis=0, tiled=True),
        lax.all_gather(w_unit, AXIS, axis=0, tiled=True),
        lax.all_gather(w_output, AXIS, axis=0, tiled=True),
        lax.all_gather(norm_gain, AXIS, axis=0, tiled=True),
    )
    back_query, back_key, back_value, back_unit, back_output, back_gain = back_attention
    grad_branch = grad_middle.astype(bf16)
    grad_w_output = jnp.einsum(TD_TE, mixed_in, grad_branch, preferred_element_type=f32)
    grad_mixed = jnp.einsum(TE_DE, grad_branch, back_output, preferred_element_type=f32)
    grad_gated = grad_mixed * unit_pre
    grad_unit_pre = (grad_mixed * gated).astype(bf16)
    grad_gain = jnp.sum(grad_gated * unit_norm, axis=0)
    grad_norm_heads = (grad_gated * back_gain.astype(f32)).reshape(length, heads, head_size)
    norm_heads = unit_norm.reshape(length, heads, head_size)
    grad_att = head_scale * (
        grad_norm_heads
        - norm_heads * jnp.mean(grad_norm_heads * norm_heads, axis=-1, keepdims=True)
    )
    grad_att_blocks = grad_att.astype(bf16).reshape(block_shape)
    grad_mixing = jnp.einsum(
        "nthf,nshf->nhts", grad_att_blocks, value_blocks, preferred_element_type=f32
    )
    grad_scores = (grad_mixing * within).astype(bf16)
    grad_query_blocks = (
        jnp.einsum("nhts,nshe->nthe", grad_scores, key_blocks, preferred_element_type=f32)
        + jnp.einsum("nthf,nhef->nthe", grad_att_blocks, state_low, preferred_element_type=f32)
        * entry[..., None]
    )
    grad_key_blocks = jnp.einsum(
        "nhts,nthe->nshe", grad_scores, query_blocks, preferred_element_type=f32
    )
    grad_value_blocks = jnp.einsum(
        "nhts,nthf->nshf", mixing, grad_att_blocks, preferred_element_type=f32
    )
    direct = jnp.einsum("nthe,nthf->nhef", query_held, grad_att_blocks, preferred_element_type=f32)
    leaving_sum = jnp.sum(arrival[:, :, None, None] * direct, axis=0)
    later = entering((through, leaving_sum), AXIS, chain_states, start_pair, True)[1]
    next_grads = [later]
    grad_increment = jnp.stack(next_grads[::-1]).astype(bf16)
    grad_keys_held = jnp.einsum(
        "nhef,nshf->nshe", grad_increment, value_blocks, preferred_element_type=f32
    )
    grad_key_blocks = grad_key_blocks + grad_keys_held * leaving[..., None]
    grad_value_blocks = grad_value_blocks + jnp.einsum(
        "nshe,nhef->nshf", keys_held, grad_increment, preferred_element_type=f32
    )
    grad_query_pre = (grad_query_blocks.reshape(length, width) * silu_slope(query_pre)).astype(bf16)
    grad_key_pre = (grad_key_blocks.reshape(length, width) * silu_slope(key_pre)).astype(bf16)
    grad_value_pre = grad_value_blocks.reshape(length, width).astype(bf16)
    grad_w_query = jnp.einsum(TD_TE, hidden, grad_query_pre, preferred_element_type=f32)
    grad_w_key = jnp.einsum(TD_TE, hidden, grad_key_pre, preferred_element_type=f32)
    grad_w_value = jnp.einsum(TD_TE, hidden, grad_value_pre, preferred_element_type=f32)
    grad_w_unit = jnp.einsum(TD_TE, hidden, grad_unit_pre, preferred_element_type=f32)
    attention_grads = (
        lax.psum_scatter(grad_w_query, AXIS, scatter_dimension=0, tiled=True),
        lax.psum_scatter(grad_w_key, AXIS, scatter_dimension=0, tiled=True),
        lax.psum_scatter(grad_w_value, AXIS, scatter_dimension=0, tiled=True),
        lax.psum_scatter(grad_w_unit, AXIS, scatter_dimension=0, tiled=True),
        lax.psum_scatter(grad_w_output, AXIS, scatter_dimension=0, tiled=True),
        lax.psum_scatter(grad_gain, AXIS, scatter_dimension=0, tiled=True),
    )
    grad_hidden = (
        jnp.einsum(TE_DE, grad_query_pre, back_query, preferred_element_type=f32)
        + jnp.einsum(TE_DE, grad_key_pre, back_key, preferred_element_type=f32)
        + jnp.einsum(TE_DE, grad_value_pre, back_value, preferred_element_type=f32)
        + jnp.einsum(TE_DE, grad_unit_pre, back_unit, preferred_element_type=f32)
    )
    grad_inputs = grad_middle + first_scale * (
        grad_hidden - normed * jnp.mean(grad_hidden * normed, axis=-1, keepdims=True)
    )
    return (
        result,
        grad_inputs,
        attention_grads[0],
        attention_grads[1],
        attention_grads[2],
        attention_grads[3],
        attention_grads[4],
        attention_grads[5],
        feed_grads[0],
        feed_grads[1],
        feed_grads[2],
    )


def body_kernels(
    tokens,
    lengths,
    seq_order,
    decay_rate,
    w_query,
    w_key,
    w_value,
    w_unit,
    w_output,
    norm_gain,
    w_left,
    w_right,
    w_down,
    cotangent,
):
    full, saved = forward(
        lengths,
        seq_order,
        decay_rate,
        tokens,
        cotangent,
        norm_gain.reshape(1, -1),
        [w_key, w_value, w_query, w_unit, w_output, w_left, w_right, w_down],
    )
    grads, result, grad_inputs = backward(
        lengths, seq_order, decay_rate, tokens, cotangent, saved, full[:4] + full[5:]
    )
    return deliver(result, grad_inputs, grads)


def solution(mesh):
    placed = (
        P(AXIS, None),
        P(),
        P(),
        P(),
        P(AXIS, None),
        P(AXIS, None),
        P(AXIS, None),
        P(AXIS, None),
        P(AXIS, None),
        P(AXIS),
        P(AXIS, None),
        P(AXIS, None),
        P(AXIS, None),
        P(AXIS, None),
    )
    return jax.shard_map(
        body_kernels if mesh.size == 32 else body,
        mesh=mesh,
        in_specs=placed,
        out_specs=(
            P(AXIS, None),
            P(AXIS, None),
            P(AXIS, None),
            P(AXIS, None),
            P(AXIS, None),
            P(AXIS, None),
            P(AXIS, None),
            P(AXIS),
            P(AXIS, None),
            P(AXIS, None),
            P(AXIS, None),
        ),
        check_vma=False,
    )
```

```python
import functools

import jax
import jax.numpy as jnp
from jax import lax
from jax.experimental import pallas as pl
from jax.experimental.pallas import tpu as pltpu
from jax.sharding import PartitionSpec as P

SPAN = 256
AXIS = "fsdp"
TE_DE = "te,de->td"
TD_TE = "td,te->de"
EPSILON = 1e-05
LOGICAL = pl.DeviceIdType.LOGICAL
VMEM_LIMIT = 64000000


class Place:
    def __init__(self):
        me = lax.axis_index(AXIS)
        self.me = me
        self.c = lax.rem(me, 2)
        self.x = lax.rem(me // 2, 2)
        self.y = lax.rem(me // 4, 2)
        self.z = me // 8
        self.inner = (self.z == 1) | (self.z == 2)
        self.even = lax.rem(self.z, 2) == 0
        self.sib = self.z + 1 - 2 * lax.rem(self.z, 2)
        half = self.z // 2
        self.near = 2 - half
        self.far = 3 - 3 * half
        self.cross = 3 - self.z
        self.x1 = 1 - self.x
        self.y1 = 1 - self.y
        self.c1 = 1 - self.c
        self.to = {
            "S": self.dev(self.sib, self.y, self.x, self.c),
            "K": self.dev(self.cross, self.y, self.x, self.c),
            "x": self.dev(self.z, self.y, self.x1, self.c),
            "y": self.dev(self.z, self.y1, self.x, self.c),
            "p": self.dev(self.z, self.y, self.x, self.c1),
        }

    def dev(self, z, y, x, c):
        return ((z * 2 + y) * 2 + x) * 2 + c


def arrived(ref, send, recv, place):
    pltpu.make_async_remote_copy(
        src_ref=ref,
        dst_ref=ref,
        send_sem=send,
        recv_sem=recv,
        device_id=place.to["p"],
        device_id_type=LOGICAL,
    ).wait_recv()


class Gather:
    RECV = ("Cs", "Cn", "Cf", "Xo", "Xs", "Xn", "Xf", "Yo", "Ys", "Yn", "Yf", "D0", "D1", "En", "Ef")
    GROUPS = ("C", "X", "Y", "D")
    NRECV = 19
    NSEND = 25

    def __init__(self, place, own, full, send, recv, index):
        self.p, self.own, self.full = place, own, full
        self.send, self.recv, self.index = send, recv, index
        self.sent = []
        p = place
        self.where = {}
        for g, y, x in (("C", p.y, p.x), ("X", p.y, p.x1), ("Y", p.y1, p.x), ("D", p.y1, p.x1)):
            for k, z in (("o", p.z), ("s", p.sib), ("n", p.near), ("f", p.far)):
                self.where[g + k] = (z, y, x, p.c)
        for a, b in (("D0", "Do"), ("D1", "Ds"), ("En", "Dn"), ("Ef", "Df")):
            self.where[a] = self.where[b]

    def slot(self, name):
        return self.full.at[self.where[name]]

    def copy(self, name, link, landing):
        src = self.own if name == "Co" else self.slot(name)
        k = len(self.sent)
        made = pltpu.make_async_remote_copy(
            src_ref=src,
            dst_ref=self.slot(name),
            send_sem=self.send.at[self.index, k],
            recv_sem=self.recv.at[self.index, self.RECV.index(landing)],
            device_id=self.p.to[link],
            device_id_type=LOGICAL,
        )
        return made

    def go(self, name, link, landing, cond=None):
        made = self.copy(name, link, landing)
        self.sent.append((made, cond))
        if cond is None:
            made.start()
        else:
            pl.when(cond)(made.start)

    def wait(self, name):
        arrived(self.slot(name), self.send.at[self.index, 0], self.recv.at[self.index, self.RECV.index(name)], self.p)

    def group(self, g):
        p = self.p
        y = p.y if g in "CX" else p.y1
        x = p.x if g in "CY" else p.x1
        return y, x

    def pair(self, g):
        y, x = self.group(g)
        ref = self.full.at[:, y, x, self.p.c]
        k = len(self.sent)
        made = pltpu.make_async_remote_copy(
            src_ref=ref,
            dst_ref=ref,
            send_sem=self.send.at[self.index, k],
            recv_sem=self.recv.at[self.index, 15 + self.GROUPS.index(g)],
            device_id=self.p.to["p"],
            device_id_type=LOGICAL,
        )
        self.sent.append((made, None))
        made.start()

    def round(self, r):
        p = self.p
        inner, even = p.inner, p.even
        odd = jnp.logical_not(even)
        if r == 0:
            keep = pltpu.make_async_copy(self.own, self.slot("Co"), self.send.at[self.index, self.NSEND])
            self.keep = keep
            keep.start()
            self.go("Co", "S", "Cs")
            self.go("Co", "K", "Cn", inner)
            self.go("Co", "x", "Xo")
            self.go("Co", "y", "Yo")
        outer = jnp.logical_not(inner)
        if r == 1:
            self.wait("Cs")
            self.go("Cs", "K", "Cf", inner)
            self.go("Cs", "x", "Xs")
            self.go("Cs", "y", "Ys")
            self.wait("Xo")
            self.go("Xo", "y", "D0", even)
            self.wait("Yo")
            self.go("Yo", "x", "D0", odd)
            self.relay("Cn")
        if r == 2:
            pl.when(outer)(lambda: self.wait("Cn"))
            self.go("Cn", "x", "Xn")
            self.go("Cn", "y", "Yn")
            self.wait("Xs")
            self.go("Xs", "y", "D1", odd)
            self.wait("Ys")
            self.go("Ys", "x", "D1", even)
            self.wait("D0")
            self.go("D0", "K", "En", inner)
            self.relay("Cf")
        if r == 3:
            pl.when(outer)(lambda: self.wait("Cf"))
            self.go("Cf", "x", "Xf")
            self.go("Cf", "y", "Yf")
            self.keep.wait()
            self.pair("C")
            self.wait("D1")
            self.go("D1", "K", "Ef", inner)
            self.wait("Xn")
            self.wait("Yn")
            self.relay("En")
        if r == 4:
            pl.when(outer)(lambda: self.wait("En"))
            self.wait("Xf")
            self.pair("X")
            self.wait("Yf")
            self.pair("Y")
            self.relay("Ef")
        if r == 5:
            pl.when(outer)(lambda: self.wait("Ef"))
            self.pair("D")

    def relay(self, name):
        pl.when(self.p.inner)(lambda: self.wait(name))
        self.go(name, "S", name, self.p.inner)

    def pairs(self):
        for g in self.GROUPS:
            y, x = self.group(g)
            ref = self.full.at[:, y, x, self.p.c1]
            arrived(ref, self.send.at[self.index, 0], self.recv.at[self.index, 15 + self.GROUPS.index(g)], self.p)

    def finish(self):
        for made, cond in self.sent:
            if cond is None:
                made.wait_send()
            else:
                pl.when(cond)(made.wait_send)


def add_into(out, parts):
    rows = out.shape[0]
    step = 8 if rows % 16 else 16

    @pl.loop(0, rows // step)
    def _(i):
        at = pl.ds(pl.multiple_of(i * step, step), step)
        total = parts[0][at, :].astype(jnp.float32)
        for part in parts[1:]:
            total = total + part[at, :].astype(jnp.float32)
        out[at, :] = total.astype(out.dtype)


class Scatter:
    NRECV = 20
    NSEND = 22
    SLOTS = ("x0", "x1", "x2", "x3", "Fx", "y0", "y1", "y2", "y3", "Fy", "En", "Ef", "Cn", "Cf", "Co", "De", "Do", "KCs", "KCo")

    def __init__(self, place, part, acc, term, came, out, send, recv, index):
        self.p, self.part, self.acc, self.term, self.came, self.out = place, part, acc, term, came, out
        self.send, self.recv, self.index = send, recv, index
        self.sent = []
        p = place
        half = p.z // 2
        self.ze, self.zo = 2 * half, 2 * half + 1
        self.C = lambda z: (z, p.y, p.x)
        self.X = lambda z: (z, p.y, p.x1)
        self.Y = lambda z: (z, p.y1, p.x)
        self.D = lambda z: (z, p.y1, p.x1)

    def go(self, where, link, slot, cond=None):
        k = len(self.sent)
        at = self.SLOTS.index(slot) if isinstance(slot, str) else slot
        made = pltpu.make_async_remote_copy(
            src_ref=self.acc.at[where],
            dst_ref=self.came.at[at],
            send_sem=self.send.at[self.index, k],
            recv_sem=self.recv.at[self.index, at],
            device_id=self.p.to[link],
            device_id_type=LOGICAL,
        )
        self.sent.append((made, cond))
        if cond is None:
            made.start()
        else:
            pl.when(cond)(made.start)

    def wait(self, slot):
        at = self.SLOTS.index(slot) if isinstance(slot, str) else slot
        arrived(self.came.at[at], self.send.at[self.index, 0], self.recv.at[self.index, at], self.p)
        return self.came.at[at]

    def add(self, where, slots):
        parts = [self.wait(s) for s in slots]
        add_into(self.acc.at[where], [self.acc.at[where]] + parts)

    def round(self, r):
        p = self.p
        inner = p.inner
        outer = jnp.logical_not(inner)
        ze, zo, near, far = self.ze, self.zo, p.near, p.far
        if r == 0:
            if self.term is None:
                self.given = pltpu.make_async_copy(self.part, self.acc, self.send.at[self.index, self.NSEND])
                self.given.start()
                return
            self.given = pltpu.make_async_remote_copy(
                src_ref=self.part,
                dst_ref=self.acc,
                send_sem=self.send.at[self.index, self.NSEND],
                recv_sem=self.recv.at[self.index, 19],
                device_id=p.to["p"],
                device_id_type=LOGICAL,
            )
            self.given.start()
        if r == 1:
            if self.term is None:
                self.given.wait()
            else:
                arrived(self.acc, self.send.at[self.index, 0], self.recv.at[self.index, 19], p)
                self.term.second(self.acc)
            self.go(self.D(far), "S", "Ef", outer)
            self.go(self.D(near), "S", "En", outer)
            self.go(self.X(far), "x", far)
            self.go(self.Y(far), "y", far + 5)
            self.go(self.D(ze), "y", "Fy", outer)
            self.go(self.D(zo), "x", "Fx", outer)
            self.go(self.X(near), "x", near)
            self.go(self.Y(near), "y", near + 5)
            self.go(self.X(zo), "x", zo)
            self.go(self.Y(ze), "y", ze + 5)
        if r == 2:

            @pl.when(inner)
            def _():
                self.add(self.D(far), ["Ef"])
                self.add(self.D(near), ["En"])

            self.go(self.D(far), "K", jnp.where(p.z == 1, self.SLOTS.index("Do"), self.SLOTS.index("De")), inner)
            self.go(self.D(near), "K", jnp.where(p.z == 1, self.SLOTS.index("De"), self.SLOTS.index("Do")), inner)
            parts = [self.wait(far), self.wait(far + 5)]
            add_into(self.acc.at[self.C(far)], [self.acc.at[self.C(far)]] + parts)
            self.go(self.C(far), "S", "Cf", outer)
        if r == 3:

            @pl.when(inner)
            def _():
                self.add(self.D(ze), ["De"])
                self.add(self.D(zo), ["Do"])
                self.add(self.C(far), ["Cf"])

            self.go(self.D(ze), "y", "Fy", inner)
            self.go(self.D(zo), "x", "Fx", inner)
            self.go(self.C(far), "K", "KCs", inner)
            parts = [self.wait(near), self.wait(near + 5)]
            add_into(self.acc.at[self.C(near)], [self.acc.at[self.C(near)]] + parts)
            self.go(self.C(near), "S", "Cn", outer)
        if r == 4:
            self.add(self.X(ze), ["Fy"])
            self.add(self.Y(zo), ["Fx"])
            self.go(self.X(ze), "x", ze)
            self.go(self.Y(zo), "y", zo + 5)

            @pl.when(inner)
            def _():
                self.add(self.C(near), ["Cn"])

            self.go(self.C(near), "K", "KCo", inner)
        if r == 5:
            self.add(self.C(p.sib), [p.sib, p.sib + 5])

            @pl.when(inner)
            def _():
                self.add(self.C(p.sib), ["KCs"])

            self.go(self.C(p.sib), "S", "Co")
        if r == 6:
            slots = [p.z, p.z + 5, "Co"]
            parts = [self.acc.at[self.C(p.z)]] + [self.wait(s) for s in slots]
            add_into(self.out, parts)

            @pl.when(inner)
            def _():
                add_into(self.out, [self.out, self.wait("KCo")])

    def handed(self):
        self.given.wait_send()

    def finish(self):
        for made, cond in self.sent:
            if cond is None:
                made.wait_send()
            else:
                pl.when(cond)(made.wait_send)


def bounds_of(lengths, order):
    total, found = jnp.int32(0), []
    for j in range(lengths.shape[0]):
        total = total + lengths[order[j]]
        found.append(total)
    return found


def segment_at(bounds, places):
    found = jnp.zeros_like(places)
    for bound in bounds:
        found = found + jnp.where(bound <= places, 1, 0)
    return found


def same_segment(bounds, earlier, later):
    same = jnp.int32(0)
    for bound in bounds:
        same = same + jnp.where((bound <= earlier) != (bound <= later), 1, 0)
    return jnp.where((earlier >= 0) & (same == 0), 1.0, 0.0).astype(jnp.float32)


def spans_of(first, bounds, dist, entry, leaving):
    size = dist.shape[0]
    t = lax.broadcasted_iota(jnp.int32, (size, size), 0)
    s = lax.broadcasted_iota(jnp.int32, (size, size), 1)
    same = segment_at(bounds, t + first) == segment_at(bounds, s + first)
    dist[...] = jnp.where(same & (s <= t), t - s, -1).astype(jnp.float32)
    t = lax.broadcasted_iota(jnp.int32, entry.shape, 0)
    here = segment_at(bounds, t + first)
    ahead = segment_at(bounds, jnp.full(entry.shape, first - 1, jnp.int32))
    ahead = jnp.where(jnp.full(entry.shape, first, jnp.int32) == 0, -1, ahead)
    last = segment_at(bounds, jnp.full(entry.shape, first + size - 1, jnp.int32))
    entry[...] = jnp.where(here == ahead, t, -1).astype(jnp.float32)
    leaving[...] = jnp.where(here == last, size - t, -1).astype(jnp.float32)


def decay(distance, rate):
    return jnp.where(distance >= 0, jnp.exp(-rate * distance), 0.0)


def mm(a, b):
    return jnp.dot(a, b, preferred_element_type=jnp.float32)


def mm_nt(a, b):
    return lax.dot_general(a, b, (((1,), (1,)), ((), ())), preferred_element_type=jnp.float32)


def mm_tn(a, b):
    return lax.dot_general(a, b, (((0,), (0,)), ((), ())), preferred_element_type=jnp.float32)


def head_of(h):
    return pl.ds(pl.multiple_of(h * 128, 128), 128)


def norm_scale(values):
    return lax.rsqrt(jnp.mean(values * values, axis=-1, keepdims=True) + EPSILON)


def slope(a):
    sigma = 1.0 / (1.0 + jnp.exp(-a))
    return sigma * (1.0 + a * (1.0 - sigma))


def flat_rows(value):
    return value.astype(jnp.float32).reshape(-1, value.shape[-1]).astype(jnp.bfloat16)


GATHERED = (2, 2, 2, 2)


def gathered(width):
    sizes = [width * part // 8 for part in GATHERED]
    return [(sum(sizes[:i]), size) for i, size in enumerate(sizes)]


SAVED_BACK = 20
FIRST = 1
ORDER = (FIRST, 2, 0)


def parts_of(width, last):
    cuts = (0, width // 2, width - last, width)
    return [(a, b - a) for a, b in zip(cuts, cuts[1:])]


class States:
    def __init__(self, place, bounds, rate, reverse, value, buffers, send, recv):
        self.bounds, self.reverse, self.rate = bounds, reverse, rate
        self.value = value
        self.theirs, self.sums, self.met, self.planes, self.ready, self.entered, self.give, self.out, self.sum = buffers
        self.send, self.recv = send, recv
        self.z, self.c, self.c1 = place.z, place.c, place.c1
        self.me, self.partner = place.me, place.to["p"]
        self.q = lax.rem(place.me // 2, 4)
        self.chip = [self.at(self.z, lax.bitwise_xor(self.q, k)) for k in range(4)]
        self.level = [self.at(lax.rem(self.z + k, 4), self.q) for k in range(4)]
        self.order = range(3, -1, -1) if reverse else range(4)
        lead = 1 if reverse else 0
        self.lead = jnp.where(self.c == lead, 1.0, 0.0).astype(jnp.float32)
        base = self.me - self.c
        self.lead_through = self.through(base + lead, 1)
        self.last_through = self.through(base + 1 - lead, 1)
        mine = rate[4 * self.c + self.q]
        self.chip_step = jnp.exp(jnp.full((1, 128), -2 * SPAN * mine, jnp.float32))
        self.plane_step = jnp.exp(jnp.full((1, 128), -8 * SPAN * mine, jnp.float32))

    def at(self, z, q):
        return (z * 4 + q) * 2 + self.c

    def through(self, device, count):
        return same_segment(self.bounds, device * SPAN - 1, (device + count) * SPAN - 1)

    def step(self, k):
        return jnp.exp(jnp.full((1, 128), -SPAN * self.rate[4 * self.c + k], jnp.float32))

    def copy(self, src, dst, k, peer):
        return pltpu.make_async_remote_copy(
            src_ref=src,
            dst_ref=dst,
            send_sem=self.send.at[k],
            recv_sem=self.recv.at[k],
            device_id=peer,
            device_id_type=LOGICAL,
        )

    def other(self, k):
        return lax.bitwise_xor(self.q, k)

    def begin(self, made):
        for one in made:
            one.start()
        return made

    def terms(self, k):
        mine, theirs = self.value[4 * self.c + k], self.theirs[k]
        rest = 1.0 - self.lead
        return self.lead * mine + rest * theirs, rest * mine + self.lead * theirs

    def spread(self):
        half = self.value.at[pl.ds(4 * self.c1, 4)]
        self.sent = self.begin([self.copy(half, self.theirs, 0, self.partner)])

    def join(self):
        self.copy(self.theirs, self.theirs, 0, self.partner).wait_recv()
        for k in range(4):
            first, last = self.terms(k)
            self.sums[k] = (self.last_through * self.step(k) * first + last).astype(jnp.bfloat16)
        self.sent += self.begin(
            [
                self.copy(self.sums.at[self.other(k)], self.met.at[self.q], k, self.chip[k])
                for k in range(1, 4)
            ]
        )
        self.met[self.q] = self.sums[self.q]

    def total(self):
        for k in range(1, 4):
            self.copy(self.sums.at[0], self.met.at[self.other(k)], k, self.chip[k]).wait_recv()
        total = jnp.zeros(self.met.shape[1:], jnp.float32)
        for i in self.order:
            through = self.through(self.z * 8 + 2 * i, 2)
            total = through * self.chip_step * total + self.met[i].astype(jnp.float32)
        self.planes[self.z] = total.astype(jnp.bfloat16)
        self.second = []
        for k in range(1, 4):
            far = self.z - k if self.reverse else self.z + k
            cond = far >= 0 if self.reverse else far <= 3
            made = self.copy(
                self.planes.at[self.z], self.planes.at[self.z], 3 + k, self.at(far, self.q)
            )
            self.second.append((made, cond))
            pl.when(cond)(made.start)

    def back(self):
        self.sum[...] = jnp.zeros(self.sum.shape, jnp.float32)
        for k in range(3, 0, -1):
            far = self.z + k if self.reverse else self.z - k
            cond = far <= 3 if self.reverse else far >= 0

            @pl.when(cond)
            def _():
                self.copy(
                    self.planes.at[self.z], self.planes.at[far], 3 + k, self.partner
                ).wait_recv()
                kept = self.through(far * 8, 8) * self.plane_step
                self.sum[...] = kept * self.sum[...] + self.planes[far].astype(jnp.float32)

        total = self.sum[...]
        for i in self.order:
            self.ready[i] = total.astype(jnp.bfloat16)
            through = self.through(self.z * 8 + 2 * i, 2)
            total = through * self.chip_step * total + self.met[i].astype(jnp.float32)
        self.sent += self.begin(
            [
                self.copy(self.ready.at[self.other(k)], self.entered.at[self.q], 6 + k, self.chip[k])
                for k in range(1, 4)
            ]
        )
        self.entered[self.q] = self.ready[self.q]

    def part(self):
        for k in range(1, 4):
            self.copy(self.ready.at[0], self.entered.at[self.other(k)], 6 + k, self.chip[k]).wait_recv()
        rest = 1.0 - self.lead
        for k in range(4):
            first, _ = self.terms(k)
            entering = self.entered[k].astype(jnp.float32)
            later = self.lead_through * self.step(k) * entering + first
            self.out[4 * self.c + k] = (self.lead * entering + rest * later).astype(jnp.bfloat16)
            self.give[k] = (self.lead * later + rest * entering).astype(jnp.bfloat16)
        at = pl.ds(4 * self.c, 4)
        self.sent += self.begin([self.copy(self.give, self.out.at[at], 10, self.partner)])

    def done(self):
        at = pl.ds(4 * self.c1, 4)
        self.copy(self.give, self.out.at[at], 10, self.partner).wait_recv()

    def finish(self):
        for one in self.sent:
            one.wait_send()
        for made, cond in self.second:
            pl.when(cond)(made.wait_send)


def state_buffers():
    cube, low = (4, 128, 128), jnp.bfloat16
    return (
        [pltpu.VMEM(cube, jnp.float32)]
        + [pltpu.VMEM(cube, low)] * 6
        + [pltpu.VMEM((8, 128, 128), low), pltpu.VMEM((128, 128), jnp.float32)]
    )


def greeted(place):
    r = lax.rem(place.me, 8)
    peers = [place.z * 8 + lax.bitwise_xor(r, k) for k in range(1, 8)]
    return peers + [lax.rem(place.z + k, 4) * 8 + r for k in range(1, 4)]


def greet(place):
    barrier = pltpu.get_barrier_semaphore()
    for peer in greeted(place):
        pl.semaphore_signal(barrier, inc=1, device_id=peer, device_id_type=LOGICAL)


def met_all(place):
    pl.semaphore_wait(pltpu.get_barrier_semaphore(), len(greeted(place)))


def forward_kernel(lengths, order, rate, gain_own, *refs):
    inputs, refs = refs[:10], refs[10:]
    f32, bf16 = jnp.float32, jnp.bfloat16
    n = 10 + len(GATHERED)
    full, refs = refs[:n], refs[n:]
    saved, refs = refs[:SAVED_BACK], refs[SAVED_BACK:]
    kept, refs = refs[:SAVED_BACK], refs[SAVED_BACK:]
    (hidden_rows, keys, values, queries, key_pre, query_pre, unit_pre, probs) = kept[:8]
    (attended, state_low, mixed_rows, middle, second_rows, left, right, product) = kept[8:16]
    gain, down_terms = kept[16], kept[17:]
    held, refs = refs[:10], refs[10:]
    (s_key, s_value, s_query, s_unit, s_output, tokens, s_left, s_right, s_down, cot) = held
    (in_sem, first_send, first_recv, down_first), refs = refs[:4], refs[4:]
    (hidden, mixed, second, turned, gain_tile) = refs[:5]
    refs = refs[1:]
    place = Place()
    greet(place)
    fetched = [
        pltpu.make_async_copy(src, dst, in_sem.at[i])
        for i, (src, dst) in enumerate(zip(inputs, held))
    ]
    for copy in fetched:
        copy.start()
    (dist, entry, leaving, gains, value) = refs[4:9]
    state_refs, arriving = refs[9:18], refs[16]
    (narrow, wide, send, recv, state_send, state_recv, load_sem, save_sem) = refs[18:]
    half = s_left.shape[1] // 2
    own = [s_key, s_value, s_query, s_unit, gain_tile, s_output]
    own += [s_left.at[:, pl.ds(0, half)], s_left.at[:, pl.ds(half, half)]]
    own += [s_right.at[:, pl.ds(0, half)], s_right.at[:, pl.ds(half, half)]]
    parts = parts_of(s_down.shape[1], 128)
    own += [s_down.at[:, pl.ds(a, size)] for a, size in gathered(s_down.shape[1])]
    lane = lax.broadcasted_iota(jnp.int32, gain_tile.shape, 1)
    line = lax.broadcasted_iota(jnp.int32, gain_tile.shape, 0)
    row = jnp.concatenate([gain_own[...].astype(f32)] * 4, axis=1)
    here = (lane // 32 == lax.rem(place.me, 4)) & (line == place.me // 4)
    gain_tile[...] = jnp.where(here, jnp.broadcast_to(row, gain_tile.shape), 0.0)
    met_all(place)
    made = [Gather(place, own[i], full[i], send, recv, i) for i in range(n)]
    bounds = bounds_of(lengths, order)
    states = States(
        place, bounds, rate, False, value, state_refs, state_send, state_recv
    )
    slots = {0: narrow.at[0], 1: narrow.at[1], 2: narrow.at[0], 3: narrow.at[1], 4: gains}
    slots.update({5: narrow.at[0], 6: wide.at[0], 7: wide.at[1], 8: wide.at[0], 9: wide.at[1]})
    saves = []

    def save(*numbers):
        for i in numbers:
            copy = pltpu.make_async_copy(kept[i], saved[i], save_sem.at[i])
            copy.start()
            saves.append(copy)

    def weight(i):
        ref = slots[i]
        return ref[...].reshape(-1, ref.shape[-1])

    def turn(ref, rows):
        @pl.loop(0, 8)
        def _(i):
            block = ref[:, head_of(i)].astype(f32).T
            rows[i // 2, i % 2] = block.reshape((2, 2) + rows.shape[4:]).astype(bf16)

    def start():
        fetched[5].wait()
        fetched[9].wait()
        x = tokens[...].astype(f32)
        hidden[...] = (x * norm_scale(x)).astype(bf16)
        spans_of(place.me * SPAN, bounds, dist, entry, leaving)
        turn(hidden, hidden_rows)
        save(0)

    def project(i, pre, low):
        out = mm(hidden[...], weight(i))
        if pre is not None:
            pre[...] = out
            out = out / (1.0 + jnp.exp(-out))
        low[...] = out.astype(bf16)

    def key():
        project(0, key_pre, keys)
        save(1, 4)

    def increments():
        project(1, None, values)

        @pl.loop(0, 8)
        def _(h):
            at = head_of(h)
            held = (keys[:, at].astype(f32) * decay(leaving[...], rate[h])).astype(bf16)
            value[h] = mm_tn(held, values[:, at])

        states.spread()
        save(2)

    def query():
        project(2, query_pre, queries)

        @pl.loop(0, 8)
        def _(h):
            at = head_of(h)
            scores = mm_nt(queries[:, at], keys[:, at])
            low = (scores * decay(dist[...], rate[h])).astype(bf16)
            probs[h] = low
            attended[:, at] = mm(low, values[:, at])

        save(3, 5, 7)

    def unit():
        unit_pre[...] = mm(hidden[...], weight(3))
        save(6)

    def attend():
        gain[...] = jnp.sum(gains[...].reshape(-1, 8, 128), axis=0)

        @pl.loop(0, 8)
        def _(h):
            at = head_of(h)
            low = arriving[h].astype(bf16)
            state_low[h] = low
            held = (queries[:, at].astype(f32) * decay(entry[...], rate[h])).astype(bf16)
            out = attended[:, at] + mm(held, low)
            attended[:, at] = out
            mixed[:, at] = (
                out * norm_scale(out) * gain[pl.ds(h, 1), :] * unit_pre[:, at]
            ).astype(bf16)

        turn(mixed, mixed_rows)
        save(8, 9, 10, 16)

    def output():
        out = tokens[...].astype(f32) + mm(mixed[...], weight(5))
        middle[...] = out
        second[...] = (out * norm_scale(out)).astype(bf16)
        turn(second, second_rows)
        save(11, 12)

    def gate(i, side, part):
        side[:, pl.ds(part * half, half)] = mm(second[...], weight(i))

    def multiply(j):
        @pl.loop(0, half // 128)
        def _(i):
            at = pl.ds(pl.multiple_of(j * half + i * 128, 128), 128)
            block = (left[:, at] * right[:, at]).astype(bf16).astype(f32)
            turned[pl.ds(pl.multiple_of(i * 128, 128), 128), :] = block.T

        both = pl.ds(2 * j, 2)
        block = turned[...].reshape((2,) + product.shape[1:])
        product[both] = block.astype(bf16)
        rows = flat_rows(product[both, :, :, place.c1])
        for m, (a, size) in enumerate(parts):
            out = down_first if m == FIRST else down_terms[m]
            term = mm(rows, cot[:, pl.ds(a, size)])
            out[both] = term.reshape((2,) + out.shape[1:]).astype(bf16)
        exchange(j).start()

    def exchange(j):
        both = pl.ds(2 * j, 2)
        return pltpu.make_async_remote_copy(
            src_ref=down_first.at[both],
            dst_ref=down_terms[FIRST].at[both],
            send_sem=first_send.at[j],
            recv_sem=first_recv.at[j],
            device_id=place.to["p"],
            device_id_type=LOGICAL,
        )

    def joined(j):
        exchange(j).wait_recv()
        both, out = pl.ds(2 * j, 2), down_terms[FIRST]
        a, size = parts[FIRST]
        rows = flat_rows(product[both, :, :, place.c])
        term = mm(rows, cot[:, pl.ds(a, size)]).reshape((2,) + out.shape[1:])
        out[both] = (out[both].astype(f32) + term).astype(bf16)

    tasks = {2: [start], 7: [key], 8: [increments], 8.5: [states.join], 9: [query], 9.5: [states.total]}
    tasks.update({10: [unit], 10.5: [states.back], 11.5: [states.part], 12: [states.done, attend]})
    tasks[12.5] = [output]
    tasks[13] = [lambda: gate(6, left, 0)]
    tasks[14] = [lambda: gate(7, left, 1), lambda: save(13)]
    tasks[15] = [lambda: gate(8, right, 0), lambda: multiply(0)]
    tasks[16] = [lambda: gate(9, right, 1), lambda: multiply(1), lambda: save(19, 17, 15, 14)]
    tasks[16] += [lambda: joined(0)]
    tasks[18] = [lambda: joined(1), lambda: save(18)]
    needs = {0: 0, 1: 1, 2: 2, 3: 3, 5: 4, 6: 6, 8: 7, 10: 8}
    loads = {}
    for step in range(n + 6):
        i = step - 6
        for r in range(6):
            if r == 0:
                for k in range(3) if step == 0 else [step + 2]:
                    if k in needs:
                        fetched[needs[k]].wait()
                    if k < n:
                        made[k].round(0)
            elif 0 <= step - r < n:
                made[step - r].round(r)
            if r == 0:
                if i - 1 in loads:
                    loads[i - 1].wait()
                for task in tasks.get(step, []):
                    task()
            if r == 3:
                for task in tasks.get(step + 0.5, []):
                    task()
        if 0 <= i < n:
            made[i].pairs()
        if i in slots:
            loads[i] = pltpu.make_async_copy(full[i], slots[i], load_sem.at[i])
            loads[i].start()
    for one in made:
        one.finish()
    states.finish()
    for j in range(2):
        exchange(j).wait_send()
    for copy in saves:
        copy.wait()


def forward(lengths, order, rate, tokens, cot, gain, shards):
    f32, bf16 = jnp.float32, jnp.bfloat16
    size, width = tokens.shape
    wide = shards[5].shape[1]
    half = wide // 2
    blocks = [(s.shape, s.dtype) for s in shards[:4]] + [((8, 128), f32)]
    blocks += [(shards[4].shape, bf16)] + [((32, half), bf16)] * 4
    parts = parts_of(width, 128)
    blocks += [((shards[7].shape[0], p), bf16) for _, p in gathered(width)]
    square, cube = (size, width), (8, 128, 128)
    rows, down_rows = shards[4].shape[0], shards[7].shape[0]
    across = ((4, 2, 2, 2, rows, size), bf16)
    kept = [across] + [(square, bf16)] * 3 + [(square, f32)] * 3 + [((8, size, size), bf16)]
    kept += [(square, f32), (cube, bf16), across, (square, f32), across]
    kept += [((size, wide), f32)] * 2 + [((4, 2, 2, 2, down_rows, size), bf16), ((8, 128), f32)]
    kept += [((4, 2, 2, down_rows, p), bf16) for _, p in parts]
    vmem, hbm = pl.BlockSpec(memory_space=pltpu.VMEM), pl.BlockSpec(memory_space=pltpu.HBM)
    smem = pl.BlockSpec(memory_space=pltpu.SMEM)
    n = len(blocks)
    inputs = [*shards[:5], tokens, *shards[5:], cot]
    out = pl.pallas_call(
        forward_kernel,
        out_shape=[jax.ShapeDtypeStruct((4, 2, 2, 2) + s, t) for s, t in blocks]
        + [jax.ShapeDtypeStruct(s, t) for s, t in kept],
        in_specs=[smem] * 3 + [vmem] + [hbm] * 10,
        out_specs=[hbm] * (n + len(kept)),
        scratch_shapes=[pltpu.VMEM(s, t) for s, t in kept]
        + [pltpu.VMEM(s.shape, s.dtype) for s in inputs]
        + [pltpu.SemaphoreType.DMA((10,))]
        + [pltpu.SemaphoreType.DMA((2,))] * 2
        + [pltpu.VMEM((4, 2, 2, down_rows, parts[FIRST][1]), bf16)]
        + [pltpu.VMEM(square, bf16)] * 3
        + [pltpu.VMEM((half, size), f32), pltpu.VMEM((8, 128), f32)]
        + [pltpu.VMEM((size, size), f32), pltpu.VMEM((size, 128), f32), pltpu.VMEM((size, 128), f32)]
        + [pltpu.VMEM((4, 2, 2, 2, 8, 128), f32)]
        + [pltpu.VMEM(cube, f32)]
        + state_buffers()
        + [
            pltpu.VMEM((2, 4, 2, 2, 2, 32, width), bf16),
            pltpu.VMEM((2, 4, 2, 2, 2, 32, half), bf16),
            pltpu.SemaphoreType.DMA((n, Gather.NSEND + 1)),
            pltpu.SemaphoreType.DMA((n, Gather.NRECV)),
            pltpu.SemaphoreType.DMA((18,)),
            pltpu.SemaphoreType.DMA((18,)),
            pltpu.SemaphoreType.DMA((n,)),
            pltpu.SemaphoreType.DMA((len(kept),)),
        ],
        compiler_params=pltpu.CompilerParams(
            collective_id=0, has_side_effects=True, vmem_limit_bytes=VMEM_LIMIT
        ),
        name="forward",
    )(lengths, order, rate, gain, *inputs)
    return out[:n], out[n:]

def backward_kernel(lengths, order, rate, h_tokens, h_cot, *refs):
    f32, bf16 = jnp.float32, jnp.bfloat16
    n = 14
    saved, refs = refs[:SAVED_BACK], refs[SAVED_BACK:]
    (h_hidden, h_keys, h_values, h_queries, h_key_pre, h_query_pre, h_unit_pre, h_probs) = saved[:8]
    (h_attended, h_state_low, h_mixed, h_middle, h_second, h_left, h_right, h_product) = saved[8:16]
    h_gain, h_down = saved[16], saved[17:]
    w_in, refs = refs[: 9 + len(GATHERED)], refs[9 + len(GATHERED) :]
    (w_key, w_value, w_query, w_unit, w_output, w_l0, w_l1, w_r0, w_r1) = w_in[:9]
    w_down = w_in[9:]
    sums, result_out, tokens_out, refs = refs[:n], refs[n], refs[n + 1], refs[n + 2 :]
    out, tokens, cot, refs = refs[:n], refs[n], refs[n + 1], refs[n + 2 :]
    acc, came, refs = refs[:n], refs[n : 2 * n], refs[2 * n :]
    (part, gain_part, wd, down, wl, left, right, f1, f2, f3, f4) = refs[:11]
    (branch, ga, gup, gkp, gvp, result, glp, grp, rows, mixed, product) = refs[11:22]
    (probs, state_low, gain, gg, dist, entry, leaving) = refs[22:29]
    value, state_refs, arriving = refs[29], refs[30:39], refs[37]
    (send, recv, state_send, state_recv, load_sem, out_sem) = refs[39:]
    place = Place()
    half = h_left.shape[1] // 2
    width = tokens.shape[1]
    left_w, right_w = left.at[:, pl.ds(0, width)], right.at[:, pl.ds(0, width)]
    queries, keys = glp.at[:, pl.ds(0, width)], glp.at[:, pl.ds(width, width)]
    values, gqp = grp.at[:, pl.ds(0, width)], grp.at[:, pl.ds(width, width)]
    wn = wl.at[:, :, :, :, :, pl.ds(0, width)]
    greet(place)
    bounds = bounds_of(lengths, order)
    states = States(
        place, bounds, rate, True, value, state_refs, state_send, state_recv
    )
    loads = {}

    def load(name, src, dst):
        copy = pltpu.make_async_copy(src, dst, load_sem.at[len(loads)])
        loads[name] = copy
        copy.start()

    def load_down(i):
        for m, (a, size) in enumerate(gathered(width)):
            dst = wd.at[:, :, :, :, :, pl.ds(a, size)]
            load("down%d%d" % (i, m), w_down[m].at[pl.ds(2 * i, 2)], dst)

    def loaded(*names):
        for name in names:
            loads[name].wait()

    def weight(cols):
        return wl[:, :, :, :, :, pl.ds(0, cols)].reshape(-1, cols)

    def side(i):
        return pl.ds(i * half, half)

    def product_of(i):
        return flat_rows(product[pl.ds(2 * i, 2)])

    class Piece:
        def __init__(self, rows, core_rows, grad, cols, need=()):
            self.rows, self.core_rows, self.grad, self.cols, self.need = rows, core_rows, grad, cols, need

        def term(self, zh, core):
            lhs = self.rows[pl.ds(zh * 2, 2), :, :, core]
            lhs = flat_rows(lhs) if self.core_rows % 16 else lhs.reshape(-1, lhs.shape[-1])
            out = mm(lhs, self.grad[...])
            return out.reshape(2, 2, 2, self.core_rows, self.cols)

        def first(self):
            @pl.loop(0, 2)
            def _(zh):
                part[pl.ds(zh * 2, 2), :, :, :, pl.ds(0, self.cols)] = self.term(
                    zh, place.c1
                ).astype(bf16)

        def second(self, acc):
            @pl.loop(0, 2)
            def _(zh):
                at = pl.ds(zh * 2, 2)
                acc[at] = (acc[at].astype(f32) + self.term(zh, place.c)).astype(bf16)

    class Gain:
        def first(self):
            gain_part[...] = jnp.broadcast_to(gg[...][None, None, None], gain_part.shape)

        def second(self, acc):
            acc[...] = acc[...] + gg[...][None, None, None]

    wide = part.at[:, :, :, :, pl.ds(0, half)]
    narrow = part.at[:, :, :, :, pl.ds(0, width)]
    parts = parts_of(width, 128)
    pieces = []
    for m in ORDER:
        a, size = parts[m]
        piece = None if m == FIRST else Piece(product, 88, cot.at[:, pl.ds(a, size)], size)
        pieces.append((h_down[m], piece))
    pieces += [(wide, Piece(rows, 32, glp.at[:, side(i)], half)) for i in (0, 1)]
    pieces += [(wide, Piece(rows, 32, grp.at[:, side(i)], half)) for i in (0, 1)]
    pieces += [(narrow, Piece(mixed, 32, branch, width)), (gain_part, Gain())]
    pieces += [(narrow, Piece(rows, 32, g, width)) for g in (gup, gqp, gvp)]
    last = width // 4
    for a, size in ((0, width - last), (width - last, last)):
        view = part.at[:, :, :, :, pl.ds(0, size)]
        pieces.append((view, Piece(rows, 32, gkp.at[:, pl.ds(a, size)], size)))
    made = [
        Scatter(place, pieces[i][0], acc[i], pieces[i][1], came[i], out[i], send, recv, i)
        for i in range(n)
    ]

    def begin():
        spans_of(place.me * SPAN, bounds, dist, entry, leaving)

    def gates(i):
        loaded(*["down%d%d" % (i, m) for m in range(len(GATHERED))])
        loaded("left%d" % i, "right%d" % i)
        pair = 2 * wd.shape[4]

        @pl.loop(0, 8)
        def _(k):
            at = pl.ds(pl.multiple_of(k * pair, 16), pair)
            down[at, :] = flat_rows(wd[k // 4, (k // 2) % 2, k % 2])

        grad = mm_nt(cot[...], down[...])
        glp[:, side(i)] = (grad * right[...]).astype(bf16)
        grp[:, side(i)] = (grad * left[...]).astype(bf16)
        if i == 0:
            loaded("middle")
            f3[...] = f2[...] + mm_tn(product_of(0), down[...])
            load_down(1)
            load("left1", h_left.at[:, side(1)], left)
            load("right1", h_right.at[:, side(1)], right)
        else:
            result[...] = (f3[...] + mm_tn(product_of(1), down[...])).astype(bf16)
            load("unit_pre", h_unit_pre, left_w)
            load("result", result, result_out)

    def second_part(name, grad, i, following, start):
        loaded(name)
        term = mm_nt(grad[:, side(i)], weight(half))
        f1[...] = term if start else f1[...] + term
        load(*following)

    def middle():
        @pl.loop(0, SPAN // 16)
        def _(i):
            at = pl.ds(pl.multiple_of(i * 16, 16), 16)
            x, g = f2[at, :], f1[at, :]
            scale = norm_scale(x)
            unit = x * scale
            grad = cot[at, :].astype(f32) + scale * (
                g - unit * jnp.mean(g * unit, axis=-1, keepdims=True)
            )
            f3[at, :] = grad
            branch[at, :] = grad.astype(bf16)

        load("attended", h_attended, f2)

    def spare():
        load("queries", h_queries, queries)
        load("keys", h_keys, keys)
        load("values", h_values, values)
        load("hidden", h_hidden, rows)

    def attention():
        loaded("output")
        f1[...] = mm_nt(branch[...], weight(width))
        load("unit", w_unit, wn)
        loaded("attended", "unit_pre", "queries", "gain")

        @pl.loop(0, 8)
        def _(h):
            at = head_of(h)
            att, up, gm = f2[:, at], left_w[:, at], f1[:, at]
            scale = norm_scale(att)
            unit = att * scale
            row = gain[pl.ds(h, 1), :]
            gated = gm * up
            gg[pl.ds(h, 1), :] = jnp.sum(gated * unit, axis=0, keepdims=True)
            gup[:, at] = (gm * unit * row).astype(bf16)
            g = gated * row
            low = (
                scale * (g - unit * jnp.mean(g * unit, axis=-1, keepdims=True))
            ).astype(bf16)
            ga[:, at] = low
            held = (queries[:, at].astype(f32) * decay(entry[...], rate[h])).astype(bf16)
            value[h] = mm_tn(held, low)

        states.spread()
        load("key_pre", h_key_pre, f2)

    def scores():
        loaded("keys", "values", "query_pre", "probs", "state_low")

        @pl.loop(0, 8)
        def _(h):
            at = head_of(h)
            low = ga[:, at]
            grads = (mm_nt(low, values[:, at]) * decay(dist[...], rate[h])).astype(bf16)
            grad_q = mm(grads, keys[:, at])
            grad_q = grad_q + mm_nt(low, state_low[h]) * decay(entry[...], rate[h])
            gqp[:, at] = (grad_q * slope(f4[:, at])).astype(bf16)
            f1[:, at] = mm_tn(grads, queries[:, at])
            right_w[:, at] = mm_tn(probs[h], low)

    def hidden_part(name, grad, following, start):
        loaded(name)
        term = mm_nt(grad[...], weight(width))
        f4[...] = term if start else f4[...] + term
        if following:
            load(*following)

    def unit_rest():
        hidden_part("unit", gup, ("query", w_query, wn), True)

    def last_grads():
        hidden_part("query", gqp, ("value", w_value, wn), False)
        states.done()
        loaded("key_pre")

        @pl.loop(0, 8)
        def _(h):
            at = head_of(h)
            grad = arriving[h].astype(bf16)
            fall = decay(leaving[...], rate[h])
            held = (keys[:, at].astype(f32) * fall).astype(bf16)
            grad_k = f1[:, at] + mm_nt(values[:, at], grad) * fall
            gkp[:, at] = (grad_k * slope(f2[:, at])).astype(bf16)
            gvp[:, at] = (right_w[:, at] + mm(held, grad)).astype(bf16)

    def value_rest():
        hidden_part("value", gvp, ("key", w_key, wn), False)

    def inputs():
        hidden_part("key", gkp, None, False)
        loaded("input")

        @pl.loop(0, SPAN // 16)
        def _(i):
            at = pl.ds(pl.multiple_of(i * 16, 16), 16)
            x, g = tokens[at, :].astype(f32), f4[at, :]
            scale = norm_scale(x)
            unit = x * scale
            f3[at, :] = f3[at, :] + scale * (g - unit * jnp.mean(g * unit, axis=-1, keepdims=True))

        load("tokens", f3, tokens_out)

    before = {2: lambda: loaded("product", "cot"), 3: lambda: loaded("second"), 7: lambda: loaded("mixed")}
    before[9] = lambda: loaded("hidden")
    tasks = {0: [lambda: rest()], 2: [lambda: gates(0)], 3: [lambda: gates(1)]}
    tasks[4] = [lambda: second_part("l0", glp, 0, ("l1", w_l1, wl), True)]
    tasks[5] = [lambda: second_part("l1", glp, 1, ("r0", w_r0, wl), False)]
    tasks[6] = [
        lambda: second_part("r0", grp, 0, ("r1", w_r1, wl), False),
        lambda: second_part("r1", grp, 1, ("output", w_output, wn), False),
        middle,
    ]
    tasks[7] = [spare, attention]
    tasks[7.5] = [states.join]
    tasks[8] = [scores]
    tasks[8.5] = [states.total]
    tasks[9] = [unit_rest, states.back]
    tasks[9.5] = [states.part]
    tasks[10] = [last_grads]
    tasks[11] = [value_rest]
    tasks[12] = [inputs]
    made[0].round(0)
    load("product", h_product, product)
    load("cot", h_cot, cot)
    load_down(0)
    load("left0", h_left.at[:, side(0)], left)
    load("right0", h_right.at[:, side(0)], right)
    met_all(place)
    made[1].round(0)
    made[2].round(0)
    made[0].round(1)

    def rest():
        load("middle", h_middle, f2)
        load("second", h_second, rows)
        load("l0", w_l0, wl)
        load("mixed", h_mixed, mixed)
        load("gain", h_gain, gain)
        load("query_pre", h_query_pre, f4)
        load("probs", h_probs, probs)
        load("state_low", h_state_low, state_low)
        load("input", h_tokens, tokens)
        begin()

    def given(i):
        return pltpu.make_async_copy(out[i], sums[i], out_sem.at[i])

    for step in range(n + 6):
        if step in before:
            before[step]()
        if 2 < step < n:
            if step > 3:
                made[step - 1].handed()
            pieces[step][1].first()
            made[step].round(0)
        if 1 < step <= n:
            made[step - 1].round(1)
        for task in tasks.get(step, []):
            task()
        for r in range(2, 7):
            if 0 <= step - r < n:
                made[step - r].round(r)
                if r == 6:
                    given(step - r).start()
            if r == 4:
                for task in tasks.get(step + 0.5, []):
                    task()
    for i, one in enumerate(made):
        if i in (1, 2, n - 1):
            one.handed()
        given(i).wait()
        one.finish()
    states.finish()
    loaded("result", "tokens")


def backward(lengths, order, rate, tokens, cot, saved, weights):
    f32, bf16 = jnp.float32, jnp.bfloat16
    size, width = tokens.shape
    wide = saved[13].shape[1]
    half = wide // 2
    rows = width // 32
    down_rows = wide // 32
    parts, last = parts_of(width, 128), width // 4
    blocks = [((down_rows, parts[m][1]), bf16) for m in ORDER] + [((rows, half), bf16)] * 4
    blocks += [((rows, width), bf16), ((8, 128), f32)] + [((rows, width), bf16)] * 3
    blocks += [((rows, width - last), bf16), ((rows, last), bf16)]
    n = len(blocks)
    square, cube = (size, width), (8, 128, 128)
    hbm = pl.BlockSpec(memory_space=pltpu.HBM)
    smem = pl.BlockSpec(memory_space=pltpu.SMEM)
    out = pl.pallas_call(
        backward_kernel,
        out_shape=[jax.ShapeDtypeStruct(b, f32) for b, _ in blocks]
        + [jax.ShapeDtypeStruct(square, bf16), jax.ShapeDtypeStruct(square, f32)],
        in_specs=[smem] * 3 + [hbm] * (2 + len(saved) + len(weights)),
        out_specs=[hbm] * (n + 2),
        scratch_shapes=[pltpu.VMEM(b, f32) for b, _ in blocks]
        + [pltpu.VMEM(square, bf16)] * 2
        + [pltpu.VMEM((4, 2, 2) + b, t) for b, t in blocks]
        + [pltpu.VMEM((19,) + b, t) for b, t in blocks]
        + [
            pltpu.VMEM((4, 2, 2, rows, half), bf16),
            pltpu.VMEM((4, 2, 2, 8, 128), f32),
            pltpu.VMEM((2, 2, 2, 2, down_rows, width), bf16),
            pltpu.VMEM((half, width), bf16),
            pltpu.VMEM((4, 2, 2, 2, rows, half), bf16),
            pltpu.VMEM((size, half), f32),
            pltpu.VMEM((size, half), f32),
        ]
        + [pltpu.VMEM(square, f32)] * 4
        + [pltpu.VMEM(square, bf16)] * 6
        + [pltpu.VMEM((size, wide), bf16)] * 2
        + [pltpu.VMEM((4, 2, 2, 2, rows, size), bf16)] * 2
        + [pltpu.VMEM((4, 2, 2, 2, down_rows, size), bf16)]
        + [pltpu.VMEM((8, size, size), bf16), pltpu.VMEM(cube, bf16)]
        + [pltpu.VMEM((8, 128), f32)] * 2
        + [pltpu.VMEM((size, size), f32), pltpu.VMEM((size, 128), f32), pltpu.VMEM((size, 128), f32)]
        + [pltpu.VMEM(cube, f32)]
        + state_buffers()
        + [
            pltpu.SemaphoreType.DMA((n, Scatter.NSEND + 1)),
            pltpu.SemaphoreType.DMA((n, Scatter.NRECV)),
            pltpu.SemaphoreType.DMA((18,)),
            pltpu.SemaphoreType.DMA((18,)),
            pltpu.SemaphoreType.DMA((60,)),
            pltpu.SemaphoreType.DMA((n,)),
        ],
        compiler_params=pltpu.CompilerParams(
            collective_id=3, has_side_effects=True, vmem_limit_bytes=67000000
        ),
        name="backward",
    )(lengths, order, rate, tokens, cot, *saved, *weights)
    return out[:n], out[n], out[n + 1]


RESULTS = ((10,), (12, 13), (11,), (9,), (7,), (8,), (3, 4), (5, 6), (2, 0, 1))


def deliver_kernel(*refs):
    given, out, held, gain, own = refs[:16], refs[16:27], refs[27:38], refs[38], refs[39]
    in_sem, out_sem = refs[40:]
    sources = [(0,), (1,)] + [tuple(k + 2 for k in found) for found in RESULTS]
    copies = []
    for dst, found in zip(held, sources):
        at, mine = 0, []
        for k in found:
            size = given[k].shape[1]
            place = gain if k == 10 else dst.at[:, pl.ds(at, size)]
            mine.append(pltpu.make_async_copy(given[k], place, in_sem.at[k]))
            at += size
        for copy in mine:
            copy.start()
        copies.append(mine)
    made = []
    for i, mine in enumerate(copies):
        for copy in mine:
            copy.wait()
        src = held[i]
        if i == 7:
            me = lax.axis_index(AXIS)
            row = gain[pl.ds(me // 4, 1), :]
            found = jnp.zeros((1, 32), jnp.float32)
            for k in range(4):
                found = found + jnp.where(lax.rem(me, 4) == k, 1.0, 0.0) * row[:, 32 * k : 32 * k + 32]
            own[...] = found
            src = own
        copy = pltpu.make_async_copy(src, out[i], out_sem.at[i])
        copy.start()
        made.append(copy)
    for copy in made:
        copy.wait()


def deliver(result, inputs, grads):
    f32 = jnp.float32
    shapes = [(grads[k[0]].shape[0], sum(grads[i].shape[1] for i in k)) for k in RESULTS]
    shapes[5] = (1, 32)
    shapes = [(result.shape, result.dtype), (inputs.shape, f32)] + [(s, f32) for s in shapes]
    hbm = pl.BlockSpec(memory_space=pltpu.HBM)
    out = pl.pallas_call(
        deliver_kernel,
        out_shape=[jax.ShapeDtypeStruct(s, t) for s, t in shapes],
        in_specs=[hbm] * 16,
        out_specs=[hbm] * 11,
        scratch_shapes=[pltpu.VMEM(s, t) for s, t in shapes]
        + [
            pltpu.VMEM((8, 128), f32),
            pltpu.VMEM((1, 32), f32),
            pltpu.SemaphoreType.DMA((16,)),
            pltpu.SemaphoreType.DMA((11,)),
        ],
        name="deliver",
    )(result, inputs, *grads)
    return (*out[:7], out[7].reshape(-1), *out[8:])


def entering(value, axis, combine, identity, reverse):
    length, here = (lax.axis_size(axis), lax.axis_index(axis))
    everything = jax.tree.map(lambda part: lax.all_gather(part, axis), value)
    start = jax.tree.map(
        lambda part, zero: jnp.broadcast_to(jnp.asarray(zero, part.dtype), part.shape),
        value,
        identity,
    )

    def hop(k, before):
        at = length - 1 - k if reverse else k
        reached = at > here if reverse else at < here
        new = combine(before, jax.tree.map(lambda part: part[at], everything))
        return jax.tree.map(lambda a, b: jnp.where(reached, a, b), new, before)

    return lax.fori_loop(0, length, hop, start)


def segment_of(places, lengths, seq_order):
    number = lengths.shape[0]
    picked = seq_order[:, None] == jnp.arange(number, dtype=jnp.int32)[None, :]
    packed = jnp.sum(jnp.where(picked, lengths[None, :], 0), axis=1, dtype=jnp.int32)
    bounds = jnp.cumsum(packed, dtype=jnp.int32)
    found = jnp.sum((bounds[None, :] <= places[:, None]).astype(jnp.int32), axis=1, dtype=jnp.int32)
    return jnp.where(places < 0, -1, found)


def decay_tables(segments, before, rate, block):
    length = segments.shape[0]
    count = length // block
    spans = segments.reshape(count, block)
    priors = jnp.concatenate([before.reshape(1), spans[:-1, -1]])
    steps = jnp.arange(block, dtype=jnp.int32)
    distance = steps[:, None] - steps[None, :]
    same = (spans[:, :, None] == spans[:, None, :]) & (distance >= 0)[None]
    powers = jnp.exp(-rate[:, None, None] * jnp.maximum(distance, 0).astype(jnp.float32)[None])
    within = jnp.where(same[:, None], powers[None], 0.0)
    entry = jnp.where(
        (spans == priors[:, None])[:, :, None],
        jnp.exp(-rate[None, :] * steps.astype(jnp.float32)[:, None])[None],
        0.0,
    )
    leaving = jnp.where(
        (spans == spans[:, -1:])[:, :, None],
        jnp.exp(-rate[None, :] * (block - steps).astype(jnp.float32)[:, None])[None],
        0.0,
    )
    passing = jnp.where((spans[:, -1] == priors)[:, None], jnp.exp(-rate * block)[None], 0.0)
    offsets = (jnp.arange(count, dtype=jnp.int32) * block).astype(jnp.float32)
    arrival = jnp.where(
        (priors == before)[:, None], jnp.exp(-rate[None, :] * offsets[:, None]), 0.0
    )
    through = jnp.where(segments[-1] == before, jnp.exp(-rate * length), 0.0)
    return (within, entry, leaving, passing, arrival, through)


def chain_states(earlier, later):
    return (earlier[0] * later[0], later[0][:, None, None] * earlier[1] + later[1])


def silu_slope(values):
    sigma = jax.nn.sigmoid(values)
    return sigma * (1.0 + values * (1.0 - sigma))


def row_scale(values):
    return lax.rsqrt(jnp.mean(values * values, axis=-1, keepdims=True) + EPSILON)


def body(
    tokens,
    lengths,
    seq_order,
    decay_rate,
    w_query,
    w_key,
    w_value,
    w_unit,
    w_output,
    norm_gain,
    w_left,
    w_right,
    w_down,
    cotangent,
):
    f32 = jnp.float32
    bf16 = jnp.bfloat16
    length, width = tokens.shape
    heads = decay_rate.shape[0]
    head_size = width // heads
    count = length // SPAN
    first = lax.axis_index(AXIS) * length
    places = first + jnp.arange(length, dtype=jnp.int32)
    segments = segment_of(places, lengths, seq_order)
    before = segment_of(jnp.reshape(first - 1, (1,)), lengths, seq_order)[0]
    within, entry, leaving, passing, arrival, through = decay_tables(
        segments, before, decay_rate, SPAN
    )
    attention_set = (
        lax.all_gather(w_query, AXIS, axis=0, tiled=True),
        lax.all_gather(w_key, AXIS, axis=0, tiled=True),
        lax.all_gather(w_value, AXIS, axis=0, tiled=True),
        lax.all_gather(w_unit, AXIS, axis=0, tiled=True),
        lax.all_gather(w_output, AXIS, axis=0, tiled=True),
        lax.all_gather(norm_gain, AXIS, axis=0, tiled=True),
    )
    feed_set = (
        lax.all_gather(w_left, AXIS, axis=0, tiled=True),
        lax.all_gather(w_right, AXIS, axis=0, tiled=True),
        lax.all_gather(w_down, AXIS, axis=0, tiled=True),
    )
    full_query, full_key, full_value, full_unit, full_output, full_gain = attention_set
    full_left, full_right, full_down = feed_set
    inputs = tokens.astype(f32)
    first_scale = row_scale(inputs)
    normed = inputs * first_scale
    hidden = normed.astype(bf16)
    query_pre = jnp.dot(hidden, full_query, preferred_element_type=f32)
    key_pre = jnp.dot(hidden, full_key, preferred_element_type=f32)
    value_pre = jnp.dot(hidden, full_value, preferred_element_type=f32)
    unit_pre = jnp.dot(hidden, full_unit, preferred_element_type=f32)
    block_shape = (count, SPAN, heads, head_size)
    query_blocks = jax.nn.silu(query_pre).astype(bf16).reshape(block_shape)
    key_blocks = jax.nn.silu(key_pre).astype(bf16).reshape(block_shape)
    value_blocks = value_pre.astype(bf16).reshape(block_shape)
    scores = jnp.einsum("nthe,nshe->nhts", query_blocks, key_blocks, preferred_element_type=f32)
    mixing = (scores * within).astype(bf16)
    local_out = jnp.einsum("nhts,nshe->nthe", mixing, value_blocks, preferred_element_type=f32)
    keys_held = (key_blocks * leaving[..., None]).astype(bf16)
    increments = jnp.einsum("nshe,nshf->nhef", keys_held, value_blocks, preferred_element_type=f32)
    local_states = [jnp.zeros((heads, head_size, head_size), f32)]
    local_states.append(passing[0][:, None, None] * local_states[-1] + increments[0])
    end_state = local_states[count]
    start_pair = (jnp.ones_like(through), jnp.zeros_like(end_state))
    arriving = entering((through, end_state), AXIS, chain_states, start_pair, False)[1]
    states = jnp.stack(local_states[:count]) + arrival[:, :, None, None] * arriving[None]
    state_low = states.astype(bf16)
    query_held = (query_blocks * entry[..., None]).astype(bf16)
    attended = local_out + jnp.einsum(
        "nthe,nhef->nthf", query_held, state_low, preferred_element_type=f32
    )
    attended_heads = attended.reshape(length, heads, head_size)
    head_scale = row_scale(attended_heads)
    unit_norm = (attended_heads * head_scale).reshape(length, width)
    gain = full_gain.astype(f32)
    gated = unit_norm * gain
    mixed_in = (gated * unit_pre).astype(bf16)
    middle = inputs + jnp.dot(mixed_in, full_output, preferred_element_type=f32)
    second_scale = row_scale(middle)
    second_unit = middle * second_scale
    second = second_unit.astype(bf16)
    left_pre = jnp.dot(second, full_left, preferred_element_type=f32)
    right_pre = jnp.dot(second, full_right, preferred_element_type=f32)
    product = (left_pre * right_pre).astype(bf16)
    result = (middle + jnp.dot(product, full_down, preferred_element_type=f32)).astype(bf16)
    back_feed = (
        lax.all_gather(w_left, AXIS, axis=0, tiled=True),
        lax.all_gather(w_right, AXIS, axis=0, tiled=True),
        lax.all_gather(w_down, AXIS, axis=0, tiled=True),
    )
    back_left, back_right, back_down = back_feed
    grad_product = jnp.einsum("td,fd->tf", cotangent, back_down, preferred_element_type=f32)
    grad_left_pre = (grad_product * right_pre).astype(bf16)
    grad_right_pre = (grad_product * left_pre).astype(bf16)
    grad_w_down = jnp.einsum("tf,td->fd", product, cotangent, preferred_element_type=f32)
    grad_w_left = jnp.einsum("td,tf->df", second, grad_left_pre, preferred_element_type=f32)
    grad_w_right = jnp.einsum("td,tf->df", second, grad_right_pre, preferred_element_type=f32)
    feed_grads = (
        lax.psum_scatter(grad_w_left, AXIS, scatter_dimension=0, tiled=True),
        lax.psum_scatter(grad_w_right, AXIS, scatter_dimension=0, tiled=True),
        lax.psum_scatter(grad_w_down, AXIS, scatter_dimension=0, tiled=True),
    )
    grad_second = jnp.einsum(
        "tf,df->td", grad_left_pre, back_left, preferred_element_type=f32
    ) + jnp.einsum("tf,df->td", grad_right_pre, back_right, preferred_element_type=f32)
    grad_middle = cotangent.astype(f32) + second_scale * (
        grad_second - second_unit * jnp.mean(grad_second * second_unit, axis=-1, keepdims=True)
    )
    back_attention = (
        lax.all_gather(w_query, AXIS, axis=0, tiled=True),
        lax.all_gather(w_key, AXIS, axis=0, tiled=True),
        lax.all_gather(w_value, AXIS, axis=0, tiled=True),
        lax.all_gather(w_unit, AXIS, axis=0, tiled=True),
        lax.all_gather(w_output, AXIS, axis=0, tiled=True),
        lax.all_gather(norm_gain, AXIS, axis=0, tiled=True),
    )
    back_query, back_key, back_value, back_unit, back_output, back_gain = back_attention
    grad_branch = grad_middle.astype(bf16)
    grad_w_output = jnp.einsum(TD_TE, mixed_in, grad_branch, preferred_element_type=f32)
    grad_mixed = jnp.einsum(TE_DE, grad_branch, back_output, preferred_element_type=f32)
    grad_gated = grad_mixed * unit_pre
    grad_unit_pre = (grad_mixed * gated).astype(bf16)
    grad_gain = jnp.sum(grad_gated * unit_norm, axis=0)
    grad_norm_heads = (grad_gated * back_gain.astype(f32)).reshape(length, heads, head_size)
    norm_heads = unit_norm.reshape(length, heads, head_size)
    grad_att = head_scale * (
        grad_norm_heads
        - norm_heads * jnp.mean(grad_norm_heads * norm_heads, axis=-1, keepdims=True)
    )
    grad_att_blocks = grad_att.astype(bf16).reshape(block_shape)
    grad_mixing = jnp.einsum(
        "nthf,nshf->nhts", grad_att_blocks, value_blocks, preferred_element_type=f32
    )
    grad_scores = (grad_mixing * within).astype(bf16)
    grad_query_blocks = (
        jnp.einsum("nhts,nshe->nthe", grad_scores, key_blocks, preferred_element_type=f32)
        + jnp.einsum("nthf,nhef->nthe", grad_att_blocks, state_low, preferred_element_type=f32)
        * entry[..., None]
    )
    grad_key_blocks = jnp.einsum(
        "nhts,nthe->nshe", grad_scores, query_blocks, preferred_element_type=f32
    )
    grad_value_blocks = jnp.einsum(
        "nhts,nthf->nshf", mixing, grad_att_blocks, preferred_element_type=f32
    )
    direct = jnp.einsum("nthe,nthf->nhef", query_held, grad_att_blocks, preferred_element_type=f32)
    leaving_sum = jnp.sum(arrival[:, :, None, None] * direct, axis=0)
    later = entering((through, leaving_sum), AXIS, chain_states, start_pair, True)[1]
    next_grads = [later]
    grad_increment = jnp.stack(next_grads[::-1]).astype(bf16)
    grad_keys_held = jnp.einsum(
        "nhef,nshf->nshe", grad_increment, value_blocks, preferred_element_type=f32
    )
    grad_key_blocks = grad_key_blocks + grad_keys_held * leaving[..., None]
    grad_value_blocks = grad_value_blocks + jnp.einsum(
        "nshe,nhef->nshf", keys_held, grad_increment, preferred_element_type=f32
    )
    grad_query_pre = (grad_query_blocks.reshape(length, width) * silu_slope(query_pre)).astype(bf16)
    grad_key_pre = (grad_key_blocks.reshape(length, width) * silu_slope(key_pre)).astype(bf16)
    grad_value_pre = grad_value_blocks.reshape(length, width).astype(bf16)
    grad_w_query = jnp.einsum(TD_TE, hidden, grad_query_pre, preferred_element_type=f32)
    grad_w_key = jnp.einsum(TD_TE, hidden, grad_key_pre, preferred_element_type=f32)
    grad_w_value = jnp.einsum(TD_TE, hidden, grad_value_pre, preferred_element_type=f32)
    grad_w_unit = jnp.einsum(TD_TE, hidden, grad_unit_pre, preferred_element_type=f32)
    attention_grads = (
        lax.psum_scatter(grad_w_query, AXIS, scatter_dimension=0, tiled=True),
        lax.psum_scatter(grad_w_key, AXIS, scatter_dimension=0, tiled=True),
        lax.psum_scatter(grad_w_value, AXIS, scatter_dimension=0, tiled=True),
        lax.psum_scatter(grad_w_unit, AXIS, scatter_dimension=0, tiled=True),
        lax.psum_scatter(grad_w_output, AXIS, scatter_dimension=0, tiled=True),
        lax.psum_scatter(grad_gain, AXIS, scatter_dimension=0, tiled=True),
    )
    grad_hidden = (
        jnp.einsum(TE_DE, grad_query_pre, back_query, preferred_element_type=f32)
        + jnp.einsum(TE_DE, grad_key_pre, back_key, preferred_element_type=f32)
        + jnp.einsum(TE_DE, grad_value_pre, back_value, preferred_element_type=f32)
        + jnp.einsum(TE_DE, grad_unit_pre, back_unit, preferred_element_type=f32)
    )
    grad_inputs = grad_middle + first_scale * (
        grad_hidden - normed * jnp.mean(grad_hidden * normed, axis=-1, keepdims=True)
    )
    return (
        result,
        grad_inputs,
        attention_grads[0],
        attention_grads[1],
        attention_grads[2],
        attention_grads[3],
        attention_grads[4],
        attention_grads[5],
        feed_grads[0],
        feed_grads[1],
        feed_grads[2],
    )


def body_kernels(
    tokens,
    lengths,
    seq_order,
    decay_rate,
    w_query,
    w_key,
    w_value,
    w_unit,
    w_output,
    norm_gain,
    w_left,
    w_right,
    w_down,
    cotangent,
):
    full, saved = forward(
        lengths,
        seq_order,
        decay_rate,
        tokens,
        cotangent,
        norm_gain.reshape(1, -1),
        [w_key, w_value, w_query, w_unit, w_output, w_left, w_right, w_down],
    )
    grads, result, grad_inputs = backward(
        lengths, seq_order, decay_rate, tokens, cotangent, saved, full[:4] + full[5:]
    )
    return deliver(result, grad_inputs, grads)


def solution(mesh):
    placed = (
        P(AXIS, None),
        P(),
        P(),
        P(),
        P(AXIS, None),
        P(AXIS, None),
        P(AXIS, None),
        P(AXIS, None),
        P(AXIS, None),
        P(AXIS),
        P(AXIS, None),
        P(AXIS, None),
        P(AXIS, None),
        P(AXIS, None),
    )
    return jax.shard_map(
        body_kernels if mesh.size == 32 else body,
        mesh=mesh,
        in_specs=placed,
        out_specs=(
            P(AXIS, None),
            P(AXIS, None),
            P(AXIS, None),
            P(AXIS, None),
            P(AXIS, None),
            P(AXIS, None),
            P(AXIS, None),
            P(AXIS),
            P(AXIS, None),
            P(AXIS, None),
            P(AXIS, None),
        ),
        check_vma=False,
    )
```
